32 devices in a mesh: dp: 2 (over core), seq: 16 (over z, y, x).
Axes of the slice: x: 2, y: 2, z: 4, core: 2. Of those that a mesh axis runs over, the one named last changes fastest.
Arguments:
- tokens: bfloat16 [32768, 768], P(('dp', 'seq')), may hold values from -6 to 6
- cotangent: bfloat16 [16384, 768], P(('dp', 'seq')), may hold values from -6 to 6
- lengths: int32 [256], replicated, may hold values from 1 to 256, 16384 in all
- w_query: float32 [768, 768], P('seq'), may hold values from -0.4375 to 0.4375
- b_query: float32 [768], P('seq'), may hold values from -3 to 3
- w_key: float32 [768, 768], P('seq'), may hold values from -0.21875 to 0.21875
- w_value: float32 [768, 768], P('seq'), may hold values from -0.21875 to 0.21875
- b_value: float32 [768], P('seq'), may hold values from -3 to 3
- w_output: float32 [768, 768], P('seq'), may hold values from -1.75 to 1.75
- b_output: float32 [768], P('seq'), may hold values from -3 to 3
- gain_attn: float32 [768], P('seq'), may hold values from 0.1 to 1.9
- shift_attn: float32 [768], P('seq'), may hold values from -3 to 3
- w_up: float32 [768, 3072], P('seq'), may hold values from -0.21875 to 0.21875
- b_up: float32 [3072], P('seq'), may hold values from -3 to 3
- w_down: float32 [3072, 768], P('seq'), may hold values from -0.109375 to 0.109375
- b_down: float32 [768], P('seq'), may hold values from -3 to 3
- gain_ffn: float32 [768], P('seq'), may hold values from 0.1 to 1.9
- shift_ffn: float32 [768], P('seq'), may hold values from -3 to 3
- distance_slope: float32 [12], replicated, may hold values from 0.004 to 0.08
Outputs:
- pooled_out: bfloat16 [16384, 768], P(('dp', 'seq'))
- grad_tokens: float32 [32768, 768], P(('dp', 'seq'))
- grad_w_query: float32 [768, 768], P('seq')
- grad_b_query: float32 [768], P('seq')
- grad_w_key: float32 [768, 768], P('seq')
- grad_w_value: float32 [768, 768], P('seq')
- grad_b_value: float32 [768], P('seq')
- grad_w_output: float32 [768, 768], P('seq')
- grad_b_output: float32 [768], P('seq')
- grad_gain_attn: float32 [768], P('seq')
- grad_shift_attn: float32 [768], P('seq')
- grad_w_up: float32 [768, 3072], P('seq')
- grad_b_up: float32 [3072], P('seq')
- grad_w_down: float32 [3072, 768], P('seq')
- grad_b_down: float32 [768], P('seq')
- grad_gain_ffn: float32 [768], P('seq')
- grad_shift_ffn: float32 [768], P('seq')
- grad_distance_slope: float32 [12], replicated
The draws below stay inside these ranges and needn't reach their ends.
Inputs may be any that keep to these rules, and one draw needn't show every extreme that they name: Lengths count token pairs; all 256 lengths sum to 16384, so the rows fill the pack exactly.
All inputs are finite; a program needn't handle non-finite values.
Results may differ from the reference program's by a relative error of at most 0.015.
The reference program's roundings to bfloat16 on the way count: a program that leaves them out, or rounds other values in their place, can miss the bound.
Values may be sent and summed in bfloat16 or wider, within the bound.
No kernel may reach another device: no remote copies, remote signals or barrier semaphores. Data moves between devices by JAX's collectives and lax.ppermute only.
A program may use at most 384 MiB of HBM per device.

```python
import math
import jax
import jax.numpy as jnp
import numpy as np
from jax import lax

D = 768
HEADS = 12
HD = 64
FF = 3072
TOK_DEV = 1024
MOST_PAIRS = 256
TOKENS = 32768
POOLED = 16384
ROWS = 256


def block_levels(rng, extent, shards, least, high):
    def one(dim, shards_of):
        steps = jax.random.uniform(jax.random.fold_in(jax.random.fold_in(rng, 6), dim), (shards_of,), jnp.float32, least / len(shards), high / len(shards))
        return jnp.repeat(jnp.exp(steps), extent[dim] // shards_of).reshape((-1,) + (1,) * (len(extent) - dim - 1))

    level = one(*shards[0])
    for cut in shards[1:]:
        level = level * one(*cut)
    return level


def length_profile(number_of, total, bound, skew):
    weights = [(1 << 20) // math.isqrt(rank ** skew) + 1 for rank in range(2, number_of + 1)]
    rest, given = total - bound - (number_of - 1), [1] * (number_of - 1)
    while rest > 0:
        free = [i for i in range(number_of - 1) if given[i] < bound]
        whole, left = sum([weights[i] for i in free]), rest
        for i in free:
            extra = min(bound - given[i], max(1, left * weights[i] // whole), rest)
            given[i] = given[i] + extra
            rest = rest - extra
    return np.array([bound] + given)


def uneven(own_key, amount, total, bound, slope):
    if amount == 2:
        one = jax.random.randint(own_key, (), max(1, total - bound), min(bound, total - 1) + 1)
        return jnp.stack([one, total - one])
    sizes = jnp.asarray(length_profile(amount, total, bound, slope), jnp.int32)
    twos = (amount - 1) // 2
    source_of, sink = sizes[1:1 + 2 * twos:2], sizes[2:2 + 2 * twos:2]
    margin = jnp.minimum(source_of - 1, bound - sink)
    shifted = jax.random.randint(jax.random.fold_in(own_key, 1), (twos,), 0, 1 << 20) % (margin + 1)
    sizes = sizes.at[1:1 + 2 * twos:2].set(source_of - shifted).at[2:2 + 2 * twos:2].set(sink + shifted)
    return sizes[jax.random.permutation(jax.random.fold_in(own_key, 2), amount)]


def noise(rng, shape, scale, bound, cuts=(), kind=jnp.bfloat16):
    factor_of = block_levels(rng, shape, cuts, -0.22, 0.18) if cuts else 1.0
    values = jax.random.normal(rng, shape, jnp.float32) * scale * factor_of
    return jnp.minimum(jnp.maximum(values, -bound), bound).astype(kind)


def setup_inputs(seed: int = 0) -> dict:
    splits = jax.random.split(jax.random.key(seed), 20)
    tokens = noise(splits[0], (TOKENS, D), 1.0, 6.0, ((0, 32),))
    cotangent = noise(splits[1], (POOLED, D), 1.0, 6.0, ((0, 32),))
    lengths = uneven(splits[2], ROWS, POOLED, MOST_PAIRS, 2).astype(jnp.int32)
    w_query = noise(splits[3], (D, D), (D // 4) ** -0.5, 0.4375, ((0, 16),), jnp.float32)
    b_query = noise(splits[4], (D,), 0.5, 3.0, ((0, 16),), jnp.float32)
    w_key = noise(splits[5], (D, D), D ** -0.5, 0.21875, ((0, 16),), jnp.float32)
    w_value = noise(splits[6], (D, D), D ** -0.5, 0.21875, ((0, 16),), jnp.float32)
    b_value = noise(splits[7], (D,), 0.5, 3.0, ((0, 16),), jnp.float32)
    w_output = noise(splits[8], (D, D), (D // 64) ** -0.5, 1.75, ((0, 16),), jnp.float32)
    b_output = noise(splits[9], (D,), 0.5, 3.0, ((0, 16),), jnp.float32)
    gain_attn = jnp.clip(1.0 + 0.18 * jax.random.normal(splits[10], (D,), jnp.float32), 0.1, 1.9)
    shift_attn = noise(splits[11], (D,), 0.5, 3.0, ((0, 16),), jnp.float32)
    w_up = noise(splits[12], (D, FF), D ** -0.5, 0.21875, ((0, 16),), jnp.float32)
    b_up = noise(splits[13], (FF,), 0.5, 3.0, ((0, 16),), jnp.float32)
    w_down = noise(splits[14], (FF, D), FF ** -0.5, 0.109375, ((0, 16),), jnp.float32)
    b_down = noise(splits[15], (D,), 0.5, 3.0, ((0, 16),), jnp.float32)
    gain_ffn = jnp.clip(1.0 + 0.18 * jax.random.normal(splits[16], (D,), jnp.float32), 0.1, 1.9)
    shift_ffn = noise(splits[17], (D,), 0.5, 3.0, ((0, 16),), jnp.float32)
    distance_slope = jnp.clip(jnp.exp(jax.random.uniform(splits[18], (HEADS,), jnp.float32, math.log(0.004), math.log(0.08))), 0.004, 0.08)
    return dict(tokens=tokens, cotangent=cotangent, lengths=lengths, w_query=w_query, b_query=b_query, w_key=w_key, w_value=w_value, b_value=b_value, w_output=w_output, b_output=b_output, gain_attn=gain_attn, shift_attn=shift_attn, w_up=w_up, b_up=b_up, w_down=w_down, b_down=b_down, gain_ffn=gain_ffn, shift_ffn=shift_ffn, distance_slope=distance_slope)


@jax.custom_vjp
def low(v):
    return lax.optimization_barrier(v.astype(jnp.bfloat16)).astype(jnp.float32)

@jax.custom_vjp
def low_back(v):
    return v

def low_keep(v):
    return (low(v), None)

def low_pass(kept, grad):
    return (grad,)

def back_keep(v):
    return (v, None)

def back_low(kept, grad):
    return (low(grad),)
low.defvjp(low_keep, low_pass)
low_back.defvjp(back_keep, back_low)
epsilon = 1e-05

def product(left, right):
    return jnp.dot(left, right, precision=lax.Precision.HIGHEST, preferred_element_type=jnp.float32)

def layer_norm(inputs, gain, shift):
    average = lax.optimization_barrier(jnp.mean(inputs, -1, keepdims=True))
    centred = inputs - average
    spread = lax.optimization_barrier(jnp.mean(centred * centred, -1, keepdims=True))
    return centred * lax.rsqrt(spread + epsilon) * gain + shift

def reference(tokens, cotangent, lengths, w_query, b_query, w_key, w_value, b_value, w_output, b_output, gain_attn, shift_attn, w_up, b_up, w_down, b_down, gain_ffn, shift_ffn, distance_slope):
    score_scale = HD ** (-0.5)
    pooled_rows = TOK_DEV // 2
    block_count = TOKENS // TOK_DEV
    global_rows = jnp.arange(TOKENS, dtype=jnp.int32)
    starts = (2 * (jnp.cumsum(lengths) - lengths)).astype(jnp.int32)
    before = starts[None, :] <= global_rows[:, None]
    row_of = lax.optimization_barrier(jnp.sum(before.astype(jnp.int32), 1)) - 1
    begin = lax.optimization_barrier(jnp.max(jnp.where(before, starts[None, :], 0), 1))
    place = (global_rows - begin).astype(jnp.float32)
    key_row = jnp.pad(row_of, (TOK_DEV, TOK_DEV), constant_values=-2)
    key_place = jnp.pad(place, (TOK_DEV, TOK_DEV))
    query_row = row_of[0::2]
    query_place = place[0::2] + 0.5

    def forward(params, tok_float):
        query_mat, query_bias, key_mat, value_mat, value_bias, output_mat, output_bias, attn_gain, attn_shift, up_mat, up_bias, down_mat, down_bias, ffn_gain, ffn_shift = [low(item) for item in params[:15]]
        slope_vec = params[15]
        pooled_in = lax.optimization_barrier(jnp.sum(tok_float.reshape(TOKENS // 2, 2, D), 1)) * 0.5
        query_all = low(low_back(product(low(pooled_in), query_mat) + query_bias))
        key_all = low(low_back(product(tok_float, key_mat)))
        value_all = low(low_back(product(tok_float, value_mat) + value_bias))
        key_pad = jnp.pad(key_all, ((TOK_DEV, TOK_DEV), (0, 0)))
        value_pad = jnp.pad(value_all, ((TOK_DEV, TOK_DEV), (0, 0)))

        def attend_block(block_index):
            q_part = lax.dynamic_slice_in_dim(query_all, block_index * pooled_rows, pooled_rows, 0).reshape(pooled_rows, HEADS, HD)
            k_part = lax.dynamic_slice_in_dim(key_pad, block_index * TOK_DEV, 3 * TOK_DEV, 0).reshape(3 * TOK_DEV, HEADS, HD)
            v_part = lax.dynamic_slice_in_dim(value_pad, block_index * TOK_DEV, 3 * TOK_DEV, 0).reshape(3 * TOK_DEV, HEADS, HD)
            rows_q = lax.dynamic_slice_in_dim(query_row, block_index * pooled_rows, pooled_rows, 0)
            places_q = lax.dynamic_slice_in_dim(query_place, block_index * pooled_rows, pooled_rows, 0)
            rows_k = lax.dynamic_slice_in_dim(key_row, block_index * TOK_DEV, 3 * TOK_DEV, 0)
            places_k = lax.dynamic_slice_in_dim(key_place, block_index * TOK_DEV, 3 * TOK_DEV, 0)
            same_row = rows_q[:, None] == rows_k[None, :]
            distance = jnp.abs(places_q[:, None] - places_k[None, :])
            raw_scores = jnp.einsum('qhd,khd->hqk', q_part, k_part, precision=lax.Precision.HIGHEST) * score_scale
            biased = raw_scores - slope_vec[:, None, None] * distance[None]
            masked = low_back(jnp.where(same_row[None], biased, -1000000000.0))
            highest = lax.optimization_barrier(jnp.max(masked, -1, keepdims=True))
            exponent = jnp.exp(masked - highest)
            probability = low(exponent / lax.optimization_barrier(jnp.sum(exponent, -1, keepdims=True)))
            mixed_heads = jnp.einsum('hqk,khd->qhd', probability, v_part, precision=lax.Precision.HIGHEST)
            return mixed_heads.reshape(pooled_rows, D)
        attended = lax.map(jax.checkpoint(attend_block), jnp.arange(block_count, dtype=jnp.int32))
        attended = low(low_back(attended.reshape(TOKENS // 2, D)))
        branch = low_back(product(attended, output_mat) + output_bias)
        hidden = layer_norm(pooled_in + branch, attn_gain, attn_shift)
        inner_act = low_back(product(low(hidden), up_mat) + up_bias)
        ffn_out = low_back(product(low(jax.nn.gelu(inner_act)), down_mat) + down_bias)
        return layer_norm(hidden + ffn_out, ffn_gain, ffn_shift)
    params = (w_query, b_query, w_key, w_value, b_value, w_output, b_output, gain_attn, shift_attn, w_up, b_up, w_down, b_down, gain_ffn, shift_ffn, distance_slope)
    result, backward = jax.vjp(forward, params, tokens.astype(jnp.float32))
    grad_params, grad_input = backward(cotangent.astype(jnp.float32))
    return (result.astype(jnp.bfloat16), grad_input, grad_params[0], grad_params[1], grad_params[2], grad_params[3], grad_params[4], grad_params[5], grad_params[6], grad_params[7], grad_params[8], grad_params[9], grad_params[10], grad_params[11], grad_params[12], grad_params[13], grad_params[14], grad_params[15])
```

```python
import jax
import jax.numpy as jnp
from jax import lax
from jax.experimental import pallas as pl
from jax.experimental.pallas import tpu as pltpu
from jax.sharding import PartitionSpec as P

HD = 64
NB = 16
QB = 128
KC = 256
EPS = 1e-05
FAR = 1e12
BF = jnp.bfloat16
FL = jnp.float32


def rel_a(p):
    return (p & 1) * 8 + ((p >> 1) & 1) * 4 + ((p >> 2) & 1) * 2 + ((p >> 3) & 1)


def rel_b(p):
    return (p & 1) * 8 + ((p >> 1) & 1) * 4 + ((p >> 2) & 1) + ((p >> 3) & 1) * 2


def dot(a, b):
    return jnp.dot(a, b, preferred_element_type=FL)


def dot_t(a, b):
    return lax.dot_general(a, b, (((1,), (1,)), ((), ())), preferred_element_type=FL)


def t_dot(a, b):
    return lax.dot_general(a, b, (((0,), (0,)), ((), ())), preferred_element_type=FL)


def exchange(x, stride_a, stride_b):
    n = lax.axis_size("seq")
    pairs = [(s, s ^ stride_a) for s in range(n)] + [(n + s, n + (s ^ stride_b)) for s in range(n)]
    return lax.ppermute(x, ("dp", "seq"), pairs)


def swap_core(x):
    return lax.ppermute(x, "dp", [(0, 1), (1, 0)])


def gather_set(x):
    x = jnp.concatenate([x, exchange(x, 8, 8)], 0)
    x = jnp.concatenate([x, exchange(x, 4, 4)], 0)
    low = jnp.concatenate([x, exchange(x, 2, 1)], 0)
    high = exchange(low, 1, 2)
    return low, high, swap_core(low), swap_core(high)


def add(*xs):
    total = xs[0].astype(FL)
    for x in xs[1:]:
        total = total + x.astype(FL)
    return total


def reduce_set(keep, send):
    got = swap_core(send)
    up = add(keep[8:], got[8:]).astype(BF)
    got1 = exchange(up, 1, 2)
    up = add(keep[4:8], got[4:8], got1[4:]).astype(BF)
    low = add(keep[:4], got[:4], got1[:4])
    got2 = exchange(up, 2, 1)
    up = (low[2:] + got2[2:].astype(FL)).astype(BF)
    low = low[:2] + got2[:2].astype(FL)
    got3 = exchange(up, 4, 4)
    up = (low[1:] + got3[1:].astype(FL)).astype(BF)
    low = low[:1] + got3[:1].astype(FL)
    got4 = exchange(up, 8, 8)
    mine = (low + got4.astype(FL))[0]
    other = swap_core(mine)
    first = lax.axis_index("dp") == 0
    return jnp.where(first, mine, other), jnp.where(first, other, mine)


def params(**kw):
    return pltpu.CompilerParams(vmem_limit_bytes=58 * 1024 * 1024, **kw)


ANY = pl.BlockSpec(memory_space=pl.ANY)


def load_sets(ids, low, high, olow, ohigh, copies_a, copies_b):
    def start(a_refs, b_refs):
        for p in range(NB):
            copies_a(a_refs[p // 8].at[p % 8], ids[0] ^ rel_a(p), p)
            copies_b(b_refs[p // 8].at[p % 8], ids[0] ^ rel_b(p), p)

    @pl.when(ids[1] == 0)
    def _():
        start((low, high), (olow, ohigh))

    @pl.when(ids[1] != 0)
    def _():
        start((olow, ohigh), (low, high))


def wait_all(ref, sem):
    pltpu.make_async_copy(ref, ref, sem).wait()


def spread_matrix(rows, cols, rb):
    lanes = lax.broadcasted_iota(jnp.int32, (rows, cols), 1)
    return (lax.broadcasted_iota(jnp.int32, (rows, cols), 0) == lanes - rb * div_rb(lanes)).astype(FL).astype(BF)


def div_rb(x):
    return (x * 21846) >> 20


def qkv_kernel(
    ids, tok, low, high, olow, ohigh, q_out, k_out, v_out, pool_out, wq, wk, wv, vec_out, up_out, bias, x32, sems
):
    width = tok.shape[1]
    rb = width // NB

    @pl.when(pl.program_id(0) == 0)
    def _():
        def rows(r, n):
            return pl.ds(pl.multiple_of(r, 16), n)

        def copies_a(block, s, p):
            pltpu.make_async_copy(block.at[pl.ds(0, 48)], wq.at[rows(s * rb, 48)], sems.at[0]).start()
            pltpu.make_async_copy(block.at[pl.ds(48, 32)], wk.at[rows(s * rb, 32)], sems.at[1]).start()

        def copies_b(block, s, p):
            pltpu.make_async_copy(block.at[pl.ds(0, 16)], wk.at[rows(s * rb + 32, 16)], sems.at[1]).start()
            pltpu.make_async_copy(block.at[pl.ds(16, 48)], wv.at[rows(s * rb, 48)], sems.at[2]).start()
            pltpu.make_async_copy(block.at[pl.ds(64, 16)], bias.at[pl.ds(16 * p, 16)], sems.at[3]).start()

        load_sets(ids, low, high, olow, ohigh, copies_a, copies_b)
        wait_all(wq, sems.at[0])
        wait_all(wk, sems.at[1])
        wait_all(wv, sems.at[2])
        wait_all(bias, sems.at[3])
        parts = bias[:, 0:128]
        wide = dot(parts, spread_matrix(128, width, rb))
        block_of = div_rb(lax.broadcasted_iota(jnp.int32, (16, width), 1))
        total = jnp.zeros((16, width), FL)
        for p in range(NB):
            total = total + jnp.where(block_of == (ids[0] ^ rel_b(p)), wide[16 * p : 16 * p + 16], 0.0)
        vec_out[...] = total
        ff = up_out.shape[1]
        wide = dot(parts, spread_matrix(128, ff, rb))
        block_of = div_rb(lax.broadcasted_iota(jnp.int32, (16, ff), 1))
        row = lax.broadcasted_iota(jnp.int32, (16, ff), 0)
        block_of = jnp.where((row >= 8) & (row < 12), block_of - row + 8, -1)
        total = jnp.zeros((16, ff), FL)
        for p in range(NB):
            total = total + jnp.where(block_of == 4 * (ids[0] ^ rel_b(p)), wide[16 * p : 16 * p + 16], 0.0)
        up_out[...] = jnp.broadcast_to(jnp.sum(total, 0, keepdims=True), up_out.shape)

    x = tok[...]
    half = x.shape[0] // 2
    k_out[...] = dot(x, wk[...]).astype(BF)
    v_out[...] = (dot(x, wv[...]) + vec_out[1:2]).astype(BF)
    for j in range(width // 128):
        cols = slice(128 * j, 128 * j + 128)
        x32[j] = x[:, cols].astype(FL)
        pool_out[:, cols] = (x32[j, pl.ds(0, half, stride=2)] + x32[j, pl.ds(1, half, stride=2)]) * 0.5
    q = (dot(pool_out[...].astype(BF), wq[...]) + vec_out[0:1]).astype(BF)
    q_out[...] = (q.astype(FL) * HD**-0.5).astype(BF)


def qkv(ids, tok_ext, sets, ff):
    rows, width = tok_ext.shape
    step = 512
    whole = lambda i, *_: (0, 0)
    return pl.pallas_call(
        qkv_kernel,
        name="qkv",
        grid_spec=pltpu.PrefetchScalarGridSpec(
            num_scalar_prefetch=1,
            grid=(rows // step,),
            in_specs=[pl.BlockSpec((step, width), lambda i, *_: (i, 0)), ANY, ANY, ANY, ANY],
            out_specs=[
                pl.BlockSpec((step // 2, width), lambda i, *_: (i, 0)),
                pl.BlockSpec((step, width), lambda i, *_: (i, 0)),
                pl.BlockSpec((step, width), lambda i, *_: (i, 0)),
                pl.BlockSpec((step // 2, width), lambda i, *_: (i, 0)),
                pl.BlockSpec((width, width), whole),
                pl.BlockSpec((width, width), whole),
                pl.BlockSpec((width, width), whole),
                pl.BlockSpec((16, width), whole),
                pl.BlockSpec((8, ff), whole),
            ],
            scratch_shapes=[
                pltpu.VMEM((16 * NB, width), BF),
                pltpu.VMEM((width // 128, step, 128), FL),
                pltpu.SemaphoreType.DMA((4,)),
            ],
        ),
        out_shape=[
            jax.ShapeDtypeStruct((rows // 2, width), BF),
            jax.ShapeDtypeStruct((rows, width), BF),
            jax.ShapeDtypeStruct((rows, width), BF),
            jax.ShapeDtypeStruct((rows // 2, width), FL),
            jax.ShapeDtypeStruct((width, width), BF),
            jax.ShapeDtypeStruct((width, width), BF),
            jax.ShapeDtypeStruct((width, width), BF),
            jax.ShapeDtypeStruct((16, width), FL),
            jax.ShapeDtypeStruct((8, ff), FL),
        ],
        compiler_params=params(),
    )(ids, tok_ext, *sets)


def two_heads(x):
    lane = lax.broadcasted_iota(jnp.int32, x.shape, 1)
    zero = jnp.zeros_like(x)
    return jnp.concatenate([jnp.where(lane < HD, x, zero), jnp.where(lane < HD, zero, x)], 0)


def one_block(x):
    r = x.shape[0] // 2
    lane = lax.broadcasted_iota(jnp.int32, (r, 128), 1)
    return jnp.where(lane < HD, x[:r], x[r:])


def distances(bounds, row, c):
    low = bounds[pl.ds(row, QB), 0:1]
    high = bounds[pl.ds(row, QB), 1:2]
    query = (2 * (row + lax.broadcasted_iota(jnp.int32, (QB, KC), 0))).astype(FL) + 0.5
    key = (c * KC + lax.broadcasted_iota(jnp.int32, (QB, KC), 1)).astype(FL)
    return jnp.where((key >= low) & (key < high), jnp.abs(query - key), FAR)


def twice(x):
    return jnp.concatenate([x, x], 1)


def forward_kernel(spans, slopes, q, k, v, bounds, o_out, exact_out, lse_out, s_scr, q2, top, total, acc, rest):
    pairs = q.shape[1] // 128
    head0 = pl.program_id(0) * 2 * pairs
    lane = lax.broadcasted_iota(jnp.int32, (QB, 128), 1)
    q_first = q.shape[0] // 4

    def query_block(b, _):
        row = pl.multiple_of(q_first + b * QB, QB)
        out_rows = pl.ds(pl.multiple_of(b * QB, QB), QB)
        block = row // QB
        c0 = spans[block]
        c1 = spans[spans.shape[0] // 2 + block]
        for j in range(pairs):
            q2[j] = two_heads(q[pl.ds(row, QB), 128 * j : 128 * j + 128])
        top[...] = jnp.full(top.shape, -3e38, FL)
        total[...] = jnp.zeros(total.shape, FL)
        acc[...] = jnp.zeros(acc.shape, FL)
        rest[...] = jnp.zeros(rest.shape, FL)

        def score(c, _):
            far = distances(bounds, row, c)
            keys = pl.ds(pl.multiple_of(c * KC, KC), KC)
            for j in range(pairs):
                s = dot_t(q2[j], k[keys, 128 * j : 128 * j + 128])
                s = jnp.concatenate(
                    [s[:QB] - slopes[head0 + 2 * j] * far, s[QB:] - slopes[head0 + 2 * j + 1] * far], 0
                )
                s_scr[c - c0, j] = s
                top[j] = jnp.maximum(top[j], jnp.maximum(s[:, :128], s[:, 128:]))
            return 0

        lax.fori_loop(c0, c1, score, 0)
        for j in range(pairs):
            top[j] = jnp.broadcast_to(jnp.max(top[j], 1, keepdims=True), (2 * QB, 128))

        def exponent(c, _):
            for j in range(pairs):
                e = jnp.exp(s_scr[c - c0, j] - twice(top[j]))
                s_scr[c - c0, j] = e
                total[j] = total[j] + (e[:, :128] + e[:, 128:])
            return 0

        lax.fori_loop(c0, c1, exponent, 0)
        lse = jnp.zeros((QB, 128), FL)
        for j in range(pairs):
            l = jnp.broadcast_to(jnp.sum(total[j], 1, keepdims=True), (2 * QB, 128))
            t = top[j] + jnp.log(l)
            total[j] = 1.0 / l
            lse = jnp.where(lane == 2 * j, t[:QB], jnp.where(lane == 2 * j + 1, t[QB:], lse))
        lse_out[out_rows, :] = lse

        def attend(c, _):
            keys = pl.ds(pl.multiple_of(c * KC, KC), KC)
            for j in range(pairs):
                p = s_scr[c - c0, j] * twice(total[j])
                high = p.astype(BF)
                low = (p - high.astype(FL)).astype(BF)
                values = v[keys, 128 * j : 128 * j + 128]
                acc[j] = acc[j] + dot(high, values)
                rest[j] = rest[j] + dot(low, values)
            return 0

        lax.fori_loop(c0, c1, attend, 0)
        for j in range(pairs):
            cols = slice(128 * j, 128 * j + 128)
            o_out[out_rows, cols] = one_block(acc[j]).astype(BF)
            exact_out[out_rows, cols] = one_block(acc[j] + rest[j])
        return 0

    lax.fori_loop(0, o_out.shape[0] // QB, query_block, 0)


def attend_forward(spans, slopes, q, k, v, bounds, own):
    width = q.shape[1]
    wide = width // 2
    pairs = wide // 128
    chunks = k.shape[0] // KC
    col = lambda i, *_: (0, i)
    return pl.pallas_call(
        forward_kernel,
        name="attend_forward",
        grid_spec=pltpu.PrefetchScalarGridSpec(
            num_scalar_prefetch=2,
            grid=(2,),
            in_specs=[
                pl.BlockSpec((q.shape[0], wide), col),
                pl.BlockSpec((k.shape[0], wide), col),
                pl.BlockSpec((k.shape[0], wide), col),
                pl.BlockSpec(bounds.shape, lambda i, *_: (0, 0)),
            ],
            out_specs=[
                pl.BlockSpec((own, wide), col),
                pl.BlockSpec((own, wide), col),
                pl.BlockSpec((own, 128), col),
            ],
            scratch_shapes=[
                pltpu.VMEM((chunks, pairs, 2 * QB, KC), FL),
                pltpu.VMEM((pairs, 2 * QB, 128), BF),
                pltpu.VMEM((pairs, 2 * QB, 128), FL),
                pltpu.VMEM((pairs, 2 * QB, 128), FL),
                pltpu.VMEM((pairs, 2 * QB, 128), FL),
                pltpu.VMEM((pairs, 2 * QB, 128), FL),
            ],
        ),
        out_shape=[
            jax.ShapeDtypeStruct((own, width), BF),
            jax.ShapeDtypeStruct((own, width), FL),
            jax.ShapeDtypeStruct((own, 256), FL),
        ],
        compiler_params=params(),
    )(spans, slopes, q, k, v, bounds)


def backward_kernel(
    spans, slopes, q, k, v, da, stats, bounds, dq_out, dk_out, dv_out, slope_out, q2, da2, lse2, del2, dq2, dk, dv, sl
):
    pairs = q.shape[1] // 128
    head0 = pl.program_id(0) * 2 * pairs
    blocks = q.shape[0] // QB
    dk[...] = jnp.zeros(dk.shape, FL)
    dv[...] = jnp.zeros(dv.shape, FL)
    sl[...] = jnp.zeros(sl.shape, FL)

    def query_block(b, _):
        row = pl.multiple_of(b * QB, QB)
        c0 = spans[b]
        c1 = spans[blocks + b]
        own = (b >= blocks // 4) & (b < blocks - blocks // 4)
        counted = jnp.where(own, 1.0, 0.0)
        for j in range(pairs):
            cols = slice(128 * j, 128 * j + 128)
            q2[j] = two_heads(q[pl.ds(row, QB), cols])
            da2[j] = two_heads(da[pl.ds(row, QB), cols])
            for i in range(2):
                rows = slice(QB * i, QB * i + QB)
                lse2[j, rows] = jnp.broadcast_to(stats[pl.ds(row, QB), 2 * j + i : 2 * j + i + 1], (QB, 128))
                del2[j, rows] = jnp.broadcast_to(stats[pl.ds(row, QB), 64 + 2 * j + i : 65 + 2 * j + i], (QB, 128))
        dq2[...] = jnp.zeros(dq2.shape, FL)

        def chunk(c, _):
            far = distances(bounds, row, c)
            keys = pl.ds(pl.multiple_of(c * KC, KC), KC)
            for j in range(pairs):
                cols = slice(128 * j, 128 * j + 128)
                kj = k[keys, cols]
                s = dot_t(q2[j], kj)
                s = jnp.concatenate(
                    [s[:QB] - slopes[head0 + 2 * j] * far, s[QB:] - slopes[head0 + 2 * j + 1] * far], 0
                )
                p = jnp.exp(s - twice(lse2[j]))
                dp = dot_t(da2[j], v[keys, cols])
                ds = (p * (dp - twice(del2[j]))).astype(BF)
                dv[keys, cols] = dv[keys, cols] + t_dot(p.astype(BF), da2[j])
                dk[keys, cols] = dk[keys, cols] + t_dot(ds, q2[j])
                dq2[j] = dq2[j] + dot(ds, kj)
                for i in range(2):
                    w = ds[QB * i : QB * i + QB].astype(FL) * far
                    w = jnp.sum(w.reshape(QB // 8, 8, KC), 0)
                    sl[2 * j + i] = sl[2 * j + i] + counted * (w[:, :128] + w[:, 128:])
            return 0

        lax.fori_loop(c0, c1, chunk, 0)

        @pl.when(own)
        def _():
            out_rows = pl.ds(pl.multiple_of(row - q.shape[0] // 4, QB), QB)
            for j in range(pairs):
                dq_out[out_rows, 128 * j : 128 * j + 128] = (one_block(dq2[j]) * HD**-0.5).astype(BF)

        return 0

    lax.fori_loop(0, blocks, query_block, 0)
    quarter = k.shape[0] // 4
    dk_out[...] = dk[quarter : 3 * quarter].astype(BF)
    dv_out[...] = dv[quarter : 3 * quarter].astype(BF)
    slope_out[...] = sl[...].reshape(slope_out.shape)


def attend_backward(spans, slopes, q, k, v, da, stats, bounds):
    width = q.shape[1]
    wide = width // 2
    pairs = wide // 128
    rows = q.shape[0]
    keys = k.shape[0]
    col = lambda i, *_: (0, i)
    return pl.pallas_call(
        backward_kernel,
        name="attend_backward",
        grid_spec=pltpu.PrefetchScalarGridSpec(
            num_scalar_prefetch=2,
            grid=(2,),
            in_specs=[
                pl.BlockSpec((rows, wide), col),
                pl.BlockSpec((keys, wide), col),
                pl.BlockSpec((keys, wide), col),
                pl.BlockSpec((rows, wide), col),
                pl.BlockSpec((rows, 128), col),
                pl.BlockSpec(bounds.shape, lambda i, *_: (0, 0)),
            ],
            out_specs=[
                pl.BlockSpec((rows // 2, wide), col),
                pl.BlockSpec((keys // 2, wide), col),
                pl.BlockSpec((keys // 2, wide), col),
                pl.BlockSpec((16 * pairs, 128), lambda i, *_: (i, 0)),
            ],
            scratch_shapes=[
                pltpu.VMEM((pairs, 2 * QB, 128), BF),
                pltpu.VMEM((pairs, 2 * QB, 128), BF),
                pltpu.VMEM((pairs, 2 * QB, 128), FL),
                pltpu.VMEM((pairs, 2 * QB, 128), FL),
                pltpu.VMEM((pairs, 2 * QB, 128), FL),
                pltpu.VMEM((keys, wide), FL),
                pltpu.VMEM((keys, wide), FL),
                pltpu.VMEM((2 * pairs, 8, 128), FL),
            ],
        ),
        out_shape=[
            jax.ShapeDtypeStruct((rows // 2, width), BF),
            jax.ShapeDtypeStruct((keys // 2, width), BF),
            jax.ShapeDtypeStruct((keys // 2, width), BF),
            jax.ShapeDtypeStruct((32 * pairs, 128), FL),
        ],
        compiler_params=params(),
    )(spans, slopes, q, k, v, da, stats, bounds)


def normalize(z):
    centred = z - jnp.mean(z, -1, keepdims=True)
    scale = lax.rsqrt(jnp.mean(centred * centred, -1, keepdims=True) + EPS)
    return centred * scale, scale


def normalize_back(d, unit, scale):
    return scale * (d - jnp.mean(d, -1, keepdims=True) - unit * jnp.mean(d * unit, -1, keepdims=True))


def rows_sum(x):
    return jnp.sum(x, 0, keepdims=True)


def middle_kernel(
    ids,
    pool,
    att,
    exact,
    lse,
    cot,
    vec,
    upb,
    low,
    high,
    olow,
    ohigh,
    out,
    pay,
    stats,
    mixed,
    gvec,
    gup,
    keep,
    send,
    wo,
    w1,
    w2,
    active,
    slope,
    unit1,
    hid,
    hid_low,
    z,
    d2,
    dw1,
    dw2,
    dwo,
    sems,
):
    n, width = att.shape
    rb = width // NB
    fb = w2.shape[0] // NB
    parts = w1.shape[0]

    def rows(r, size):
        return pl.ds(pl.multiple_of(r, 16), size)

    def copies_a(block, s, p):
        pltpu.make_async_copy(block.at[pl.ds(192, 32)], wo.at[rows(s * rb, 32)], sems.at[0]).start()
        pltpu.make_async_copy(block.at[pl.ds(0, 192)], w2.at[rows(s * fb, 192)], sems.at[2]).start()

    def copies_b(block, s, p):
        pltpu.make_async_copy(block.at[pl.ds(192, 16)], wo.at[rows(s * rb + 32, 16)], sems.at[0]).start()
        for c in range(parts):
            pltpu.make_async_copy(block.at[pl.ds(48 * c, 48)], w1.at[c, rows(s * rb, 48)], sems.at[1]).start()

    load_sets(ids, low, high, olow, ohigh, copies_a, copies_b)
    wait_all(wo, sems.at[0])
    z[...] = dot(att[...], wo[...])
    rc = 128

    def row_loop(f):
        def body(i, _):
            f(pl.ds(pl.multiple_of(i * rc, rc), rc), i)
            return 0

        lax.fori_loop(0, n // rc, body, 0)

    def first_norm(r, i):
        unit, scale = normalize(pool[r, :] + z[r, :] + vec[2:3])
        h = unit * vec[3:4] + vec[4:5]
        unit1[r, :] = unit
        d2[r, 0:128] = jnp.broadcast_to(scale, (rc, 128))
        hid[r, :] = h
        hid_low[r, :] = h.astype(BF)

    row_loop(first_norm)
    wait_all(w1, sems.at[1])
    wait_all(w2, sems.at[2])
    c0 = 0.7978845608028654

    def up(c, _):
        inner = dot(hid_low[...], w1[c]) + upb[pl.ds(0, 1), pl.ds(pl.multiple_of(c * width, 128), width)]
        sq = inner * inner
        t = jnp.tanh(c0 * (inner + 0.044715 * (inner * sq)))
        cdf = 0.5 * (1.0 + t)
        active[c] = (inner * cdf).astype(BF)
        slope[c] = cdf + inner * (0.5 * (1.0 - t * t)) * (c0 + (3 * 0.044715 * c0) * sq)
        return 0

    lax.fori_loop(0, parts, up, 0)
    z[...] = dot(active[0], w2[pl.ds(0, width), :])
    for c in range(1, parts):
        z[...] = z[...] + dot(active[c], w2[pl.ds(c * width, width), :])
    gvec[...] = jnp.zeros(gvec.shape, FL)

    def second_norm(r, i):
        unit, scale = normalize(hid[r, :] + (z[r, :] + vec[5:6]))
        out[r, :] = (unit * vec[6:7] + vec[7:8]).astype(BF)
        dy = cot[r, :].astype(FL)
        gvec[6:7] = gvec[6:7] + rows_sum(dy * unit)
        gvec[7:8] = gvec[7:8] + rows_sum(dy)
        d = normalize_back(dy * vec[6:7], unit, scale)
        hid[r, :] = d
        d_low = d.astype(BF)
        att_like[r, :] = d_low
        gvec[5:6] = gvec[5:6] + rows_sum(d_low.astype(FL))

    att_like = pay.at[:, 0:width]
    scale1 = d2[:, 0:1]
    row_loop(second_norm)
    z[...] = jnp.zeros(z.shape, FL)

    def down(c, _):
        ffn = pay[:, 0:width]
        far = pl.ds(pl.multiple_of(c * width, 128), width)
        d_inner = (dot_t(ffn, w2[far, :]) * slope[c]).astype(BF)
        gup[:, far] = jnp.broadcast_to(rows_sum(d_inner.astype(FL)), (8, width))
        dw2[far, :] = t_dot(active[c], ffn).astype(BF)
        dw1[c] = t_dot(hid_low[...], d_inner).astype(BF)
        z[...] = z[...] + dot_t(d_inner, w1[c])
        return 0

    lax.fori_loop(0, parts, down, 0)

    def store_sets(a_ref, b_ref):
        for p in range(NB):
            s = ids[0] ^ rel_a(p)
            pltpu.make_async_copy(dw2.at[rows(s * fb, 192)], a_ref.at[p, pl.ds(0, 192)], sems.at[3]).start()
            s = ids[0] ^ rel_b(p)
            for c in range(parts):
                pltpu.make_async_copy(
                    dw1.at[c, rows(s * rb, 48)], b_ref.at[p, pl.ds(48 * c, 48)], sems.at[3]
                ).start()

    @pl.when(ids[1] == 0)
    def _():
        store_sets(keep, send)

    @pl.when(ids[1] != 0)
    def _():
        store_sets(send, keep)

    def first_back(r, i):
        unit = unit1[r, :]
        d = hid[r, :] + z[r, :]
        gvec[3:4] = gvec[3:4] + rows_sum(d * unit)
        gvec[4:5] = gvec[4:5] + rows_sum(d)
        d = normalize_back(d * vec[3:4], unit, d2[r, 0:1])
        mixed[r, :] = d
        d_low = d.astype(BF)
        hid_low[r, :] = d_low
        gvec[2:3] = gvec[2:3] + rows_sum(d_low.astype(FL))

    row_loop(first_back)
    dwo[...] = t_dot(att[...], hid_low[...]).astype(BF)

    def store_wo(a_ref, b_ref):
        for p in range(NB):
            s = ids[0] ^ rel_a(p)
            pltpu.make_async_copy(dwo.at[rows(s * rb, 32)], a_ref.at[p, pl.ds(192, 32)], sems.at[3]).start()
            s = ids[0] ^ rel_b(p)
            pltpu.make_async_copy(dwo.at[rows(s * rb + 32, 16)], b_ref.at[p, pl.ds(192, 16)], sems.at[3]).start()
            pltpu.make_async_copy(dwo.at[rows(s * rb + 32, 16)], b_ref.at[p, pl.ds(208, 16)], sems.at[3]).start()

    @pl.when(ids[1] == 0)
    def _():
        store_wo(keep, send)

    @pl.when(ids[1] != 0)
    def _():
        store_wo(send, keep)

    z[...] = dot_t(hid_low[...], wo[...])
    heads = width // HD
    head_of = (lax.broadcasted_iota(jnp.int32, (width, 256), 0)) // HD
    spot = lax.broadcasted_iota(jnp.int32, (width, 256), 1)
    half = heads // 2
    spot_of = jnp.where(head_of < half, head_of + 64, head_of - half + 128 + 64)
    pick = (spot == spot_of).astype(FL).astype(BF)

    def last(r, i):
        d_low = z[r, :].astype(BF)
        prod = d_low.astype(FL) * exact[r, :]
        delta = jnp.zeros((rc, 256), FL)
        for _ in range(3):
            piece = prod.astype(BF)
            delta = delta + dot(piece, pick)
            prod = prod - piece.astype(FL)
        st = jnp.where(lax.broadcasted_iota(jnp.int32, (rc, 256), 1) % 128 < 64, lse[r, :], delta)
        stats[r, :] = st
        pay[r, 0:width] = d_low
        for j in range(3):
            piece = st.astype(BF)
            pay[r, width + 256 * j : width + 256 * j + 256] = piece
            st = st - piece.astype(FL)

    row_loop(last)
    wait_all(keep, sems.at[3])
    wait_all(send, sems.at[3])


def middle(ids, pool, att, exact, lse, cot, vec, upb, sets, set_rows):
    n, width = att.shape
    ff = upb.shape[1]
    parts = ff // width
    whole = lambda i, *_: (0, 0)
    full = lambda x: pl.BlockSpec(x.shape, whole)
    shapes = [
        jax.ShapeDtypeStruct((n, width), BF),
        jax.ShapeDtypeStruct((n, width + 768), BF),
        jax.ShapeDtypeStruct((n, 256), FL),
        jax.ShapeDtypeStruct((n, width), FL),
        jax.ShapeDtypeStruct((8, width), FL),
        jax.ShapeDtypeStruct((8, ff), FL),
    ]
    big = jax.ShapeDtypeStruct((NB, set_rows, width), BF)
    return pl.pallas_call(
        middle_kernel,
        name="middle",
        grid_spec=pltpu.PrefetchScalarGridSpec(
            num_scalar_prefetch=1,
            grid=(1,),
            in_specs=[full(pool)]
            + [full(x) for x in (att, exact, lse, cot, vec, upb)]
            + [ANY] * 4,
            out_specs=[full(x) for x in shapes] + [ANY, ANY],
            scratch_shapes=[
                pltpu.VMEM((width, width), BF),
                pltpu.VMEM((parts, width, width), BF),
                pltpu.VMEM((ff, width), BF),
                pltpu.VMEM((parts, n, width), BF),
                pltpu.VMEM((parts, n, width), FL),
                pltpu.VMEM((n, width), FL),
                pltpu.VMEM((n, width), FL),
                pltpu.VMEM((n, width), BF),
                pltpu.VMEM((n, width), FL),
                pltpu.VMEM((n, 128), FL),
                pltpu.VMEM((parts, width, width), BF),
                pltpu.VMEM((ff, width), BF),
                pltpu.VMEM((width, width), BF),
                pltpu.SemaphoreType.DMA((4,)),
            ],
        ),
        out_shape=shapes + [big, big],
        compiler_params=params(),
    )(ids, pool, att, exact, lse, cot, vec, upb, *sets)


def weights_kernel(ids, pool, tok, dq, dk, dv, gvec, gup, sl, keep, send, dwq, dwk, dwv, bias, sems):
    width = tok.shape[1]
    ff = gup.shape[1]
    rb = width // NB
    dwq[...] = t_dot(pool[...].astype(BF), dq[...]).astype(BF)
    dwk[...] = t_dot(tok[...], dk[...]).astype(BF)
    dwv[...] = t_dot(tok[...], dv[...]).astype(BF)
    row = lax.broadcasted_iota(jnp.int32, (16, width), 0)
    g = jnp.concatenate([gvec[...], jnp.zeros((8, width), FL)], 0)
    g = jnp.where(row == 0, rows_sum(dq[...].astype(FL)), g)
    g = jnp.where(row == 1, rows_sum(dv[...].astype(FL)), g)
    block_of = div_rb(lax.broadcasted_iota(jnp.int32, (16, width), 1))
    parts = []
    for p in range(NB):
        parts.append(jnp.where(block_of == (ids[0] ^ rel_b(p)), g, 0.0).astype(BF))
    total = dot_t(jnp.concatenate(parts, 0), spread_matrix(128, width, rb))
    row = lax.broadcasted_iota(jnp.int32, (16, ff), 0)
    block_of = div_rb(lax.broadcasted_iota(jnp.int32, (16, ff), 1))
    block_of = jnp.where((row >= 8) & (row < 12), block_of - row + 8, -1)
    up = jnp.concatenate([gup[...], gup[...]], 0)
    parts = []
    for p in range(NB):
        parts.append(jnp.where(block_of == 4 * (ids[0] ^ rel_b(p)), up, 0.0).astype(BF))
    total = total + dot_t(jnp.concatenate(parts, 0), spread_matrix(128, ff, rb))
    heads = sl.shape[0] // 8
    per_head = jnp.sum(jnp.sum(sl[...].reshape(heads, 8, 128), 1), 1, keepdims=True)
    at = lax.broadcasted_iota(jnp.int32, (heads, 128), 0) == lax.broadcasted_iota(jnp.int32, (heads, 128), 1)
    line = -jnp.sum(jnp.where(at, per_head, 0.0), 0, keepdims=True)
    row = lax.broadcasted_iota(jnp.int32, (16 * NB, 128), 0)
    total = jnp.where((row & 15) == 12, line, total)
    bias[...] = jnp.zeros(bias.shape, BF)
    bias[:, 0:128] = total.astype(BF)

    def rows(r, size):
        return pl.ds(pl.multiple_of(r, 16), size)

    def store_sets(a_ref, b_ref):
        def go(src, dst):
            pltpu.make_async_copy(src, dst, sems.at[0]).start()

        for p in range(NB):
            s = ids[0] ^ rel_a(p)
            go(dwq.at[rows(s * rb, 48)], a_ref.at[p, pl.ds(0, 48)])
            go(dwk.at[rows(s * rb, 32)], a_ref.at[p, pl.ds(48, 32)])
            s = ids[0] ^ rel_b(p)
            go(dwk.at[rows(s * rb + 32, 16)], b_ref.at[p, pl.ds(0, 16)])
            go(dwv.at[rows(s * rb, 48)], b_ref.at[p, pl.ds(16, 48)])
            go(bias.at[pl.ds(16 * p, 16)], b_ref.at[p, pl.ds(64, 16)])

    @pl.when(ids[1] == 0)
    def _():
        store_sets(keep, send)

    @pl.when(ids[1] != 0)
    def _():
        store_sets(send, keep)

    wait_all(keep, sems.at[0])
    wait_all(send, sems.at[0])


def weight_grads(ids, pool, tok, dq, dk, dv, gvec, gup, sl, set_rows):
    width = tok.shape[1]
    full = lambda x: pl.BlockSpec(x.shape, lambda i, *_: (0, 0))
    big = jax.ShapeDtypeStruct((NB, set_rows, width), BF)
    square = pltpu.VMEM((width, width), BF)
    return pl.pallas_call(
        weights_kernel,
        name="weight_grads",
        grid_spec=pltpu.PrefetchScalarGridSpec(
            num_scalar_prefetch=1,
            grid=(1,),
            in_specs=[full(x) for x in (pool, tok, dq, dk, dv, gvec, gup, sl)],
            out_specs=[ANY, ANY],
            scratch_shapes=[
                square,
                square,
                square,
                pltpu.VMEM((16 * NB, width), BF),
                pltpu.SemaphoreType.DMA((1,)),
            ],
        ),
        out_shape=[big, big],
        compiler_params=params(),
    )(ids, pool, tok, dq, dk, dv, gvec, gup, sl)


def tokens_kernel(mixed, dq, dk, dv, wq, wk, wv, out, acc):
    half = mixed.shape[0]
    up = 0.5 * (mixed[...] + dot_t(dq[...], wq[...]))
    down = dot_t(dk[...], wk[...]) + dot_t(dv[...], wv[...])
    for j in range(mixed.shape[1] // 128):
        cols = slice(128 * j, 128 * j + 128)
        for i in range(2):
            acc[j, pl.ds(i, half, stride=2)] = up[:, cols]
        out[:, cols] = acc[j] + down[:, cols]


def token_grads(mixed, dq, dk, dv, wq, wk, wv):
    rows, width = dk.shape
    step = 512
    half = pl.BlockSpec((step // 2, width), lambda i: (i, 0))
    block = pl.BlockSpec((step, width), lambda i: (i, 0))
    whole = pl.BlockSpec((width, width), lambda i: (0, 0))
    return pl.pallas_call(
        tokens_kernel,
        name="token_grads",
        grid=(rows // step,),
        in_specs=[half, half, block, block, whole, whole, whole],
        out_specs=block,
        out_shape=jax.ShapeDtypeStruct((rows, width), FL),
        scratch_shapes=[pltpu.VMEM((width // 128, step, 128), FL)],
        compiler_params=params(),
    )(mixed, dq, dk, dv, wq, wk, wv)


def blocks_of(x):
    return x.reshape(NB, x.shape[0] // NB, x.shape[1])


def column_parts(x, width):
    return jnp.concatenate([x[..., width * c : width * c + width] for c in range(x.shape[-1] // width)], -2)


def bias_block(small, up, width):
    rb = small[0].shape[-1]
    rows = jnp.stack(list(small) + [up[..., rb * c : rb * c + rb] for c in range(4)], -2)
    pad = [(0, 0)] * (rows.ndim - 2) + [(0, 4), (0, width - rb)]
    return jnp.pad(rows, pad)


def pack(wq, wk, wv, wo, w1, w2, bias, width):
    a1 = jnp.concatenate([wq, wk[..., :32, :]], -2)
    b1 = jnp.concatenate([wk[..., 32:, :], wv, bias], -2)
    a2 = jnp.concatenate([w2, wo[..., :32, :]], -2)
    b2 = jnp.concatenate([column_parts(w1, width), wo[..., 32:, :], wo[..., 32:, :]], -2)
    return a1, b1, a2, b2


def unpack(a1, b1, a2, b2, width):
    wq = a1[..., :48, :]
    wk = jnp.concatenate([a1[..., 48:, :], b1[..., :16, :]], -2)
    wv = b1[..., 16:64, :]
    bias = b1[..., 64:, :]
    wo = jnp.concatenate([a2[..., 192:, :], b2[..., 192:208, :]], -2)
    w2 = a2[..., :192, :]
    parts = 4
    w1 = jnp.concatenate([b2[..., 48 * c : 48 * c + 48, :] for c in range(parts)], -1)
    return wq, wk, wv, wo, w1, w2, bias


def local(
    tokens,
    cotangent,
    lengths,
    w_query,
    b_query,
    w_key,
    w_value,
    b_value,
    w_output,
    b_output,
    gain_attn,
    shift_attn,
    w_up,
    b_up,
    w_down,
    b_down,
    gain_ffn,
    shift_ffn,
    distance_slope,
):
    rows_here, width = tokens.shape
    ff = w_up.shape[1]
    own = rows_here // 2
    halo = rows_here // 2
    seq = lax.axis_size("seq")
    devices = seq * lax.axis_size("dp")
    direct = seq == NB
    order = ("dp", "seq")
    up_pairs = [(i, i + 1) for i in range(devices - 1)]
    down_pairs = [(i + 1, i) for i in range(devices - 1)]

    masters = (w_query, w_key, w_value, w_output, w_up, w_down)
    vectors = (b_query, b_value, b_output, gain_attn, shift_attn, b_down, gain_ffn, shift_ffn)
    if direct:
        core = lax.axis_index("dp")
        ids = jnp.stack([lax.axis_index("seq"), core]).astype(jnp.int32)
        a1, b1, a2, b2 = pack(*masters, bias_block(vectors, b_up, width), width)
        first = jnp.where(core == 0, a1, b1).astype(BF)[None]
        second = jnp.where(core == 0, a2, b2).astype(BF)[None]
        sets1 = gather_set(first)
        sets2 = gather_set(second)
    else:
        ids = jnp.zeros((2,), jnp.int32)
        gather = lambda x: lax.all_gather(x.astype(BF), "seq", axis=0, tiled=True)
        full = [blocks_of(gather(x)) for x in masters]
        small = [gather(x).reshape(NB, -1) for x in vectors]
        bias = bias_block(small, gather(b_up).reshape(NB, -1), width)
        a1, b1, a2, b2 = pack(*full, bias, width)
        at_a = jnp.array([rel_a(p) for p in range(NB)])
        at_b = jnp.array([rel_b(p) for p in range(NB)])
        sets1 = (a1[at_a[:8]], a1[at_a[8:]], b1[at_b[:8]], b1[at_b[8:]])
        sets2 = (a2[at_a[:8]], a2[at_a[8:]], b2[at_b[:8]], b2[at_b[8:]])

    first_row = lax.axis_index(order) * rows_here
    total = devices * rows_here
    starts = 2 * (jnp.cumsum(lengths) - lengths)
    place = first_row - halo + 2 * jnp.arange(2 * own, dtype=jnp.int32)
    before = starts[None, :] <= place[:, None]
    begin = jnp.max(jnp.where(before, starts[None, :], 0), 1)
    end = jnp.min(jnp.where(before, total, starts[None, :]), 1)
    inside = (place >= 0) & (place < total)
    shift = first_row - halo
    begin = jnp.where(inside, begin - shift, 0)
    end = jnp.where(inside, end - shift, 0)
    bounds = jnp.stack([begin, end], 1).astype(FL)
    bounds = jnp.pad(bounds, ((0, 0), (0, 126)))
    blocks = 2 * own // QB
    chunks = (rows_here + 2 * halo) // KC
    low_chunk = jnp.min(jnp.where(inside, begin, 4 * total).reshape(blocks, QB), 1) // KC
    high_chunk = (jnp.max(end.reshape(blocks, QB), 1) + KC - 1) // KC
    index = jnp.arange(blocks)
    away = (index < blocks // 4) | (index >= blocks - blocks // 4)
    low_chunk = jnp.clip(low_chunk, jnp.where(away, chunks // 4, 0), chunks)
    high_chunk = jnp.clip(high_chunk, 0, jnp.where(away, chunks - chunks // 4, chunks))
    spans = jnp.concatenate([low_chunk, high_chunk]).astype(jnp.int32)

    low_tokens = lax.ppermute(tokens[rows_here - halo :], order, up_pairs)
    high_tokens = lax.ppermute(tokens[:halo], order, down_pairs)
    tok_ext = jnp.concatenate([low_tokens, tokens, high_tokens], 0)

    q, k, v, pool, wq, wk, wv, vec, upb = qkv(ids, tok_ext, sets1, ff)
    pool = pool[own // 2 : own // 2 + own]
    att, exact, lse = attend_forward(spans, distance_slope, q, k, v, bounds, own)
    out, pay, stats, mixed, gvec, gup, keep2, send2 = middle(
        ids, pool, att, exact, lse, cotangent, vec, upb, sets2, 224
    )
    low_pay = lax.ppermute(pay[own // 2 :], order, up_pairs)
    high_pay = lax.ppermute(pay[: own // 2], order, down_pairs)

    def stats_of(x):
        return add(*[x[:, width + 256 * j : width + 256 * j + 256] for j in range(3)])

    da = jnp.concatenate([low_pay[:, :width], pay[:, :width], high_pay[:, :width]], 0)
    stats_ext = jnp.concatenate([stats_of(low_pay), stats, stats_of(high_pay)], 0)
    dq, dk, dv, sl = attend_backward(spans, distance_slope, q, k, v, da, stats_ext, bounds)
    keep1, send1 = weight_grads(ids, pool, tokens, dq, dk, dv, gvec, gup, sl, 80)
    grad_tokens = token_grads(mixed, dq, dk, dv, wq, wk, wv)

    if direct:
        a2, b2 = reduce_set(keep2, send2)
        a1, b1 = reduce_set(keep1, send1)
        gq, gk, gv, go, g1, g2, gb = unpack(a1, b1, a2, b2, width)
        rb = width // NB
        small = [gb[i, :rb] for i in range(8)]
        g_up = jnp.concatenate([gb[8 + c, :rb] for c in range(4)], 0)
        g_slope = gb[12, : distance_slope.shape[0]]
    else:
        inv_a = [0] * NB
        inv_b = [0] * NB
        for p in range(NB):
            inv_a[rel_a(p)] = p
            inv_b[rel_b(p)] = p
        inv_a = jnp.array(inv_a)
        inv_b = jnp.array(inv_b)
        gq, gk, gv, go, g1, g2, gb = unpack(keep1[inv_a], send1[inv_b], keep2[inv_a], send2[inv_b], width)
        rb = width // NB

        def share(x):
            x = lax.psum(x.astype(FL), "dp")
            return lax.psum_scatter(x, "seq", scatter_dimension=0, tiled=True)

        gq, gk, gv, go, g1, g2 = [share(x.reshape(-1, x.shape[-1])) for x in (gq, gk, gv, go, g1, g2)]
        small = [share(gb[:, i, :rb].reshape(-1)) for i in range(8)]
        g_up = share(gb[:, 8:12, :rb].reshape(-1))
        g_slope = lax.psum(gb[0, 12, : distance_slope.shape[0]].astype(FL), order)
    return (
        out,
        grad_tokens,
        gq,
        small[0],
        gk,
        gv,
        small[1],
        go,
        small[2],
        small[3],
        small[4],
        g1,
        g_up,
        g2,
        small[5],
        small[6],
        small[7],
        g_slope,
    )


def solution(mesh):
    tall = P(("dp", "seq"), None)
    mat = P("seq", None)
    vec = P("seq")
    return jax.shard_map(
        local,
        mesh=mesh,
        in_specs=(tall, tall, P(), mat, vec, mat, mat, vec, mat, vec, vec, vec, mat, vec, mat, vec, vec, vec, P()),
        out_specs=(tall, tall, mat, vec, mat, mat, vec, mat, vec, vec, vec, mat, vec, mat, vec, vec, vec, P()),
        check_vma=False,
    )
```

```python
import functools

import jax
import jax.numpy as jnp
from jax import lax
from jax.experimental import pallas as pl
from jax.experimental.pallas import tpu as pltpu
from jax.sharding import PartitionSpec as P

HD = 64
NB = 16
QB = 128
KC = 256
EPS = 1e-05
FAR = 1e12
BF = jnp.bfloat16
FL = jnp.float32


def rel_a(p):
    return (p & 1) * 8 + ((p >> 1) & 1) * 4 + ((p >> 2) & 1) * 2 + ((p >> 3) & 1)


def rel_b(p):
    return (p & 1) * 8 + ((p >> 1) & 1) * 4 + ((p >> 2) & 1) + ((p >> 3) & 1) * 2


def dot(a, b):
    return jnp.dot(a, b, preferred_element_type=FL)


def dot_t(a, b):
    return lax.dot_general(a, b, (((1,), (1,)), ((), ())), preferred_element_type=FL)


def t_dot(a, b):
    return lax.dot_general(a, b, (((0,), (0,)), ((), ())), preferred_element_type=FL)


def exchange(x, stride_a, stride_b):
    n = lax.axis_size("seq")
    pairs = [(s, s ^ stride_a) for s in range(n)] + [(n + s, n + (s ^ stride_b)) for s in range(n)]
    return lax.ppermute(x, ("dp", "seq"), pairs)


def swap_core(x):
    return lax.ppermute(x, "dp", [(0, 1), (1, 0)])


def add(*xs):
    total = xs[0].astype(FL)
    for x in xs[1:]:
        total = total + x.astype(FL)
    return total


def params(**kw):
    return pltpu.CompilerParams(vmem_limit_bytes=58 * 1024 * 1024, **kw)


ANY = pl.BlockSpec(memory_space=pl.ANY)


def load_sets(ids, low, high, olow, ohigh, copies_a, copies_b):
    def start(a_refs, b_refs):
        for p in range(NB):
            copies_a(a_refs[p // 8].at[p % 8], ids[0] ^ rel_a(p), p)
            copies_b(b_refs[p // 8].at[p % 8], ids[0] ^ rel_b(p), p)

    @pl.when(ids[1] == 0)
    def _():
        start((low, high), (olow, ohigh))

    @pl.when(ids[1] != 0)
    def _():
        start((olow, ohigh), (low, high))


def wait_all(ref, sem):
    pltpu.make_async_copy(ref, ref, sem).wait()


def spread_matrix(rows, cols, rb):
    lanes = lax.broadcasted_iota(jnp.int32, (rows, cols), 1)
    return (lax.broadcasted_iota(jnp.int32, (rows, cols), 0) == lanes - rb * div_rb(lanes)).astype(FL).astype(BF)


def div_rb(x):
    return (x * 21846) >> 20


def qkv_kernel(
    ids, tok, low, high, olow, ohigh, q_out, k_out, v_out, pool_out, wq, wk, wv, vec_out, up_out, bias, x32, pool, sems
):
    width = tok.shape[1]
    rb = width // NB

    @pl.when(pl.program_id(0) == 0)
    def _():
        def rows(r, n):
            return pl.ds(pl.multiple_of(r, 16), n)

        def copies_a(block, s, p):
            pltpu.make_async_copy(block.at[pl.ds(0, 48)], wq.at[rows(s * rb, 48)], sems.at[0]).start()
            pltpu.make_async_copy(block.at[pl.ds(48, 32)], wk.at[rows(s * rb, 32)], sems.at[1]).start()

        def copies_b(block, s, p):
            pltpu.make_async_copy(block.at[pl.ds(0, 16)], wk.at[rows(s * rb + 32, 16)], sems.at[1]).start()
            pltpu.make_async_copy(block.at[pl.ds(16, 48)], wv.at[rows(s * rb, 48)], sems.at[2]).start()
            pltpu.make_async_copy(block.at[pl.ds(64, 16)], bias.at[pl.ds(16 * p, 16)], sems.at[3]).start()

        load_sets(ids, low, high, olow, ohigh, copies_a, copies_b)
        wait_all(wq, sems.at[0])
        wait_all(wk, sems.at[1])
        wait_all(wv, sems.at[2])
        wait_all(bias, sems.at[3])
        parts = bias[:, 0:128]
        wide = dot(parts, spread_matrix(128, width, rb))
        block_of = div_rb(lax.broadcasted_iota(jnp.int32, (16, width), 1))
        total = jnp.zeros((16, width), FL)
        for p in range(NB):
            total = total + jnp.where(block_of == (ids[0] ^ rel_b(p)), wide[16 * p : 16 * p + 16], 0.0)
        vec_out[...] = total
        ff = up_out.shape[1]
        wide = dot(parts, spread_matrix(128, ff, rb))
        block_of = div_rb(lax.broadcasted_iota(jnp.int32, (16, ff), 1))
        row = lax.broadcasted_iota(jnp.int32, (16, ff), 0)
        block_of = jnp.where((row >= 8) & (row < 12), block_of - row + 8, -1)
        total = jnp.zeros((16, ff), FL)
        for p in range(NB):
            total = total + jnp.where(block_of == 4 * (ids[0] ^ rel_b(p)), wide[16 * p : 16 * p + 16], 0.0)
        up_out[...] = jnp.broadcast_to(jnp.sum(total, 0, keepdims=True), up_out.shape)

    x = tok[...]
    half = x.shape[0] // 2
    k_out[...] = dot(x, wk[...]).astype(BF)
    v_out[...] = (dot(x, wv[...]) + vec_out[1:2]).astype(BF)
    for j in range(width // 128):
        cols = slice(128 * j, 128 * j + 128)
        x32[j] = x[:, cols].astype(FL)
        pool[:, cols] = (x32[j, pl.ds(0, half, stride=2)] + x32[j, pl.ds(1, half, stride=2)]) * 0.5
    step = pl.program_id(0)

    @pl.when((step > 0) & (step < pl.num_programs(0) - 1))
    def _():
        pool_out[...] = pool[...]

    q = (dot(pool[...].astype(BF), wq[...]) + vec_out[0:1]).astype(BF)
    q_out[...] = (q.astype(FL) * HD**-0.5).astype(BF)


def qkv(ids, tok_ext, sets, ff):
    rows, width = tok_ext.shape
    step = 512
    whole = lambda i, *_: (0, 0)
    return pl.pallas_call(
        qkv_kernel,
        name="qkv",
        grid_spec=pltpu.PrefetchScalarGridSpec(
            num_scalar_prefetch=1,
            grid=(rows // step,),
            in_specs=[pl.BlockSpec((step, width), lambda i, *_: (i, 0)), ANY, ANY, ANY, ANY],
            out_specs=[
                pl.BlockSpec((step // 2, width), lambda i, *_: (i, 0)),
                pl.BlockSpec((step, width), lambda i, *_: (i, 0)),
                pl.BlockSpec((step, width), lambda i, *_: (i, 0)),
                pl.BlockSpec((step // 2, width), lambda i, *_: (jnp.clip(i - 1, 0, rows // step - 3), 0)),
                pl.BlockSpec((width, width), whole),
                pl.BlockSpec((width, width), whole),
                pl.BlockSpec((width, width), whole),
                pl.BlockSpec((16, width), whole),
                pl.BlockSpec((8, ff), whole),
            ],
            scratch_shapes=[
                pltpu.VMEM((16 * NB, width), BF),
                pltpu.VMEM((width // 128, step, 128), FL),
                pltpu.VMEM((step // 2, width), FL),
                pltpu.SemaphoreType.DMA((4,)),
            ],
        ),
        out_shape=[
            jax.ShapeDtypeStruct((rows // 2, width), BF),
            jax.ShapeDtypeStruct((rows, width), BF),
            jax.ShapeDtypeStruct((rows, width), BF),
            jax.ShapeDtypeStruct((rows // 4, width), FL),
            jax.ShapeDtypeStruct((width, width), BF),
            jax.ShapeDtypeStruct((width, width), BF),
            jax.ShapeDtypeStruct((width, width), BF),
            jax.ShapeDtypeStruct((16, width), FL),
            jax.ShapeDtypeStruct((8, ff), FL),
        ],
        compiler_params=params(),
    )(ids, tok_ext, *sets)


def two_heads(x):
    lane = lax.broadcasted_iota(jnp.int32, x.shape, 1)
    zero = jnp.zeros_like(x)
    return jnp.concatenate([jnp.where(lane < HD, x, zero), jnp.where(lane < HD, zero, x)], 0)


def one_block(x):
    r = x.shape[1] // 2
    line = lax.broadcasted_iota(jnp.int32, (128, r), 0)
    return jnp.where(line < HD, x[:, :r], x[:, r:]).T


def distances(bounds, row, c):
    low = bounds[0:1, pl.ds(row, QB)]
    high = bounds[1:2, pl.ds(row, QB)]
    query = (2 * (row + lax.broadcasted_iota(jnp.int32, (KC, QB), 1))).astype(FL) + 0.5
    key = (c * KC + lax.broadcasted_iota(jnp.int32, (KC, QB), 0)).astype(FL)
    far = jnp.where((key >= low) & (key < high), jnp.abs(query - key), FAR)
    return jnp.concatenate([far, far], 1)


def fold(x, f):
    n = x.shape[0] // 8
    parts = [x[8 * i : 8 * i + 8] for i in range(n)]
    while len(parts) > 1:
        parts = [f(parts[2 * i], parts[2 * i + 1]) for i in range(len(parts) // 2)]
    return parts[0]


def slope_line(slopes, head):
    lane = lax.broadcasted_iota(jnp.int32, (1, 2 * QB), 1)
    return jnp.where(lane < QB, slopes[head], slopes[head + 1])


def forward_kernel(half, spans, slopes, q, k, v, bounds, o_out, exact_out, lse_out, s_scr, vt, q2, top, total, acc, rest):
    pairs = q.shape[1] // 128
    head0 = half * 2 * pairs
    q_first = q.shape[0] // 4
    slope = [slope_line(slopes, head0 + 2 * j) for j in range(pairs)]
    for c in range(k.shape[0] // KC):
        for j in range(pairs):
            vt[c, j] = v[KC * c : KC * c + KC, 128 * j : 128 * j + 128].T

    def query_block(b, _):
        row = pl.multiple_of(q_first + b * QB, QB)
        out_rows = pl.ds(pl.multiple_of(b * QB, QB), QB)
        block = row // QB
        c0 = spans[block]
        c1 = spans[spans.shape[0] // 2 + block]
        for j in range(pairs):
            q2[j] = two_heads(q[pl.ds(row, QB), 128 * j : 128 * j + 128])
        top[...] = jnp.full(top.shape, -3e38, FL)
        total[...] = jnp.zeros(total.shape, FL)
        acc[...] = jnp.zeros(acc.shape, FL)
        rest[...] = jnp.zeros(rest.shape, FL)

        def score(c, _):
            far = distances(bounds, row, c)
            keys = pl.ds(pl.multiple_of(c * KC, KC), KC)
            for j in range(pairs):
                s = dot_t(k[keys, 128 * j : 128 * j + 128], q2[j]) - slope[j] * far
                s_scr[c - c0, j] = s
                top[j] = jnp.maximum(top[j], fold(s, jnp.maximum))
            return 0

        lax.fori_loop(c0, c1, score, 0)
        peak = [jnp.max(top[j], 0, keepdims=True) for j in range(pairs)]

        def exponent(c, _):
            for j in range(pairs):
                e = jnp.exp(s_scr[c - c0, j] - peak[j])
                s_scr[c - c0, j] = e
                total[j] = total[j] + fold(e, jnp.add)
            return 0

        lax.fori_loop(c0, c1, exponent, 0)
        inverse = []
        for j in range(pairs):
            l = jnp.sum(total[j], 0, keepdims=True)
            t = peak[j] + jnp.log(l)
            inverse.append(1.0 / l)
            lse_out[2 * j : 2 * j + 1, out_rows] = t[:, :QB]
            lse_out[2 * j + 1 : 2 * j + 2, out_rows] = t[:, QB:]

        def attend(c, _):
            for j in range(pairs):
                p = s_scr[c - c0, j] * inverse[j]
                high = p.astype(BF)
                low = (p - high.astype(FL)).astype(BF)
                values = vt[c, j]
                acc[j] = acc[j] + dot(values, high)
                rest[j] = rest[j] + dot(values, low)
            return 0

        lax.fori_loop(c0, c1, attend, 0)
        for j in range(pairs):
            cols = slice(128 * j, 128 * j + 128)
            o_out[out_rows, cols] = one_block(acc[j]).astype(BF)
            exact_out[out_rows, cols] = one_block(acc[j] + rest[j])
        return 0

    lse_out[...] = jnp.zeros(lse_out.shape, FL)
    lax.fori_loop(0, o_out.shape[0] // QB, query_block, 0)


def attend_forward(half, spans, slopes, q, k, v, bounds, own):
    wide = q.shape[1] // 2
    pairs = wide // 128
    chunks = k.shape[0] // KC
    col = lambda i, *_: (0, half)
    zero = lambda i, *_: (0, 0)
    return pl.pallas_call(
        functools.partial(forward_kernel, half),
        name=f"attend_forward_{half}",
        grid_spec=pltpu.PrefetchScalarGridSpec(
            num_scalar_prefetch=2,
            grid=(1,),
            in_specs=[
                pl.BlockSpec((q.shape[0], wide), col),
                pl.BlockSpec((k.shape[0], wide), col),
                pl.BlockSpec((k.shape[0], wide), col),
                pl.BlockSpec(bounds.shape, zero),
            ],
            out_specs=[
                pl.BlockSpec((own, wide), zero),
                pl.BlockSpec((own, wide), zero),
                pl.BlockSpec((8, own), zero),
            ],
            scratch_shapes=[
                pltpu.VMEM((chunks, pairs, KC, 2 * QB), FL),
                pltpu.VMEM((chunks, pairs, 128, KC), BF),
                pltpu.VMEM((pairs, 2 * QB, 128), BF),
                pltpu.VMEM((pairs, 8, 2 * QB), FL),
                pltpu.VMEM((pairs, 8, 2 * QB), FL),
                pltpu.VMEM((pairs, 128, 2 * QB), FL),
                pltpu.VMEM((pairs, 128, 2 * QB), FL),
            ],
        ),
        out_shape=[
            jax.ShapeDtypeStruct((own, wide), BF),
            jax.ShapeDtypeStruct((own, wide), FL),
            jax.ShapeDtypeStruct((8, own), FL),
        ],
        compiler_params=params(),
    )(spans, slopes, q, k, v, bounds)


def chunk_step(q2, da2, far, slope, lse, delta, kj, vj):
    p = jnp.exp(dot_t(kj, q2) - slope * far - lse)
    ds = (p * (dot_t(vj, da2) - delta)).astype(BF)
    return p.astype(BF), ds


def own_kernel(
    half, spans, slopes, q, k, v, da, stats, bounds, dq_out, dk, dv, slope_out, kt, q2, da2, dq2, sl
):
    pairs = q.shape[1] // 128
    head0 = half * 2 * pairs
    total_blocks = bounds.shape[1] // QB
    quarter = k.shape[0] // KC // 4
    first = total_blocks // 4
    slope = [slope_line(slopes, head0 + 2 * j) for j in range(pairs)]
    dk[...] = jnp.zeros(dk.shape, FL)
    dv[...] = jnp.zeros(dv.shape, FL)
    sl[...] = jnp.zeros(sl.shape, FL)
    for c in range(k.shape[0] // KC):
        for j in range(pairs):
            kt[c, j] = k[KC * c : KC * c + KC, 128 * j : 128 * j + 128].T

    def query_block(b, _):
        row = pl.multiple_of((first + b) * QB, QB)
        rows = pl.ds(pl.multiple_of(b * QB, QB), QB)
        c0 = spans[first + b]
        c1 = spans[total_blocks + first + b]
        lse = []
        delta = []
        for j in range(pairs):
            cols = slice(128 * j, 128 * j + 128)
            q2[j] = two_heads(q[pl.ds(row, QB), cols])
            da2[j] = two_heads(da[rows, cols])
            h = head0 + 2 * j
            lse.append(jnp.concatenate([stats[h : h + 1, rows], stats[h + 1 : h + 2, rows]], 1))
            delta.append(jnp.concatenate([stats[16 + h : 17 + h, rows], stats[17 + h : 18 + h, rows]], 1))
        dq2[...] = jnp.zeros(dq2.shape, FL)

        def step(c, grads):
            far = distances(bounds, row, c)
            keys = pl.ds(pl.multiple_of(c * KC, KC), KC)
            for j in range(pairs):
                cols = slice(128 * j, 128 * j + 128)
                p, ds = chunk_step(q2[j], da2[j], far, slope[j], lse[j], delta[j], k[keys, cols], v[keys, cols])
                if grads:
                    mine = pl.ds(pl.multiple_of((c - quarter) * KC, KC), KC)
                    dv[mine, cols] = dv[mine, cols] + dot(p, da2[j])
                    dk[mine, cols] = dk[mine, cols] + dot(ds, q2[j])
                dq2[j] = dq2[j] + dot(kt[c, j], ds)
                sl[j] = sl[j] + fold(ds.astype(FL) * far, jnp.add)

        def inside(c, _):
            step(c, True)
            return 0

        left = jnp.maximum(jnp.minimum(c1, quarter) - c0, 0)
        right0 = jnp.maximum(c0, 3 * quarter)

        def outside(i, _):
            step(jnp.where(i < left, c0 + i, right0 + i - left), False)
            return 0

        lax.fori_loop(jnp.maximum(c0, quarter), jnp.minimum(c1, 3 * quarter), inside, 0)
        lax.fori_loop(0, left + jnp.maximum(c1 - right0, 0), outside, 0)
        for j in range(pairs):
            dq_out[rows, 128 * j : 128 * j + 128] = (one_block(dq2[j]) * HD**-0.5).astype(BF)
        return 0

    lax.fori_loop(0, da.shape[0] // QB, query_block, 0)
    slope_out[...] = sl[...].reshape(slope_out.shape)


def attend_own(half, spans, slopes, q, k, v, da, stats, bounds):
    own = stats.shape[1]
    wide = q.shape[1] // 2
    pairs = wide // 128
    keys = k.shape[0]
    chunks = keys // KC
    col = lambda i, *_: (0, half)
    zero = lambda i, *_: (0, 0)
    return pl.pallas_call(
        functools.partial(own_kernel, half),
        name=f"attend_own_{half}",
        grid_spec=pltpu.PrefetchScalarGridSpec(
            num_scalar_prefetch=2,
            grid=(1,),
            in_specs=[
                pl.BlockSpec((q.shape[0], wide), col),
                pl.BlockSpec((keys, wide), col),
                pl.BlockSpec((keys, wide), col),
                pl.BlockSpec((own, wide), col),
                pl.BlockSpec(stats.shape, zero),
                pl.BlockSpec(bounds.shape, zero),
            ],
            out_specs=[
                pl.BlockSpec((own, wide), zero),
                pl.BlockSpec((keys // 2, wide), zero),
                pl.BlockSpec((keys // 2, wide), zero),
                pl.BlockSpec((8 * pairs, 2 * QB), zero),
            ],
            scratch_shapes=[
                pltpu.VMEM((chunks, pairs, 128, KC), BF),
                pltpu.VMEM((pairs, 2 * QB, 128), BF),
                pltpu.VMEM((pairs, 2 * QB, 128), BF),
                pltpu.VMEM((pairs, 128, 2 * QB), FL),
                pltpu.VMEM((pairs, 8, 2 * QB), FL),
            ],
        ),
        out_shape=[
            jax.ShapeDtypeStruct((own, wide), BF),
            jax.ShapeDtypeStruct((keys // 2, wide), FL),
            jax.ShapeDtypeStruct((keys // 2, wide), FL),
            jax.ShapeDtypeStruct((8 * pairs, 2 * QB), FL),
        ],
        compiler_params=params(),
    )(spans, slopes, q, k, v, da, stats, bounds)


def halo_kernel(spans, slopes, q, k, v, low_pay, high_pay, bounds, dk0, dv0, dk1, dv1, dk_out, dv_out, q2, da2, st, dk, dv):
    wide = dk0.shape[1]
    width = q.shape[1]
    pairs = width // 128
    total_blocks = bounds.shape[1] // QB
    quarter = k.shape[0] // KC // 4
    count = low_pay.shape[0] // QB
    dk[:, :wide] = dk0[...]
    dk[:, wide:] = dk1[...]
    dv[:, :wide] = dv0[...]
    dv[:, wide:] = dv1[...]
    for side, pay in enumerate((low_pay, high_pay)):
        x = pay[:, width : width + 128].astype(FL)
        x = x + pltpu.roll(x, 96, 1) + pltpu.roll(x, 64, 1)
        st[...] = x.T
        for i in range(count):
            block = i if side == 0 else total_blocks - count + i
            row = block * QB
            rows = slice(i * QB, i * QB + QB)
            c0 = spans[block]
            c1 = spans[total_blocks + block]

            @pl.when(c0 < c1)
            def _():
                for j in range(pairs):
                    cols = slice(128 * j, 128 * j + 128)
                    q2[j] = two_heads(q[row : row + QB, cols])
                    da2[j] = two_heads(pay[rows, cols])

                def step(c, _):
                    far = distances(bounds, row, c)
                    keys = pl.ds(pl.multiple_of(c * KC, KC), KC)
                    mine = pl.ds(pl.multiple_of((c - quarter) * KC, KC), KC)
                    for j in range(pairs):
                        cols = slice(128 * j, 128 * j + 128)
                        h = 2 * j
                        lse = jnp.concatenate([st[h : h + 1, rows], st[h + 1 : h + 2, rows]], 1)
                        delta = jnp.concatenate([st[16 + h : 17 + h, rows], st[17 + h : 18 + h, rows]], 1)
                        p, ds = chunk_step(
                            q2[j], da2[j], far, slope_line(slopes, h), lse, delta, k[keys, cols], v[keys, cols]
                        )
                        dv[mine, cols] = dv[mine, cols] + dot(p, da2[j])
                        dk[mine, cols] = dk[mine, cols] + dot(ds, q2[j])
                    return 0

                lax.fori_loop(c0, c1, step, 0)

    dk_out[...] = dk[...].astype(BF)
    dv_out[...] = dv[...].astype(BF)


def attend_halo(spans, slopes, q, k, v, low_pay, high_pay, bounds, dk0, dv0, dk1, dv1):
    width = q.shape[1]
    pairs = width // 128
    keys = k.shape[0]
    full = lambda x: pl.BlockSpec(x.shape, lambda i, *_: (0, 0))
    shape = jax.ShapeDtypeStruct((keys // 2, width), BF)
    return pl.pallas_call(
        halo_kernel,
        name="attend_halo",
        grid_spec=pltpu.PrefetchScalarGridSpec(
            num_scalar_prefetch=2,
            grid=(1,),
            in_specs=[full(x) for x in (q, k, v, low_pay, high_pay, bounds, dk0, dv0, dk1, dv1)],
            out_specs=[full(shape), full(shape)],
            scratch_shapes=[
                pltpu.VMEM((pairs, 2 * QB, 128), BF),
                pltpu.VMEM((pairs, 2 * QB, 128), BF),
                pltpu.VMEM((128, low_pay.shape[0]), FL),
                pltpu.VMEM((keys // 2, width), FL),
                pltpu.VMEM((keys // 2, width), FL),
            ],
        ),
        out_shape=[shape, shape],
        compiler_params=params(),
    )(spans, slopes, q, k, v, low_pay, high_pay, bounds, dk0, dv0, dk1, dv1)


def normalize(z):
    centred = z - jnp.mean(z, -1, keepdims=True)
    scale = lax.rsqrt(jnp.mean(centred * centred, -1, keepdims=True) + EPS)
    return centred * scale, scale


def normalize_back(d, unit, scale):
    return scale * (d - jnp.mean(d, -1, keepdims=True) - unit * jnp.mean(d * unit, -1, keepdims=True))


def rows_sum(x):
    return jnp.sum(x, 0, keepdims=True)


def middle_kernel(
    ids,
    pool,
    att0,
    att1,
    exact0,
    exact1,
    lse0,
    lse1,
    cot,
    vec,
    upb,
    low,
    high,
    olow,
    ohigh,
    out,
    pay,
    stats,
    mixed,
    gvec,
    gup,
    keep,
    send,
    wo,
    w1,
    w2,
    active,
    slope,
    unit1,
    hid,
    hid_low,
    z,
    d2,
    dw1,
    dw2,
    dwo,
    att,
    sems,
):
    n, width = att.shape
    att[:, : width // 2] = att0[...]
    att[:, width // 2 :] = att1[...]
    rb = width // NB
    fb = w2.shape[0] // NB
    parts = w1.shape[0]

    def rows(r, size):
        return pl.ds(pl.multiple_of(r, 16), size)

    def copies_a(block, s, p):
        pltpu.make_async_copy(block.at[pl.ds(192, 32)], wo.at[rows(s * rb, 32)], sems.at[0]).start()
        pltpu.make_async_copy(block.at[pl.ds(0, 192)], w2.at[rows(s * fb, 192)], sems.at[2]).start()

    def copies_b(block, s, p):
        pltpu.make_async_copy(block.at[pl.ds(192, 16)], wo.at[rows(s * rb + 32, 16)], sems.at[0]).start()
        for c in range(parts):
            pltpu.make_async_copy(block.at[pl.ds(48 * c, 48)], w1.at[c, rows(s * rb, 48)], sems.at[1]).start()

    load_sets(ids, low, high, olow, ohigh, copies_a, copies_b)
    wait_all(wo, sems.at[0])
    z[...] = dot(att[...], wo[...])
    rc = 128

    def row_loop(f):
        def body(i, _):
            f(pl.ds(pl.multiple_of(i * rc, rc), rc), i)
            return 0

        lax.fori_loop(0, n // rc, body, 0)

    def first_norm(r, i):
        unit, scale = normalize(pool[r, :] + z[r, :] + vec[2:3])
        h = unit * vec[3:4] + vec[4:5]
        unit1[r, :] = unit
        d2[r, 0:128] = jnp.broadcast_to(scale, (rc, 128))
        hid[r, :] = h
        hid_low[r, :] = h.astype(BF)

    row_loop(first_norm)
    wait_all(w1, sems.at[1])
    wait_all(w2, sems.at[2])
    c0 = 0.7978845608028654

    def up(c, _):
        inner = dot(hid_low[...], w1[c]) + upb[pl.ds(0, 1), pl.ds(pl.multiple_of(c * width, 128), width)]
        sq = inner * inner
        t = jnp.tanh(c0 * (inner + 0.044715 * (inner * sq)))
        cdf = 0.5 * (1.0 + t)
        active[c] = (inner * cdf).astype(BF)
        slope[c] = cdf + inner * (0.5 * (1.0 - t * t)) * (c0 + (3 * 0.044715 * c0) * sq)
        return 0

    lax.fori_loop(0, parts, up, 0)
    z[...] = dot(active[0], w2[pl.ds(0, width), :])
    for c in range(1, parts):
        z[...] = z[...] + dot(active[c], w2[pl.ds(c * width, width), :])
    gvec[...] = jnp.zeros(gvec.shape, FL)

    def second_norm(r, i):
        unit, scale = normalize(hid[r, :] + (z[r, :] + vec[5:6]))
        out[r, :] = (unit * vec[6:7] + vec[7:8]).astype(BF)
        dy = cot[r, :].astype(FL)
        gvec[6:7] = gvec[6:7] + rows_sum(dy * unit)
        gvec[7:8] = gvec[7:8] + rows_sum(dy)
        d = normalize_back(dy * vec[6:7], unit, scale)
        hid[r, :] = d
        d_low = d.astype(BF)
        att_like[r, :] = d_low
        gvec[5:6] = gvec[5:6] + rows_sum(d_low.astype(FL))

    att_like = pay.at[:, 0:width]
    scale1 = d2[:, 0:1]
    row_loop(second_norm)
    z[...] = jnp.zeros(z.shape, FL)

    def down(c, _):
        ffn = pay[:, 0:width]
        far = pl.ds(pl.multiple_of(c * width, 128), width)
        d_inner = (dot_t(ffn, w2[far, :]) * slope[c]).astype(BF)
        gup[:, far] = jnp.broadcast_to(rows_sum(d_inner.astype(FL)), (8, width))
        dw2[far, :] = t_dot(active[c], ffn).astype(BF)
        dw1[c] = t_dot(hid_low[...], d_inner).astype(BF)
        z[...] = z[...] + dot_t(d_inner, w1[c])
        return 0

    lax.fori_loop(0, parts, down, 0)

    def store_sets(a_ref, b_ref):
        for p in range(NB):
            s = ids[0] ^ rel_a(p)
            pltpu.make_async_copy(dw2.at[rows(s * fb, 192)], a_ref.at[p, pl.ds(0, 192)], sems.at[3]).start()
            s = ids[0] ^ rel_b(p)
            for c in range(parts):
                pltpu.make_async_copy(
                    dw1.at[c, rows(s * rb, 48)], b_ref.at[p, pl.ds(48 * c, 48)], sems.at[3]
                ).start()

    @pl.when(ids[1] == 0)
    def _():
        store_sets(keep, send)

    @pl.when(ids[1] != 0)
    def _():
        store_sets(send, keep)

    def first_back(r, i):
        unit = unit1[r, :]
        d = hid[r, :] + z[r, :]
        gvec[3:4] = gvec[3:4] + rows_sum(d * unit)
        gvec[4:5] = gvec[4:5] + rows_sum(d)
        d = normalize_back(d * vec[3:4], unit, d2[r, 0:1])
        mixed[r, :] = d
        d_low = d.astype(BF)
        hid_low[r, :] = d_low
        gvec[2:3] = gvec[2:3] + rows_sum(d_low.astype(FL))

    row_loop(first_back)
    dwo[...] = t_dot(att[...], hid_low[...]).astype(BF)

    def store_wo(a_ref, b_ref):
        for p in range(NB):
            s = ids[0] ^ rel_a(p)
            pltpu.make_async_copy(dwo.at[rows(s * rb, 32)], a_ref.at[p, pl.ds(192, 32)], sems.at[3]).start()
            s = ids[0] ^ rel_b(p)
            pltpu.make_async_copy(dwo.at[rows(s * rb + 32, 16)], b_ref.at[p, pl.ds(192, 16)], sems.at[3]).start()
            pltpu.make_async_copy(dwo.at[rows(s * rb + 32, 16)], b_ref.at[p, pl.ds(208, 16)], sems.at[3]).start()

    @pl.when(ids[1] == 0)
    def _():
        store_wo(keep, send)

    @pl.when(ids[1] != 0)
    def _():
        store_wo(send, keep)

    z[...] = dot_t(hid_low[...], wo[...])
    heads = width // HD
    head_of = lax.broadcasted_iota(jnp.int32, (16, width), 1) // HD
    pick = (head_of == lax.broadcasted_iota(jnp.int32, (16, width), 0)).astype(FL).astype(BF)
    stats[...] = jnp.zeros(stats.shape, FL)
    stats[0 : heads // 2, :] = lse0[0 : heads // 2, :]
    stats[heads // 2 : heads, :] = lse1[0 : heads // 2, :]

    def last(r, i):
        d_low = z[r, :].astype(BF)
        pay[r, 0:width] = d_low
        exact = jnp.concatenate([exact0[r, :], exact1[r, :]], 1)
        prod = d_low.astype(FL) * exact
        delta = jnp.zeros((16, rc), FL)
        for _ in range(3):
            piece = prod.astype(BF)
            delta = delta + dot_t(pick, piece)
            prod = prod - piece.astype(FL)
        stats[16:32, r] = delta

    row_loop(last)
    st = stats[...].T
    pieces = []
    for _ in range(3):
        piece = st.astype(BF).astype(FL)
        pieces.append(piece)
        st = st - piece
    pieces.append(jnp.zeros_like(st))
    pay[:, width:] = jnp.concatenate(pieces, 1).astype(BF)
    wait_all(keep, sems.at[3])
    wait_all(send, sems.at[3])


def middle(ids, pool, att0, att1, exact0, exact1, lse0, lse1, cot, vec, upb, sets, set_rows):
    n, width = pool.shape
    ff = upb.shape[1]
    parts = ff // width
    whole = lambda i, *_: (0, 0)
    full = lambda x: pl.BlockSpec(x.shape, whole)
    shapes = [
        jax.ShapeDtypeStruct((n, width), BF),
        jax.ShapeDtypeStruct((n, width + 128), BF),
        jax.ShapeDtypeStruct((32, n), FL),
        jax.ShapeDtypeStruct((n, width), FL),
        jax.ShapeDtypeStruct((8, width), FL),
        jax.ShapeDtypeStruct((8, ff), FL),
    ]
    big = jax.ShapeDtypeStruct((NB, set_rows, width), BF)
    return pl.pallas_call(
        middle_kernel,
        name="middle",
        grid_spec=pltpu.PrefetchScalarGridSpec(
            num_scalar_prefetch=1,
            grid=(1,),
            in_specs=[full(pool)]
            + [full(x) for x in (att0, att1, exact0, exact1, lse0, lse1, cot, vec, upb)]
            + [ANY] * 4,
            out_specs=[full(x) for x in shapes] + [ANY, ANY],
            scratch_shapes=[
                pltpu.VMEM((width, width), BF),
                pltpu.VMEM((parts, width, width), BF),
                pltpu.VMEM((ff, width), BF),
                pltpu.VMEM((parts, n, width), BF),
                pltpu.VMEM((parts, n, width), FL),
                pltpu.VMEM((n, width), FL),
                pltpu.VMEM((n, width), FL),
                pltpu.VMEM((n, width), BF),
                pltpu.VMEM((n, width), FL),
                pltpu.VMEM((n, 128), FL),
                pltpu.VMEM((parts, width, width), BF),
                pltpu.VMEM((ff, width), BF),
                pltpu.VMEM((width, width), BF),
                pltpu.VMEM((n, width), BF),
                pltpu.SemaphoreType.DMA((4,)),
            ],
        ),
        out_shape=shapes + [big, big],
        compiler_params=params(),
    )(ids, pool, att0, att1, exact0, exact1, lse0, lse1, cot, vec, upb, *sets)


def weights_kernel(ids, pool, tok, dq0, dq1, dk, dv, gvec, gup, sl0, sl1, keep, send, dwq, dwk, dwv, bias, sems):
    width = tok.shape[1]
    ff = gup.shape[1]
    rb = width // NB
    dq = jnp.concatenate([dq0[...], dq1[...]], 1)
    dwq[...] = t_dot(pool[...].astype(BF), dq).astype(BF)
    dwk[...] = t_dot(tok[...], dk[...]).astype(BF)
    dwv[...] = t_dot(tok[...], dv[...]).astype(BF)
    row = lax.broadcasted_iota(jnp.int32, (16, width), 0)
    g = jnp.concatenate([gvec[...], jnp.zeros((8, width), FL)], 0)
    g = jnp.where(row == 0, rows_sum(dq.astype(FL)), g)
    g = jnp.where(row == 1, rows_sum(dv[...].astype(FL)), g)
    block_of = div_rb(lax.broadcasted_iota(jnp.int32, (16, width), 1))
    parts = []
    for p in range(NB):
        parts.append(jnp.where(block_of == (ids[0] ^ rel_b(p)), g, 0.0).astype(BF))
    total = dot_t(jnp.concatenate(parts, 0), spread_matrix(128, width, rb))
    row = lax.broadcasted_iota(jnp.int32, (16, ff), 0)
    block_of = div_rb(lax.broadcasted_iota(jnp.int32, (16, ff), 1))
    block_of = jnp.where((row >= 8) & (row < 12), block_of - row + 8, -1)
    up = jnp.concatenate([gup[...], gup[...]], 0)
    parts = []
    for p in range(NB):
        parts.append(jnp.where(block_of == 4 * (ids[0] ^ rel_b(p)), up, 0.0).astype(BF))
    total = total + dot_t(jnp.concatenate(parts, 0), spread_matrix(128, ff, rb))
    line = jnp.zeros((1, 128), FL)
    lane = lax.broadcasted_iota(jnp.int32, (1, 128), 1)
    for half, sl in enumerate((sl0, sl1)):
        pairs = sl.shape[0] // 8
        for j in range(pairs):
            x = rows_sum(sl[8 * j : 8 * j + 8, :])
            for i in range(2):
                value = jnp.sum(x[:, QB * i : QB * i + QB], 1, keepdims=True)
                line = jnp.where(lane == 2 * pairs * half + 2 * j + i, -value, line)
    row = lax.broadcasted_iota(jnp.int32, (16 * NB, 128), 0)
    total = jnp.where((row & 15) == 12, line, total)
    bias[...] = jnp.zeros(bias.shape, BF)
    bias[:, 0:128] = total.astype(BF)

    def rows(r, size):
        return pl.ds(pl.multiple_of(r, 16), size)

    def store_sets(a_ref, b_ref):
        def go(src, dst):
            pltpu.make_async_copy(src, dst, sems.at[0]).start()

        for p in range(NB):
            s = ids[0] ^ rel_a(p)
            go(dwq.at[rows(s * rb, 48)], a_ref.at[p, pl.ds(0, 48)])
            go(dwk.at[rows(s * rb, 32)], a_ref.at[p, pl.ds(48, 32)])
            s = ids[0] ^ rel_b(p)
            go(dwk.at[rows(s * rb + 32, 16)], b_ref.at[p, pl.ds(0, 16)])
            go(dwv.at[rows(s * rb, 48)], b_ref.at[p, pl.ds(16, 48)])
            go(bias.at[pl.ds(16 * p, 16)], b_ref.at[p, pl.ds(64, 16)])

    @pl.when(ids[1] == 0)
    def _():
        store_sets(keep, send)

    @pl.when(ids[1] != 0)
    def _():
        store_sets(send, keep)

    wait_all(keep, sems.at[0])
    wait_all(send, sems.at[0])


def weight_grads(ids, pool, tok, dq0, dq1, dk, dv, gvec, gup, sl0, sl1, set_rows):
    width = tok.shape[1]
    full = lambda x: pl.BlockSpec(x.shape, lambda i, *_: (0, 0))
    big = jax.ShapeDtypeStruct((NB, set_rows, width), BF)
    square = pltpu.VMEM((width, width), BF)
    return pl.pallas_call(
        weights_kernel,
        name="weight_grads",
        grid_spec=pltpu.PrefetchScalarGridSpec(
            num_scalar_prefetch=1,
            grid=(1,),
            in_specs=[full(x) for x in (pool, tok, dq0, dq1, dk, dv, gvec, gup, sl0, sl1)],
            out_specs=[ANY, ANY],
            scratch_shapes=[
                square,
                square,
                square,
                pltpu.VMEM((16 * NB, width), BF),
                pltpu.SemaphoreType.DMA((1,)),
            ],
        ),
        out_shape=[big, big],
        compiler_params=params(),
    )(ids, pool, tok, dq0, dq1, dk, dv, gvec, gup, sl0, sl1)


def tokens_kernel(mixed, dq0, dq1, dk, dv, wq, wk, wv, out, acc):
    half = mixed.shape[0]
    dq = jnp.concatenate([dq0[...], dq1[...]], 1)
    up = 0.5 * (mixed[...] + dot_t(dq, wq[...]))
    down = dot_t(dk[...], wk[...]) + dot_t(dv[...], wv[...])
    for j in range(mixed.shape[1] // 128):
        cols = slice(128 * j, 128 * j + 128)
        for i in range(2):
            acc[j, pl.ds(i, half, stride=2)] = up[:, cols]
        out[:, cols] = acc[j] + down[:, cols]


def token_grads(mixed, dq0, dq1, dk, dv, wq, wk, wv):
    rows, width = dk.shape
    step = 512
    half = pl.BlockSpec((step // 2, width), lambda i: (i, 0))
    block = pl.BlockSpec((step, width), lambda i: (i, 0))
    whole = pl.BlockSpec((width, width), lambda i: (0, 0))
    thin = pl.BlockSpec((step // 2, width // 2), lambda i: (i, 0))
    return pl.pallas_call(
        tokens_kernel,
        name="token_grads",
        grid=(rows // step,),
        in_specs=[half, thin, thin, block, block, whole, whole, whole],
        out_specs=block,
        out_shape=jax.ShapeDtypeStruct((rows, width), FL),
        scratch_shapes=[pltpu.VMEM((width // 128, step, 128), FL)],
        compiler_params=params(),
    )(mixed, dq0, dq1, dk, dv, wq, wk, wv)


def blocks_of(x):
    return x.reshape(NB, x.shape[0] // NB, x.shape[1])


def column_parts(x, width):
    return jnp.concatenate([x[..., width * c : width * c + width] for c in range(x.shape[-1] // width)], -2)


def bias_block(small, up, width):
    rb = small[0].shape[-1]
    rows = jnp.stack(list(small) + [up[..., rb * c : rb * c + rb] for c in range(4)], -2)
    pad = [(0, 0)] * (rows.ndim - 2) + [(0, 4), (0, width - rb)]
    return jnp.pad(rows, pad)


def pack(wq, wk, wv, wo, w1, w2, bias, width):
    a1 = jnp.concatenate([wq, wk[..., :32, :]], -2)
    b1 = jnp.concatenate([wk[..., 32:, :], wv, bias], -2)
    a2 = jnp.concatenate([w2, wo[..., :32, :]], -2)
    b2 = jnp.concatenate([column_parts(w1, width), wo[..., 32:, :], wo[..., 32:, :]], -2)
    return a1, b1, a2, b2


def unpack(a1, b1, a2, b2, width):
    wq = a1[..., :48, :]
    wk = jnp.concatenate([a1[..., 48:, :], b1[..., :16, :]], -2)
    wv = b1[..., 16:64, :]
    bias = b1[..., 64:, :]
    wo = jnp.concatenate([a2[..., 192:, :], b2[..., 192:208, :]], -2)
    w2 = a2[..., :192, :]
    parts = 4
    w1 = jnp.concatenate([b2[..., 48 * c : 48 * c + 48, :] for c in range(parts)], -1)
    return wq, wk, wv, wo, w1, w2, bias


def pack_kernel(ids, wq, wk, wv, wo, w1, w2, b_up, *refs):
    vectors, (first, second, bias) = refs[:8], refs[8:]
    rb, width = wq.shape

    @pl.when(ids[1] == 0)
    def _():
        first[0, 0:48] = wq[...].astype(BF)
        first[0, 48:80] = wk[0:32].astype(BF)
        second[0, 0:192] = w2[...].astype(BF)
        second[0, 192:224] = wo[0:32].astype(BF)

    @pl.when(ids[1] != 0)
    def _():
        bias[...] = jnp.zeros(bias.shape, FL)
        for i, x in enumerate(vectors):
            bias[i : i + 1, 0:rb] = x[...]
        for c in range(4):
            bias[8 + c : 9 + c, 0:rb] = b_up[:, rb * c : rb * c + rb]
        first[0, 0:16] = wk[32:48].astype(BF)
        first[0, 16:64] = wv[...].astype(BF)
        first[0, 64:80] = bias[...].astype(BF)
        for c in range(4):
            second[0, 48 * c : 48 * c + 48] = w1[:, width * c : width * c + width].astype(BF)
        second[0, 192:208] = wo[32:48].astype(BF)
        second[0, 208:224] = wo[32:48].astype(BF)


def pack_own(ids, masters, b_up, vectors):
    width = masters[0].shape[1]
    args = list(masters) + [b_up[None]] + [x[None] for x in vectors]
    full = lambda x: pl.BlockSpec(x.shape, lambda i, *_: (0,) * len(x.shape))
    shapes = [jax.ShapeDtypeStruct((1, 80, width), BF), jax.ShapeDtypeStruct((1, 224, width), BF)]
    return pl.pallas_call(
        pack_kernel,
        name="pack",
        grid_spec=pltpu.PrefetchScalarGridSpec(
            num_scalar_prefetch=1,
            grid=(1,),
            in_specs=[full(x) for x in args],
            out_specs=[full(x) for x in shapes],
            scratch_shapes=[pltpu.VMEM((16, width), FL)],
        ),
        out_shape=shapes,
        compiler_params=params(),
    )(ids, *args)


def after(x, *done):
    return lax.optimization_barrier((x,) + done)[0]


def local(
    tokens,
    cotangent,
    lengths,
    w_query,
    b_query,
    w_key,
    w_value,
    b_value,
    w_output,
    b_output,
    gain_attn,
    shift_attn,
    w_up,
    b_up,
    w_down,
    b_down,
    gain_ffn,
    shift_ffn,
    distance_slope,
):
    rows_here, width = tokens.shape
    ff = w_up.shape[1]
    own = rows_here // 2
    halo = rows_here // 2
    seq = lax.axis_size("seq")
    devices = seq * lax.axis_size("dp")
    direct = seq == NB
    order = ("dp", "seq")
    up_pairs = [(i, i + 1) for i in range(devices - 1)]
    down_pairs = [(i + 1, i) for i in range(devices - 1)]

    masters = (w_query, w_key, w_value, w_output, w_up, w_down)
    vectors = (b_query, b_value, b_output, gain_attn, shift_attn, b_down, gain_ffn, shift_ffn)
    if direct:
        core = lax.axis_index("dp")
        ids = jnp.stack([lax.axis_index("seq"), core]).astype(jnp.int32)
        first, second = pack_own(ids, masters, b_up, vectors)
        low_tokens = lax.ppermute(tokens[rows_here - halo :], order, up_pairs)
        x = jnp.concatenate([first, exchange(first, 8, 8)], 0)
        x = jnp.concatenate([x, exchange(x, 4, 4)], 0)
        y0 = after(second, x)
        x1, y1, low_tokens = lax.optimization_barrier((exchange(x, 2, 1), exchange(y0, 8, 8), low_tokens))
        low1 = jnp.concatenate([x, x1], 0)
        y = jnp.concatenate([y0, y1], 0)
        high_tokens = lax.ppermute(after(tokens[:halo], x1), order, down_pairs)
        high1, olow1, y1, high_tokens = lax.optimization_barrier(
            (exchange(low1, 1, 2), swap_core(low1), exchange(y, 4, 4), high_tokens)
        )
        sets1 = (low1, high1, olow1, swap_core(high1))
        y = jnp.concatenate([y, y1], 0)
    else:
        ids = jnp.zeros((2,), jnp.int32)
        gather = lambda x: lax.all_gather(x.astype(BF), "seq", axis=0, tiled=True)
        full = [blocks_of(gather(x)) for x in masters]
        small = [gather(x).reshape(NB, -1) for x in vectors]
        bias = bias_block(small, gather(b_up).reshape(NB, -1), width)
        a1, b1, a2, b2 = pack(*full, bias, width)
        at_a = jnp.array([rel_a(p) for p in range(NB)])
        at_b = jnp.array([rel_b(p) for p in range(NB)])
        sets1 = (a1[at_a[:8]], a1[at_a[8:]], b1[at_b[:8]], b1[at_b[8:]])
        sets2 = (a2[at_a[:8]], a2[at_a[8:]], b2[at_b[:8]], b2[at_b[8:]])
        low_tokens = lax.ppermute(tokens[rows_here - halo :], order, up_pairs)
        high_tokens = lax.ppermute(tokens[:halo], order, down_pairs)

    first_row = lax.axis_index(order) * rows_here
    total = devices * rows_here
    starts = 2 * (jnp.cumsum(lengths) - lengths)
    place = first_row - halo + 2 * jnp.arange(2 * own, dtype=jnp.int32)
    before = starts[None, :] <= place[:, None]
    begin = jnp.max(jnp.where(before, starts[None, :], 0), 1)
    end = jnp.min(jnp.where(before, total, starts[None, :]), 1)
    inside = (place >= 0) & (place < total)
    shift = first_row - halo
    begin = jnp.where(inside, begin - shift, 0)
    end = jnp.where(inside, end - shift, 0)
    bounds = jnp.pad(jnp.stack([begin, end], 0).astype(FL), ((0, 6), (0, 0)))
    blocks = 2 * own // QB
    chunks = (rows_here + 2 * halo) // KC
    low_chunk = jnp.min(jnp.where(inside, begin, 4 * total).reshape(blocks, QB), 1) // KC
    high_chunk = (jnp.max(end.reshape(blocks, QB), 1) + KC - 1) // KC
    index = jnp.arange(blocks)
    away = (index < blocks // 4) | (index >= blocks - blocks // 4)
    low_chunk = jnp.clip(low_chunk, jnp.where(away, chunks // 4, 0), chunks)
    high_chunk = jnp.clip(high_chunk, 0, jnp.where(away, chunks - chunks // 4, chunks))
    spans = jnp.concatenate([low_chunk, high_chunk]).astype(jnp.int32)

    tok_ext = jnp.concatenate([low_tokens, tokens, high_tokens], 0)

    slopes = distance_slope
    q, k, v, pool, wq, wk, wv, vec, upb = qkv(ids, tok_ext, sets1, ff)
    if direct:
        y1, k = lax.optimization_barrier((exchange(y, 2, 1), k))
        low2 = jnp.concatenate([y, y1], 0)
        bounds = after(bounds, low2)
    att0, exact0, lse0 = attend_forward(0, spans, slopes, q, k, v, bounds, own)
    att1, exact1, lse1 = attend_forward(1, spans, slopes, q, k, v, after(bounds, lse0), own)
    if direct:
        high2, lse1 = lax.optimization_barrier((exchange(low2, 1, 2), lse1))
        sets2 = (low2, high2, swap_core(low2), swap_core(high2))
    out, pay, stats, mixed, gvec, gup, keep2, send2 = middle(
        ids, pool, att0, att1, exact0, exact1, lse0, lse1, cotangent, vec, upb, sets2, 224
    )
    low_pay = lax.ppermute(pay[own // 2 :], order, up_pairs)
    high_pay = lax.ppermute(pay[: own // 2], order, down_pairs)
    dq0, dk0, dv0, sl0 = attend_own(0, spans, slopes, q, k, v, pay, stats, bounds)
    if direct:
        got = swap_core(send2)
        got, keep2, dq0, low_pay, high_pay = lax.optimization_barrier((got, keep2, dq0, low_pay, high_pay))
        up = add(keep2[8:], got[8:]).astype(BF)
        bounds = after(bounds, up)
    dq1, dk1, dv1, sl1 = attend_own(1, spans, slopes, q, k, v, pay, stats, bounds)
    if direct:
        got1 = exchange(up, 1, 2)
        got1, dq1 = lax.optimization_barrier((got1, dq1))
        up = add(keep2[4:8], got[4:8], got1[4:]).astype(BF)
        bounds = after(bounds, up)
    dk, dv = attend_halo(spans, slopes, q, k, v, low_pay, high_pay, bounds, dk0, dv0, dk1, dv1)
    if direct:
        got2 = exchange(up, 2, 1)
        got2, dk = lax.optimization_barrier((got2, dk))
        low = add(keep2[:4], got[:4], got1[:4])
        up = (low[2:] + got2[2:].astype(FL)).astype(BF)
        sl0 = after(sl0, up)
    keep1, send1 = weight_grads(ids, pool, tokens, dq0, dq1, dk, dv, gvec, gup, sl0, sl1, 80)
    if direct:
        core0 = lax.axis_index("dp") == 0
        got3 = exchange(up, 4, 4)
        got3, send1 = lax.optimization_barrier((got3, send1))
        low = low[:2] + got2[:2].astype(FL)
        up = (low[1:] + got3[1:].astype(FL)).astype(BF)
        low = low[:1] + got3[:1].astype(FL)
        got = swap_core(send1)
        got4 = exchange(up, 8, 8)
        part = add(keep1[8:], got[8:]).astype(BF)
        got1 = exchange(part, 1, 2)
        mixed = after(mixed, part)
    grad_tokens = token_grads(mixed, dq0, dq1, dk, dv, wq, wk, wv)

    if direct:
        got1, grad_tokens = lax.optimization_barrier((got1, grad_tokens))
        part = add(keep1[4:8], got[4:8], got1[4:]).astype(BF)
        got2 = exchange(part, 2, 1)
        mine = (low + got4.astype(FL))[0]
        other = swap_core(mine)
        a2, b2 = jnp.where(core0, mine, other), jnp.where(core0, other, mine)
        low = add(keep1[:4], got[:4], got1[:4])
        part = (low[2:] + got2[2:].astype(FL)).astype(BF)
        low = low[:2] + got2[:2].astype(FL)
        got3 = exchange(part, 4, 4)
        part = (low[1:] + got3[1:].astype(FL)).astype(BF)
        low = low[:1] + got3[:1].astype(FL)
        mine = (low + exchange(part, 8, 8).astype(FL))[0]
        other = swap_core(mine)
        a1, b1 = jnp.where(core0, mine, other), jnp.where(core0, other, mine)
        gq, gk, gv, go, g1, g2, gb = unpack(a1, b1, a2, b2, width)
        rb = width // NB
        small = [gb[i, :rb] for i in range(8)]
        g_up = jnp.concatenate([gb[8 + c, :rb] for c in range(4)], 0)
        g_slope = gb[12, : distance_slope.shape[0]]
    else:
        inv_a = [0] * NB
        inv_b = [0] * NB
        for p in range(NB):
            inv_a[rel_a(p)] = p
            inv_b[rel_b(p)] = p
        inv_a = jnp.array(inv_a)
        inv_b = jnp.array(inv_b)
        gq, gk, gv, go, g1, g2, gb = unpack(keep1[inv_a], send1[inv_b], keep2[inv_a], send2[inv_b], width)
        rb = width // NB

        def share(x):
            x = lax.psum(x.astype(FL), "dp")
            return lax.psum_scatter(x, "seq", scatter_dimension=0, tiled=True)

        gq, gk, gv, go, g1, g2 = [share(x.reshape(-1, x.shape[-1])) for x in (gq, gk, gv, go, g1, g2)]
        small = [share(gb[:, i, :rb].reshape(-1)) for i in range(8)]
        g_up = share(gb[:, 8:12, :rb].reshape(-1))
        g_slope = lax.psum(gb[0, 12, : distance_slope.shape[0]].astype(FL), order)
    return (
        out,
        grad_tokens,
        gq,
        small[0],
        gk,
        gv,
        small[1],
        go,
        small[2],
        small[3],
        small[4],
        g1,
        g_up,
        g2,
        small[5],
        small[6],
        small[7],
        g_slope,
    )


def solution(mesh):
    tall = P(("dp", "seq"), None)
    mat = P("seq", None)
    vec = P("seq")
    return jax.shard_map(
        local,
        mesh=mesh,
        in_specs=(tall, tall, P(), mat, vec, mat, mat, vec, mat, vec, vec, vec, mat, vec, mat, vec, vec, vec, P()),
        out_specs=(tall, tall, mat, vec, mat, mat, vec, mat, vec, vec, vec, mat, vec, mat, vec, vec, vec, P()),
        check_vma=False,
    )
```

```python
import functools

import jax
import jax.numpy as jnp
from jax import lax
from jax.experimental import pallas as pl
from jax.experimental.pallas import tpu as pltpu
from jax.sharding import PartitionSpec as P

HD = 64
NB = 16
QB = 128
KC = 256
EPS = 1e-05
FAR = 1e12
BF = jnp.bfloat16
FL = jnp.float32


def rel_a(p):
    return (p & 1) * 8 + ((p >> 1) & 1) * 4 + ((p >> 2) & 1) * 2 + ((p >> 3) & 1)


def rel_b(p):
    return (p & 1) * 4 + ((p >> 1) & 1) * 8 + ((p >> 2) & 1) + ((p >> 3) & 1) * 2


def dot(a, b):
    return jnp.dot(a, b, preferred_element_type=FL)


def dot_t(a, b):
    return lax.dot_general(a, b, (((1,), (1,)), ((), ())), preferred_element_type=FL)


def t_dot(a, b):
    return lax.dot_general(a, b, (((0,), (0,)), ((), ())), preferred_element_type=FL)


def exchange(x, stride_a, stride_b):
    n = lax.axis_size("seq")
    pairs = [(s, s ^ stride_a) for s in range(n)] + [(n + s, n + (s ^ stride_b)) for s in range(n)]
    return lax.ppermute(x, ("dp", "seq"), pairs)


def swap_core(x):
    return lax.ppermute(x, "dp", [(0, 1), (1, 0)])


def add(*xs):
    total = xs[0].astype(FL)
    for x in xs[1:]:
        total = total + x.astype(FL)
    return total


def params(**kw):
    return pltpu.CompilerParams(vmem_limit_bytes=58 * 1024 * 1024, **kw)


def takes(us):
    return pl.CostEstimate(flops=us * 1150 * 10**6, transcendentals=0, bytes_accessed=us * 3600 * 10**3)


ANY = pl.BlockSpec(memory_space=pl.ANY)


def load_sets(ids, low, high, olow, ohigh, copies_a, copies_b):
    def start(a_refs, b_refs):
        for p in range(NB):
            copies_a(a_refs[p // 8].at[p % 8], ids[0] ^ rel_a(p), p)
            copies_b(b_refs[p // 8].at[p % 8], ids[0] ^ rel_b(p), p)

    @pl.when(ids[1] == 0)
    def _():
        start((low, high), (olow, ohigh))

    @pl.when(ids[1] != 0)
    def _():
        start((olow, ohigh), (low, high))


def wait_all(ref, sem):
    pltpu.make_async_copy(ref, ref, sem).wait()


def spread_matrix(rows, cols, rb):
    lanes = lax.broadcasted_iota(jnp.int32, (rows, cols), 1)
    return (lax.broadcasted_iota(jnp.int32, (rows, cols), 0) == lanes - rb * div_rb(lanes)).astype(FL).astype(BF)


def div_rb(x):
    return (x * 21846) >> 20


def qkv_kernel(
    ids, tok, low, high, olow, ohigh, q_out, k_out, v_out, pool_out, wq, wk, wv, vec_out, up_out, bias, x32, sems
):
    width = tok.shape[1]
    rb = width // NB

    @pl.when(pl.program_id(0) == 0)
    def _():
        def rows(r, n):
            return pl.ds(pl.multiple_of(r, 16), n)

        def copies_a(block, s, p):
            pltpu.make_async_copy(block.at[pl.ds(0, 48)], wq.at[rows(s * rb, 48)], sems.at[0]).start()
            pltpu.make_async_copy(block.at[pl.ds(48, 32)], wk.at[rows(s * rb, 32)], sems.at[1]).start()

        def copies_b(block, s, p):
            pltpu.make_async_copy(block.at[pl.ds(0, 16)], wk.at[rows(s * rb + 32, 16)], sems.at[1]).start()
            pltpu.make_async_copy(block.at[pl.ds(16, 48)], wv.at[rows(s * rb, 48)], sems.at[2]).start()
            pltpu.make_async_copy(block.at[pl.ds(64, 16)], bias.at[pl.ds(16 * p, 16)], sems.at[3]).start()

        load_sets(ids, low, high, olow, ohigh, copies_a, copies_b)
        wait_all(wq, sems.at[0])
        wait_all(wk, sems.at[1])
        wait_all(wv, sems.at[2])
        wait_all(bias, sems.at[3])
        parts = bias[:, 0:128]
        wide = dot(parts, spread_matrix(128, width, rb))
        block_of = div_rb(lax.broadcasted_iota(jnp.int32, (16, width), 1))
        total = jnp.zeros((16, width), FL)
        for p in range(NB):
            total = total + jnp.where(block_of == (ids[0] ^ rel_b(p)), wide[16 * p : 16 * p + 16], 0.0)
        vec_out[...] = total
        ff = up_out.shape[1]
        wide = dot(parts, spread_matrix(128, ff, rb))
        block_of = div_rb(lax.broadcasted_iota(jnp.int32, (16, ff), 1))
        row = lax.broadcasted_iota(jnp.int32, (16, ff), 0)
        block_of = jnp.where((row >= 8) & (row < 12), block_of - row + 8, -1)
        total = jnp.zeros((16, ff), FL)
        for p in range(NB):
            total = total + jnp.where(block_of == 4 * (ids[0] ^ rel_b(p)), wide[16 * p : 16 * p + 16], 0.0)
        up_out[...] = jnp.broadcast_to(jnp.sum(total, 0, keepdims=True), up_out.shape)

    pooled = project(tok, wq, wk, wv, vec_out, q_out, k_out, v_out, x32)
    pool_out[...] = pooled


def project(tok, wq, wk, wv, vec, q_out, k_out, v_out, x32):
    x = tok[...]
    width = x.shape[1]
    half = x.shape[0] // 2
    k_out[...] = dot(x, wk[...]).astype(BF)
    v_out[...] = (dot(x, wv[...]) + vec[1:2]).astype(BF)
    pooled = []
    for j in range(width // 128):
        x32[j] = x[:, 128 * j : 128 * j + 128].astype(FL)
        pooled.append((x32[j, pl.ds(0, half, stride=2)] + x32[j, pl.ds(1, half, stride=2)]) * 0.5)
    pooled = jnp.concatenate(pooled, 1)
    q = (dot(pooled.astype(BF), wq[...]) + vec[0:1]).astype(BF)
    q_out[...] = (q.astype(FL) * HD**-0.5).astype(BF)
    return pooled


def qkv(ids, tokens, sets, ff):
    rows, width = tokens.shape
    step = 512
    whole = lambda i, *_: (0, 0)
    square = jax.ShapeDtypeStruct((width, width), BF)
    thin = pl.BlockSpec((step // 2, width), lambda i, *_: (i, 0))
    block = pl.BlockSpec((step, width), lambda i, *_: (i, 0))
    return pl.pallas_call(
        qkv_kernel,
        name="qkv",
        cost_estimate=takes(9),
        grid_spec=pltpu.PrefetchScalarGridSpec(
            num_scalar_prefetch=1,
            grid=(rows // step,),
            in_specs=[block, ANY, ANY, ANY, ANY],
            out_specs=[thin, block, block, thin]
            + [pl.BlockSpec((width, width), whole)] * 3
            + [pl.BlockSpec((16, width), whole), pl.BlockSpec((8, ff), whole)],
            scratch_shapes=[
                pltpu.VMEM((16 * NB, width), BF),
                pltpu.VMEM((width // 128, step, 128), FL),
                pltpu.SemaphoreType.DMA((4,)),
            ],
        ),
        out_shape=[
            jax.ShapeDtypeStruct((rows // 2, width), BF),
            jax.ShapeDtypeStruct((rows, width), BF),
            jax.ShapeDtypeStruct((rows, width), BF),
            jax.ShapeDtypeStruct((rows // 2, width), FL),
            square,
            square,
            square,
            jax.ShapeDtypeStruct((16, width), FL),
            jax.ShapeDtypeStruct((8, ff), FL),
        ],
        compiler_params=params(),
    )(ids, tokens, *sets)


def halo_qkv_kernel(low_a, low_b, high_a, high_b, wq, wk, wv, vec, q_out, k_out, v_out, x32):
    for side, parts in enumerate(((low_a, low_b), (high_a, high_b))):
        tok = jnp.concatenate([x[...] for x in parts], 0)
        project(tok, wq, wk, wv, vec, q_out.at[side], k_out.at[side], v_out.at[side], x32)


def halo_qkv(low_a, low_b, high_a, high_b, wq, wk, wv, vec):
    rows, width = low_a.shape
    rows = 2 * rows
    full = lambda x: pl.BlockSpec(x.shape, lambda i: (0,) * len(x.shape))
    args = (low_a, low_b, high_a, high_b, wq, wk, wv, vec)
    shapes = [
        jax.ShapeDtypeStruct((2, rows // 2, width), BF),
        jax.ShapeDtypeStruct((2, rows, width), BF),
        jax.ShapeDtypeStruct((2, rows, width), BF),
    ]
    return pl.pallas_call(
        halo_qkv_kernel,
        name="halo_qkv",
        cost_estimate=takes(7),
        grid=(1,),
        in_specs=[full(x) for x in args],
        out_specs=[full(x) for x in shapes],
        out_shape=shapes,
        scratch_shapes=[pltpu.VMEM((width // 128, rows, 128), FL)],
        compiler_params=params(),
    )(*args)


def two_heads(x):
    lane = lax.broadcasted_iota(jnp.int32, x.shape, 1)
    zero = jnp.zeros_like(x)
    return jnp.concatenate([jnp.where(lane < HD, x, zero), jnp.where(lane < HD, zero, x)], 0)


def one_block(x):
    r = x.shape[1] // 2
    line = lax.broadcasted_iota(jnp.int32, (128, r), 0)
    return jnp.where(line < HD, x[:, :r], x[:, r:]).T


def distances(bounds, row, c):
    low = bounds[0:1, pl.ds(row, QB)]
    high = bounds[1:2, pl.ds(row, QB)]
    query = (2 * (row + lax.broadcasted_iota(jnp.int32, (KC, QB), 1))).astype(FL) + 0.5
    key = (c * KC + lax.broadcasted_iota(jnp.int32, (KC, QB), 0)).astype(FL)
    far = jnp.where((key >= low) & (key < high), jnp.abs(query - key), FAR)
    return jnp.concatenate([far, far], 1)


def fold(x, f):
    n = x.shape[0] // 8
    parts = [x[8 * i : 8 * i + 8] for i in range(n)]
    while len(parts) > 1:
        parts = [f(parts[2 * i], parts[2 * i + 1]) for i in range(len(parts) // 2)]
    return parts[0]


def slope_line(slopes, head):
    lane = lax.broadcasted_iota(jnp.int32, (1, 2 * QB), 1)
    return jnp.where(lane < QB, slopes[head], slopes[head + 1])


def span_of(own, halo, into):
    edge = halo.shape[1]
    into[0:edge] = halo[0]
    into[edge : edge + own.shape[0]] = own[...]
    into[edge + own.shape[0] :] = halo[1]


def forward_kernel(
    half, spans, slopes, q, ko, kh, vo, vh, bounds, o_out, exact_out, lse_out, s_scr, k, v, vt, q2, top, total, acc, rest
):
    pairs = q.shape[1] // 128
    head0 = half * 2 * pairs
    span_of(ko, kh, k)
    span_of(vo, vh, v)
    q_first = q.shape[0] // 2
    slope = [slope_line(slopes, head0 + 2 * j) for j in range(pairs)]
    for c in range(k.shape[0] // KC):
        for j in range(pairs):
            vt[c, j] = v[KC * c : KC * c + KC, 128 * j : 128 * j + 128].T

    def query_block(b, _):
        row = pl.multiple_of(q_first + b * QB, QB)
        out_rows = pl.ds(pl.multiple_of(b * QB, QB), QB)
        block = row // QB
        c0 = spans[block]
        c1 = spans[spans.shape[0] // 2 + block]
        for j in range(pairs):
            q2[j] = two_heads(q[out_rows, 128 * j : 128 * j + 128])
        top[...] = jnp.full(top.shape, -3e38, FL)
        total[...] = jnp.zeros(total.shape, FL)
        acc[...] = jnp.zeros(acc.shape, FL)
        rest[...] = jnp.zeros(rest.shape, FL)

        def score(c, _):
            far = distances(bounds, row, c)
            keys = pl.ds(pl.multiple_of(c * KC, KC), KC)
            for j in range(pairs):
                s = dot_t(k[keys, 128 * j : 128 * j + 128], q2[j]) - slope[j] * far
                s_scr[c - c0, j] = s
                top[j] = jnp.maximum(top[j], fold(s, jnp.maximum))
            return 0

        lax.fori_loop(c0, c1, score, 0)
        peak = [jnp.max(top[j], 0, keepdims=True) for j in range(pairs)]

        def exponent(c, _):
            for j in range(pairs):
                e = jnp.exp(s_scr[c - c0, j] - peak[j])
                s_scr[c - c0, j] = e
                total[j] = total[j] + fold(e, jnp.add)
            return 0

        lax.fori_loop(c0, c1, exponent, 0)
        inverse = []
        for j in range(pairs):
            l = jnp.sum(total[j], 0, keepdims=True)
            t = peak[j] + jnp.log(l)
            inverse.append(1.0 / l)
            lse_out[2 * j : 2 * j + 1, out_rows] = t[:, :QB]
            lse_out[2 * j + 1 : 2 * j + 2, out_rows] = t[:, QB:]

        def attend(c, _):
            for j in range(pairs):
                p = s_scr[c - c0, j] * inverse[j]
                high = p.astype(BF)
                low = (p - high.astype(FL)).astype(BF)
                values = vt[c, j]
                acc[j] = acc[j] + dot(values, high)
                rest[j] = rest[j] + dot(values, low)
            return 0

        lax.fori_loop(c0, c1, attend, 0)
        for j in range(pairs):
            cols = slice(128 * j, 128 * j + 128)
            o_out[out_rows, cols] = one_block(acc[j]).astype(BF)
            exact_out[out_rows, cols] = one_block(acc[j] + rest[j])
        return 0

    lse_out[...] = jnp.zeros(lse_out.shape, FL)
    lax.fori_loop(0, o_out.shape[0] // QB, query_block, 0)


def key_specs(keys, halos, wide, half):
    return [
        pl.BlockSpec((keys.shape[0], wide), lambda i, *_: (0, half)),
        pl.BlockSpec((2, halos.shape[1], wide), lambda i, *_: (0, 0, half)),
    ]


def attend_forward(half, spans, slopes, q, k, kh, v, vh, bounds):
    own = q.shape[0]
    wide = q.shape[1] // 2
    pairs = wide // 128
    keys = k.shape[0] + 2 * kh.shape[1]
    chunks = keys // KC
    col = lambda i, *_: (0, half)
    zero = lambda i, *_: (0, 0)
    return pl.pallas_call(
        functools.partial(forward_kernel, half),
        name=f"attend_forward_{half}",
        cost_estimate=takes(15),
        grid_spec=pltpu.PrefetchScalarGridSpec(
            num_scalar_prefetch=2,
            grid=(1,),
            in_specs=[pl.BlockSpec((own, wide), col)]
            + key_specs(k, kh, wide, half)
            + key_specs(v, vh, wide, half)
            + [pl.BlockSpec(bounds.shape, zero)],
            out_specs=[
                pl.BlockSpec((own, wide), zero),
                pl.BlockSpec((own, wide), zero),
                pl.BlockSpec((8, own), zero),
            ],
            scratch_shapes=[
                pltpu.VMEM((chunks, pairs, KC, 2 * QB), FL),
                pltpu.VMEM((keys, wide), BF),
                pltpu.VMEM((keys, wide), BF),
                pltpu.VMEM((chunks, pairs, 128, KC), BF),
                pltpu.VMEM((pairs, 2 * QB, 128), BF),
                pltpu.VMEM((pairs, 8, 2 * QB), FL),
                pltpu.VMEM((pairs, 8, 2 * QB), FL),
                pltpu.VMEM((pairs, 128, 2 * QB), FL),
                pltpu.VMEM((pairs, 128, 2 * QB), FL),
            ],
        ),
        out_shape=[
            jax.ShapeDtypeStruct((own, wide), BF),
            jax.ShapeDtypeStruct((own, wide), FL),
            jax.ShapeDtypeStruct((8, own), FL),
        ],
        compiler_params=params(),
    )(spans, slopes, q, k, kh, v, vh, bounds)


def pieces(x):
    out = []
    for _ in range(3):
        y = x.astype(BF).astype(FL)
        out.append(y)
        x = x - y
    return out


def key_lines(side, kind):
    lane = lax.broadcasted_iota(jnp.int32, (KC, 128), 1)
    key = lax.broadcasted_iota(jnp.int32, (KC, 128), 0).astype(FL)
    x = jnp.where(lane < 3, 1.0, jnp.where(lane < 6, -side, jnp.where(lane < 9, side * key, 0.0)))
    return jnp.where(lane == kind, 1.0, x) if kind else x


def chunk_lines(base, away, side, limit):
    lane = lax.broadcasted_iota(jnp.int32, (KC, 128), 1)
    key = lax.broadcasted_iota(jnp.int32, (KC, 128), 0).astype(FL) + KC * away
    other = jnp.where(side * key < side * limit, 1.0, 0.0)
    x = base + jnp.where((lane >= 9) & (lane < 12), side * KC * away, 0.0)
    return jnp.where(lane == 12, other, x).astype(BF)


def value_lines():
    lane = lax.broadcasted_iota(jnp.int32, (KC, 128), 1)
    return (lane < 3).astype(FL).astype(BF)


def query_rows(lse, slope, spots, out_left, out_right):
    one = jnp.ones_like(lse)
    rows = pieces(-lse) + pieces(slope * spots) + pieces(slope * one) * 2
    rows += [-FAR * one, -FAR * out_left, -FAR * out_right, 0.0 * one]
    return jnp.concatenate(rows, 0).astype(BF)


def two_heads_t(x):
    line = lax.broadcasted_iota(jnp.int32, x.shape, 0)
    zero = jnp.zeros_like(x)
    return jnp.concatenate([jnp.where(line < HD, x, zero), jnp.where(line < HD, zero, x)], 1)


def block_setup(bounds, row):
    low = bounds[0:1, pl.ds(row, QB)]
    high = bounds[1:2, pl.ds(row, QB)]
    first = low[:, 0:1]
    last = high[:, QB - 1 : QB]
    base = (2 * row).astype(FL) if hasattr(row, "astype") else float(2 * row)
    out_left = jnp.where(low == first, 0.0, 1.0)
    out_right = jnp.where(high == last, 0.0, 1.0)
    spots = 2.0 * lax.broadcasted_iota(jnp.int32, (1, QB), 1).astype(FL) + 0.5
    return low - base, high - base, first - base, last - base - 0.5, twice(out_left), twice(out_right), twice(spots)


def twice(x):
    return jnp.concatenate([x, x], 1)


def fill_queries(j, q, da, lse, delta, slope, setup, q2, da2, qt, dat):
    out_left, out_right, spots = setup[4:]
    q2[j] = two_heads(q)
    da2[j] = two_heads(da)
    qt[j, 0:128] = two_heads_t(q.T)
    dat[j, 0:128] = two_heads_t(da.T)
    qt[j, 128:144] = query_rows(lse, slope, spots, out_left, out_right)
    rows = pieces(-delta) + [jnp.zeros((13, 2 * QB), FL)]
    dat[j, 128:144] = jnp.concatenate(rows, 0).astype(BF)


def own_kernel(
    half,
    spans,
    slopes,
    q,
    ko,
    kh,
    vo,
    vh,
    da,
    stats,
    bounds,
    dq_out,
    dk,
    dv,
    slope_out,
    k,
    v,
    kt,
    q2,
    da2,
    qt,
    dat,
    dq2,
    sl,
    base,
):
    pairs = q.shape[1] // 128
    head0 = half * 2 * pairs
    total_blocks = bounds.shape[1] // QB
    quarter = k.shape[0] // KC // 4
    first = total_blocks // 4
    slope = [slope_line(slopes, head0 + 2 * j) for j in range(pairs)]
    dk[...] = jnp.zeros(dk.shape, FL)
    dv[...] = jnp.zeros(dv.shape, FL)
    sl[...] = jnp.zeros(sl.shape, FL)
    qt[...] = jnp.zeros(qt.shape, BF)
    dat[...] = jnp.zeros(dat.shape, BF)
    span_of(ko, kh, k)
    span_of(vo, vh, v)
    line = lax.broadcasted_iota(jnp.int32, (16, KC), 0)
    spot = lax.broadcasted_iota(jnp.int32, (16, KC), 1).astype(FL)
    extra = jnp.where(line == 0, 1.0, jnp.where(line == 1, spot, 0.0)).astype(BF)
    for c in range(k.shape[0] // KC):
        for j in range(pairs):
            kt[c, j, 0:128] = k[KC * c : KC * c + KC, 128 * j : 128 * j + 128].T
            kt[c, j, 128:144] = extra
    base[0] = key_lines(1.0, 13)
    base[1] = key_lines(-1.0, 14)
    own_lines = key_lines(1.0, 0).astype(BF)
    ones = value_lines()

    def query_block(b, _):
        block = first + b
        row = pl.multiple_of(block * QB, QB)
        rows = pl.ds(pl.multiple_of(b * QB, QB), QB)
        c0 = spans[block]
        c1 = spans[total_blocks + block]
        setup = block_setup(bounds, row)
        low, high, limit_left, limit_right = setup[:4]
        spots = setup[6]
        for j in range(pairs):
            cols = slice(128 * j, 128 * j + 128)
            h = head0 + 2 * j
            lse = jnp.concatenate([stats[h : h + 1, rows], stats[h + 1 : h + 2, rows]], 1)
            delta = jnp.concatenate([stats[16 + h : 17 + h, rows], stats[17 + h : 18 + h, rows]], 1)
            fill_queries(j, q[rows, cols], da[rows, cols], lse, delta, slope[j], setup, q2, da2, qt, dat)
        dq2[...] = jnp.zeros(dq2.shape, FL)

        def step(c, lines, side, away, grads, wide):
            keys = pl.ds(pl.multiple_of(c * KC, KC), KC)
            col = [slice(128 * j, 128 * j + 128) for j in range(pairs)]
            s = [dot(jnp.concatenate([k[keys, col[j]], lines], 1), qt[j]) for j in range(pairs)]
            dp = [dot(jnp.concatenate([v[keys, col[j]], ones], 1), dat[j]) for j in range(pairs)]
            if wide is not None:
                s = [s[j] - slope[j] * wide for j in range(pairs)]
            p = [jnp.exp(x) for x in s]
            ds = [(p[j] * dp[j]).astype(BF) for j in range(pairs)]
            if grads:
                mine = pl.ds(pl.multiple_of((c - quarter) * KC, KC), KC)
                new_v = [dot(p[j].astype(BF), da2[j]) for j in range(pairs)]
                new_k = [dot(ds[j], q2[j]) for j in range(pairs)]
            r = [dot(kt[c, j], ds[j]) for j in range(pairs)]
            for j in range(pairs):
                if grads:
                    dv[mine, col[j]] = dv[mine, col[j]] + new_v[j]
                    dk[mine, col[j]] = dk[mine, col[j]] + new_k[j]
                dq2[j] = dq2[j] + r[j][0:128]
                part = side * ((spots - KC * away) * r[j][128:129] - r[j][129:130])
                if wide is not None:
                    part = part + jnp.sum(ds[j].astype(FL) * wide, 0, keepdims=True)
                sl[j] = sl[j] + part

        key = lax.broadcasted_iota(jnp.int32, (KC, QB), 0).astype(FL)
        over = 2.0 * jnp.maximum(key - spots[:, :QB], 0.0)
        wide = twice(jnp.where((key >= low) & (key < high), over, FAR))
        step(block, own_lines, 1.0, 0.0, True, wide)

        def other(c, grads):
            before = c < block
            side = jnp.where(before, 1.0, -1.0)
            away = (c - block).astype(FL)
            limit = jnp.where(before, limit_left, limit_right)
            step(c, chunk_lines(base[jnp.where(before, 0, 1)], away, side, limit), side, away, grads, None)

        def inside(i, _):
            other(jnp.where(i < block, i, i + 1), True)
            return 0

        left = jnp.maximum(jnp.minimum(c1, quarter) - c0, 0)
        right0 = jnp.maximum(c0, 3 * quarter)

        def outside(i, _):
            other(jnp.where(i < left, c0 + i, right0 + i - left), False)
            return 0

        lax.fori_loop(jnp.maximum(c0, quarter), jnp.minimum(c1, 3 * quarter) - 1, inside, 0)
        lax.fori_loop(0, left + jnp.maximum(c1 - right0, 0), outside, 0)
        for j in range(pairs):
            dq_out[rows, 128 * j : 128 * j + 128] = (one_block(dq2[j]) * HD**-0.5).astype(BF)
        return 0

    lax.fori_loop(0, da.shape[0] // QB, query_block, 0)
    slope_out[...] = jnp.zeros(slope_out.shape, FL)
    for j in range(pairs):
        slope_out[8 * j : 8 * j + 1] = sl[j]


def attend_own(half, spans, slopes, q, k, kh, v, vh, da, stats, bounds):
    own = stats.shape[1]
    wide = q.shape[1] // 2
    pairs = wide // 128
    keys = k.shape[0] + 2 * kh.shape[1]
    chunks = keys // KC
    col = lambda i, *_: (0, half)
    zero = lambda i, *_: (0, 0)
    return pl.pallas_call(
        functools.partial(own_kernel, half),
        name=f"attend_own_{half}",
        cost_estimate=takes(19),
        grid_spec=pltpu.PrefetchScalarGridSpec(
            num_scalar_prefetch=2,
            grid=(1,),
            in_specs=[pl.BlockSpec((own, wide), col)]
            + key_specs(k, kh, wide, half)
            + key_specs(v, vh, wide, half)
            + [
                pl.BlockSpec((own, wide), col),
                pl.BlockSpec(stats.shape, zero),
                pl.BlockSpec(bounds.shape, zero),
            ],
            out_specs=[
                pl.BlockSpec((own, wide), zero),
                pl.BlockSpec((keys // 2, wide), zero),
                pl.BlockSpec((keys // 2, wide), zero),
                pl.BlockSpec((8 * pairs, 2 * QB), zero),
            ],
            scratch_shapes=[
                pltpu.VMEM((keys, wide), BF),
                pltpu.VMEM((keys, wide), BF),
                pltpu.VMEM((chunks, pairs, 144, KC), BF),
                pltpu.VMEM((pairs, 2 * QB, 128), BF),
                pltpu.VMEM((pairs, 2 * QB, 128), BF),
                pltpu.VMEM((pairs, 256, 2 * QB), BF),
                pltpu.VMEM((pairs, 256, 2 * QB), BF),
                pltpu.VMEM((pairs, 128, 2 * QB), FL),
                pltpu.VMEM((pairs, 1, 2 * QB), FL),
                pltpu.VMEM((2, KC, 128), FL),
            ],
        ),
        out_shape=[
            jax.ShapeDtypeStruct((own, wide), BF),
            jax.ShapeDtypeStruct((keys // 2, wide), FL),
            jax.ShapeDtypeStruct((keys // 2, wide), FL),
            jax.ShapeDtypeStruct((8 * pairs, 2 * QB), FL),
        ],
        compiler_params=params(),
    )(spans, slopes, q, k, kh, v, vh, da, stats, bounds)


def halo_kernel(
    spans, slopes, q, k, v, low_pay, high_pay, bounds, dk0, dv0, dk1, dv1, dk_out, dv_out, q2, da2, qt, dat, st, dk, dv
):
    wide = dk0.shape[1]
    width = q.shape[2]
    pairs = width // 128
    total_blocks = bounds.shape[1] // QB
    quarter = k.shape[0] // KC // 2
    count = low_pay.shape[0] // QB
    dk[:, :wide] = dk0[...]
    dk[:, wide:] = dk1[...]
    dv[:, :wide] = dv0[...]
    dv[:, wide:] = dv1[...]
    qt[...] = jnp.zeros(qt.shape, BF)
    dat[...] = jnp.zeros(dat.shape, BF)
    ones = value_lines()
    for side, pay in enumerate((low_pay, high_pay)):
        x = pay[:, width : width + 128].astype(FL)
        st[side] = (x + pltpu.roll(x, 96, 1) + pltpu.roll(x, 64, 1)).T

    def query_block(i, _):
        side = i // count
        at = i - side * count
        block = jnp.where(side == 0, i, total_blocks - 2 * count + i)
        row = pl.multiple_of(block * QB, QB)
        rows = pl.ds(pl.multiple_of(at * QB, QB), QB)
        c0 = spans[block]
        c1 = spans[total_blocks + block]

        @pl.when(c0 < c1)
        def _():
            setup = block_setup(bounds, row)
            limit = jnp.where(side == 0, setup[3], setup[2])
            sign = jnp.where(side == 0, -1.0, 1.0)
            base = jnp.where(side == 0, key_lines(-1.0, 14), key_lines(1.0, 13))
            for j in range(pairs):
                cols = slice(128 * j, 128 * j + 128)
                h = 2 * j
                lse = jnp.concatenate([st[side, h : h + 1, rows], st[side, h + 1 : h + 2, rows]], 1)
                delta = jnp.concatenate([st[side, 16 + h : 17 + h, rows], st[side, 17 + h : 18 + h, rows]], 1)
                d = jnp.where(side == 0, low_pay[rows, cols], high_pay[rows, cols])
                fill_queries(
                    j, q[side, rows, cols], d, lse, delta, slope_line(slopes, h), setup, q2, da2, qt, dat
                )

            def step(c, _):
                mine = pl.ds(pl.multiple_of((c - quarter) * KC, KC), KC)
                lines = chunk_lines(base, (c - block).astype(FL), sign, limit)
                for j in range(pairs):
                    cols = slice(128 * j, 128 * j + 128)
                    p = jnp.exp(dot(jnp.concatenate([k[mine, cols], lines], 1), qt[j]))
                    dp = dot(jnp.concatenate([v[mine, cols], ones], 1), dat[j])
                    dv[mine, cols] = dv[mine, cols] + dot(p.astype(BF), da2[j])
                    dk[mine, cols] = dk[mine, cols] + dot((p * dp).astype(BF), q2[j])
                return 0

            lax.fori_loop(c0, c1, step, 0)

        return 0

    lax.fori_loop(0, 2 * count, query_block, 0)
    dk_out[...] = dk[...].astype(BF)
    dv_out[...] = dv[...].astype(BF)


def attend_halo(spans, slopes, q, k, v, low_pay, high_pay, bounds, dk0, dv0, dk1, dv1):
    width = q.shape[2]
    pairs = width // 128
    keys = k.shape[0]
    full = lambda x: pl.BlockSpec(x.shape, lambda i, *_: (0,) * len(x.shape))
    shape = jax.ShapeDtypeStruct((keys, width), BF)
    return pl.pallas_call(
        halo_kernel,
        name="attend_halo",
        cost_estimate=takes(12),
        grid_spec=pltpu.PrefetchScalarGridSpec(
            num_scalar_prefetch=2,
            grid=(1,),
            in_specs=[full(x) for x in (q, k, v, low_pay, high_pay, bounds, dk0, dv0, dk1, dv1)],
            out_specs=[full(shape), full(shape)],
            scratch_shapes=[
                pltpu.VMEM((pairs, 2 * QB, 128), BF),
                pltpu.VMEM((pairs, 2 * QB, 128), BF),
                pltpu.VMEM((pairs, 256, 2 * QB), BF),
                pltpu.VMEM((pairs, 256, 2 * QB), BF),
                pltpu.VMEM((2, 128, low_pay.shape[0]), FL),
                pltpu.VMEM((keys, width), FL),
                pltpu.VMEM((keys, width), FL),
            ],
        ),
        out_shape=[shape, shape],
        compiler_params=params(),
    )(spans, slopes, q, k, v, low_pay, high_pay, bounds, dk0, dv0, dk1, dv1)


def normalize(z):
    centred = z - jnp.mean(z, -1, keepdims=True)
    scale = lax.rsqrt(jnp.mean(centred * centred, -1, keepdims=True) + EPS)
    return centred * scale, scale


def normalize_back(d, unit, scale):
    return scale * (d - jnp.mean(d, -1, keepdims=True) - unit * jnp.mean(d * unit, -1, keepdims=True))


def rows_sum(x):
    return jnp.sum(x, 0, keepdims=True)


def middle_kernel(
    ids,
    pool,
    att0,
    att1,
    exact0,
    exact1,
    lse0,
    lse1,
    cot,
    vec,
    upb,
    low,
    high,
    olow,
    ohigh,
    out,
    pay,
    stats,
    mixed,
    gvec,
    gup,
    keep,
    send,
    wo,
    w1,
    w2,
    active,
    slope,
    unit1,
    hid,
    hid_low,
    z,
    d2,
    dw1,
    dw2,
    dwo,
    att,
    sems,
):
    n, width = att.shape
    att[:, : width // 2] = att0[...]
    att[:, width // 2 :] = att1[...]
    rb = width // NB
    fb = w2.shape[0] // NB
    parts = w1.shape[0]

    def rows(r, size):
        return pl.ds(pl.multiple_of(r, 16), size)

    def copies_a(block, s, p):
        pltpu.make_async_copy(block.at[pl.ds(192, 32)], wo.at[rows(s * rb, 32)], sems.at[0]).start()
        pltpu.make_async_copy(block.at[pl.ds(0, 192)], w2.at[rows(s * fb, 192)], sems.at[2]).start()

    def copies_b(block, s, p):
        pltpu.make_async_copy(block.at[pl.ds(192, 16)], wo.at[rows(s * rb + 32, 16)], sems.at[0]).start()
        for c in range(parts):
            pltpu.make_async_copy(block.at[pl.ds(48 * c, 48)], w1.at[c, rows(s * rb, 48)], sems.at[1]).start()

    load_sets(ids, low, high, olow, ohigh, copies_a, copies_b)
    wait_all(wo, sems.at[0])
    z[...] = dot(att[...], wo[...])
    rc = 128

    def row_loop(f):
        def body(i, _):
            f(pl.ds(pl.multiple_of(i * rc, rc), rc), i)
            return 0

        lax.fori_loop(0, n // rc, body, 0)

    def first_norm(r, i):
        unit, scale = normalize(pool[r, :] + z[r, :] + vec[2:3])
        h = unit * vec[3:4] + vec[4:5]
        unit1[r, :] = unit
        d2[r, 0:128] = jnp.broadcast_to(scale, (rc, 128))
        hid[r, :] = h
        hid_low[r, :] = h.astype(BF)

    row_loop(first_norm)
    wait_all(w1, sems.at[1])
    wait_all(w2, sems.at[2])
    c0 = 0.7978845608028654

    def up(c, _):
        inner = dot(hid_low[...], w1[c]) + upb[pl.ds(0, 1), pl.ds(pl.multiple_of(c * width, 128), width)]
        sq = inner * inner
        t = jnp.tanh(c0 * (inner + 0.044715 * (inner * sq)))
        cdf = 0.5 * (1.0 + t)
        active[c] = (inner * cdf).astype(BF)
        slope[c] = cdf + inner * (0.5 * (1.0 - t * t)) * (c0 + (3 * 0.044715 * c0) * sq)
        return 0

    lax.fori_loop(0, parts, up, 0)
    z[...] = dot(active[0], w2[pl.ds(0, width), :])
    for c in range(1, parts):
        z[...] = z[...] + dot(active[c], w2[pl.ds(c * width, width), :])
    gvec[...] = jnp.zeros(gvec.shape, FL)

    def second_norm(r, i):
        unit, scale = normalize(hid[r, :] + (z[r, :] + vec[5:6]))
        out[r, :] = (unit * vec[6:7] + vec[7:8]).astype(BF)
        dy = cot[r, :].astype(FL)
        gvec[6:7] = gvec[6:7] + rows_sum(dy * unit)
        gvec[7:8] = gvec[7:8] + rows_sum(dy)
        d = normalize_back(dy * vec[6:7], unit, scale)
        hid[r, :] = d
        d_low = d.astype(BF)
        att_like[r, :] = d_low
        gvec[5:6] = gvec[5:6] + rows_sum(d_low.astype(FL))

    att_like = pay.at[:, 0:width]
    scale1 = d2[:, 0:1]
    row_loop(second_norm)
    z[...] = jnp.zeros(z.shape, FL)

    def down(c, _):
        ffn = pay[:, 0:width]
        far = pl.ds(pl.multiple_of(c * width, 128), width)
        d_inner = (dot_t(ffn, w2[far, :]) * slope[c]).astype(BF)
        gup[:, far] = jnp.broadcast_to(rows_sum(d_inner.astype(FL)), (8, width))
        dw2[far, :] = t_dot(active[c], ffn).astype(BF)
        dw1[c] = t_dot(hid_low[...], d_inner).astype(BF)
        z[...] = z[...] + dot_t(d_inner, w1[c])
        return 0

    lax.fori_loop(0, parts, down, 0)

    def store_sets(a_ref, b_ref):
        for p in range(NB):
            s = ids[0] ^ rel_a(p)
            pltpu.make_async_copy(dw2.at[rows(s * fb, 192)], a_ref.at[p, pl.ds(0, 192)], sems.at[3]).start()
            s = ids[0] ^ rel_b(p)
            for c in range(parts):
                pltpu.make_async_copy(
                    dw1.at[c, rows(s * rb, 48)], b_ref.at[p, pl.ds(48 * c, 48)], sems.at[3]
                ).start()

    @pl.when(ids[1] == 0)
    def _():
        store_sets(keep, send)

    @pl.when(ids[1] != 0)
    def _():
        store_sets(send, keep)

    def first_back(r, i):
        unit = unit1[r, :]
        d = hid[r, :] + z[r, :]
        gvec[3:4] = gvec[3:4] + rows_sum(d * unit)
        gvec[4:5] = gvec[4:5] + rows_sum(d)
        d = normalize_back(d * vec[3:4], unit, d2[r, 0:1])
        mixed[r, :] = d
        d_low = d.astype(BF)
        hid_low[r, :] = d_low
        gvec[2:3] = gvec[2:3] + rows_sum(d_low.astype(FL))

    row_loop(first_back)
    dwo[...] = t_dot(att[...], hid_low[...]).astype(BF)

    def store_wo(a_ref, b_ref):
        for p in range(NB):
            s = ids[0] ^ rel_a(p)
            pltpu.make_async_copy(dwo.at[rows(s * rb, 32)], a_ref.at[p, pl.ds(192, 32)], sems.at[3]).start()
            s = ids[0] ^ rel_b(p)
            pltpu.make_async_copy(dwo.at[rows(s * rb + 32, 16)], b_ref.at[p, pl.ds(192, 16)], sems.at[3]).start()
            pltpu.make_async_copy(dwo.at[rows(s * rb + 32, 16)], b_ref.at[p, pl.ds(208, 16)], sems.at[3]).start()

    @pl.when(ids[1] == 0)
    def _():
        store_wo(keep, send)

    @pl.when(ids[1] != 0)
    def _():
        store_wo(send, keep)

    z[...] = dot_t(hid_low[...], wo[...])
    heads = width // HD
    head_of = lax.broadcasted_iota(jnp.int32, (16, width), 1) // HD
    pick = (head_of == lax.broadcasted_iota(jnp.int32, (16, width), 0)).astype(FL).astype(BF)
    stats[...] = jnp.zeros(stats.shape, FL)
    stats[0 : heads // 2, :] = lse0[0 : heads // 2, :]
    stats[heads // 2 : heads, :] = lse1[0 : heads // 2, :]

    def last(r, i):
        d_low = z[r, :].astype(BF)
        pay[r, 0:width] = d_low
        exact = jnp.concatenate([exact0[r, :], exact1[r, :]], 1)
        prod = d_low.astype(FL) * exact
        delta = jnp.zeros((16, rc), FL)
        for _ in range(3):
            piece = prod.astype(BF)
            delta = delta + dot_t(pick, piece)
            prod = prod - piece.astype(FL)
        stats[16:32, r] = delta

    row_loop(last)
    st = stats[...].T
    pieces = []
    for _ in range(3):
        piece = st.astype(BF).astype(FL)
        pieces.append(piece)
        st = st - piece
    pieces.append(jnp.zeros_like(st))
    pay[:, width:] = jnp.concatenate(pieces, 1).astype(BF)
    wait_all(keep, sems.at[3])
    wait_all(send, sems.at[3])


def middle(ids, pool, att0, att1, exact0, exact1, lse0, lse1, cot, vec, upb, sets, set_rows):
    n, width = pool.shape
    ff = upb.shape[1]
    parts = ff // width
    whole = lambda i, *_: (0, 0)
    full = lambda x: pl.BlockSpec(x.shape, whole)
    shapes = [
        jax.ShapeDtypeStruct((n, width), BF),
        jax.ShapeDtypeStruct((n, width + 128), BF),
        jax.ShapeDtypeStruct((32, n), FL),
        jax.ShapeDtypeStruct((n, width), FL),
        jax.ShapeDtypeStruct((8, width), FL),
        jax.ShapeDtypeStruct((8, ff), FL),
    ]
    big = jax.ShapeDtypeStruct((NB, set_rows, width), BF)
    return pl.pallas_call(
        middle_kernel,
        name="middle",
        cost_estimate=takes(36),
        grid_spec=pltpu.PrefetchScalarGridSpec(
            num_scalar_prefetch=1,
            grid=(1,),
            in_specs=[full(pool)]
            + [full(x) for x in (att0, att1, exact0, exact1, lse0, lse1, cot, vec, upb)]
            + [ANY] * 4,
            out_specs=[full(x) for x in shapes] + [ANY, ANY],
            scratch_shapes=[
                pltpu.VMEM((width, width), BF),
                pltpu.VMEM((parts, width, width), BF),
                pltpu.VMEM((ff, width), BF),
                pltpu.VMEM((parts, n, width), BF),
                pltpu.VMEM((parts, n, width), FL),
                pltpu.VMEM((n, width), FL),
                pltpu.VMEM((n, width), FL),
                pltpu.VMEM((n, width), BF),
                pltpu.VMEM((n, width), FL),
                pltpu.VMEM((n, 128), FL),
                pltpu.VMEM((parts, width, width), BF),
                pltpu.VMEM((ff, width), BF),
                pltpu.VMEM((width, width), BF),
                pltpu.VMEM((n, width), BF),
                pltpu.SemaphoreType.DMA((4,)),
            ],
        ),
        out_shape=shapes + [big, big],
        compiler_params=params(),
    )(ids, pool, att0, att1, exact0, exact1, lse0, lse1, cot, vec, upb, *sets)


def weights_kernel(ids, pool, tok, dq0, dq1, dk, dv, gvec, gup, sl0, sl1, keep, send, dwq, dwk, dwv, bias, sems):
    width = tok.shape[1]
    ff = gup.shape[1]
    rb = width // NB
    dq = jnp.concatenate([dq0[...], dq1[...]], 1)
    dwq[...] = t_dot(pool[...].astype(BF), dq).astype(BF)
    dwk[...] = t_dot(tok[...], dk[...]).astype(BF)
    dwv[...] = t_dot(tok[...], dv[...]).astype(BF)
    row = lax.broadcasted_iota(jnp.int32, (16, width), 0)
    g = jnp.concatenate([gvec[...], jnp.zeros((8, width), FL)], 0)
    g = jnp.where(row == 0, rows_sum(dq.astype(FL)), g)
    g = jnp.where(row == 1, rows_sum(dv[...].astype(FL)), g)
    block_of = div_rb(lax.broadcasted_iota(jnp.int32, (16, width), 1))
    parts = []
    for p in range(NB):
        parts.append(jnp.where(block_of == (ids[0] ^ rel_b(p)), g, 0.0).astype(BF))
    total = dot_t(jnp.concatenate(parts, 0), spread_matrix(128, width, rb))
    row = lax.broadcasted_iota(jnp.int32, (16, ff), 0)
    block_of = div_rb(lax.broadcasted_iota(jnp.int32, (16, ff), 1))
    block_of = jnp.where((row >= 8) & (row < 12), block_of - row + 8, -1)
    up = jnp.concatenate([gup[...], gup[...]], 0)
    parts = []
    for p in range(NB):
        parts.append(jnp.where(block_of == 4 * (ids[0] ^ rel_b(p)), up, 0.0).astype(BF))
    total = total + dot_t(jnp.concatenate(parts, 0), spread_matrix(128, ff, rb))
    line = jnp.zeros((1, 128), FL)
    lane = lax.broadcasted_iota(jnp.int32, (1, 128), 1)
    for half, sl in enumerate((sl0, sl1)):
        pairs = sl.shape[0] // 8
        for j in range(pairs):
            x = rows_sum(sl[8 * j : 8 * j + 8, :])
            for i in range(2):
                value = jnp.sum(x[:, QB * i : QB * i + QB], 1, keepdims=True)
                line = jnp.where(lane == 2 * pairs * half + 2 * j + i, -value, line)
    row = lax.broadcasted_iota(jnp.int32, (16 * NB, 128), 0)
    total = jnp.where((row & 15) == 12, line, total)
    bias[...] = jnp.zeros(bias.shape, BF)
    bias[:, 0:128] = total.astype(BF)

    def rows(r, size):
        return pl.ds(pl.multiple_of(r, 16), size)

    def store_sets(a_ref, b_ref):
        def go(src, dst):
            pltpu.make_async_copy(src, dst, sems.at[0]).start()

        for p in range(NB):
            s = ids[0] ^ rel_a(p)
            go(dwq.at[rows(s * rb, 48)], a_ref.at[p, pl.ds(0, 48)])
            go(dwk.at[rows(s * rb, 32)], a_ref.at[p, pl.ds(48, 32)])
            s = ids[0] ^ rel_b(p)
            go(dwk.at[rows(s * rb + 32, 16)], b_ref.at[p, pl.ds(0, 16)])
            go(dwv.at[rows(s * rb, 48)], b_ref.at[p, pl.ds(16, 48)])
            go(bias.at[pl.ds(16 * p, 16)], b_ref.at[p, pl.ds(64, 16)])

    @pl.when(ids[1] == 0)
    def _():
        store_sets(keep, send)

    @pl.when(ids[1] != 0)
    def _():
        store_sets(send, keep)

    wait_all(keep, sems.at[0])
    wait_all(send, sems.at[0])


def weight_grads(ids, pool, tok, dq0, dq1, dk, dv, gvec, gup, sl0, sl1, set_rows):
    width = tok.shape[1]
    full = lambda x: pl.BlockSpec(x.shape, lambda i, *_: (0, 0))
    big = jax.ShapeDtypeStruct((NB, set_rows, width), BF)
    square = pltpu.VMEM((width, width), BF)
    return pl.pallas_call(
        weights_kernel,
        name="weight_grads",
        cost_estimate=takes(9),
        grid_spec=pltpu.PrefetchScalarGridSpec(
            num_scalar_prefetch=1,
            grid=(1,),
            in_specs=[full(x) for x in (pool, tok, dq0, dq1, dk, dv, gvec, gup, sl0, sl1)],
            out_specs=[ANY, ANY],
            scratch_shapes=[
                square,
                square,
                square,
                pltpu.VMEM((16 * NB, width), BF),
                pltpu.SemaphoreType.DMA((1,)),
            ],
        ),
        out_shape=[big, big],
        compiler_params=params(),
    )(ids, pool, tok, dq0, dq1, dk, dv, gvec, gup, sl0, sl1)


def tokens_kernel(mixed, dq0, dq1, dk, dv, wq, wk, wv, out, acc):
    half = mixed.shape[0]
    dq = jnp.concatenate([dq0[...], dq1[...]], 1)
    up = 0.5 * (mixed[...] + dot_t(dq, wq[...]))
    down = dot_t(dk[...], wk[...]) + dot_t(dv[...], wv[...])
    for j in range(mixed.shape[1] // 128):
        cols = slice(128 * j, 128 * j + 128)
        for i in range(2):
            acc[j, pl.ds(i, half, stride=2)] = up[:, cols]
        out[:, cols] = acc[j] + down[:, cols]


def token_grads(mixed, dq0, dq1, dk, dv, wq, wk, wv):
    rows, width = dk.shape
    step = 512
    half = pl.BlockSpec((step // 2, width), lambda i: (i, 0))
    block = pl.BlockSpec((step, width), lambda i: (i, 0))
    whole = pl.BlockSpec((width, width), lambda i: (0, 0))
    thin = pl.BlockSpec((step // 2, width // 2), lambda i: (i, 0))
    return pl.pallas_call(
        tokens_kernel,
        name="token_grads",
        cost_estimate=takes(8),
        grid=(rows // step,),
        in_specs=[half, thin, thin, block, block, whole, whole, whole],
        out_specs=block,
        out_shape=jax.ShapeDtypeStruct((rows, width), FL),
        scratch_shapes=[pltpu.VMEM((width // 128, step, 128), FL)],
        compiler_params=params(),
    )(mixed, dq0, dq1, dk, dv, wq, wk, wv)


def blocks_of(x):
    return x.reshape(NB, x.shape[0] // NB, x.shape[1])


def column_parts(x, width):
    return jnp.concatenate([x[..., width * c : width * c + width] for c in range(x.shape[-1] // width)], -2)


def bias_block(small, up, width):
    rb = small[0].shape[-1]
    rows = jnp.stack(list(small) + [up[..., rb * c : rb * c + rb] for c in range(4)], -2)
    pad = [(0, 0)] * (rows.ndim - 2) + [(0, 4), (0, width - rb)]
    return jnp.pad(rows, pad)


def pack(wq, wk, wv, wo, w1, w2, bias, width):
    a1 = jnp.concatenate([wq, wk[..., :32, :]], -2)
    b1 = jnp.concatenate([wk[..., 32:, :], wv, bias], -2)
    a2 = jnp.concatenate([w2, wo[..., :32, :]], -2)
    b2 = jnp.concatenate([column_parts(w1, width), wo[..., 32:, :], wo[..., 32:, :]], -2)
    return a1, b1, a2, b2


def unpack(a1, b1, a2, b2, width):
    wq = a1[..., :48, :]
    wk = jnp.concatenate([a1[..., 48:, :], b1[..., :16, :]], -2)
    wv = b1[..., 16:64, :]
    bias = b1[..., 64:, :]
    wo = jnp.concatenate([a2[..., 192:, :], b2[..., 192:208, :]], -2)
    w2 = a2[..., :192, :]
    parts = 4
    w1 = jnp.concatenate([b2[..., 48 * c : 48 * c + 48, :] for c in range(parts)], -1)
    return wq, wk, wv, wo, w1, w2, bias


def pack_kernel(ids, wq, wk, wv, wo, w1, w2, b_up, *refs):
    vectors, (out, bias) = refs[:8], refs[8:]
    first = out.at[:, 0:80]
    second = out.at[:, 80:304]
    rb, width = wq.shape

    @pl.when(ids[1] == 0)
    def _():
        first[0, 0:48] = wq[...].astype(BF)
        first[0, 48:80] = wk[0:32].astype(BF)
        second[0, 0:192] = w2[...].astype(BF)
        second[0, 192:224] = wo[0:32].astype(BF)

    @pl.when(ids[1] != 0)
    def _():
        bias[...] = jnp.zeros(bias.shape, FL)
        for i, x in enumerate(vectors):
            bias[i : i + 1, 0:rb] = x[...]
        for c in range(4):
            bias[8 + c : 9 + c, 0:rb] = b_up[:, rb * c : rb * c + rb]
        first[0, 0:16] = wk[32:48].astype(BF)
        first[0, 16:64] = wv[...].astype(BF)
        first[0, 64:80] = bias[...].astype(BF)
        for c in range(4):
            second[0, 48 * c : 48 * c + 48] = w1[:, width * c : width * c + width].astype(BF)
        second[0, 192:208] = wo[32:48].astype(BF)
        second[0, 208:224] = wo[32:48].astype(BF)


def pack_own(ids, masters, b_up, vectors):
    width = masters[0].shape[1]
    args = list(masters) + [b_up[None]] + [x[None] for x in vectors]
    full = lambda x: pl.BlockSpec(x.shape, lambda i, *_: (0,) * len(x.shape))
    shape = jax.ShapeDtypeStruct((1, 304, width), BF)
    return pl.pallas_call(
        pack_kernel,
        name="pack",
        cost_estimate=takes(3),
        grid_spec=pltpu.PrefetchScalarGridSpec(
            num_scalar_prefetch=1,
            grid=(1,),
            in_specs=[full(x) for x in args],
            out_specs=full(shape),
            scratch_shapes=[pltpu.VMEM((16, width), FL)],
        ),
        out_shape=shape,
        compiler_params=params(),
    )(ids, *args)


def unpack_kernel(ids, mine1, other1, mine2, other2, wq, wk, wv, wo, w1, w2, *vectors):
    width = wq.shape[1]
    rb = wq.shape[0]

    def store(a1, b1, a2, b2):
        wq[...] = a1[0:48]
        wk[0:32] = a1[48:80]
        wk[32:48] = b1[0:16]
        wv[...] = b1[16:64]
        for i in range(8):
            vectors[i][...] = b1[64 + i : 65 + i, 0:rb]
        for c in range(4):
            vectors[8][:, rb * c : rb * c + rb] = b1[72 + c : 73 + c, 0:rb]
            w1[:, width * c : width * c + width] = b2[48 * c : 48 * c + 48]
        vectors[9][...] = b1[76:77, 0:128]
        w2[...] = a2[0:192]
        wo[0:32] = a2[192:224]
        wo[32:48] = b2[192:208]

    @pl.when(ids[1] == 0)
    def _():
        store(mine1, other1, mine2, other2)

    @pl.when(ids[1] != 0)
    def _():
        store(other1, mine1, other2, mine2)


def unpack_own(ids, args, ff):
    width = args[0].shape[1]
    rb = width // NB
    dims = [(rb, width)] * 4 + [(rb, ff), (ff // NB, width)] + [(1, rb)] * 8 + [(1, ff // NB), (1, 128)]
    shapes = [jax.ShapeDtypeStruct(d, FL) for d in dims]
    full = lambda x: pl.BlockSpec(x.shape, lambda i, *_: (0, 0))
    return pl.pallas_call(
        unpack_kernel,
        name="unpack",
        cost_estimate=takes(3),
        grid_spec=pltpu.PrefetchScalarGridSpec(
            num_scalar_prefetch=1,
            grid=(1,),
            in_specs=[full(x) for x in args],
            out_specs=[full(x) for x in shapes],
        ),
        out_shape=shapes,
        compiler_params=params(),
    )(ids, *args)


def after(x, *done):
    return lax.optimization_barrier((x,) + done)[0]


def local(
    tokens,
    cotangent,
    lengths,
    w_query,
    b_query,
    w_key,
    w_value,
    b_value,
    w_output,
    b_output,
    gain_attn,
    shift_attn,
    w_up,
    b_up,
    w_down,
    b_down,
    gain_ffn,
    shift_ffn,
    distance_slope,
):
    rows_here, width = tokens.shape
    ff = w_up.shape[1]
    own = rows_here // 2
    halo = rows_here // 2
    seq = lax.axis_size("seq")
    devices = seq * lax.axis_size("dp")
    direct = seq == NB
    order = ("dp", "seq")
    up_pairs = [(i, i + 1) for i in range(devices - 1)]
    down_pairs = [(i + 1, i) for i in range(devices - 1)]

    masters = (w_query, w_key, w_value, w_output, w_up, w_down)
    vectors = (b_query, b_value, b_output, gain_attn, shift_attn, b_down, gain_ffn, shift_ffn)
    if direct:
        core = lax.axis_index("dp")
        ids = jnp.stack([lax.axis_index("seq"), core]).astype(jnp.int32)
        x = pack_own(ids, masters, b_up, vectors)
        y = x[:, 80:]
        x = x[:, :80]
        x = jnp.concatenate([x, exchange(x, 8, 4)], 0)
        x1, low_a = lax.optimization_barrier(
            (exchange(x, 4, 8), lax.ppermute(tokens[rows_here - halo : rows_here - halo // 2], order, up_pairs))
        )
        x = jnp.concatenate([x, x1], 0)
        y, part = lax.optimization_barrier((y, tokens[rows_here - halo // 2 :], x1))[:2]
        x1, y1, low_b = lax.optimization_barrier(
            (exchange(x, 2, 1), exchange(y, 8, 4), lax.ppermute(part, order, up_pairs))
        )
        low1 = jnp.concatenate([x, x1], 0)
        y = jnp.concatenate([y, y1], 0)
        high1, olow1, y1, high_a = lax.optimization_barrier(
            (
                exchange(low1, 1, 2),
                swap_core(low1),
                exchange(y, 4, 8),
                lax.ppermute(after(tokens[: halo // 2], x1), order, down_pairs),
            )
        )
        y = jnp.concatenate([y, y1], 0)
        sets1 = (low1, high1, olow1, swap_core(high1))
        y1 = exchange(y, 2, 1)
        high_b = lax.ppermute(after(tokens[halo // 2 : halo], high1), order, down_pairs)
    else:
        ids = jnp.zeros((2,), jnp.int32)
        gather = lambda x: lax.all_gather(x.astype(BF), "seq", axis=0, tiled=True)
        full = [blocks_of(gather(x)) for x in masters]
        small = [gather(x).reshape(NB, -1) for x in vectors]
        bias = bias_block(small, gather(b_up).reshape(NB, -1), width)
        a1, b1, a2, b2 = pack(*full, bias, width)
        at_a = jnp.array([rel_a(p) for p in range(NB)])
        at_b = jnp.array([rel_b(p) for p in range(NB)])
        sets1 = (a1[at_a[:8]], a1[at_a[8:]], b1[at_b[:8]], b1[at_b[8:]])
        sets2 = (a2[at_a[:8]], a2[at_a[8:]], b2[at_b[:8]], b2[at_b[8:]])
        low_a = lax.ppermute(tokens[rows_here - halo : rows_here - halo // 2], order, up_pairs)
        low_b = lax.ppermute(tokens[rows_here - halo // 2 :], order, up_pairs)
        high_a = lax.ppermute(tokens[: halo // 2], order, down_pairs)
        high_b = lax.ppermute(tokens[halo // 2 : halo], order, down_pairs)

    first_row = lax.axis_index(order) * rows_here
    total = devices * rows_here
    starts = 2 * (jnp.cumsum(lengths) - lengths)
    place = first_row - halo + 2 * jnp.arange(2 * own, dtype=jnp.int32)
    before = starts[None, :] <= place[:, None]
    begin = jnp.max(jnp.where(before, starts[None, :], 0), 1)
    end = jnp.min(jnp.where(before, total, starts[None, :]), 1)
    inside = (place >= 0) & (place < total)
    shift = first_row - halo
    begin = jnp.where(inside, begin - shift, 0)
    end = jnp.where(inside, end - shift, 0)
    bounds = jnp.pad(jnp.stack([begin, end], 0).astype(FL), ((0, 6), (0, 0)))
    blocks = 2 * own // QB
    chunks = (rows_here + 2 * halo) // KC
    low_chunk = jnp.min(jnp.where(inside, begin, 4 * total).reshape(blocks, QB), 1) // KC
    high_chunk = (jnp.max(end.reshape(blocks, QB), 1) + KC - 1) // KC
    index = jnp.arange(blocks)
    away = (index < blocks // 4) | (index >= blocks - blocks // 4)
    low_chunk = jnp.clip(low_chunk, jnp.where(away, chunks // 4, 0), chunks)
    high_chunk = jnp.clip(high_chunk, 0, jnp.where(away, chunks - chunks // 4, chunks))
    spans = jnp.concatenate([low_chunk, high_chunk]).astype(jnp.int32)

    slopes = distance_slope
    q, k, v, pool, wq, wk, wv, vec, upb = qkv(ids, tokens, sets1, ff)
    if direct:
        k, high_b = lax.optimization_barrier((k, high_b))
    qh, kh, vh = halo_qkv(low_a, low_b, high_a, high_b, wq, wk, wv, vec)
    if direct:
        y1, kh = lax.optimization_barrier((y1, kh))
        low2 = jnp.concatenate([y, y1], 0)
        bounds = after(bounds, low2)
    att0, exact0, lse0 = attend_forward(0, spans, slopes, q, k, kh, v, vh, bounds)
    att1, exact1, lse1 = attend_forward(1, spans, slopes, q, k, kh, v, vh, after(bounds, lse0))
    if direct:
        high2, lse1 = lax.optimization_barrier((exchange(low2, 1, 2), lse1))
        sets2 = (low2, high2, swap_core(low2), swap_core(high2))
    out, pay, stats, mixed, gvec, gup, keep2, send2 = middle(
        ids, pool, att0, att1, exact0, exact1, lse0, lse1, cotangent, vec, upb, sets2, 224
    )
    low_pay = lax.ppermute(pay[own // 2 :], order, up_pairs)
    high_pay = lax.ppermute(pay[: own // 2], order, down_pairs)
    if direct:
        got = swap_core(send2)
        up = add(keep2[8:], got[8:]).astype(BF)
        bounds = after(bounds, up)
    dq0, dk0, dv0, sl0 = attend_own(0, spans, slopes, q, k, kh, v, vh, pay, stats, bounds)
    bounds = after(bounds, dq0)
    dq1, dk1, dv1, sl1 = attend_own(1, spans, slopes, q, k, kh, v, vh, pay, stats, bounds)
    if direct:
        got1, dq1, low_pay, high_pay = lax.optimization_barrier((exchange(up, 1, 2), dq1, low_pay, high_pay))
        up = add(keep2[4:8], got[4:8], got1[4:]).astype(BF)
        bounds = after(bounds, up)
    dk, dv = attend_halo(spans, slopes, qh, k, v, low_pay, high_pay, after(bounds, dq1), dk0, dv0, dk1, dv1)
    keep1, send1 = weight_grads(ids, pool, tokens, dq0, dq1, dk, dv, gvec, gup, sl0, sl1, 80)
    if direct:
        got2, keep1, send1 = lax.optimization_barrier((exchange(up, 2, 1), keep1, send1))
        low = add(keep2[:4], got[:4], got1[:4])
        up = (low[2:] + got2[2:].astype(FL)).astype(BF)
        low = low[:2] + got2[:2].astype(FL)
        got, up = lax.optimization_barrier((swap_core(send1), up))
        part = add(keep1[8:], got[8:]).astype(BF)
        mixed = after(mixed, part)
    grad_tokens = token_grads(mixed, dq0, dq1, dk, dv, wq, wk, wv)

    if direct:
        got3, got1, grad_tokens = lax.optimization_barrier((exchange(up, 4, 8), exchange(part, 1, 2), grad_tokens))
        part = add(keep1[4:8], got[4:8], got1[4:]).astype(BF)
        up = (low[1:] + got3[1:].astype(FL)).astype(BF)
        low = low[:1] + got3[:1].astype(FL)
        got4, got2 = lax.optimization_barrier((exchange(up, 8, 4), exchange(part, 2, 1)))
        mine = (low + got4.astype(FL))[0]
        low = add(keep1[:4], got[:4], got1[:4])
        part = (low[2:] + got2[2:].astype(FL)).astype(BF)
        low = low[:2] + got2[:2].astype(FL)
        got3, other = lax.optimization_barrier((exchange(part, 4, 8), swap_core(mine)))
        second = (mine, other)
        part = (low[1:] + got3[1:].astype(FL)).astype(BF)
        low = low[:1] + got3[:1].astype(FL)
        mine = (low + exchange(part, 8, 4).astype(FL))[0]
        other = swap_core(mine)
        gq, gk, gv, go, g1, g2, *small = unpack_own(ids, (mine, other) + second, ff)
        g_up, g_slope = small[8][0], small[9][0, : distance_slope.shape[0]]
        small = [x[0] for x in small[:8]]
    else:
        inv_a = [0] * NB
        inv_b = [0] * NB
        for p in range(NB):
            inv_a[rel_a(p)] = p
            inv_b[rel_b(p)] = p
        inv_a = jnp.array(inv_a)
        inv_b = jnp.array(inv_b)
        gq, gk, gv, go, g1, g2, gb = unpack(keep1[inv_a], send1[inv_b], keep2[inv_a], send2[inv_b], width)
        rb = width // NB

        def share(x):
            x = lax.psum(x.astype(FL), "dp")
            return lax.psum_scatter(x, "seq", scatter_dimension=0, tiled=True)

        gq, gk, gv, go, g1, g2 = [share(x.reshape(-1, x.shape[-1])) for x in (gq, gk, gv, go, g1, g2)]
        small = [share(gb[:, i, :rb].reshape(-1)) for i in range(8)]
        g_up = share(gb[:, 8:12, :rb].reshape(-1))
        g_slope = lax.psum(gb[0, 12, : distance_slope.shape[0]].astype(FL), order)
    return (
        out,
        grad_tokens,
        gq,
        small[0],
        gk,
        gv,
        small[1],
        go,
        small[2],
        small[3],
        small[4],
        g1,
        g_up,
        g2,
        small[5],
        small[6],
        small[7],
        g_slope,
    )


def solution(mesh):
    tall = P(("dp", "seq"), None)
    mat = P("seq", None)
    vec = P("seq")
    return jax.shard_map(
        local,
        mesh=mesh,
        in_specs=(tall, tall, P(), mat, vec, mat, mat, vec, mat, vec, vec, vec, mat, vec, mat, vec, vec, vec, P()),
        out_specs=(tall, tall, mat, vec, mat, mat, vec, mat, vec, vec, vec, mat, vec, mat, vec, vec, vec, P()),
        check_vma=False,
    )
```

```python
import functools

import jax
import jax.numpy as jnp
from jax import lax
from jax.experimental import pallas as pl
from jax.experimental.pallas import tpu as pltpu
from jax.sharding import PartitionSpec as P

HD = 64
NB = 16
QB = 128
KC = 256
EPS = 1e-05
FAR = 1e12
BF = jnp.bfloat16
FL = jnp.float32


def rel_a(p):
    return (p & 1) * 8 + ((p >> 1) & 1) * 4 + ((p >> 2) & 1) * 2 + ((p >> 3) & 1)


def rel_b(p):
    return (p & 1) * 4 + ((p >> 1) & 1) * 8 + ((p >> 2) & 1) + ((p >> 3) & 1) * 2


def dot(a, b):
    return jnp.dot(a, b, preferred_element_type=FL)


def dot_t(a, b):
    return lax.dot_general(a, b, (((1,), (1,)), ((), ())), preferred_element_type=FL)


def t_dot(a, b):
    return lax.dot_general(a, b, (((0,), (0,)), ((), ())), preferred_element_type=FL)


def exchange(x, stride_a, stride_b):
    n = lax.axis_size("seq")
    pairs = [(s, s ^ stride_a) for s in range(n)] + [(n + s, n + (s ^ stride_b)) for s in range(n)]
    return lax.ppermute(x, ("dp", "seq"), pairs)


def swap_core(x):
    return lax.ppermute(x, "dp", [(0, 1), (1, 0)])


def add(*xs):
    total = xs[0].astype(FL)
    for x in xs[1:]:
        total = total + x.astype(FL)
    return total


def params(**kw):
    return pltpu.CompilerParams(vmem_limit_bytes=58 * 1024 * 1024, **kw)


def takes(us):
    return pl.CostEstimate(flops=us * 1150 * 10**6, transcendentals=0, bytes_accessed=us * 3600 * 10**3)


ANY = pl.BlockSpec(memory_space=pl.ANY)


def load_sets(ids, low, high, olow, ohigh, copies_a, copies_b):
    def start(a_refs, b_refs):
        for p in range(NB):
            copies_a(a_refs[p // 8].at[p % 8], ids[0] ^ rel_a(p), p)
            copies_b(b_refs[p // 8].at[p % 8], ids[0] ^ rel_b(p), p)

    @pl.when(ids[1] == 0)
    def _():
        start((low, high), (olow, ohigh))

    @pl.when(ids[1] != 0)
    def _():
        start((olow, ohigh), (low, high))


def wait_all(ref, sem):
    pltpu.make_async_copy(ref, ref, sem).wait()


def spread_matrix(rows, cols, rb):
    lanes = lax.broadcasted_iota(jnp.int32, (rows, cols), 1)
    return (lax.broadcasted_iota(jnp.int32, (rows, cols), 0) == lanes - rb * div_rb(lanes)).astype(FL).astype(BF)


def div_rb(x):
    return (x * 21846) >> 20


def qkv_kernel(
    ids, tok, low, high, olow, ohigh, q_out, k_out, v_out, kt_out, vt_out, pool_out, wq, wk, wv, vec_out, up_out, bias, x32, sems
):
    width = tok.shape[1]
    rb = width // NB

    @pl.when(pl.program_id(0) == 0)
    def _():
        def rows(r, n):
            return pl.ds(pl.multiple_of(r, 16), n)

        def copies_a(block, s, p):
            pltpu.make_async_copy(block.at[pl.ds(0, 48)], wq.at[rows(s * rb, 48)], sems.at[0]).start()
            pltpu.make_async_copy(block.at[pl.ds(48, 32)], wk.at[rows(s * rb, 32)], sems.at[1]).start()

        def copies_b(block, s, p):
            pltpu.make_async_copy(block.at[pl.ds(0, 16)], wk.at[rows(s * rb + 32, 16)], sems.at[1]).start()
            pltpu.make_async_copy(block.at[pl.ds(16, 48)], wv.at[rows(s * rb, 48)], sems.at[2]).start()
            pltpu.make_async_copy(block.at[pl.ds(64, 16)], bias.at[pl.ds(16 * p, 16)], sems.at[3]).start()

        load_sets(ids, low, high, olow, ohigh, copies_a, copies_b)
        wait_all(wq, sems.at[0])
        wait_all(wk, sems.at[1])
        wait_all(wv, sems.at[2])
        wait_all(bias, sems.at[3])
        parts = bias[:, 0:128]
        wide = dot(parts, spread_matrix(128, width, rb))
        block_of = div_rb(lax.broadcasted_iota(jnp.int32, (16, width), 1))
        total = jnp.zeros((16, width), FL)
        for p in range(NB):
            total = total + jnp.where(block_of == (ids[0] ^ rel_b(p)), wide[16 * p : 16 * p + 16], 0.0)
        vec_out[...] = total
        ff = up_out.shape[1]
        wide = dot(parts, spread_matrix(128, ff, rb))
        block_of = div_rb(lax.broadcasted_iota(jnp.int32, (16, ff), 1))
        row = lax.broadcasted_iota(jnp.int32, (16, ff), 0)
        block_of = jnp.where((row >= 8) & (row < 12), block_of - row + 8, -1)
        total = jnp.zeros((16, ff), FL)
        for p in range(NB):
            total = total + jnp.where(block_of == 4 * (ids[0] ^ rel_b(p)), wide[16 * p : 16 * p + 16], 0.0)
        up_out[...] = jnp.broadcast_to(jnp.sum(total, 0, keepdims=True), up_out.shape)

    pool_out[...] = project(tok[...], wq, wk, wv, vec_out, q_out, k_out, v_out, kt_out, vt_out, x32)


def project(x, wq, wk, wv, vec, q_out, k_out, v_out, kt_out, vt_out, x32):
    width = x.shape[1]
    half = x.shape[0] // 2
    k_out[...] = dot(x, wk[...]).astype(BF)
    v_out[...] = (dot(x, wv[...]) + vec[1:2]).astype(BF)
    for c in range(x.shape[0] // KC):
        kt_out[c] = k_out[KC * c : KC * c + KC].T
        vt_out[c] = v_out[KC * c : KC * c + KC].T
    pooled = []
    for j in range(width // 128):
        x32[j] = x[:, 128 * j : 128 * j + 128].astype(FL)
        pooled.append((x32[j, pl.ds(0, half, stride=2)] + x32[j, pl.ds(1, half, stride=2)]) * 0.5)
    pooled = jnp.concatenate(pooled, 1)
    q = (dot(pooled.astype(BF), wq[...]) + vec[0:1]).astype(BF)
    q_out[...] = (q.astype(FL) * HD**-0.5).astype(BF)
    return pooled


def qkv(ids, tokens, sets, ff):
    rows, width = tokens.shape
    step = 512
    whole = lambda i, *_: (0, 0)
    square = jax.ShapeDtypeStruct((width, width), BF)
    thin = pl.BlockSpec((step // 2, width), lambda i, *_: (i, 0))
    block = pl.BlockSpec((step, width), lambda i, *_: (i, 0))
    inner = pl.BlockSpec((step, width), lambda i, *_: (i + 1, 0))
    tall = pl.BlockSpec((step // KC, width, KC), lambda i, *_: (i + 1, 0, 0))
    return pl.pallas_call(
        qkv_kernel,
        name="qkv",
        cost_estimate=takes(9),
        grid_spec=pltpu.PrefetchScalarGridSpec(
            num_scalar_prefetch=1,
            grid=(rows // step,),
            in_specs=[block, ANY, ANY, ANY, ANY],
            out_specs=[thin, inner, inner, tall, tall, thin]
            + [pl.BlockSpec((width, width), whole)] * 3
            + [pl.BlockSpec((16, width), whole), pl.BlockSpec((8, ff), whole)],
            scratch_shapes=[
                pltpu.VMEM((16 * NB, width), BF),
                pltpu.VMEM((width // 128, step, 128), FL),
                pltpu.SemaphoreType.DMA((4,)),
            ],
        ),
        out_shape=[
            jax.ShapeDtypeStruct((rows // 2, width), BF),
            jax.ShapeDtypeStruct((2 * rows, width), BF),
            jax.ShapeDtypeStruct((2 * rows, width), BF),
            jax.ShapeDtypeStruct((2 * rows // KC, width, KC), BF),
            jax.ShapeDtypeStruct((2 * rows // KC, width, KC), BF),
            jax.ShapeDtypeStruct((rows // 2, width), FL),
            square,
            square,
            square,
            jax.ShapeDtypeStruct((16, width), FL),
            jax.ShapeDtypeStruct((8, ff), FL),
        ],
        compiler_params=params(),
    )(ids, tokens, *sets)


def halo_qkv_kernel(
    low_a, low_b, high_a, high_b, wq, wk, wv, vec, k, v, kt, vt, q_out, k_out, v_out, kt_out, vt_out, x32
):
    low = pl.program_id(0) == 0
    parts = [jnp.where(low, a[...], b[...]) for a, b in ((low_a, high_a), (low_b, high_b))]
    project(jnp.concatenate(parts, 0), wq, wk, wv, vec, q_out, k_out, v_out, kt_out, vt_out, x32)


def halo_qkv(low_a, low_b, high_a, high_b, wq, wk, wv, vec, k, v, kt, vt):
    rows, width = low_a.shape
    rows = 2 * rows
    full = lambda x: pl.BlockSpec(x.shape, lambda i: (0,) * len(x.shape))
    args = (low_a, low_b, high_a, high_b, wq, wk, wv, vec)
    edge = pl.BlockSpec((rows, width), lambda i: (3 * i, 0))
    tall = pl.BlockSpec((rows // KC, width, KC), lambda i: (3 * i, 0, 0))
    return pl.pallas_call(
        halo_qkv_kernel,
        name="halo_qkv",
        cost_estimate=takes(7),
        grid=(2,),
        in_specs=[full(x) for x in args] + [ANY] * 4,
        out_specs=[pl.BlockSpec((None, rows // 2, width), lambda i: (i, 0, 0)), edge, edge, tall, tall],
        out_shape=[jax.ShapeDtypeStruct((2, rows // 2, width), BF)]
        + [jax.ShapeDtypeStruct(x.shape, x.dtype) for x in (k, v, kt, vt)],
        input_output_aliases={8: 1, 9: 2, 10: 3, 11: 4},
        scratch_shapes=[pltpu.VMEM((width // 128, rows, 128), FL)],
        compiler_params=params(),
    )(*args, k, v, kt, vt)


def two_heads(x):
    lane = lax.broadcasted_iota(jnp.int32, x.shape, 1)
    zero = jnp.zeros_like(x)
    return jnp.concatenate([jnp.where(lane < HD, x, zero), jnp.where(lane < HD, zero, x)], 0)


def one_block(x):
    r = x.shape[1] // 2
    line = lax.broadcasted_iota(jnp.int32, (128, r), 0)
    return jnp.where(line < HD, x[:, :r], x[:, r:]).T


def distances(bounds, row, c):
    low = bounds[0:1, pl.ds(row, QB)]
    high = bounds[1:2, pl.ds(row, QB)]
    query = (2 * (row + lax.broadcasted_iota(jnp.int32, (KC, QB), 1))).astype(FL) + 0.5
    key = (c * KC + lax.broadcasted_iota(jnp.int32, (KC, QB), 0)).astype(FL)
    far = jnp.where((key >= low) & (key < high), jnp.abs(query - key), FAR)
    return jnp.concatenate([far, far], 1)


def fold(x, f):
    n = x.shape[0] // 8
    parts = [x[8 * i : 8 * i + 8] for i in range(n)]
    while len(parts) > 1:
        parts = [f(parts[2 * i], parts[2 * i + 1]) for i in range(len(parts) // 2)]
    return parts[0]


def slope_line(slopes, head):
    lane = lax.broadcasted_iota(jnp.int32, (1, 2 * QB), 1)
    return jnp.where(lane < QB, slopes[head], slopes[head + 1])


def forward_kernel(
    spans, slopes, q, k, vt, bounds, o_out, exact_out, lse_out, s_scr, q2, top, total, acc, rest
):
    pairs = q.shape[1] // 128
    head0 = pl.program_id(0) * 2 * pairs
    q_first = q.shape[0] // 2
    slope = [slope_line(slopes, head0 + 2 * j) for j in range(pairs)]

    def query_block(b, _):
        row = pl.multiple_of(q_first + b * QB, QB)
        out_rows = pl.ds(pl.multiple_of(b * QB, QB), QB)
        block = row // QB
        c0 = spans[block]
        c1 = spans[spans.shape[0] // 2 + block]
        for j in range(pairs):
            q2[j] = two_heads(q[out_rows, 128 * j : 128 * j + 128])
        top[...] = jnp.full(top.shape, -3e38, FL)
        total[...] = jnp.zeros(total.shape, FL)
        acc[...] = jnp.zeros(acc.shape, FL)
        rest[...] = jnp.zeros(rest.shape, FL)

        def score(c, _):
            far = distances(bounds, row, c)
            keys = pl.ds(pl.multiple_of(c * KC, KC), KC)
            for j in range(pairs):
                s = dot_t(k[keys, 128 * j : 128 * j + 128], q2[j]) - slope[j] * far
                s_scr[c - c0, j] = s
                top[j] = jnp.maximum(top[j], fold(s, jnp.maximum))
            return 0

        lax.fori_loop(c0, c1, score, 0)
        peak = [jnp.max(top[j], 0, keepdims=True) for j in range(pairs)]

        def exponent(c, _):
            for j in range(pairs):
                e = jnp.exp(s_scr[c - c0, j] - peak[j])
                s_scr[c - c0, j] = e
                total[j] = total[j] + fold(e, jnp.add)
            return 0

        lax.fori_loop(c0, c1, exponent, 0)
        inverse = []
        for j in range(pairs):
            l = jnp.sum(total[j], 0, keepdims=True)
            t = peak[j] + jnp.log(l)
            inverse.append(1.0 / l)
            lse_out[2 * j : 2 * j + 1, out_rows] = t[:, :QB]
            lse_out[2 * j + 1 : 2 * j + 2, out_rows] = t[:, QB:]

        def attend(c, _):
            for j in range(pairs):
                p = s_scr[c - c0, j] * inverse[j]
                high = p.astype(BF)
                low = (p - high.astype(FL)).astype(BF)
                values = vt[c, 128 * j : 128 * j + 128]
                acc[j] = acc[j] + dot(values, high)
                rest[j] = rest[j] + dot(values, low)
            return 0

        lax.fori_loop(c0, c1, attend, 0)
        for j in range(pairs):
            cols = slice(128 * j, 128 * j + 128)
            o_out[out_rows, cols] = one_block(acc[j]).astype(BF)
            exact_out[out_rows, cols] = one_block(acc[j] + rest[j])
        return 0

    lse_out[...] = jnp.zeros(lse_out.shape, FL)
    lax.fori_loop(0, o_out.shape[0] // QB, query_block, 0)


def attend_forward(spans, slopes, q, k, vt, bounds):
    own, width = q.shape
    wide = width // 2
    pairs = wide // 128
    keys = k.shape[0]
    chunks = keys // KC
    col = lambda i, *_: (0, i)
    return pl.pallas_call(
        forward_kernel,
        name="attend_forward",
        cost_estimate=takes(30),
        grid_spec=pltpu.PrefetchScalarGridSpec(
            num_scalar_prefetch=2,
            grid=(2,),
            in_specs=[
                pl.BlockSpec((own, wide), col),
                pl.BlockSpec((keys, wide), col),
                pl.BlockSpec((chunks, wide, KC), lambda i, *_: (0, i, 0)),
                pl.BlockSpec(bounds.shape, lambda i, *_: (0, 0)),
            ],
            out_specs=[
                pl.BlockSpec((own, wide), col),
                pl.BlockSpec((own, wide), col),
                pl.BlockSpec((8, own), lambda i, *_: (i, 0)),
            ],
            scratch_shapes=[
                pltpu.VMEM((chunks, pairs, KC, 2 * QB), FL),
                pltpu.VMEM((pairs, 2 * QB, 128), BF),
                pltpu.VMEM((pairs, 8, 2 * QB), FL),
                pltpu.VMEM((pairs, 8, 2 * QB), FL),
                pltpu.VMEM((pairs, 128, 2 * QB), FL),
                pltpu.VMEM((pairs, 128, 2 * QB), FL),
            ],
        ),
        out_shape=[
            jax.ShapeDtypeStruct((own, width), BF),
            jax.ShapeDtypeStruct((own, width), FL),
            jax.ShapeDtypeStruct((16, own), FL),
        ],
        compiler_params=params(),
    )(spans, slopes, q, k, vt, bounds)


def pieces(x):
    out = []
    for _ in range(3):
        y = x.astype(BF).astype(FL)
        out.append(y)
        x = x - y
    return out


def key_lines(side, kind):
    lane = lax.broadcasted_iota(jnp.int32, (KC, 128), 1)
    key = lax.broadcasted_iota(jnp.int32, (KC, 128), 0).astype(FL)
    x = jnp.where(lane < 3, 1.0, jnp.where(lane < 6, -side, jnp.where(lane < 9, side * key, 0.0)))
    return jnp.where(lane == kind, 1.0, x) if kind else x


def chunk_lines(base, away, side, limit):
    lane = lax.broadcasted_iota(jnp.int32, (KC, 128), 1)
    key = lax.broadcasted_iota(jnp.int32, (KC, 128), 0).astype(FL) + KC * away
    other = jnp.where(side * key < side * limit, 1.0, 0.0)
    x = base + jnp.where((lane >= 9) & (lane < 12), side * KC * away, 0.0)
    return jnp.where(lane == 12, other, x).astype(BF)


def value_lines():
    lane = lax.broadcasted_iota(jnp.int32, (KC, 128), 1)
    return (lane < 3).astype(FL).astype(BF)


def query_rows(lse, slope, spots, out_left, out_right):
    one = jnp.ones_like(lse)
    rows = pieces(-lse) + pieces(slope * spots) + pieces(slope * one) * 2
    rows += [-FAR * one, -FAR * out_left, -FAR * out_right, 0.0 * one]
    return jnp.concatenate(rows, 0).astype(BF)


def two_heads_t(x):
    line = lax.broadcasted_iota(jnp.int32, x.shape, 0)
    zero = jnp.zeros_like(x)
    return jnp.concatenate([jnp.where(line < HD, x, zero), jnp.where(line < HD, zero, x)], 1)


def block_setup(bounds, row):
    low = bounds[0:1, pl.ds(row, QB)]
    high = bounds[1:2, pl.ds(row, QB)]
    first = low[:, 0:1]
    last = high[:, QB - 1 : QB]
    base = (2 * row).astype(FL) if hasattr(row, "astype") else float(2 * row)
    out_left = jnp.where(low == first, 0.0, 1.0)
    out_right = jnp.where(high == last, 0.0, 1.0)
    spots = 2.0 * lax.broadcasted_iota(jnp.int32, (1, QB), 1).astype(FL) + 0.5
    return low - base, high - base, first - base, last - base - 0.5, twice(out_left), twice(out_right), twice(spots)


def twice(x):
    return jnp.concatenate([x, x], 1)


def fill_queries(j, q, da, lse, delta, slope, setup, q2, da2, qt, dat):
    out_left, out_right, spots = setup[4:]
    q2[j] = two_heads(q)
    da2[j] = two_heads(da)
    qt[j, 0:128] = two_heads_t(q.T)
    dat[j, 0:128] = two_heads_t(da.T)
    qt[j, 128:144] = query_rows(lse, slope, spots, out_left, out_right)
    rows = pieces(-delta) + [jnp.zeros((13, 2 * QB), FL)]
    dat[j, 128:144] = jnp.concatenate(rows, 0).astype(BF)


def own_kernel(
    spans, slopes, q, k, v, kt, da, stats, bounds, dq_out, dk, dv, slope_out, q2, da2, qt, dat, dq2, sl, base
):
    pairs = q.shape[1] // 128
    head0 = pl.program_id(0) * 2 * pairs
    total_blocks = bounds.shape[1] // QB
    quarter = k.shape[0] // KC // 4
    first = total_blocks // 4
    slope = [slope_line(slopes, head0 + 2 * j) for j in range(pairs)]
    dk[...] = jnp.zeros(dk.shape, FL)
    dv[...] = jnp.zeros(dv.shape, FL)
    sl[...] = jnp.zeros(sl.shape, FL)
    qt[...] = jnp.zeros(qt.shape, BF)
    dat[...] = jnp.zeros(dat.shape, BF)
    line = lax.broadcasted_iota(jnp.int32, (16, KC), 0)
    spot = lax.broadcasted_iota(jnp.int32, (16, KC), 1).astype(FL)
    extra = jnp.where(line == 0, 1.0, jnp.where(line == 1, spot, 0.0)).astype(BF)
    base[0] = key_lines(1.0, 13)
    base[1] = key_lines(-1.0, 14)
    own_lines = key_lines(1.0, 0).astype(BF)
    ones = value_lines()

    def query_block(b, _):
        block = first + b
        row = pl.multiple_of(block * QB, QB)
        rows = pl.ds(pl.multiple_of(b * QB, QB), QB)
        c0 = spans[block]
        c1 = spans[total_blocks + block]
        setup = block_setup(bounds, row)
        low, high, limit_left, limit_right = setup[:4]
        spots = setup[6]
        for j in range(pairs):
            cols = slice(128 * j, 128 * j + 128)
            h = 2 * j
            lse = jnp.concatenate([stats[h : h + 1, rows], stats[h + 1 : h + 2, rows]], 1)
            delta = jnp.concatenate([stats[8 + h : 9 + h, rows], stats[9 + h : 10 + h, rows]], 1)
            fill_queries(j, q[rows, cols], da[rows, cols], lse, delta, slope[j], setup, q2, da2, qt, dat)
        dq2[...] = jnp.zeros(dq2.shape, FL)

        def step(c, lines, side, away, grads, wide):
            keys = pl.ds(pl.multiple_of(c * KC, KC), KC)
            col = [slice(128 * j, 128 * j + 128) for j in range(pairs)]
            s = [dot(jnp.concatenate([k[keys, col[j]], lines], 1), qt[j]) for j in range(pairs)]
            dp = [dot(jnp.concatenate([v[keys, col[j]], ones], 1), dat[j]) for j in range(pairs)]
            if wide is not None:
                s = [s[j] - slope[j] * wide for j in range(pairs)]
            p = [jnp.exp(x) for x in s]
            ds = [(p[j] * dp[j]).astype(BF) for j in range(pairs)]
            if grads:
                mine = pl.ds(pl.multiple_of((c - quarter) * KC, KC), KC)
                new_v = [dot(p[j].astype(BF), da2[j]) for j in range(pairs)]
                new_k = [dot(ds[j], q2[j]) for j in range(pairs)]
            r = [dot(jnp.concatenate([kt[c, col[j]], extra], 0), ds[j]) for j in range(pairs)]
            for j in range(pairs):
                if grads:
                    dv[mine, col[j]] = dv[mine, col[j]] + new_v[j]
                    dk[mine, col[j]] = dk[mine, col[j]] + new_k[j]
                dq2[j] = dq2[j] + r[j][0:128]
                part = side * ((spots - KC * away) * r[j][128:129] - r[j][129:130])
                if wide is not None:
                    part = part + jnp.sum(ds[j].astype(FL) * wide, 0, keepdims=True)
                sl[j] = sl[j] + part

        key = lax.broadcasted_iota(jnp.int32, (KC, QB), 0).astype(FL)
        over = 2.0 * jnp.maximum(key - spots[:, :QB], 0.0)
        wide = twice(jnp.where((key >= low) & (key < high), over, FAR))
        step(block, own_lines, 1.0, 0.0, True, wide)

        def other(c, grads):
            before = c < block
            side = jnp.where(before, 1.0, -1.0)
            away = (c - block).astype(FL)
            limit = jnp.where(before, limit_left, limit_right)
            step(c, chunk_lines(base[jnp.where(before, 0, 1)], away, side, limit), side, away, grads, None)

        def inside(i, _):
            other(jnp.where(i < block, i, i + 1), True)
            return 0

        left = jnp.maximum(jnp.minimum(c1, quarter) - c0, 0)
        right0 = jnp.maximum(c0, 3 * quarter)

        def outside(i, _):
            other(jnp.where(i < left, c0 + i, right0 + i - left), False)
            return 0

        lax.fori_loop(jnp.maximum(c0, quarter), jnp.minimum(c1, 3 * quarter) - 1, inside, 0)
        lax.fori_loop(0, left + jnp.maximum(c1 - right0, 0), outside, 0)
        for j in range(pairs):
            dq_out[rows, 128 * j : 128 * j + 128] = (one_block(dq2[j]) * HD**-0.5).astype(BF)
        return 0

    lax.fori_loop(0, da.shape[0] // QB, query_block, 0)
    slope_out[...] = jnp.zeros(slope_out.shape, FL)
    for j in range(pairs):
        slope_out[8 * j : 8 * j + 1] = sl[j]


def attend_own(spans, slopes, q, k, v, kt, da, stats, bounds):
    own, width = q.shape
    wide = width // 2
    pairs = wide // 128
    keys = k.shape[0]
    chunks = keys // KC
    col = lambda i, *_: (0, i)
    zero = lambda i, *_: (0, 0)
    return pl.pallas_call(
        own_kernel,
        name="attend_own",
        cost_estimate=takes(30),
        grid_spec=pltpu.PrefetchScalarGridSpec(
            num_scalar_prefetch=2,
            grid=(2,),
            in_specs=[
                pl.BlockSpec((own, wide), col),
                pl.BlockSpec((keys, wide), col),
                pl.BlockSpec((keys, wide), col),
                pl.BlockSpec((chunks, wide, KC), lambda i, *_: (0, i, 0)),
                pl.BlockSpec((own, wide), col),
                pl.BlockSpec((16, own), lambda i, *_: (i, 0)),
                pl.BlockSpec(bounds.shape, zero),
            ],
            out_specs=[
                pl.BlockSpec((own, wide), col),
                pl.BlockSpec((keys // 2, wide), col),
                pl.BlockSpec((keys // 2, wide), col),
                pl.BlockSpec((8 * pairs, 2 * QB), lambda i, *_: (i, 0)),
            ],
            scratch_shapes=[
                pltpu.VMEM((pairs, 2 * QB, 128), BF),
                pltpu.VMEM((pairs, 2 * QB, 128), BF),
                pltpu.VMEM((pairs, 256, 2 * QB), BF),
                pltpu.VMEM((pairs, 256, 2 * QB), BF),
                pltpu.VMEM((pairs, 128, 2 * QB), FL),
                pltpu.VMEM((pairs, 1, 2 * QB), FL),
                pltpu.VMEM((2, KC, 128), FL),
            ],
        ),
        out_shape=[
            jax.ShapeDtypeStruct((own, width), BF),
            jax.ShapeDtypeStruct((keys // 2, width), FL),
            jax.ShapeDtypeStruct((keys // 2, width), FL),
            jax.ShapeDtypeStruct((16 * pairs, 2 * QB), FL),
        ],
        compiler_params=params(),
    )(spans, slopes, q, k, v, kt, da, stats, bounds)


def halo_kernel(
    spans, slopes, q, k, v, low_pay, high_pay, bounds, dk0, dv0, dk_out, dv_out, q2, da2, qt, dat, st, dk, dv
):
    width = q.shape[2]
    pairs = width // 128
    total_blocks = bounds.shape[1] // QB
    quarter = k.shape[0] // KC // 4
    count = low_pay.shape[0] // QB
    dk[...] = dk0[...]
    dv[...] = dv0[...]
    qt[...] = jnp.zeros(qt.shape, BF)
    dat[...] = jnp.zeros(dat.shape, BF)
    ones = value_lines()
    for side, pay in enumerate((low_pay, high_pay)):
        x = pay[:, width : width + 128].astype(FL)
        st[side] = (x + pltpu.roll(x, 96, 1) + pltpu.roll(x, 64, 1)).T

    def query_block(i, _):
        side = i // count
        nth = i - side * count
        block = jnp.where(side == 0, i, total_blocks - 2 * count + i)
        row = pl.multiple_of(block * QB, QB)
        rows = pl.ds(pl.multiple_of(nth * QB, QB), QB)
        c0 = spans[block]
        c1 = spans[total_blocks + block]

        @pl.when(c0 < c1)
        def _():
            setup = block_setup(bounds, row)
            limit = jnp.where(side == 0, setup[3], setup[2])
            sign = jnp.where(side == 0, -1.0, 1.0)
            base = jnp.where(side == 0, key_lines(-1.0, 14), key_lines(1.0, 13))
            for j in range(pairs):
                cols = slice(128 * j, 128 * j + 128)
                h = 2 * j
                at = 16 * (h // (width // 128)) + h % (width // 128)
                lse = jnp.concatenate([st[side, at : at + 1, rows], st[side, at + 1 : at + 2, rows]], 1)
                delta = jnp.concatenate([st[side, at + 8 : at + 9, rows], st[side, at + 9 : at + 10, rows]], 1)
                d = jnp.where(side == 0, low_pay[rows, cols], high_pay[rows, cols])
                fill_queries(
                    j, q[side, rows, cols], d, lse, delta, slope_line(slopes, h), setup, q2, da2, qt, dat
                )

            def step(c, _):
                keys = pl.ds(pl.multiple_of(c * KC, KC), KC)
                mine = pl.ds(pl.multiple_of((c - quarter) * KC, KC), KC)
                lines = chunk_lines(base, (c - block).astype(FL), sign, limit)
                for g in range(0, pairs, 3):
                    js = range(g, g + 3)
                    col = {j: slice(128 * j, 128 * j + 128) for j in js}
                    p = [jnp.exp(dot(jnp.concatenate([k[keys, col[j]], lines], 1), qt[j])) for j in js]
                    dp = [dot(jnp.concatenate([v[keys, col[j]], ones], 1), dat[j]) for j in js]
                    new_v = [dot(x.astype(BF), da2[j]) for x, j in zip(p, js)]
                    new_k = [dot((x * y).astype(BF), q2[j]) for x, y, j in zip(p, dp, js)]
                    for j, x, y in zip(js, new_v, new_k):
                        dv[mine, col[j]] = dv[mine, col[j]] + x
                        dk[mine, col[j]] = dk[mine, col[j]] + y
                return 0

            lax.fori_loop(c0, c1, step, 0)

        return 0

    lax.fori_loop(0, 2 * count, query_block, 0)
    dk_out[...] = dk[...].astype(BF)
    dv_out[...] = dv[...].astype(BF)


def attend_halo(spans, slopes, q, k, v, low_pay, high_pay, bounds, dk0, dv0):
    width = q.shape[2]
    pairs = width // 128
    keys = dk0.shape[0]
    full = lambda x: pl.BlockSpec(x.shape, lambda i, *_: (0,) * len(x.shape))
    shape = jax.ShapeDtypeStruct((keys, width), BF)
    return pl.pallas_call(
        halo_kernel,
        name="attend_halo",
        cost_estimate=takes(12),
        grid_spec=pltpu.PrefetchScalarGridSpec(
            num_scalar_prefetch=2,
            grid=(1,),
            in_specs=[full(x) for x in (q, k, v, low_pay, high_pay, bounds, dk0, dv0)],
            out_specs=[full(shape), full(shape)],
            scratch_shapes=[
                pltpu.VMEM((pairs, 2 * QB, 128), BF),
                pltpu.VMEM((pairs, 2 * QB, 128), BF),
                pltpu.VMEM((pairs, 256, 2 * QB), BF),
                pltpu.VMEM((pairs, 256, 2 * QB), BF),
                pltpu.VMEM((2, 128, low_pay.shape[0]), FL),
                pltpu.VMEM((keys, width), FL),
                pltpu.VMEM((keys, width), FL),
            ],
        ),
        out_shape=[shape, shape],
        compiler_params=params(),
    )(spans, slopes, q, k, v, low_pay, high_pay, bounds, dk0, dv0)


def normalize(z):
    centred = z - jnp.mean(z, -1, keepdims=True)
    scale = lax.rsqrt(jnp.mean(centred * centred, -1, keepdims=True) + EPS)
    return centred * scale, scale


def normalize_back(d, unit, scale):
    return scale * (d - jnp.mean(d, -1, keepdims=True) - unit * jnp.mean(d * unit, -1, keepdims=True))


def rows_sum(x):
    return jnp.sum(x, 0, keepdims=True)


def middle_kernel(
    ids,
    pool,
    att,
    exact,
    lse,
    cot,
    vec,
    upb,
    low,
    high,
    olow,
    ohigh,
    out,
    pay,
    stats,
    mixed,
    gvec,
    gup,
    keep,
    send,
    wo,
    w1,
    w2,
    active,
    slope,
    unit1,
    hid,
    hid_low,
    z,
    d2,
    dw1,
    dw2,
    dwo,
    sems,
):
    n, width = att.shape
    rb = width // NB
    fb = w2.shape[0] // NB
    parts = w1.shape[0]

    def rows(r, size):
        return pl.ds(pl.multiple_of(r, 16), size)

    def copies_a(block, s, p):
        pltpu.make_async_copy(block.at[pl.ds(192, 32)], wo.at[rows(s * rb, 32)], sems.at[0]).start()
        pltpu.make_async_copy(block.at[pl.ds(0, 192)], w2.at[rows(s * fb, 192)], sems.at[2]).start()

    def copies_b(block, s, p):
        pltpu.make_async_copy(block.at[pl.ds(192, 16)], wo.at[rows(s * rb + 32, 16)], sems.at[0]).start()
        for c in range(parts):
            pltpu.make_async_copy(block.at[pl.ds(48 * c, 48)], w1.at[c, rows(s * rb, 48)], sems.at[1]).start()

    load_sets(ids, low, high, olow, ohigh, copies_a, copies_b)
    wait_all(wo, sems.at[0])
    z[...] = dot(att[...], wo[...])
    rc = 128

    def row_loop(f):
        def body(i, _):
            f(pl.ds(pl.multiple_of(i * rc, rc), rc), i)
            return 0

        lax.fori_loop(0, n // rc, body, 0)

    def first_norm(r, i):
        unit, scale = normalize(pool[r, :] + z[r, :] + vec[2:3])
        h = unit * vec[3:4] + vec[4:5]
        unit1[r, :] = unit
        d2[r, 0:128] = jnp.broadcast_to(scale, (rc, 128))
        hid[r, :] = h
        hid_low[r, :] = h.astype(BF)

    row_loop(first_norm)
    wait_all(w1, sems.at[1])
    wait_all(w2, sems.at[2])
    c0 = 0.7978845608028654

    def up(c, _):
        inner = dot(hid_low[...], w1[c]) + upb[pl.ds(0, 1), pl.ds(pl.multiple_of(c * width, 128), width)]
        sq = inner * inner
        t = jnp.tanh(c0 * (inner + 0.044715 * (inner * sq)))
        cdf = 0.5 * (1.0 + t)
        active[c] = (inner * cdf).astype(BF)
        slope[c] = cdf + inner * (0.5 * (1.0 - t * t)) * (c0 + (3 * 0.044715 * c0) * sq)
        part = dot(active[c], w2[pl.ds(pl.multiple_of(c * width, 128), width), :])
        z[...] = jnp.where(c == 0, part, z[...] + part)
        return 0

    lax.fori_loop(0, parts, up, 0)
    gvec[...] = jnp.zeros(gvec.shape, FL)

    def second_norm(r, i):
        unit, scale = normalize(hid[r, :] + (z[r, :] + vec[5:6]))
        out[r, :] = (unit * vec[6:7] + vec[7:8]).astype(BF)
        dy = cot[r, :].astype(FL)
        gvec[6:7] = gvec[6:7] + rows_sum(dy * unit)
        gvec[7:8] = gvec[7:8] + rows_sum(dy)
        d = normalize_back(dy * vec[6:7], unit, scale)
        hid[r, :] = d
        d_low = d.astype(BF)
        att_like[r, :] = d_low
        gvec[5:6] = gvec[5:6] + rows_sum(d_low.astype(FL))

    att_like = pay.at[:, 0:width]
    scale1 = d2[:, 0:1]
    row_loop(second_norm)
    z[...] = jnp.zeros(z.shape, FL)

    def down(c, _):
        ffn = pay[:, 0:width]
        far = pl.ds(pl.multiple_of(c * width, 128), width)
        d_inner = (dot_t(ffn, w2[far, :]) * slope[c]).astype(BF)
        gup[:, far] = jnp.broadcast_to(rows_sum(d_inner.astype(FL)), (8, width))
        dw2[far, :] = t_dot(active[c], ffn).astype(BF)
        dw1[c] = t_dot(hid_low[...], d_inner).astype(BF)
        z[...] = z[...] + dot_t(d_inner, w1[c])
        return 0

    lax.fori_loop(0, parts, down, 0)

    def store_sets(a_ref, b_ref):
        for p in range(NB):
            s = ids[0] ^ rel_a(p)
            pltpu.make_async_copy(dw2.at[rows(s * fb, 192)], a_ref.at[p, pl.ds(0, 192)], sems.at[3]).start()
            s = ids[0] ^ rel_b(p)
            for c in range(parts):
                pltpu.make_async_copy(
                    dw1.at[c, rows(s * rb, 48)], b_ref.at[p, pl.ds(48 * c, 48)], sems.at[3]
                ).start()

    @pl.when(ids[1] == 0)
    def _():
        store_sets(keep, send)

    @pl.when(ids[1] != 0)
    def _():
        store_sets(send, keep)

    def first_back(r, i):
        unit = unit1[r, :]
        d = hid[r, :] + z[r, :]
        gvec[3:4] = gvec[3:4] + rows_sum(d * unit)
        gvec[4:5] = gvec[4:5] + rows_sum(d)
        d = normalize_back(d * vec[3:4], unit, d2[r, 0:1])
        mixed[r, :] = d
        d_low = d.astype(BF)
        hid_low[r, :] = d_low
        gvec[2:3] = gvec[2:3] + rows_sum(d_low.astype(FL))

    row_loop(first_back)
    dwo[...] = t_dot(att[...], hid_low[...]).astype(BF)

    def store_wo(a_ref, b_ref):
        for p in range(NB):
            s = ids[0] ^ rel_a(p)
            pltpu.make_async_copy(dwo.at[rows(s * rb, 32)], a_ref.at[p, pl.ds(192, 32)], sems.at[3]).start()
            s = ids[0] ^ rel_b(p)
            pltpu.make_async_copy(dwo.at[rows(s * rb + 32, 16)], b_ref.at[p, pl.ds(192, 16)], sems.at[3]).start()
            pltpu.make_async_copy(dwo.at[rows(s * rb + 32, 16)], b_ref.at[p, pl.ds(208, 16)], sems.at[3]).start()

    @pl.when(ids[1] == 0)
    def _():
        store_wo(keep, send)

    @pl.when(ids[1] != 0)
    def _():
        store_wo(send, keep)

    z[...] = dot_t(hid_low[...], wo[...])
    heads = width // HD
    head_of = lax.broadcasted_iota(jnp.int32, (16, width), 1) // HD
    head_of = jnp.where(head_of < heads // 2, head_of, head_of - heads // 2 + 8)
    pick = (head_of == lax.broadcasted_iota(jnp.int32, (16, width), 0)).astype(FL).astype(BF)
    stats[0:8, :] = lse[0:8, :]
    stats[16:24, :] = lse[8:16, :]

    def last(r, i):
        d_low = z[r, :].astype(BF)
        pay[r, 0:width] = d_low
        prod = d_low.astype(FL) * exact[r, :]
        delta = jnp.zeros((16, rc), FL)
        for _ in range(3):
            piece = prod.astype(BF)
            delta = delta + dot_t(pick, piece)
            prod = prod - piece.astype(FL)
        stats[8:16, r] = delta[0:8]
        stats[24:32, r] = delta[8:16]

    row_loop(last)
    st = stats[...].T
    pieces = []
    for _ in range(3):
        piece = st.astype(BF).astype(FL)
        pieces.append(piece)
        st = st - piece
    pieces.append(jnp.zeros_like(st))
    pay[:, width:] = jnp.concatenate(pieces, 1).astype(BF)
    wait_all(keep, sems.at[3])
    wait_all(send, sems.at[3])


def middle(ids, pool, att, exact, lse, cot, vec, upb, sets, set_rows):
    n, width = pool.shape
    ff = upb.shape[1]
    parts = ff // width
    whole = lambda i, *_: (0, 0)
    full = lambda x: pl.BlockSpec(x.shape, whole)
    shapes = [
        jax.ShapeDtypeStruct((n, width), BF),
        jax.ShapeDtypeStruct((n, width + 128), BF),
        jax.ShapeDtypeStruct((32, n), FL),
        jax.ShapeDtypeStruct((n, width), FL),
        jax.ShapeDtypeStruct((8, width), FL),
        jax.ShapeDtypeStruct((8, ff), FL),
    ]
    big = jax.ShapeDtypeStruct((NB, set_rows, width), BF)
    return pl.pallas_call(
        middle_kernel,
        name="middle",
        cost_estimate=takes(36),
        grid_spec=pltpu.PrefetchScalarGridSpec(
            num_scalar_prefetch=1,
            grid=(1,),
            in_specs=[full(pool)]
            + [full(x) for x in (att, exact, lse, cot, vec, upb)]
            + [ANY] * 4,
            out_specs=[full(x) for x in shapes] + [ANY, ANY],
            scratch_shapes=[
                pltpu.VMEM((width, width), BF),
                pltpu.VMEM((parts, width, width), BF),
                pltpu.VMEM((ff, width), BF),
                pltpu.VMEM((parts, n, width), BF),
                pltpu.VMEM((parts, n, width), FL),
                pltpu.VMEM((n, width), FL),
                pltpu.VMEM((n, width), FL),
                pltpu.VMEM((n, width), BF),
                pltpu.VMEM((n, width), FL),
                pltpu.VMEM((n, 128), FL),
                pltpu.VMEM((parts, width, width), BF),
                pltpu.VMEM((ff, width), BF),
                pltpu.VMEM((width, width), BF),
                pltpu.SemaphoreType.DMA((4,)),
            ],
        ),
        out_shape=shapes + [big, big],
        compiler_params=params(),
    )(ids, pool, att, exact, lse, cot, vec, upb, *sets)


def weights_kernel(ids, pool, tok, dq, dk, dv, gvec, gup, sl, keep, send, dwq, dwk, dwv, bias, tt, sems):
    width = tok.shape[1]
    ff = gup.shape[1]
    rb = width // NB
    tt[...] = tok[...].T
    dwq[...] = t_dot(pool[...].astype(BF), dq[...]).astype(BF)

    def columns(c, _):
        cols = pl.ds(pl.multiple_of(c * 256, 256), 256)
        dwk[:, cols] = dot(tt[...], dk[:, cols]).astype(BF)
        dwv[:, cols] = dot(tt[...], dv[:, cols]).astype(BF)
        return 0

    lax.fori_loop(0, width // 256, columns, 0)

    def rows(r, size):
        return pl.ds(pl.multiple_of(r, 16), size)

    def go(src, dst):
        pltpu.make_async_copy(src, dst, sems.at[0]).start()

    def store_sets(a_ref, b_ref):
        for p in range(NB):
            s = ids[0] ^ rel_a(p)
            go(dwq.at[rows(s * rb, 48)], a_ref.at[p, pl.ds(0, 48)])
            go(dwk.at[rows(s * rb, 32)], a_ref.at[p, pl.ds(48, 32)])
            s = ids[0] ^ rel_b(p)
            go(dwk.at[rows(s * rb + 32, 16)], b_ref.at[p, pl.ds(0, 16)])
            go(dwv.at[rows(s * rb, 48)], b_ref.at[p, pl.ds(16, 48)])

    @pl.when(ids[1] == 0)
    def _():
        store_sets(keep, send)

    @pl.when(ids[1] != 0)
    def _():
        store_sets(send, keep)

    row = lax.broadcasted_iota(jnp.int32, (16, width), 0)
    g = jnp.concatenate([gvec[...], jnp.zeros((8, width), FL)], 0)
    g = jnp.where(row == 0, rows_sum(dq[...].astype(FL)), g)
    g = jnp.where(row == 1, rows_sum(dv[...].astype(FL)), g)
    block_of = div_rb(lax.broadcasted_iota(jnp.int32, (16, width), 1))
    parts = []
    for p in range(NB):
        parts.append(jnp.where(block_of == (ids[0] ^ rel_b(p)), g, 0.0).astype(BF))
    total = dot_t(jnp.concatenate(parts, 0), spread_matrix(128, width, rb))
    row = lax.broadcasted_iota(jnp.int32, (16, ff), 0)
    block_of = div_rb(lax.broadcasted_iota(jnp.int32, (16, ff), 1))
    block_of = jnp.where((row >= 8) & (row < 12), block_of - row + 8, -1)
    up = jnp.concatenate([gup[...], gup[...]], 0)
    parts = []
    for p in range(NB):
        parts.append(jnp.where(block_of == 4 * (ids[0] ^ rel_b(p)), up, 0.0).astype(BF))
    total = total + dot_t(jnp.concatenate(parts, 0), spread_matrix(128, ff, rb))
    line = jnp.zeros((1, 128), FL)
    lane = lax.broadcasted_iota(jnp.int32, (1, 128), 1)
    for j in range(sl.shape[0] // 8):
        for i in range(2):
            value = jnp.sum(sl[8 * j : 8 * j + 1, QB * i : QB * i + QB], 1, keepdims=True)
            line = jnp.where(lane == 2 * j + i, -value, line)
    row = lax.broadcasted_iota(jnp.int32, (16 * NB, 128), 0)
    total = jnp.where((row & 15) == 12, line, total)
    bias[...] = jnp.zeros(bias.shape, BF)
    bias[:, 0:128] = total.astype(BF)

    def store_bias(b_ref):
        for p in range(NB):
            go(bias.at[pl.ds(16 * p, 16)], b_ref.at[p, pl.ds(64, 16)])

    @pl.when(ids[1] == 0)
    def _():
        store_bias(send)

    @pl.when(ids[1] != 0)
    def _():
        store_bias(keep)

    wait_all(keep, sems.at[0])
    wait_all(send, sems.at[0])


def weight_grads(ids, pool, tok, dq, dk, dv, gvec, gup, sl, set_rows):
    width = tok.shape[1]
    full = lambda x: pl.BlockSpec(x.shape, lambda i, *_: (0, 0))
    big = jax.ShapeDtypeStruct((NB, set_rows, width), BF)
    square = pltpu.VMEM((width, width), BF)
    return pl.pallas_call(
        weights_kernel,
        name="weight_grads",
        cost_estimate=takes(9),
        grid_spec=pltpu.PrefetchScalarGridSpec(
            num_scalar_prefetch=1,
            grid=(1,),
            in_specs=[full(x) for x in (pool, tok, dq, dk, dv, gvec, gup, sl)],
            out_specs=[ANY, ANY],
            scratch_shapes=[
                square,
                square,
                square,
                pltpu.VMEM((16 * NB, width), BF),
                pltpu.VMEM((width, tok.shape[0]), BF),
                pltpu.SemaphoreType.DMA((1,)),
            ],
        ),
        out_shape=[big, big],
        compiler_params=params(),
    )(ids, pool, tok, dq, dk, dv, gvec, gup, sl)


def tokens_kernel(mixed, dq, dk, dv, wq, wk, wv, out, acc):
    half = mixed.shape[0]
    up = 0.5 * (mixed[...] + dot_t(dq[...], wq[...]))
    down = dot_t(dk[...], wk[...]) + dot_t(dv[...], wv[...])
    for j in range(mixed.shape[1] // 128):
        cols = slice(128 * j, 128 * j + 128)
        for i in range(2):
            acc[j, pl.ds(i, half, stride=2)] = up[:, cols]
        out[:, cols] = acc[j] + down[:, cols]


def token_grads(mixed, dq, dk, dv, wq, wk, wv):
    rows, width = dk.shape
    step = 512
    half = pl.BlockSpec((step // 2, width), lambda i: (i, 0))
    block = pl.BlockSpec((step, width), lambda i: (i, 0))
    whole = pl.BlockSpec((width, width), lambda i: (0, 0))
    return pl.pallas_call(
        tokens_kernel,
        name="token_grads",
        cost_estimate=takes(8),
        grid=(rows // step,),
        in_specs=[half, half, block, block, whole, whole, whole],
        out_specs=block,
        out_shape=jax.ShapeDtypeStruct((rows, width), FL),
        scratch_shapes=[pltpu.VMEM((width // 128, step, 128), FL)],
        compiler_params=params(),
    )(mixed, dq, dk, dv, wq, wk, wv)


def blocks_of(x):
    return x.reshape(NB, x.shape[0] // NB, x.shape[1])


def column_parts(x, width):
    return jnp.concatenate([x[..., width * c : width * c + width] for c in range(x.shape[-1] // width)], -2)


def bias_block(small, up, width):
    rb = small[0].shape[-1]
    rows = jnp.stack(list(small) + [up[..., rb * c : rb * c + rb] for c in range(4)], -2)
    pad = [(0, 0)] * (rows.ndim - 2) + [(0, 4), (0, width - rb)]
    return jnp.pad(rows, pad)


def pack(wq, wk, wv, wo, w1, w2, bias, width):
    a1 = jnp.concatenate([wq, wk[..., :32, :]], -2)
    b1 = jnp.concatenate([wk[..., 32:, :], wv, bias], -2)
    a2 = jnp.concatenate([w2, wo[..., :32, :]], -2)
    b2 = jnp.concatenate([column_parts(w1, width), wo[..., 32:, :], wo[..., 32:, :]], -2)
    return a1, b1, a2, b2


def unpack(a1, b1, a2, b2, width):
    wq = a1[..., :48, :]
    wk = jnp.concatenate([a1[..., 48:, :], b1[..., :16, :]], -2)
    wv = b1[..., 16:64, :]
    bias = b1[..., 64:, :]
    wo = jnp.concatenate([a2[..., 192:, :], b2[..., 192:208, :]], -2)
    w2 = a2[..., :192, :]
    parts = 4
    w1 = jnp.concatenate([b2[..., 48 * c : 48 * c + 48, :] for c in range(parts)], -1)
    return wq, wk, wv, wo, w1, w2, bias


def pack_kernel(ids, wq, wk, wv, wo, w1, w2, b_up, *refs):
    vectors, (out, bias) = refs[:8], refs[8:]
    first = out.at[:, 0:80]
    second = out.at[:, 80:304]
    rb, width = wq.shape

    @pl.when(ids[1] == 0)
    def _():
        first[0, 0:48] = wq[...].astype(BF)
        first[0, 48:80] = wk[0:32].astype(BF)
        second[0, 0:192] = w2[...].astype(BF)
        second[0, 192:224] = wo[0:32].astype(BF)

    @pl.when(ids[1] != 0)
    def _():
        bias[...] = jnp.zeros(bias.shape, FL)
        for i, x in enumerate(vectors):
            bias[i : i + 1, 0:rb] = x[...]
        for c in range(4):
            bias[8 + c : 9 + c, 0:rb] = b_up[:, rb * c : rb * c + rb]
        first[0, 0:16] = wk[32:48].astype(BF)
        first[0, 16:64] = wv[...].astype(BF)
        first[0, 64:80] = bias[...].astype(BF)
        for c in range(4):
            second[0, 48 * c : 48 * c + 48] = w1[:, width * c : width * c + width].astype(BF)
        second[0, 192:208] = wo[32:48].astype(BF)
        second[0, 208:224] = wo[32:48].astype(BF)


def pack_own(ids, masters, b_up, vectors):
    width = masters[0].shape[1]
    args = list(masters) + [b_up[None]] + [x[None] for x in vectors]
    full = lambda x: pl.BlockSpec(x.shape, lambda i, *_: (0,) * len(x.shape))
    shape = jax.ShapeDtypeStruct((1, 304, width), BF)
    return pl.pallas_call(
        pack_kernel,
        name="pack",
        cost_estimate=takes(3),
        grid_spec=pltpu.PrefetchScalarGridSpec(
            num_scalar_prefetch=1,
            grid=(1,),
            in_specs=[full(x) for x in args],
            out_specs=full(shape),
            scratch_shapes=[pltpu.VMEM((16, width), FL)],
        ),
        out_shape=shape,
        compiler_params=params(),
    )(ids, *args)


def unpack_kernel(ids, mine1, other1, mine2, other2, wq, wk, wv, wo, w1, w2, *vectors):
    width = wq.shape[1]
    rb = wq.shape[0]

    def store(a1, b1, a2, b2):
        wq[...] = a1[0:48]
        wk[0:32] = a1[48:80]
        wk[32:48] = b1[0:16]
        wv[...] = b1[16:64]
        for i in range(8):
            vectors[i][...] = b1[64 + i : 65 + i, 0:rb]
        for c in range(4):
            vectors[8][:, rb * c : rb * c + rb] = b1[72 + c : 73 + c, 0:rb]
            w1[:, width * c : width * c + width] = b2[48 * c : 48 * c + 48]
        vectors[9][...] = b1[76:77, 0:128]
        w2[...] = a2[0:192]
        wo[0:32] = a2[192:224]
        wo[32:48] = b2[192:208]

    @pl.when(ids[1] == 0)
    def _():
        store(mine1, other1, mine2, other2)

    @pl.when(ids[1] != 0)
    def _():
        store(other1, mine1, other2, mine2)


def unpack_own(ids, args, ff):
    width = args[0].shape[1]
    rb = width // NB
    dims = [(rb, width)] * 4 + [(rb, ff), (ff // NB, width)] + [(1, rb)] * 8 + [(1, ff // NB), (1, 128)]
    shapes = [jax.ShapeDtypeStruct(d, FL) for d in dims]
    full = lambda x: pl.BlockSpec(x.shape, lambda i, *_: (0, 0))
    return pl.pallas_call(
        unpack_kernel,
        name="unpack",
        cost_estimate=takes(3),
        grid_spec=pltpu.PrefetchScalarGridSpec(
            num_scalar_prefetch=1,
            grid=(1,),
            in_specs=[full(x) for x in args],
            out_specs=[full(x) for x in shapes],
        ),
        out_shape=shapes,
        compiler_params=params(),
    )(ids, *args)


def after(x, *done):
    return lax.optimization_barrier((x,) + done)[0]


def local(
    tokens,
    cotangent,
    lengths,
    w_query,
    b_query,
    w_key,
    w_value,
    b_value,
    w_output,
    b_output,
    gain_attn,
    shift_attn,
    w_up,
    b_up,
    w_down,
    b_down,
    gain_ffn,
    shift_ffn,
    distance_slope,
):
    rows_here, width = tokens.shape
    ff = w_up.shape[1]
    own = rows_here // 2
    halo = rows_here // 2
    seq = lax.axis_size("seq")
    devices = seq * lax.axis_size("dp")
    direct = seq == NB
    order = ("dp", "seq")
    up_pairs = [(i, i + 1) for i in range(devices - 1)]
    down_pairs = [(i + 1, i) for i in range(devices - 1)]

    masters = (w_query, w_key, w_value, w_output, w_up, w_down)
    vectors = (b_query, b_value, b_output, gain_attn, shift_attn, b_down, gain_ffn, shift_ffn)
    if direct:
        core = lax.axis_index("dp")
        ids = jnp.stack([lax.axis_index("seq"), core]).astype(jnp.int32)
        x = pack_own(ids, masters, b_up, vectors)
        y = x[:, 80:]
        x = x[:, :80]
        x = jnp.concatenate([x, exchange(x, 8, 4)], 0)
        x1, low_a = lax.optimization_barrier(
            (exchange(x, 4, 8), lax.ppermute(tokens[rows_here - halo : rows_here - halo // 2], order, up_pairs))
        )
        x = jnp.concatenate([x, x1], 0)
        y, part = lax.optimization_barrier((y, tokens[rows_here - halo // 2 :], x1))[:2]
        x1, y1, low_b = lax.optimization_barrier(
            (exchange(x, 2, 1), exchange(y, 8, 4), lax.ppermute(part, order, up_pairs))
        )
        low1 = jnp.concatenate([x, x1], 0)
        y = jnp.concatenate([y, y1], 0)
        high1, olow1, y1, high_a = lax.optimization_barrier(
            (
                exchange(low1, 1, 2),
                swap_core(low1),
                exchange(y, 4, 8),
                lax.ppermute(after(tokens[: halo // 2], x1), order, down_pairs),
            )
        )
        y = jnp.concatenate([y, y1], 0)
        sets1 = (low1, high1, olow1, swap_core(high1))
        y1 = exchange(y, 2, 1)
        high_b = lax.ppermute(after(tokens[halo // 2 : halo], high1), order, down_pairs)
    else:
        ids = jnp.zeros((2,), jnp.int32)
        gather = lambda x: lax.all_gather(x.astype(BF), "seq", axis=0, tiled=True)
        full = [blocks_of(gather(x)) for x in masters]
        small = [gather(x).reshape(NB, -1) for x in vectors]
        bias = bias_block(small, gather(b_up).reshape(NB, -1), width)
        a1, b1, a2, b2 = pack(*full, bias, width)
        at_a = jnp.array([rel_a(p) for p in range(NB)])
        at_b = jnp.array([rel_b(p) for p in range(NB)])
        sets1 = (a1[at_a[:8]], a1[at_a[8:]], b1[at_b[:8]], b1[at_b[8:]])
        sets2 = (a2[at_a[:8]], a2[at_a[8:]], b2[at_b[:8]], b2[at_b[8:]])
        low_a = lax.ppermute(tokens[rows_here - halo : rows_here - halo // 2], order, up_pairs)
        low_b = lax.ppermute(tokens[rows_here - halo // 2 :], order, up_pairs)
        high_a = lax.ppermute(tokens[: halo // 2], order, down_pairs)
        high_b = lax.ppermute(tokens[halo // 2 : halo], order, down_pairs)

    first_row = lax.axis_index(order) * rows_here
    total = devices * rows_here
    starts = 2 * (jnp.cumsum(lengths) - lengths)
    place = first_row - halo + 2 * jnp.arange(2 * own, dtype=jnp.int32)
    before = starts[None, :] <= place[:, None]
    begin = jnp.max(jnp.where(before, starts[None, :], 0), 1)
    end = jnp.min(jnp.where(before, total, starts[None, :]), 1)
    inside = (place >= 0) & (place < total)
    shift = first_row - halo
    begin = jnp.where(inside, begin - shift, 0)
    end = jnp.where(inside, end - shift, 0)
    bounds = jnp.pad(jnp.stack([begin, end], 0).astype(FL), ((0, 6), (0, 0)))
    blocks = 2 * own // QB
    chunks = (rows_here + 2 * halo) // KC
    low_chunk = jnp.min(jnp.where(inside, begin, 4 * total).reshape(blocks, QB), 1) // KC
    high_chunk = (jnp.max(end.reshape(blocks, QB), 1) + KC - 1) // KC
    index = jnp.arange(blocks)
    away = (index < blocks // 4) | (index >= blocks - blocks // 4)
    low_chunk = jnp.clip(low_chunk, jnp.where(away, chunks // 4, 0), chunks)
    high_chunk = jnp.clip(high_chunk, 0, jnp.where(away, chunks - chunks // 4, chunks))
    spans = jnp.concatenate([low_chunk, high_chunk]).astype(jnp.int32)

    slopes = distance_slope
    q, k, v, kt, vt, pool, wq, wk, wv, vec, upb = qkv(ids, tokens, sets1, ff)
    if direct:
        k, high_b = lax.optimization_barrier((k, high_b))
    qh, k, v, kt, vt = halo_qkv(low_a, low_b, high_a, high_b, wq, wk, wv, vec, k, v, kt, vt)
    if direct:
        y1, qh = lax.optimization_barrier((y1, qh))
        low2 = jnp.concatenate([y, y1], 0)
        bounds = after(bounds, low2)
    att, exact, lse = attend_forward(spans, slopes, q, k, vt, bounds)
    if direct:
        high2, lse = lax.optimization_barrier((exchange(low2, 1, 2), lse))
        sets2 = (low2, high2, swap_core(low2), swap_core(high2))
    out, pay, stats, mixed, gvec, gup, keep2, send2 = middle(
        ids, pool, att, exact, lse, cotangent, vec, upb, sets2, 224
    )
    low_pay = lax.ppermute(pay[own // 2 :], order, up_pairs)
    high_pay = lax.ppermute(pay[: own // 2], order, down_pairs)
    if direct:
        got = swap_core(send2)
        up = add(keep2[8:], got[8:]).astype(BF)
        bounds = after(bounds, up)
    dq, dk, dv, sl = attend_own(spans, slopes, q, k, v, kt, pay, stats, bounds)
    if direct:
        got1, dq, low_pay, high_pay = lax.optimization_barrier((exchange(up, 1, 2), dq, low_pay, high_pay))
        up = add(keep2[4:8], got[4:8], got1[4:]).astype(BF)
        bounds = after(bounds, up)
    dk, dv = attend_halo(spans, slopes, qh, k, v, low_pay, high_pay, bounds, dk, dv)
    keep1, send1 = weight_grads(ids, pool, tokens, dq, dk, dv, gvec, gup, sl, 80)
    if direct:
        got2, keep1, send1 = lax.optimization_barrier((exchange(up, 2, 1), keep1, send1))
        low = add(keep2[:4], got[:4], got1[:4])
        up = (low[2:] + got2[2:].astype(FL)).astype(BF)
        low = low[:2] + got2[:2].astype(FL)
        got, up = lax.optimization_barrier((swap_core(send1), up))
        part = add(keep1[8:], got[8:]).astype(BF)
        mixed = after(mixed, part)
    grad_tokens = token_grads(mixed, dq, dk, dv, wq, wk, wv)

    if direct:
        got3, got1, grad_tokens = lax.optimization_barrier((exchange(up, 4, 8), exchange(part, 1, 2), grad_tokens))
        part = add(keep1[4:8], got[4:8], got1[4:]).astype(BF)
        up = (low[1:] + got3[1:].astype(FL)).astype(BF)
        low = low[:1] + got3[:1].astype(FL)
        got4, got2 = lax.optimization_barrier((exchange(up, 8, 4), exchange(part, 2, 1)))
        mine = (low + got4.astype(FL))[0]
        low = add(keep1[:4], got[:4], got1[:4])
        part = (low[2:] + got2[2:].astype(FL)).astype(BF)
        low = low[:2] + got2[:2].astype(FL)
        got3, other = lax.optimization_barrier((exchange(part, 4, 8), swap_core(mine)))
        second = (mine, other)
        part = (low[1:] + got3[1:].astype(FL)).astype(BF)
        low = low[:1] + got3[:1].astype(FL)
        mine = (low + exchange(part, 8, 4).astype(FL))[0]
        other = swap_core(mine)
        gq, gk, gv, go, g1, g2, *small = unpack_own(ids, (mine, other) + second, ff)
        g_up, g_slope = small[8][0], small[9][0, : distance_slope.shape[0]]
        small = [x[0] for x in small[:8]]
    else:
        inv_a = [0] * NB
        inv_b = [0] * NB
        for p in range(NB):
            inv_a[rel_a(p)] = p
            inv_b[rel_b(p)] = p
        inv_a = jnp.array(inv_a)
        inv_b = jnp.array(inv_b)
        gq, gk, gv, go, g1, g2, gb = unpack(keep1[inv_a], send1[inv_b], keep2[inv_a], send2[inv_b], width)
        rb = width // NB

        def share(x):
            x = lax.psum(x.astype(FL), "dp")
            return lax.psum_scatter(x, "seq", scatter_dimension=0, tiled=True)

        gq, gk, gv, go, g1, g2 = [share(x.reshape(-1, x.shape[-1])) for x in (gq, gk, gv, go, g1, g2)]
        small = [share(gb[:, i, :rb].reshape(-1)) for i in range(8)]
        g_up = share(gb[:, 8:12, :rb].reshape(-1))
        g_slope = lax.psum(gb[0, 12, : distance_slope.shape[0]].astype(FL), order)
    return (
        out,
        grad_tokens,
        gq,
        small[0],
        gk,
        gv,
        small[1],
        go,
        small[2],
        small[3],
        small[4],
        g1,
        g_up,
        g2,
        small[5],
        small[6],
        small[7],
        g_slope,
    )


def solution(mesh):
    tall = P(("dp", "seq"), None)
    mat = P("seq", None)
    vec = P("seq")
    return jax.shard_map(
        local,
        mesh=mesh,
        in_specs=(tall, tall, P(), mat, vec, mat, mat, vec, mat, vec, vec, vec, mat, vec, mat, vec, vec, vec, P()),
        out_specs=(tall, tall, mat, vec, mat, mat, vec, mat, vec, vec, vec, mat, vec, mat, vec, vec, vec, P()),
        check_vma=False,
    )
```

```python
import functools

import jax
import jax.numpy as jnp
from jax import lax
from jax.experimental import pallas as pl
from jax.experimental.pallas import tpu as pltpu
from jax.sharding import PartitionSpec as P

HD = 64
NB = 16
QB = 128
KC = 256
EPS = 1e-05
FAR = 1e12
BF = jnp.bfloat16
FL = jnp.float32


def rel_a(p):
    return (p & 1) * 8 + ((p >> 1) & 1) * 4 + ((p >> 2) & 1) * 2 + ((p >> 3) & 1)


def rel_b(p):
    return (p & 1) * 4 + ((p >> 1) & 1) * 8 + ((p >> 2) & 1) + ((p >> 3) & 1) * 2


def dot(a, b):
    return jnp.dot(a, b, preferred_element_type=FL)


def dot_t(a, b):
    return lax.dot_general(a, b, (((1,), (1,)), ((), ())), preferred_element_type=FL)


def t_dot(a, b):
    return lax.dot_general(a, b, (((0,), (0,)), ((), ())), preferred_element_type=FL)


def exchange(x, stride_a, stride_b):
    n = lax.axis_size("seq")
    pairs = [(s, s ^ stride_a) for s in range(n)] + [(n + s, n + (s ^ stride_b)) for s in range(n)]
    return lax.ppermute(x, ("dp", "seq"), pairs)


def swap_core(x):
    return lax.ppermute(x, "dp", [(0, 1), (1, 0)])


def add(*xs):
    total = xs[0].astype(FL)
    for x in xs[1:]:
        total = total + x.astype(FL)
    return total


def params(**kw):
    return pltpu.CompilerParams(vmem_limit_bytes=58 * 1024 * 1024, **kw)


def takes(us):
    return pl.CostEstimate(flops=us * 1150 * 10**6, transcendentals=0, bytes_accessed=us * 3600 * 10**3)


ANY = pl.BlockSpec(memory_space=pl.ANY)


def load_sets(ids, low, high, olow, ohigh, copies_a, copies_b):
    def start(a_refs, b_refs):
        for p in range(NB):
            copies_a(a_refs[p // 8].at[p % 8], ids[0] ^ rel_a(p), p)
            copies_b(b_refs[p // 8].at[p % 8], ids[0] ^ rel_b(p), p)

    @pl.when(ids[1] == 0)
    def _():
        start((low, high), (olow, ohigh))

    @pl.when(ids[1] != 0)
    def _():
        start((olow, ohigh), (low, high))


def wait_all(ref, sem):
    pltpu.make_async_copy(ref, ref, sem).wait()


def spread_matrix(rows, cols, rb):
    lanes = lax.broadcasted_iota(jnp.int32, (rows, cols), 1)
    return (lax.broadcasted_iota(jnp.int32, (rows, cols), 0) == lanes - rb * div_rb(lanes)).astype(FL).astype(BF)


def div_rb(x):
    return (x * 21846) >> 20


def qkv_kernel(
    ids, tok, low, high, olow, ohigh, q_out, k_out, v_out, kt_out, vt_out, pool_out, wq, wk, wv, vec_out, up_out, bias, x32, sems
):
    width = tok.shape[1]
    rb = width // NB

    @pl.when(pl.program_id(0) == 0)
    def _():
        def rows(r, n):
            return pl.ds(pl.multiple_of(r, 16), n)

        def copies_a(block, s, p):
            pltpu.make_async_copy(block.at[pl.ds(0, 48)], wq.at[rows(s * rb, 48)], sems.at[0]).start()
            pltpu.make_async_copy(block.at[pl.ds(48, 32)], wk.at[rows(s * rb, 32)], sems.at[1]).start()

        def copies_b(block, s, p):
            pltpu.make_async_copy(block.at[pl.ds(0, 16)], wk.at[rows(s * rb + 32, 16)], sems.at[1]).start()
            pltpu.make_async_copy(block.at[pl.ds(16, 48)], wv.at[rows(s * rb, 48)], sems.at[2]).start()
            pltpu.make_async_copy(block.at[pl.ds(64, 16)], bias.at[pl.ds(16 * p, 16)], sems.at[3]).start()

        load_sets(ids, low, high, olow, ohigh, copies_a, copies_b)
        wait_all(wq, sems.at[0])
        wait_all(wk, sems.at[1])
        wait_all(wv, sems.at[2])
        wait_all(bias, sems.at[3])
        parts = bias[:, 0:128]
        wide = dot(parts, spread_matrix(128, width, rb))
        block_of = div_rb(lax.broadcasted_iota(jnp.int32, (16, width), 1))
        total = jnp.zeros((16, width), FL)
        for p in range(NB):
            total = total + jnp.where(block_of == (ids[0] ^ rel_b(p)), wide[16 * p : 16 * p + 16], 0.0)
        vec_out[...] = total
        ff = up_out.shape[1]
        wide = dot(parts, spread_matrix(128, ff, rb))
        block_of = div_rb(lax.broadcasted_iota(jnp.int32, (16, ff), 1))
        row = lax.broadcasted_iota(jnp.int32, (16, ff), 0)
        block_of = jnp.where((row >= 8) & (row < 12), block_of - row + 8, -1)
        total = jnp.zeros((16, ff), FL)
        for p in range(NB):
            total = total + jnp.where(block_of == 4 * (ids[0] ^ rel_b(p)), wide[16 * p : 16 * p + 16], 0.0)
        up_out[...] = jnp.broadcast_to(jnp.sum(total, 0, keepdims=True), up_out.shape)

    pool_out[...] = project(tok[...], wq, wk, wv, vec_out, q_out, k_out, v_out, kt_out, vt_out, x32)


def project(x, wq, wk, wv, vec, q_out, k_out, v_out, kt_out, vt_out, x32):
    width = x.shape[1]
    half = x.shape[0] // 2
    k_out[...] = dot(x, wk[...]).astype(BF)
    v_out[...] = (dot(x, wv[...]) + vec[1:2]).astype(BF)
    for c in range(x.shape[0] // KC):
        kt_out[c] = k_out[KC * c : KC * c + KC].T
        vt_out[c] = v_out[KC * c : KC * c + KC].T
    pooled = []
    for j in range(width // 128):
        x32[j] = x[:, 128 * j : 128 * j + 128].astype(FL)
        pooled.append((x32[j, pl.ds(0, half, stride=2)] + x32[j, pl.ds(1, half, stride=2)]) * 0.5)
    pooled = jnp.concatenate(pooled, 1)
    q = (dot(pooled.astype(BF), wq[...]) + vec[0:1]).astype(BF)
    q_out[...] = (q.astype(FL) * HD**-0.5).astype(BF)
    return pooled


def qkv(ids, tokens, sets, ff):
    rows, width = tokens.shape
    step = 512
    whole = lambda i, *_: (0, 0)
    square = jax.ShapeDtypeStruct((width, width), BF)
    thin = pl.BlockSpec((step // 2, width), lambda i, *_: (i, 0))
    block = pl.BlockSpec((step, width), lambda i, *_: (i, 0))
    inner = pl.BlockSpec((step, width), lambda i, *_: (i + 1, 0))
    tall = pl.BlockSpec((step // KC, width, KC), lambda i, *_: (i + 1, 0, 0))
    return pl.pallas_call(
        qkv_kernel,
        name="qkv",
        cost_estimate=takes(9),
        grid_spec=pltpu.PrefetchScalarGridSpec(
            num_scalar_prefetch=1,
            grid=(rows // step,),
            in_specs=[block, ANY, ANY, ANY, ANY],
            out_specs=[thin, inner, inner, tall, tall, thin]
            + [pl.BlockSpec((width, width), whole)] * 3
            + [pl.BlockSpec((16, width), whole), pl.BlockSpec((8, ff), whole)],
            scratch_shapes=[
                pltpu.VMEM((16 * NB, width), BF),
                pltpu.VMEM((width // 128, step, 128), FL),
                pltpu.SemaphoreType.DMA((4,)),
            ],
        ),
        out_shape=[
            jax.ShapeDtypeStruct((rows // 2, width), BF),
            jax.ShapeDtypeStruct((2 * rows, width), BF),
            jax.ShapeDtypeStruct((2 * rows, width), BF),
            jax.ShapeDtypeStruct((2 * rows // KC, width, KC), BF),
            jax.ShapeDtypeStruct((2 * rows // KC, width, KC), BF),
            jax.ShapeDtypeStruct((rows // 2, width), FL),
            square,
            square,
            square,
            jax.ShapeDtypeStruct((16, width), FL),
            jax.ShapeDtypeStruct((8, ff), FL),
        ],
        compiler_params=params(),
    )(ids, tokens, *sets)


def halo_qkv_kernel(
    low_a, low_b, high_a, high_b, wq, wk, wv, vec, k, v, kt, vt, q_out, k_out, v_out, kt_out, vt_out, x32
):
    low = pl.program_id(0) == 0
    parts = [jnp.where(low, a[...], b[...]) for a, b in ((low_a, high_a), (low_b, high_b))]
    project(jnp.concatenate(parts, 0), wq, wk, wv, vec, q_out, k_out, v_out, kt_out, vt_out, x32)


def halo_qkv(low_a, low_b, high_a, high_b, wq, wk, wv, vec, k, v, kt, vt):
    rows, width = low_a.shape
    rows = 2 * rows
    full = lambda x: pl.BlockSpec(x.shape, lambda i: (0,) * len(x.shape))
    args = (low_a, low_b, high_a, high_b, wq, wk, wv, vec)
    edge = pl.BlockSpec((rows, width), lambda i: (3 * i, 0))
    tall = pl.BlockSpec((rows // KC, width, KC), lambda i: (3 * i, 0, 0))
    return pl.pallas_call(
        halo_qkv_kernel,
        name="halo_qkv",
        cost_estimate=takes(7),
        grid=(2,),
        in_specs=[full(x) for x in args] + [ANY] * 4,
        out_specs=[pl.BlockSpec((None, rows // 2, width), lambda i: (i, 0, 0)), edge, edge, tall, tall],
        out_shape=[jax.ShapeDtypeStruct((2, rows // 2, width), BF)]
        + [jax.ShapeDtypeStruct(x.shape, x.dtype) for x in (k, v, kt, vt)],
        input_output_aliases={8: 1, 9: 2, 10: 3, 11: 4},
        scratch_shapes=[pltpu.VMEM((width // 128, rows, 128), FL)],
        compiler_params=params(),
    )(*args, k, v, kt, vt)


def two_heads(x):
    lane = lax.broadcasted_iota(jnp.int32, x.shape, 1)
    zero = jnp.zeros_like(x)
    return jnp.concatenate([jnp.where(lane < HD, x, zero), jnp.where(lane < HD, zero, x)], 0)


def one_block(x):
    r = x.shape[1] // 2
    line = lax.broadcasted_iota(jnp.int32, (128, r), 0)
    return jnp.where(line < HD, x[:, :r], x[:, r:]).T


def distances(bounds, row, c):
    low = bounds[0:1, pl.ds(row, QB)]
    high = bounds[1:2, pl.ds(row, QB)]
    query = (2 * (row + lax.broadcasted_iota(jnp.int32, (KC, QB), 1))).astype(FL) + 0.5
    key = (c * KC + lax.broadcasted_iota(jnp.int32, (KC, QB), 0)).astype(FL)
    far = jnp.where((key >= low) & (key < high), jnp.abs(query - key), FAR)
    return jnp.concatenate([far, far], 1)


def fold(x, f):
    n = x.shape[0] // 8
    parts = [x[8 * i : 8 * i + 8] for i in range(n)]
    while len(parts) > 1:
        parts = [f(parts[2 * i], parts[2 * i + 1]) for i in range(len(parts) // 2)]
    return parts[0]


def slope_line(slopes, head):
    lane = lax.broadcasted_iota(jnp.int32, (1, 2 * QB), 1)
    return jnp.where(lane < QB, slopes[head], slopes[head + 1])


def forward_kernel(
    spans, slopes, q, k, vt, bounds, o_out, exact_out, lse_out, s_scr, q2, top, total, acc, rest
):
    pairs = q.shape[1] // 128
    head0 = pl.program_id(0) * 2 * pairs
    q_first = q.shape[0] // 2
    slope = [slope_line(slopes, head0 + 2 * j) for j in range(pairs)]

    def query_block(b, _):
        row = pl.multiple_of(q_first + b * QB, QB)
        out_rows = pl.ds(pl.multiple_of(b * QB, QB), QB)
        block = row // QB
        c0 = spans[block]
        c1 = spans[spans.shape[0] // 2 + block]
        for j in range(pairs):
            q2[j] = two_heads(q[out_rows, 128 * j : 128 * j + 128])
        top[...] = jnp.full(top.shape, -3e38, FL)
        total[...] = jnp.zeros(total.shape, FL)
        acc[...] = jnp.zeros(acc.shape, FL)
        rest[...] = jnp.zeros(rest.shape, FL)

        def score(c, _):
            far = distances(bounds, row, c)
            keys = pl.ds(pl.multiple_of(c * KC, KC), KC)
            for j in range(pairs):
                s = dot_t(k[keys, 128 * j : 128 * j + 128], q2[j]) - slope[j] * far
                s_scr[c - c0, j] = s
                top[j] = jnp.maximum(top[j], fold(s, jnp.maximum))
            return 0

        lax.fori_loop(c0, c1, score, 0)
        peak = [jnp.max(top[j], 0, keepdims=True) for j in range(pairs)]

        def exponent(c, _):
            for j in range(pairs):
                e = jnp.exp(s_scr[c - c0, j] - peak[j])
                s_scr[c - c0, j] = e
                total[j] = total[j] + fold(e, jnp.add)
            return 0

        lax.fori_loop(c0, c1, exponent, 0)
        inverse = []
        for j in range(pairs):
            l = jnp.sum(total[j], 0, keepdims=True)
            t = peak[j] + jnp.log(l)
            inverse.append(1.0 / l)
            lse_out[2 * j : 2 * j + 1, out_rows] = t[:, :QB]
            lse_out[2 * j + 1 : 2 * j + 2, out_rows] = t[:, QB:]

        def attend(c, _):
            for j in range(pairs):
                p = s_scr[c - c0, j] * inverse[j]
                high = p.astype(BF)
                low = (p - high.astype(FL)).astype(BF)
                values = vt[c, 128 * j : 128 * j + 128]
                acc[j] = acc[j] + dot(values, high)
                rest[j] = rest[j] + dot(values, low)
            return 0

        lax.fori_loop(c0, c1, attend, 0)
        for j in range(pairs):
            cols = slice(128 * j, 128 * j + 128)
            o_out[out_rows, cols] = one_block(acc[j]).astype(BF)
            exact_out[out_rows, cols] = one_block(acc[j] + rest[j])
        return 0

    lse_out[...] = jnp.zeros(lse_out.shape, FL)
    lax.fori_loop(0, o_out.shape[0] // QB, query_block, 0)


def attend_forward(spans, slopes, q, k, vt, bounds):
    own, width = q.shape
    wide = width // 2
    pairs = wide // 128
    keys = k.shape[0]
    chunks = keys // KC
    col = lambda i, *_: (0, i)
    return pl.pallas_call(
        forward_kernel,
        name="attend_forward",
        cost_estimate=takes(30),
        grid_spec=pltpu.PrefetchScalarGridSpec(
            num_scalar_prefetch=2,
            grid=(2,),
            in_specs=[
                pl.BlockSpec((own, wide), col),
                pl.BlockSpec((keys, wide), col),
                pl.BlockSpec((chunks, wide, KC), lambda i, *_: (0, i, 0)),
                pl.BlockSpec(bounds.shape, lambda i, *_: (0, 0)),
            ],
            out_specs=[
                pl.BlockSpec((own, wide), col),
                pl.BlockSpec((own, wide), col),
                pl.BlockSpec((8, own), lambda i, *_: (i, 0)),
            ],
            scratch_shapes=[
                pltpu.VMEM((chunks, pairs, KC, 2 * QB), FL),
                pltpu.VMEM((pairs, 2 * QB, 128), BF),
                pltpu.VMEM((pairs, 8, 2 * QB), FL),
                pltpu.VMEM((pairs, 8, 2 * QB), FL),
                pltpu.VMEM((pairs, 128, 2 * QB), FL),
                pltpu.VMEM((pairs, 128, 2 * QB), FL),
            ],
        ),
        out_shape=[
            jax.ShapeDtypeStruct((own, width), BF),
            jax.ShapeDtypeStruct((own, width), FL),
            jax.ShapeDtypeStruct((16, own), FL),
        ],
        compiler_params=params(),
    )(spans, slopes, q, k, vt, bounds)


def pieces(x):
    out = []
    for _ in range(3):
        y = x.astype(BF).astype(FL)
        out.append(y)
        x = x - y
    return out


def key_lines(side, kind):
    lane = lax.broadcasted_iota(jnp.int32, (KC, 128), 1)
    key = lax.broadcasted_iota(jnp.int32, (KC, 128), 0).astype(FL)
    x = jnp.where(lane < 3, 1.0, jnp.where(lane < 6, -side, jnp.where(lane < 9, side * key, 0.0)))
    return jnp.where(lane == kind, 1.0, x) if kind else x


def chunk_lines(base, away, side, limit):
    lane = lax.broadcasted_iota(jnp.int32, (KC, 128), 1)
    key = lax.broadcasted_iota(jnp.int32, (KC, 128), 0).astype(FL) + KC * away
    other = jnp.where(side * key < side * limit, 1.0, 0.0)
    x = base + jnp.where((lane >= 9) & (lane < 12), side * KC * away, 0.0)
    return jnp.where(lane == 12, other, x).astype(BF)


def value_lines():
    lane = lax.broadcasted_iota(jnp.int32, (KC, 128), 1)
    return (lane < 3).astype(FL).astype(BF)


def query_rows(lse, slope, spots, out_left, out_right):
    one = jnp.ones_like(lse)
    rows = pieces(-lse) + pieces(slope * spots) + pieces(slope * one) * 2
    rows += [-FAR * one, -FAR * out_left, -FAR * out_right, 0.0 * one]
    return jnp.concatenate(rows, 0).astype(BF)


def two_heads_t(x):
    line = lax.broadcasted_iota(jnp.int32, x.shape, 0)
    zero = jnp.zeros_like(x)
    return jnp.concatenate([jnp.where(line < HD, x, zero), jnp.where(line < HD, zero, x)], 1)


def block_setup(bounds, row):
    low = bounds[0:1, pl.ds(row, QB)]
    high = bounds[1:2, pl.ds(row, QB)]
    first = low[:, 0:1]
    last = high[:, QB - 1 : QB]
    base = (2 * row).astype(FL) if hasattr(row, "astype") else float(2 * row)
    out_left = jnp.where(low == first, 0.0, 1.0)
    out_right = jnp.where(high == last, 0.0, 1.0)
    spots = 2.0 * lax.broadcasted_iota(jnp.int32, (1, QB), 1).astype(FL) + 0.5
    return low - base, high - base, first - base, last - base - 0.5, twice(out_left), twice(out_right), twice(spots)


def twice(x):
    return jnp.concatenate([x, x], 1)


def fill_queries(j, q, da, lse, delta, slope, setup, q2, da2, qt, dat):
    out_left, out_right, spots = setup[4:]
    q2[j] = two_heads(q)
    da2[j] = two_heads(da)
    qt[j, 0:128] = two_heads_t(q.T)
    dat[j, 0:128] = two_heads_t(da.T)
    qt[j, 128:144] = query_rows(lse, slope, spots, out_left, out_right)
    rows = pieces(-delta) + [jnp.zeros((13, 2 * QB), FL)]
    dat[j, 128:144] = jnp.concatenate(rows, 0).astype(BF)


def own_kernel(
    spans, slopes, q, k, v, kt, da, stats, bounds, dq_out, dk, dv, slope_out, q2, da2, qt, dat, dq2, sl, base
):
    pairs = q.shape[1] // 128
    head0 = pl.program_id(0) * 2 * pairs
    total_blocks = bounds.shape[1] // QB
    quarter = k.shape[0] // KC // 4
    first = total_blocks // 4
    slope = [slope_line(slopes, head0 + 2 * j) for j in range(pairs)]
    dk[...] = jnp.zeros(dk.shape, FL)
    dv[...] = jnp.zeros(dv.shape, FL)
    sl[...] = jnp.zeros(sl.shape, FL)
    qt[...] = jnp.zeros(qt.shape, BF)
    dat[...] = jnp.zeros(dat.shape, BF)
    line = lax.broadcasted_iota(jnp.int32, (16, KC), 0)
    spot = lax.broadcasted_iota(jnp.int32, (16, KC), 1).astype(FL)
    extra = jnp.where(line == 0, 1.0, jnp.where(line == 1, spot, 0.0)).astype(BF)
    base[0] = key_lines(1.0, 13)
    base[1] = key_lines(-1.0, 14)
    own_lines = key_lines(1.0, 0).astype(BF)
    ones = value_lines()

    def query_block(b, _):
        block = first + b
        row = pl.multiple_of(block * QB, QB)
        rows = pl.ds(pl.multiple_of(b * QB, QB), QB)
        c0 = spans[block]
        c1 = spans[total_blocks + block]
        setup = block_setup(bounds, row)
        low, high, limit_left, limit_right = setup[:4]
        spots = setup[6]
        for j in range(pairs):
            cols = slice(128 * j, 128 * j + 128)
            h = 2 * j
            lse = jnp.concatenate([stats[h : h + 1, rows], stats[h + 1 : h + 2, rows]], 1)
            delta = jnp.concatenate([stats[8 + h : 9 + h, rows], stats[9 + h : 10 + h, rows]], 1)
            fill_queries(j, q[rows, cols], da[rows, cols], lse, delta, slope[j], setup, q2, da2, qt, dat)
        dq2[...] = jnp.zeros(dq2.shape, FL)

        def step(c, lines, side, away, grads, wide):
            keys = pl.ds(pl.multiple_of(c * KC, KC), KC)
            col = [slice(128 * j, 128 * j + 128) for j in range(pairs)]
            s = [dot(jnp.concatenate([k[keys, col[j]], lines], 1), qt[j]) for j in range(pairs)]
            dp = [dot(jnp.concatenate([v[keys, col[j]], ones], 1), dat[j]) for j in range(pairs)]
            if wide is not None:
                s = [s[j] - slope[j] * wide for j in range(pairs)]
            p = [jnp.exp(x) for x in s]
            ds = [(p[j] * dp[j]).astype(BF) for j in range(pairs)]
            if grads:
                mine = pl.ds(pl.multiple_of((c - quarter) * KC, KC), KC)
                new_v = [dot(p[j].astype(BF), da2[j]) for j in range(pairs)]
                new_k = [dot(ds[j], q2[j]) for j in range(pairs)]
            r = [dot(jnp.concatenate([kt[c, col[j]], extra], 0), ds[j]) for j in range(pairs)]
            for j in range(pairs):
                if grads:
                    dv[mine, col[j]] = dv[mine, col[j]] + new_v[j]
                    dk[mine, col[j]] = dk[mine, col[j]] + new_k[j]
                dq2[j] = dq2[j] + r[j][0:128]
                part = side * ((spots - KC * away) * r[j][128:129] - r[j][129:130])
                if wide is not None:
                    part = part + jnp.sum(ds[j].astype(FL) * wide, 0, keepdims=True)
                sl[j] = sl[j] + part

        key = lax.broadcasted_iota(jnp.int32, (KC, QB), 0).astype(FL)
        over = 2.0 * jnp.maximum(key - spots[:, :QB], 0.0)
        wide = twice(jnp.where((key >= low) & (key < high), over, FAR))
        step(block, own_lines, 1.0, 0.0, True, wide)

        def other(c, grads):
            before = c < block
            side = jnp.where(before, 1.0, -1.0)
            away = (c - block).astype(FL)
            limit = jnp.where(before, limit_left, limit_right)
            step(c, chunk_lines(base[jnp.where(before, 0, 1)], away, side, limit), side, away, grads, None)

        def inside(i, _):
            other(jnp.where(i < block, i, i + 1), True)
            return 0

        left = jnp.maximum(jnp.minimum(c1, quarter) - c0, 0)
        right0 = jnp.maximum(c0, 3 * quarter)

        def outside(i, _):
            other(jnp.where(i < left, c0 + i, right0 + i - left), False)
            return 0

        lax.fori_loop(jnp.maximum(c0, quarter), jnp.minimum(c1, 3 * quarter) - 1, inside, 0)
        lax.fori_loop(0, left + jnp.maximum(c1 - right0, 0), outside, 0)
        for j in range(pairs):
            dq_out[rows, 128 * j : 128 * j + 128] = (one_block(dq2[j]) * HD**-0.5).astype(BF)
        return 0

    lax.fori_loop(0, da.shape[0] // QB, query_block, 0)
    slope_out[...] = jnp.zeros(slope_out.shape, FL)
    for j in range(pairs):
        slope_out[8 * j : 8 * j + 1] = sl[j]


def attend_own(spans, slopes, q, k, v, kt, da, stats, bounds):
    own, width = q.shape
    wide = width // 2
    pairs = wide // 128
    keys = k.shape[0]
    chunks = keys // KC
    col = lambda i, *_: (0, i)
    zero = lambda i, *_: (0, 0)
    return pl.pallas_call(
        own_kernel,
        name="attend_own",
        cost_estimate=takes(30),
        grid_spec=pltpu.PrefetchScalarGridSpec(
            num_scalar_prefetch=2,
            grid=(2,),
            in_specs=[
                pl.BlockSpec((own, wide), col),
                pl.BlockSpec((keys, wide), col),
                pl.BlockSpec((keys, wide), col),
                pl.BlockSpec((chunks, wide, KC), lambda i, *_: (0, i, 0)),
                pl.BlockSpec((own, wide), col),
                pl.BlockSpec((16, own), lambda i, *_: (i, 0)),
                pl.BlockSpec(bounds.shape, zero),
            ],
            out_specs=[
                pl.BlockSpec((own, wide), col),
                pl.BlockSpec((keys // 2, wide), col),
                pl.BlockSpec((keys // 2, wide), col),
                pl.BlockSpec((8 * pairs, 2 * QB), lambda i, *_: (i, 0)),
            ],
            scratch_shapes=[
                pltpu.VMEM((pairs, 2 * QB, 128), BF),
                pltpu.VMEM((pairs, 2 * QB, 128), BF),
                pltpu.VMEM((pairs, 256, 2 * QB), BF),
                pltpu.VMEM((pairs, 256, 2 * QB), BF),
                pltpu.VMEM((pairs, 128, 2 * QB), FL),
                pltpu.VMEM((pairs, 1, 2 * QB), FL),
                pltpu.VMEM((2, KC, 128), FL),
            ],
        ),
        out_shape=[
            jax.ShapeDtypeStruct((own, width), BF),
            jax.ShapeDtypeStruct((keys // 2, width), FL),
            jax.ShapeDtypeStruct((keys // 2, width), FL),
            jax.ShapeDtypeStruct((16 * pairs, 2 * QB), FL),
        ],
        compiler_params=params(),
    )(spans, slopes, q, k, v, kt, da, stats, bounds)


def halo_kernel(
    spans,
    slopes,
    q,
    ka,
    kb,
    va,
    vb,
    low_pay,
    high_pay,
    low_stats,
    high_stats,
    bounds,
    dk0,
    dv0,
    dk_out,
    dv_out,
    q2,
    da2,
    qt,
    dat,
    st,
    k,
    v,
    dk,
    dv,
):
    half = pl.program_id(0)
    pairs = q.shape[2] // 128
    total_blocks = bounds.shape[1] // QB
    edge = ka.shape[0]
    first = edge // KC
    count = low_pay.shape[0] // QB
    dk[...] = dk0[...]
    dv[...] = dv0[...]
    for into, parts in ((k, (ka, kb)), (v, (va, vb))):
        into[0:edge] = parts[0][...]
        into[edge:] = parts[1][...]
    qt[...] = jnp.zeros(qt.shape, BF)
    dat[...] = jnp.zeros(dat.shape, BF)
    ones = value_lines()
    for side, pay in enumerate((low_stats, high_stats)):
        x = pay[...].astype(FL)
        x = (x + pltpu.roll(x, 96, 1) + pltpu.roll(x, 64, 1)).T
        st[side] = jnp.where(half == 0, x[0:16], x[16:32])

    def query_block(i, _):
        side = i // count
        nth = i - side * count
        block = jnp.where(side == 0, i, total_blocks - 2 * count + i)
        row = pl.multiple_of(block * QB, QB)
        rows = pl.ds(pl.multiple_of(nth * QB, QB), QB)
        c0 = spans[block]
        c1 = spans[total_blocks + block]

        @pl.when(c0 < c1)
        def _():
            setup = block_setup(bounds, row)
            limit = jnp.where(side == 0, setup[3], setup[2])
            sign = jnp.where(side == 0, -1.0, 1.0)
            base = jnp.where(side == 0, key_lines(-1.0, 14), key_lines(1.0, 13))
            for j in range(pairs):
                cols = slice(128 * j, 128 * j + 128)
                h = 2 * j
                lse = jnp.concatenate([st[side, h : h + 1, rows], st[side, h + 1 : h + 2, rows]], 1)
                delta = jnp.concatenate([st[side, h + 8 : h + 9, rows], st[side, h + 9 : h + 10, rows]], 1)
                d = jnp.where(side == 0, low_pay[rows, cols], high_pay[rows, cols])
                slope = slope_line(slopes, 2 * pairs * half + h)
                fill_queries(j, q[side, rows, cols], d, lse, delta, slope, setup, q2, da2, qt, dat)

            def step(c, _):
                mine = pl.ds(pl.multiple_of((c - first) * KC, KC), KC)
                lines = chunk_lines(base, (c - block).astype(FL), sign, limit)
                js = range(pairs)
                col = [slice(128 * j, 128 * j + 128) for j in js]
                p = [jnp.exp(dot(jnp.concatenate([k[mine, col[j]], lines], 1), qt[j])) for j in js]
                dp = [dot(jnp.concatenate([v[mine, col[j]], ones], 1), dat[j]) for j in js]
                new_v = [dot(p[j].astype(BF), da2[j]) for j in js]
                new_k = [dot((p[j] * dp[j]).astype(BF), q2[j]) for j in js]
                for j in js:
                    dv[mine, col[j]] = dv[mine, col[j]] + new_v[j]
                    dk[mine, col[j]] = dk[mine, col[j]] + new_k[j]
                return 0

            lax.fori_loop(c0, c1, step, 0)

        return 0

    lax.fori_loop(0, 2 * count, query_block, 0)
    dk_out[...] = dk[...].astype(BF)
    dv_out[...] = dv[...].astype(BF)


def attend_halo(spans, slopes, q, k, v, low_pay, high_pay, bounds, dk0, dv0):
    width = q.shape[2]
    wide = width // 2
    pairs = wide // 128
    keys = dk0.shape[0]
    rows = low_pay.shape[0]
    shape = jax.ShapeDtypeStruct((keys, width), BF)
    col = lambda i, *_: (0, i)
    parts = [pl.BlockSpec((keys // 2, wide), lambda i, *_: (1, i)), pl.BlockSpec((keys // 2, wide), lambda i, *_: (2, i))]
    tail = pl.BlockSpec((rows, 128), lambda i, *_: (0, width // 128))
    whole = pl.BlockSpec((keys, wide), col)
    pay = pl.BlockSpec((rows, wide), col)
    return pl.pallas_call(
        halo_kernel,
        name="attend_halo",
        cost_estimate=takes(12),
        grid_spec=pltpu.PrefetchScalarGridSpec(
            num_scalar_prefetch=2,
            grid=(2,),
            in_specs=[pl.BlockSpec((2, q.shape[1], wide), lambda i, *_: (0, 0, i))]
            + parts * 2
            + [pay, pay, tail, tail, pl.BlockSpec(bounds.shape, lambda i, *_: (0, 0)), whole, whole],
            out_specs=[whole, whole],
            scratch_shapes=[
                pltpu.VMEM((pairs, 2 * QB, 128), BF),
                pltpu.VMEM((pairs, 2 * QB, 128), BF),
                pltpu.VMEM((pairs, 256, 2 * QB), BF),
                pltpu.VMEM((pairs, 256, 2 * QB), BF),
                pltpu.VMEM((2, 16, rows), FL),
                pltpu.VMEM((keys, wide), BF),
                pltpu.VMEM((keys, wide), BF),
                pltpu.VMEM((keys, wide), FL),
                pltpu.VMEM((keys, wide), FL),
            ],
        ),
        out_shape=[shape, shape],
        compiler_params=params(),
    )(spans, slopes, q, k, k, v, v, low_pay, high_pay, low_pay, high_pay, bounds, dk0, dv0)


def normalize(z):
    centred = z - jnp.mean(z, -1, keepdims=True)
    scale = lax.rsqrt(jnp.mean(centred * centred, -1, keepdims=True) + EPS)
    return centred * scale, scale


def normalize_back(d, unit, scale):
    return scale * (d - jnp.mean(d, -1, keepdims=True) - unit * jnp.mean(d * unit, -1, keepdims=True))


def rows_sum(x):
    return jnp.sum(x, 0, keepdims=True)


def middle_kernel(
    ids,
    pool,
    att,
    exact,
    lse,
    cot,
    vec,
    upb,
    low,
    high,
    olow,
    ohigh,
    out,
    pay,
    pay_low,
    pay_high,
    stats,
    mixed,
    gvec,
    gup,
    keep,
    send,
    wo,
    w1,
    w2,
    active,
    slope,
    unit1,
    hid,
    hid_low,
    z,
    d2,
    dw1,
    dw2,
    dwo,
    sems,
):
    n, width = att.shape
    rb = width // NB
    fb = w2.shape[0] // NB
    parts = w1.shape[0]

    def rows(r, size):
        return pl.ds(pl.multiple_of(r, 16), size)

    def copies_a(block, s, p):
        pltpu.make_async_copy(block.at[pl.ds(192, 32)], wo.at[rows(s * rb, 32)], sems.at[0]).start()
        pltpu.make_async_copy(block.at[pl.ds(0, 192)], w2.at[rows(s * fb, 192)], sems.at[2]).start()

    def copies_b(block, s, p):
        pltpu.make_async_copy(block.at[pl.ds(192, 16)], wo.at[rows(s * rb + 32, 16)], sems.at[0]).start()
        for c in range(parts):
            pltpu.make_async_copy(block.at[pl.ds(48 * c, 48)], w1.at[c, rows(s * rb, 48)], sems.at[1]).start()

    load_sets(ids, low, high, olow, ohigh, copies_a, copies_b)
    wait_all(wo, sems.at[0])
    z[...] = dot(att[...], wo[...])
    rc = 128

    def row_loop(f):
        def body(i, _):
            f(pl.ds(pl.multiple_of(i * rc, rc), rc), i)
            return 0

        lax.fori_loop(0, n // rc, body, 0)

    def first_norm(r, i):
        unit, scale = normalize(pool[r, :] + z[r, :] + vec[2:3])
        h = unit * vec[3:4] + vec[4:5]
        unit1[r, :] = unit
        d2[r, 0:128] = jnp.broadcast_to(scale, (rc, 128))
        hid[r, :] = h
        hid_low[r, :] = h.astype(BF)

    row_loop(first_norm)
    wait_all(w1, sems.at[1])
    wait_all(w2, sems.at[2])
    c0 = 0.7978845608028654

    def up(c, _):
        before = jnp.maximum(c - 1, 0)
        z[...] = z[...] + dot(active[before], w2[pl.ds(pl.multiple_of(before * width, 128), width), :])
        inner = dot(hid_low[...], w1[c]) + upb[pl.ds(0, 1), pl.ds(pl.multiple_of(c * width, 128), width)]
        sq = inner * inner
        t = jnp.tanh(inner * (c0 + (0.044715 * c0) * sq))
        cdf = 0.5 + 0.5 * t
        active[c] = (inner * cdf).astype(BF)
        slope[c] = cdf + (inner * (1.0 - t * t)) * (0.5 * c0 + (1.5 * 0.044715 * c0) * sq)
        return 0

    active[0] = jnp.zeros((n, width), BF)
    z[...] = jnp.zeros(z.shape, FL)
    lax.fori_loop(0, parts, up, 0)
    z[...] = z[...] + dot(active[parts - 1], w2[pl.ds((parts - 1) * width, width), :])
    gvec[...] = jnp.zeros(gvec.shape, FL)

    def second_norm(r, i):
        unit, scale = normalize(hid[r, :] + (z[r, :] + vec[5:6]))
        out[r, :] = (unit * vec[6:7] + vec[7:8]).astype(BF)
        dy = cot[r, :].astype(FL)
        gvec[6:7] = gvec[6:7] + rows_sum(dy * unit)
        gvec[7:8] = gvec[7:8] + rows_sum(dy)
        d = normalize_back(dy * vec[6:7], unit, scale)
        hid[r, :] = d
        d_low = d.astype(BF)
        att_like[r, :] = d_low
        gvec[5:6] = gvec[5:6] + rows_sum(d_low.astype(FL))

    att_like = pay.at[:, 0:width]
    scale1 = d2[:, 0:1]
    row_loop(second_norm)
    z[...] = jnp.zeros(z.shape, FL)

    def down(c, _):
        ffn = pay[:, 0:width]
        far = pl.ds(pl.multiple_of(c * width, 128), width)
        d_inner = (dot_t(ffn, w2[far, :]) * slope[c]).astype(BF)
        gup[:, far] = jnp.broadcast_to(rows_sum(d_inner.astype(FL)), (8, width))
        dw2[far, :] = t_dot(active[c], ffn).astype(BF)
        dw1[c] = t_dot(hid_low[...], d_inner).astype(BF)
        z[...] = z[...] + dot_t(d_inner, w1[c])
        return 0

    lax.fori_loop(0, parts, down, 0)

    def store_sets(a_ref, b_ref):
        for p in range(NB):
            s = ids[0] ^ rel_a(p)
            pltpu.make_async_copy(dw2.at[rows(s * fb, 192)], a_ref.at[p, pl.ds(0, 192)], sems.at[3]).start()
            s = ids[0] ^ rel_b(p)
            for c in range(parts):
                pltpu.make_async_copy(
                    dw1.at[c, rows(s * rb, 48)], b_ref.at[p, pl.ds(48 * c, 48)], sems.at[3]
                ).start()

    @pl.when(ids[1] == 0)
    def _():
        store_sets(keep, send)

    @pl.when(ids[1] != 0)
    def _():
        store_sets(send, keep)

    def first_back(r, i):
        unit = unit1[r, :]
        d = hid[r, :] + z[r, :]
        gvec[3:4] = gvec[3:4] + rows_sum(d * unit)
        gvec[4:5] = gvec[4:5] + rows_sum(d)
        d = normalize_back(d * vec[3:4], unit, d2[r, 0:1])
        mixed[r, :] = d
        d_low = d.astype(BF)
        hid_low[r, :] = d_low
        gvec[2:3] = gvec[2:3] + rows_sum(d_low.astype(FL))

    row_loop(first_back)
    dwo[...] = t_dot(att[...], hid_low[...]).astype(BF)

    def store_wo(a_ref, b_ref):
        for p in range(NB):
            s = ids[0] ^ rel_a(p)
            pltpu.make_async_copy(dwo.at[rows(s * rb, 32)], a_ref.at[p, pl.ds(192, 32)], sems.at[3]).start()
            s = ids[0] ^ rel_b(p)
            pltpu.make_async_copy(dwo.at[rows(s * rb + 32, 16)], b_ref.at[p, pl.ds(192, 16)], sems.at[3]).start()
            pltpu.make_async_copy(dwo.at[rows(s * rb + 32, 16)], b_ref.at[p, pl.ds(208, 16)], sems.at[3]).start()

    @pl.when(ids[1] == 0)
    def _():
        store_wo(keep, send)

    @pl.when(ids[1] != 0)
    def _():
        store_wo(send, keep)

    z[...] = dot_t(hid_low[...], wo[...])
    heads = width // HD
    head_of = lax.broadcasted_iota(jnp.int32, (16, width), 1) // HD
    head_of = jnp.where(head_of < heads // 2, head_of, head_of - heads // 2 + 8)
    pick = (head_of == lax.broadcasted_iota(jnp.int32, (16, width), 0)).astype(FL).astype(BF)
    stats[0:8, :] = lse[0:8, :]
    stats[16:24, :] = lse[8:16, :]

    def last(r, i):
        d_low = z[r, :].astype(BF)
        pay[r, 0:width] = d_low
        prod = d_low.astype(FL) * exact[r, :]
        delta = jnp.zeros((16, rc), FL)
        for _ in range(3):
            piece = prod.astype(BF)
            delta = delta + dot_t(pick, piece)
            prod = prod - piece.astype(FL)
        stats[8:16, r] = delta[0:8]
        stats[24:32, r] = delta[8:16]

    row_loop(last)
    st = stats[...].T
    pieces = []
    for _ in range(3):
        piece = st.astype(BF).astype(FL)
        pieces.append(piece)
        st = st - piece
    pieces.append(jnp.zeros_like(st))
    pay_low[:, width:] = jnp.concatenate(pieces, 1)[: n // 2].astype(BF)
    pay_high[:, width:] = jnp.concatenate(pieces, 1)[n // 2 :].astype(BF)
    pay_low[:, 0:width] = pay[0 : n // 2, :]
    pay_high[:, 0:width] = pay[n // 2 :, :]
    wait_all(keep, sems.at[3])
    wait_all(send, sems.at[3])


def middle(ids, pool, att, exact, lse, cot, vec, upb, sets, set_rows):
    n, width = pool.shape
    ff = upb.shape[1]
    parts = ff // width
    whole = lambda i, *_: (0, 0)
    full = lambda x: pl.BlockSpec(x.shape, whole)
    shapes = [
        jax.ShapeDtypeStruct((n, width), BF),
        jax.ShapeDtypeStruct((n, width), BF),
        jax.ShapeDtypeStruct((n // 2, width + 128), BF),
        jax.ShapeDtypeStruct((n // 2, width + 128), BF),
        jax.ShapeDtypeStruct((32, n), FL),
        jax.ShapeDtypeStruct((n, width), FL),
        jax.ShapeDtypeStruct((8, width), FL),
        jax.ShapeDtypeStruct((8, ff), FL),
    ]
    big = jax.ShapeDtypeStruct((NB, set_rows, width), BF)
    return pl.pallas_call(
        middle_kernel,
        name="middle",
        cost_estimate=takes(36),
        grid_spec=pltpu.PrefetchScalarGridSpec(
            num_scalar_prefetch=1,
            grid=(1,),
            in_specs=[full(pool)]
            + [full(x) for x in (att, exact, lse, cot, vec, upb)]
            + [ANY] * 4,
            out_specs=[full(x) for x in shapes] + [ANY, ANY],
            scratch_shapes=[
                pltpu.VMEM((width, width), BF),
                pltpu.VMEM((parts, width, width), BF),
                pltpu.VMEM((ff, width), BF),
                pltpu.VMEM((parts, n, width), BF),
                pltpu.VMEM((parts, n, width), FL),
                pltpu.VMEM((n, width), FL),
                pltpu.VMEM((n, width), FL),
                pltpu.VMEM((n, width), BF),
                pltpu.VMEM((n, width), FL),
                pltpu.VMEM((n, 128), FL),
                pltpu.VMEM((parts, width, width), BF),
                pltpu.VMEM((ff, width), BF),
                pltpu.VMEM((width, width), BF),
                pltpu.SemaphoreType.DMA((4,)),
            ],
        ),
        out_shape=shapes + [big, big],
        compiler_params=params(),
    )(ids, pool, att, exact, lse, cot, vec, upb, *sets)


def weights_kernel(
    ids, pool, tok, dq, dk, dv, gvec, gup, sl, keep_low, keep_up, send_low, send_up, dwq, dwk, dwv, bias, tt, sems
):
    keep = (keep_low, keep_up)
    send = (send_low, send_up)
    width = tok.shape[1]
    ff = gup.shape[1]
    rb = width // NB
    tt[...] = tok[...].T
    dwq[...] = t_dot(pool[...].astype(BF), dq[...]).astype(BF)

    def columns(c, _):
        cols = pl.ds(pl.multiple_of(c * 256, 256), 256)
        dwk[:, cols] = dot(tt[...], dk[:, cols]).astype(BF)
        dwv[:, cols] = dot(tt[...], dv[:, cols]).astype(BF)
        return 0

    lax.fori_loop(0, width // 256, columns, 0)

    def rows(r, size):
        return pl.ds(pl.multiple_of(r, 16), size)

    def go(src, dst):
        pltpu.make_async_copy(src, dst, sems.at[0]).start()

    def store_sets(a_ref, b_ref):
        for p in range(NB):
            s = ids[0] ^ rel_a(p)
            go(dwq.at[rows(s * rb, 48)], a_ref[p // 8].at[p % 8, pl.ds(0, 48)])
            go(dwk.at[rows(s * rb, 32)], a_ref[p // 8].at[p % 8, pl.ds(48, 32)])
            s = ids[0] ^ rel_b(p)
            go(dwk.at[rows(s * rb + 32, 16)], b_ref[p // 8].at[p % 8, pl.ds(0, 16)])
            go(dwv.at[rows(s * rb, 48)], b_ref[p // 8].at[p % 8, pl.ds(16, 48)])

    @pl.when(ids[1] == 0)
    def _():
        store_sets(keep, send)

    @pl.when(ids[1] != 0)
    def _():
        store_sets(send, keep)

    row = lax.broadcasted_iota(jnp.int32, (16, width), 0)
    g = jnp.concatenate([gvec[...], jnp.zeros((8, width), FL)], 0)
    g = jnp.where(row == 0, rows_sum(dq[...].astype(FL)), g)
    g = jnp.where(row == 1, rows_sum(dv[...].astype(FL)), g)
    block_of = div_rb(lax.broadcasted_iota(jnp.int32, (16, width), 1))
    parts = []
    for p in range(NB):
        parts.append(jnp.where(block_of == (ids[0] ^ rel_b(p)), g, 0.0).astype(BF))
    total = dot_t(jnp.concatenate(parts, 0), spread_matrix(128, width, rb))
    row = lax.broadcasted_iota(jnp.int32, (16, ff), 0)
    block_of = div_rb(lax.broadcasted_iota(jnp.int32, (16, ff), 1))
    block_of = jnp.where((row >= 8) & (row < 12), block_of - row + 8, -1)
    up = jnp.concatenate([gup[...], gup[...]], 0)
    parts = []
    for p in range(NB):
        parts.append(jnp.where(block_of == 4 * (ids[0] ^ rel_b(p)), up, 0.0).astype(BF))
    total = total + dot_t(jnp.concatenate(parts, 0), spread_matrix(128, ff, rb))
    line = jnp.zeros((1, 128), FL)
    lane = lax.broadcasted_iota(jnp.int32, (1, 128), 1)
    for j in range(sl.shape[0] // 8):
        for i in range(2):
            value = jnp.sum(sl[8 * j : 8 * j + 1, QB * i : QB * i + QB], 1, keepdims=True)
            line = jnp.where(lane == 2 * j + i, -value, line)
    row = lax.broadcasted_iota(jnp.int32, (16 * NB, 128), 0)
    total = jnp.where((row & 15) == 12, line, total)
    bias[...] = jnp.zeros(bias.shape, BF)
    bias[:, 0:128] = total.astype(BF)

    def store_bias(b_ref):
        for p in range(NB):
            go(bias.at[pl.ds(16 * p, 16)], b_ref[p // 8].at[p % 8, pl.ds(64, 16)])

    @pl.when(ids[1] == 0)
    def _():
        store_bias(send)

    @pl.when(ids[1] != 0)
    def _():
        store_bias(keep)

    for x in keep + send:
        wait_all(x, sems.at[0])


def weight_grads(ids, pool, tok, dq, dk, dv, gvec, gup, sl, set_rows):
    width = tok.shape[1]
    full = lambda x: pl.BlockSpec(x.shape, lambda i, *_: (0, 0))
    big = jax.ShapeDtypeStruct((NB // 2, set_rows, width), BF)
    square = pltpu.VMEM((width, width), BF)
    return pl.pallas_call(
        weights_kernel,
        name="weight_grads",
        cost_estimate=takes(9),
        grid_spec=pltpu.PrefetchScalarGridSpec(
            num_scalar_prefetch=1,
            grid=(1,),
            in_specs=[full(x) for x in (pool, tok, dq, dk, dv, gvec, gup, sl)],
            out_specs=[ANY] * 4,
            scratch_shapes=[
                square,
                square,
                square,
                pltpu.VMEM((16 * NB, width), BF),
                pltpu.VMEM((width, tok.shape[0]), BF),
                pltpu.SemaphoreType.DMA((1,)),
            ],
        ),
        out_shape=[big] * 4,
        compiler_params=params(),
    )(ids, pool, tok, dq, dk, dv, gvec, gup, sl)


def tokens_kernel(mixed, dq, dk, dv, wq, wk, wv, out, acc):
    half = mixed.shape[0]
    up = 0.5 * (mixed[...] + dot_t(dq[...], wq[...]))
    down = dot_t(dk[...], wk[...]) + dot_t(dv[...], wv[...])
    for j in range(mixed.shape[1] // 128):
        cols = slice(128 * j, 128 * j + 128)
        for i in range(2):
            acc[j, pl.ds(i, half, stride=2)] = up[:, cols]
        out[:, cols] = acc[j] + down[:, cols]


def token_grads(mixed, dq, dk, dv, wq, wk, wv):
    rows, width = dk.shape
    step = 512
    half = pl.BlockSpec((step // 2, width), lambda i: (i, 0))
    block = pl.BlockSpec((step, width), lambda i: (i, 0))
    whole = pl.BlockSpec((width, width), lambda i: (0, 0))
    return pl.pallas_call(
        tokens_kernel,
        name="token_grads",
        cost_estimate=takes(8),
        grid=(rows // step,),
        in_specs=[half, half, block, block, whole, whole, whole],
        out_specs=block,
        out_shape=jax.ShapeDtypeStruct((rows, width), FL),
        scratch_shapes=[pltpu.VMEM((width // 128, step, 128), FL)],
        compiler_params=params(),
    )(mixed, dq, dk, dv, wq, wk, wv)


def blocks_of(x):
    return x.reshape(NB, x.shape[0] // NB, x.shape[1])


def column_parts(x, width):
    return jnp.concatenate([x[..., width * c : width * c + width] for c in range(x.shape[-1] // width)], -2)


def bias_block(small, up, width):
    rb = small[0].shape[-1]
    rows = jnp.stack(list(small) + [up[..., rb * c : rb * c + rb] for c in range(4)], -2)
    pad = [(0, 0)] * (rows.ndim - 2) + [(0, 4), (0, width - rb)]
    return jnp.pad(rows, pad)


def pack(wq, wk, wv, wo, w1, w2, bias, width):
    a1 = jnp.concatenate([wq, wk[..., :32, :]], -2)
    b1 = jnp.concatenate([wk[..., 32:, :], wv, bias], -2)
    a2 = jnp.concatenate([w2, wo[..., :32, :]], -2)
    b2 = jnp.concatenate([column_parts(w1, width), wo[..., 32:, :], wo[..., 32:, :]], -2)
    return a1, b1, a2, b2


def unpack(a1, b1, a2, b2, width):
    wq = a1[..., :48, :]
    wk = jnp.concatenate([a1[..., 48:, :], b1[..., :16, :]], -2)
    wv = b1[..., 16:64, :]
    bias = b1[..., 64:, :]
    wo = jnp.concatenate([a2[..., 192:, :], b2[..., 192:208, :]], -2)
    w2 = a2[..., :192, :]
    parts = 4
    w1 = jnp.concatenate([b2[..., 48 * c : 48 * c + 48, :] for c in range(parts)], -1)
    return wq, wk, wv, wo, w1, w2, bias


def pack_kernel(ids, wq, wk, wv, wo, w1, w2, b_up, *refs):
    vectors, (out, bias) = refs[:8], refs[8:]
    first = out.at[:, 0:80]
    second = out.at[:, 80:304]
    rb, width = wq.shape

    @pl.when(ids[1] == 0)
    def _():
        first[0, 0:48] = wq[...].astype(BF)
        first[0, 48:80] = wk[0:32].astype(BF)
        second[0, 0:192] = w2[...].astype(BF)
        second[0, 192:224] = wo[0:32].astype(BF)

    @pl.when(ids[1] != 0)
    def _():
        bias[...] = jnp.zeros(bias.shape, FL)
        for i, x in enumerate(vectors):
            bias[i : i + 1, 0:rb] = x[...]
        for c in range(4):
            bias[8 + c : 9 + c, 0:rb] = b_up[:, rb * c : rb * c + rb]
        first[0, 0:16] = wk[32:48].astype(BF)
        first[0, 16:64] = wv[...].astype(BF)
        first[0, 64:80] = bias[...].astype(BF)
        for c in range(4):
            second[0, 48 * c : 48 * c + 48] = w1[:, width * c : width * c + width].astype(BF)
        second[0, 192:208] = wo[32:48].astype(BF)
        second[0, 208:224] = wo[32:48].astype(BF)


def pack_own(ids, masters, b_up, vectors):
    width = masters[0].shape[1]
    args = list(masters) + [b_up[None]] + [x[None] for x in vectors]
    full = lambda x: pl.BlockSpec(x.shape, lambda i, *_: (0,) * len(x.shape))
    shape = jax.ShapeDtypeStruct((1, 304, width), BF)
    return pl.pallas_call(
        pack_kernel,
        name="pack",
        cost_estimate=takes(3),
        grid_spec=pltpu.PrefetchScalarGridSpec(
            num_scalar_prefetch=1,
            grid=(1,),
            in_specs=[full(x) for x in args],
            out_specs=full(shape),
            scratch_shapes=[pltpu.VMEM((16, width), FL)],
        ),
        out_shape=shape,
        compiler_params=params(),
    )(ids, *args)


def unpack_kernel(ids, low1, got1, olow1, ogot1, mine2, other2, wq, wk, wv, wo, w1, w2, *vectors):
    width = wq.shape[1]
    rb = wq.shape[0]
    mine1 = low1[...] + got1[...].astype(FL)
    other1 = olow1[...] + ogot1[...].astype(FL)

    def store(a1, b1, a2, b2):
        wq[...] = a1[0:48]
        wk[0:32] = a1[48:80]
        wk[32:48] = b1[0:16]
        wv[...] = b1[16:64]
        for i in range(8):
            vectors[i][...] = b1[64 + i : 65 + i, 0:rb]
        for c in range(4):
            vectors[8][:, rb * c : rb * c + rb] = b1[72 + c : 73 + c, 0:rb]
            w1[:, width * c : width * c + width] = b2[48 * c : 48 * c + 48]
        vectors[9][...] = b1[76:77, 0:128]
        w2[...] = a2[0:192]
        wo[0:32] = a2[192:224]
        wo[32:48] = b2[192:208]

    @pl.when(ids[1] == 0)
    def _():
        store(mine1, other1, mine2, other2)

    @pl.when(ids[1] != 0)
    def _():
        store(other1, mine1, other2, mine2)


def unpack_own(ids, args, ff):
    width = args[0].shape[1]
    rb = width // NB
    dims = [(rb, width)] * 4 + [(rb, ff), (ff // NB, width)] + [(1, rb)] * 8 + [(1, ff // NB), (1, 128)]
    shapes = [jax.ShapeDtypeStruct(d, FL) for d in dims]
    full = lambda x: pl.BlockSpec(x.shape, lambda i, *_: (0, 0))
    return pl.pallas_call(
        unpack_kernel,
        name="unpack",
        cost_estimate=takes(3),
        grid_spec=pltpu.PrefetchScalarGridSpec(
            num_scalar_prefetch=1,
            grid=(1,),
            in_specs=[full(x) for x in args],
            out_specs=[full(x) for x in shapes],
        ),
        out_shape=shapes,
        compiler_params=params(),
    )(ids, *args)


def after(x, *done):
    return lax.optimization_barrier((x,) + done)[0]


def local(
    tokens,
    cotangent,
    lengths,
    w_query,
    b_query,
    w_key,
    w_value,
    b_value,
    w_output,
    b_output,
    gain_attn,
    shift_attn,
    w_up,
    b_up,
    w_down,
    b_down,
    gain_ffn,
    shift_ffn,
    distance_slope,
):
    rows_here, width = tokens.shape
    ff = w_up.shape[1]
    own = rows_here // 2
    halo = rows_here // 2
    seq = lax.axis_size("seq")
    devices = seq * lax.axis_size("dp")
    direct = seq == NB
    order = ("dp", "seq")
    up_pairs = [(i, i + 1) for i in range(devices - 1)]
    down_pairs = [(i + 1, i) for i in range(devices - 1)]

    masters = (w_query, w_key, w_value, w_output, w_up, w_down)
    vectors = (b_query, b_value, b_output, gain_attn, shift_attn, b_down, gain_ffn, shift_ffn)
    if direct:
        core = lax.axis_index("dp")
        ids = jnp.stack([lax.axis_index("seq"), core]).astype(jnp.int32)
        x = pack_own(ids, masters, b_up, vectors)
        y = x[:, 80:]
        x = x[:, :80]
        x = jnp.concatenate([x, exchange(x, 8, 4)], 0)
        x1, low_a = lax.optimization_barrier(
            (exchange(x, 4, 8), lax.ppermute(tokens[rows_here - halo : rows_here - halo // 2], order, up_pairs))
        )
        x = jnp.concatenate([x, x1], 0)
        y, part = lax.optimization_barrier((y, tokens[rows_here - halo // 2 :], x1))[:2]
        x1, y1, low_b = lax.optimization_barrier(
            (exchange(x, 2, 1), exchange(y, 8, 4), lax.ppermute(part, order, up_pairs))
        )
        low1 = jnp.concatenate([x, x1], 0)
        y = jnp.concatenate([y, y1], 0)
        high1, olow1, y1, high_a = lax.optimization_barrier(
            (
                exchange(low1, 1, 2),
                swap_core(low1),
                exchange(y, 4, 8),
                lax.ppermute(after(tokens[: halo // 2], x1), order, down_pairs),
            )
        )
        y = jnp.concatenate([y, y1], 0)
        sets1 = (low1, high1, olow1, swap_core(high1))
        y1 = exchange(y, 2, 1)
        high_b = lax.ppermute(after(tokens[halo // 2 : halo], high1), order, down_pairs)
    else:
        ids = jnp.zeros((2,), jnp.int32)
        gather = lambda x: lax.all_gather(x.astype(BF), "seq", axis=0, tiled=True)
        full = [blocks_of(gather(x)) for x in masters]
        small = [gather(x).reshape(NB, -1) for x in vectors]
        bias = bias_block(small, gather(b_up).reshape(NB, -1), width)
        a1, b1, a2, b2 = pack(*full, bias, width)
        at_a = jnp.array([rel_a(p) for p in range(NB)])
        at_b = jnp.array([rel_b(p) for p in range(NB)])
        sets1 = (a1[at_a[:8]], a1[at_a[8:]], b1[at_b[:8]], b1[at_b[8:]])
        sets2 = (a2[at_a[:8]], a2[at_a[8:]], b2[at_b[:8]], b2[at_b[8:]])
        low_a = lax.ppermute(tokens[rows_here - halo : rows_here - halo // 2], order, up_pairs)
        low_b = lax.ppermute(tokens[rows_here - halo // 2 :], order, up_pairs)
        high_a = lax.ppermute(tokens[: halo // 2], order, down_pairs)
        high_b = lax.ppermute(tokens[halo // 2 : halo], order, down_pairs)

    first_row = lax.axis_index(order) * rows_here
    total = devices * rows_here
    starts = 2 * (jnp.cumsum(lengths) - lengths)
    place = first_row - halo + 2 * jnp.arange(2 * own, dtype=jnp.int32)
    before = starts[None, :] <= place[:, None]
    begin = jnp.max(jnp.where(before, starts[None, :], 0), 1)
    end = jnp.min(jnp.where(before, total, starts[None, :]), 1)
    inside = (place >= 0) & (place < total)
    shift = first_row - halo
    begin = jnp.where(inside, begin - shift, 0)
    end = jnp.where(inside, end - shift, 0)
    bounds = jnp.pad(jnp.stack([begin, end], 0).astype(FL), ((0, 6), (0, 0)))
    blocks = 2 * own // QB
    chunks = (rows_here + 2 * halo) // KC
    low_chunk = jnp.min(jnp.where(inside, begin, 4 * total).reshape(blocks, QB), 1) // KC
    high_chunk = (jnp.max(end.reshape(blocks, QB), 1) + KC - 1) // KC
    index = jnp.arange(blocks)
    away = (index < blocks // 4) | (index >= blocks - blocks // 4)
    low_chunk = jnp.clip(low_chunk, jnp.where(away, chunks // 4, 0), chunks)
    high_chunk = jnp.clip(high_chunk, 0, jnp.where(away, chunks - chunks // 4, chunks))
    spans = jnp.concatenate([low_chunk, high_chunk]).astype(jnp.int32)

    slopes = distance_slope
    q, k, v, kt, vt, pool, wq, wk, wv, vec, upb = qkv(ids, tokens, sets1, ff)
    if direct:
        k, high_b = lax.optimization_barrier((k, high_b))
    qh, k, v, kt, vt = halo_qkv(low_a, low_b, high_a, high_b, wq, wk, wv, vec, k, v, kt, vt)
    if direct:
        y1, qh = lax.optimization_barrier((y1, qh))
        low2 = jnp.concatenate([y, y1], 0)
        bounds = after(bounds, low2)
    att, exact, lse = attend_forward(spans, slopes, q, k, vt, bounds)
    if direct:
        high2, lse = lax.optimization_barrier((exchange(low2, 1, 2), lse))
        sets2 = (low2, high2, swap_core(low2), swap_core(high2))
    out, pay, pay_low, pay_high, stats, mixed, gvec, gup, keep2, send2 = middle(
        ids, pool, att, exact, lse, cotangent, vec, upb, sets2, 224
    )
    low_pay = lax.ppermute(pay_high, order, up_pairs)
    high_pay = lax.ppermute(pay_low, order, down_pairs)
    if direct:
        got = swap_core(send2)
        up = add(keep2[8:], got[8:]).astype(BF)
        bounds = after(bounds, up)
    dq, dk, dv, sl = attend_own(spans, slopes, q, k, v, kt, pay, stats, bounds)
    if direct:
        dq, low_pay, high_pay = lax.optimization_barrier((dq, low_pay, high_pay))
    dk, dv = attend_halo(spans, slopes, qh, k, v, low_pay, high_pay, bounds, dk, dv)
    if direct:
        got1, dk = lax.optimization_barrier((exchange(up, 1, 2), dk))
        up = add(keep2[4:8], got[4:8], got1[4:]).astype(BF)
        sl = after(sl, up)
    keep1, keep1_up, send1, send1_up = weight_grads(ids, pool, tokens, dq, dk, dv, gvec, gup, sl, 80)
    if direct:
        gots = swap_core(send1)
        part, got2 = lax.optimization_barrier((add(keep1_up, swap_core(send1_up)).astype(BF), exchange(up, 2, 1)))
        low = add(keep2[:4], got[:4], got1[:4])
        up = (low[2:] + got2[2:].astype(FL)).astype(BF)
        low = low[:2] + got2[:2].astype(FL)
        mixed = after(mixed, part, up)
    grad_tokens = token_grads(mixed, dq, dk, dv, wq, wk, wv)

    if direct:
        got3, one, grad_tokens = lax.optimization_barrier((exchange(up, 4, 8), exchange(part, 1, 2), grad_tokens))
        part = add(keep1[4:8], gots[4:8], one[4:]).astype(BF)
        up = (low[1:] + got3[1:].astype(FL)).astype(BF)
        low = low[:1] + got3[:1].astype(FL)
        got4, two = lax.optimization_barrier((exchange(up, 8, 4), exchange(part, 2, 1)))
        mine = (low + got4.astype(FL))[0]
        rest = add(keep1[:4], gots[:4], one[:4])
        part = (rest[2:] + two[2:].astype(FL)).astype(BF)
        rest = rest[:2] + two[:2].astype(FL)
        three, other = lax.optimization_barrier((exchange(part, 4, 8), swap_core(mine)))
        second = (mine, other)
        part = (rest[1:] + three[1:].astype(FL)).astype(BF)
        rest = rest[:1] + three[:1].astype(FL)
        over = [(s, seq + (s ^ 8)) for s in range(seq)] + [(seq + s, s ^ 4) for s in range(seq)]
        first = (rest[0], exchange(part, 8, 4)[0], swap_core(rest)[0], lax.ppermute(part, order, over)[0])
        gq, gk, gv, go, g1, g2, *small = unpack_own(ids, first + second, ff)
        g_up, g_slope = small[8][0], small[9][0, : distance_slope.shape[0]]
        small = [x[0] for x in small[:8]]
    else:
        inv_a = [0] * NB
        inv_b = [0] * NB
        for p in range(NB):
            inv_a[rel_a(p)] = p
            inv_b[rel_b(p)] = p
        inv_a = jnp.array(inv_a)
        inv_b = jnp.array(inv_b)
        joined = [jnp.concatenate(x, 0) for x in ((keep1, keep1_up), (send1, send1_up))]
        gq, gk, gv, go, g1, g2, gb = unpack(joined[0][inv_a], joined[1][inv_b], keep2[inv_a], send2[inv_b], width)
        rb = width // NB

        def share(x):
            x = lax.psum(x.astype(FL), "dp")
            return lax.psum_scatter(x, "seq", scatter_dimension=0, tiled=True)

        gq, gk, gv, go, g1, g2 = [share(x.reshape(-1, x.shape[-1])) for x in (gq, gk, gv, go, g1, g2)]
        small = [share(gb[:, i, :rb].reshape(-1)) for i in range(8)]
        g_up = share(gb[:, 8:12, :rb].reshape(-1))
        g_slope = lax.psum(gb[0, 12, : distance_slope.shape[0]].astype(FL), order)
    return (
        out,
        grad_tokens,
        gq,
        small[0],
        gk,
        gv,
        small[1],
        go,
        small[2],
        small[3],
        small[4],
        g1,
        g_up,
        g2,
        small[5],
        small[6],
        small[7],
        g_slope,
    )


def solution(mesh):
    tall = P(("dp", "seq"), None)
    mat = P("seq", None)
    vec = P("seq")
    return jax.shard_map(
        local,
        mesh=mesh,
        in_specs=(tall, tall, P(), mat, vec, mat, mat, vec, mat, vec, vec, vec, mat, vec, mat, vec, vec, vec, P()),
        out_specs=(tall, tall, mat, vec, mat, mat, vec, mat, vec, vec, vec, mat, vec, mat, vec, vec, vec, P()),
        check_vma=False,
    )
```

```python
import functools

import jax
import jax.numpy as jnp
from jax import lax
from jax.experimental import pallas as pl
from jax.experimental.pallas import tpu as pltpu
from jax.sharding import PartitionSpec as P

HD = 64
NB = 16
QB = 128
KC = 256
EPS = 1e-05
FAR = 1e12
BF = jnp.bfloat16
FL = jnp.float32


def rel_a(p):
    return (p & 1) * 8 + ((p >> 1) & 1) * 4 + ((p >> 2) & 1) * 2 + ((p >> 3) & 1)


def rel_b(p):
    return (p & 1) * 4 + ((p >> 1) & 1) * 8 + ((p >> 2) & 1) + ((p >> 3) & 1) * 2


def dot(a, b):
    return jnp.dot(a, b, preferred_element_type=FL)


def dot_t(a, b):
    return lax.dot_general(a, b, (((1,), (1,)), ((), ())), preferred_element_type=FL)


def t_dot(a, b):
    return lax.dot_general(a, b, (((0,), (0,)), ((), ())), preferred_element_type=FL)


def exchange(x, stride_a, stride_b):
    n = lax.axis_size("seq")
    pairs = [(s, s ^ stride_a) for s in range(n)] + [(n + s, n + (s ^ stride_b)) for s in range(n)]
    return lax.ppermute(x, ("dp", "seq"), pairs)


def swap_core(x):
    return lax.ppermute(x, "dp", [(0, 1), (1, 0)])


def add(*xs):
    total = xs[0].astype(FL)
    for x in xs[1:]:
        total = total + x.astype(FL)
    return total


def params(**kw):
    return pltpu.CompilerParams(vmem_limit_bytes=58 * 1024 * 1024, **kw)


def takes(us):
    return pl.CostEstimate(flops=us * 1150 * 10**6, transcendentals=0, bytes_accessed=us * 3600 * 10**3)


ANY = pl.BlockSpec(memory_space=pl.ANY)


def load_sets(ids, low, high, olow, ohigh, copies_a, copies_b):
    def start(a_refs, b_refs):
        for p in range(NB):
            copies_a(a_refs[p // 8].at[p % 8], ids[0] ^ rel_a(p), p)
            copies_b(b_refs[p // 8].at[p % 8], ids[0] ^ rel_b(p), p)

    @pl.when(ids[1] == 0)
    def _():
        start((low, high), (olow, ohigh))

    @pl.when(ids[1] != 0)
    def _():
        start((olow, ohigh), (low, high))


def wait_all(ref, sem):
    pltpu.make_async_copy(ref, ref, sem).wait()


def spread_matrix(rows, cols, rb):
    lanes = lax.broadcasted_iota(jnp.int32, (rows, cols), 1)
    return (lax.broadcasted_iota(jnp.int32, (rows, cols), 0) == lanes - rb * div_rb(lanes)).astype(FL).astype(BF)


def div_rb(x):
    return (x * 21846) >> 20


def qkv_kernel(
    ids, tok, low, high, olow, ohigh, q_out, k_out, v_out, kt_out, vt_out, pool_out, wq, wk, wv, vec_out, up_out, bias, x32, sems
):
    width = tok.shape[1]
    rb = width // NB

    @pl.when(pl.program_id(0) == 0)
    def _():
        def rows(r, n):
            return pl.ds(pl.multiple_of(r, 16), n)

        def copies_a(block, s, p):
            pltpu.make_async_copy(block.at[pl.ds(0, 48)], wq.at[rows(s * rb, 48)], sems.at[0]).start()
            pltpu.make_async_copy(block.at[pl.ds(48, 32)], wk.at[rows(s * rb, 32)], sems.at[1]).start()

        def copies_b(block, s, p):
            pltpu.make_async_copy(block.at[pl.ds(0, 16)], wk.at[rows(s * rb + 32, 16)], sems.at[1]).start()
            pltpu.make_async_copy(block.at[pl.ds(16, 48)], wv.at[rows(s * rb, 48)], sems.at[2]).start()
            pltpu.make_async_copy(block.at[pl.ds(64, 16)], bias.at[pl.ds(16 * p, 16)], sems.at[3]).start()

        load_sets(ids, low, high, olow, ohigh, copies_a, copies_b)
        wait_all(wq, sems.at[0])
        wait_all(wk, sems.at[1])
        wait_all(wv, sems.at[2])
        wait_all(bias, sems.at[3])
        parts = bias[:, 0:128]
        wide = dot(parts, spread_matrix(128, width, rb))
        block_of = div_rb(lax.broadcasted_iota(jnp.int32, (16, width), 1))
        total = jnp.zeros((16, width), FL)
        for p in range(NB):
            total = total + jnp.where(block_of == (ids[0] ^ rel_b(p)), wide[16 * p : 16 * p + 16], 0.0)
        vec_out[...] = total
        ff = up_out.shape[1]
        wide = dot(parts, spread_matrix(128, ff, rb))
        block_of = div_rb(lax.broadcasted_iota(jnp.int32, (16, ff), 1))
        row = lax.broadcasted_iota(jnp.int32, (16, ff), 0)
        block_of = jnp.where((row >= 8) & (row < 12), block_of - row + 8, -1)
        total = jnp.zeros((16, ff), FL)
        for p in range(NB):
            total = total + jnp.where(block_of == 4 * (ids[0] ^ rel_b(p)), wide[16 * p : 16 * p + 16], 0.0)
        up_out[...] = jnp.broadcast_to(jnp.sum(total, 0, keepdims=True), up_out.shape)

    pool_out[...] = project(tok[...], wq, wk, wv, vec_out, q_out, k_out, v_out, kt_out, vt_out, x32)


def project(x, wq, wk, wv, vec, q_out, k_out, v_out, kt_out, vt_out, x32):
    width = x.shape[1]
    half = x.shape[0] // 2
    k_out[...] = dot(x, wk[...]).astype(BF)
    v_out[...] = (dot(x, wv[...]) + vec[1:2]).astype(BF)
    for c in range(x.shape[0] // KC):
        kt_out[c] = k_out[KC * c : KC * c + KC].T
        vt_out[c] = v_out[KC * c : KC * c + KC].T
    pooled = []
    for j in range(width // 128):
        x32[j] = x[:, 128 * j : 128 * j + 128].astype(FL)
        pooled.append((x32[j, pl.ds(0, half, stride=2)] + x32[j, pl.ds(1, half, stride=2)]) * 0.5)
    pooled = jnp.concatenate(pooled, 1)
    q = (dot(pooled.astype(BF), wq[...]) + vec[0:1]).astype(BF)
    q_out[...] = (q.astype(FL) * HD**-0.5).astype(BF)
    return pooled


def qkv(ids, tokens, sets, ff):
    rows, width = tokens.shape
    step = 512
    whole = lambda i, *_: (0, 0)
    square = jax.ShapeDtypeStruct((width, width), BF)
    thin = pl.BlockSpec((step // 2, width), lambda i, *_: (i, 0))
    block = pl.BlockSpec((step, width), lambda i, *_: (i, 0))
    inner = pl.BlockSpec((step, width), lambda i, *_: (i + 1, 0))
    tall = pl.BlockSpec((step // KC, width, KC), lambda i, *_: (i + 1, 0, 0))
    return pl.pallas_call(
        qkv_kernel,
        name="qkv",
        cost_estimate=takes(9),
        grid_spec=pltpu.PrefetchScalarGridSpec(
            num_scalar_prefetch=1,
            grid=(rows // step,),
            in_specs=[block, ANY, ANY, ANY, ANY],
            out_specs=[thin, inner, inner, tall, tall, thin]
            + [pl.BlockSpec((width, width), whole)] * 3
            + [pl.BlockSpec((16, width), whole), pl.BlockSpec((8, ff), whole)],
            scratch_shapes=[
                pltpu.VMEM((16 * NB, width), BF),
                pltpu.VMEM((width // 128, step, 128), FL),
                pltpu.SemaphoreType.DMA((4,)),
            ],
        ),
        out_shape=[
            jax.ShapeDtypeStruct((rows // 2, width), BF),
            jax.ShapeDtypeStruct((2 * rows, width), BF),
            jax.ShapeDtypeStruct((2 * rows, width), BF),
            jax.ShapeDtypeStruct((2 * rows // KC, width, KC), BF),
            jax.ShapeDtypeStruct((2 * rows // KC, width, KC), BF),
            jax.ShapeDtypeStruct((rows // 2, width), FL),
            square,
            square,
            square,
            jax.ShapeDtypeStruct((16, width), FL),
            jax.ShapeDtypeStruct((8, ff), FL),
        ],
        compiler_params=params(),
    )(ids, tokens, *sets)


def halo_qkv_kernel(
    low_a, low_b, high_a, high_b, wq, wk, wv, vec, k, v, kt, vt, q_out, k_out, v_out, kt_out, vt_out, x32
):
    low = pl.program_id(0) == 0
    parts = [jnp.where(low, a[...], b[...]) for a, b in ((low_a, high_a), (low_b, high_b))]
    project(jnp.concatenate(parts, 0), wq, wk, wv, vec, q_out, k_out, v_out, kt_out, vt_out, x32)


def halo_qkv(low_a, low_b, high_a, high_b, wq, wk, wv, vec, k, v, kt, vt):
    rows, width = low_a.shape
    rows = 2 * rows
    full = lambda x: pl.BlockSpec(x.shape, lambda i: (0,) * len(x.shape))
    args = (low_a, low_b, high_a, high_b, wq, wk, wv, vec)
    edge = pl.BlockSpec((rows, width), lambda i: (3 * i, 0))
    tall = pl.BlockSpec((rows // KC, width, KC), lambda i: (3 * i, 0, 0))
    return pl.pallas_call(
        halo_qkv_kernel,
        name="halo_qkv",
        cost_estimate=takes(7),
        grid=(2,),
        in_specs=[full(x) for x in args] + [ANY] * 4,
        out_specs=[pl.BlockSpec((None, rows // 2, width), lambda i: (i, 0, 0)), edge, edge, tall, tall],
        out_shape=[jax.ShapeDtypeStruct((2, rows // 2, width), BF)]
        + [jax.ShapeDtypeStruct(x.shape, x.dtype) for x in (k, v, kt, vt)],
        input_output_aliases={8: 1, 9: 2, 10: 3, 11: 4},
        scratch_shapes=[pltpu.VMEM((width // 128, rows, 128), FL)],
        compiler_params=params(),
    )(*args, k, v, kt, vt)


def two_heads(x):
    lane = lax.broadcasted_iota(jnp.int32, x.shape, 1)
    zero = jnp.zeros_like(x)
    return jnp.concatenate([jnp.where(lane < HD, x, zero), jnp.where(lane < HD, zero, x)], 0)


def one_block(x):
    r = x.shape[1] // 2
    line = lax.broadcasted_iota(jnp.int32, (128, r), 0)
    return jnp.where(line < HD, x[:, :r], x[:, r:]).T


def distances(bounds, row, c):
    low = bounds[0:1, pl.ds(row, QB)]
    high = bounds[1:2, pl.ds(row, QB)]
    query = (2 * (row + lax.broadcasted_iota(jnp.int32, (KC, QB), 1))).astype(FL) + 0.5
    key = (c * KC + lax.broadcasted_iota(jnp.int32, (KC, QB), 0)).astype(FL)
    far = jnp.where((key >= low) & (key < high), jnp.abs(query - key), FAR)
    return jnp.concatenate([far, far], 1)


def fold(x, f):
    n = x.shape[0] // 8
    parts = [x[8 * i : 8 * i + 8] for i in range(n)]
    while len(parts) > 1:
        parts = [f(parts[2 * i], parts[2 * i + 1]) for i in range(len(parts) // 2)]
    return parts[0]


def slope_line(slopes, head):
    lane = lax.broadcasted_iota(jnp.int32, (1, 2 * QB), 1)
    return jnp.where(lane < QB, slopes[head], slopes[head + 1])


def forward_kernel(
    spans, slopes, q, k, vt, bounds, o_out, exact_out, lse_out, s_scr, q2, top, total, acc, rest
):
    pairs = q.shape[1] // 128
    head0 = pl.program_id(0) * 2 * pairs
    q_first = q.shape[0] // 2
    slope = [slope_line(slopes, head0 + 2 * j) for j in range(pairs)]

    def query_block(b, _):
        row = pl.multiple_of(q_first + b * QB, QB)
        out_rows = pl.ds(pl.multiple_of(b * QB, QB), QB)
        block = row // QB
        c0 = spans[block]
        c1 = spans[spans.shape[0] // 2 + block]
        for j in range(pairs):
            q2[j] = two_heads(q[out_rows, 128 * j : 128 * j + 128])
        top[...] = jnp.full(top.shape, -3e38, FL)
        total[...] = jnp.zeros(total.shape, FL)
        acc[...] = jnp.zeros(acc.shape, FL)
        rest[...] = jnp.zeros(rest.shape, FL)

        def score(c, _):
            far = distances(bounds, row, c)
            keys = pl.ds(pl.multiple_of(c * KC, KC), KC)
            for j in range(pairs):
                s = dot_t(k[keys, 128 * j : 128 * j + 128], q2[j]) - slope[j] * far
                s_scr[c - c0, j] = s
                top[j] = jnp.maximum(top[j], fold(s, jnp.maximum))
            return 0

        lax.fori_loop(c0, c1, score, 0)
        peak = [jnp.max(top[j], 0, keepdims=True) for j in range(pairs)]

        def exponent(c, _):
            for j in range(pairs):
                e = jnp.exp(s_scr[c - c0, j] - peak[j])
                s_scr[c - c0, j] = e
                total[j] = total[j] + fold(e, jnp.add)
            return 0

        lax.fori_loop(c0, c1, exponent, 0)
        inverse = []
        for j in range(pairs):
            l = jnp.sum(total[j], 0, keepdims=True)
            t = peak[j] + jnp.log(l)
            inverse.append(1.0 / l)
            lse_out[2 * j : 2 * j + 1, out_rows] = t[:, :QB]
            lse_out[2 * j + 1 : 2 * j + 2, out_rows] = t[:, QB:]

        def attend(c, _):
            for j in range(pairs):
                p = s_scr[c - c0, j] * inverse[j]
                high = p.astype(BF)
                low = (p - high.astype(FL)).astype(BF)
                values = vt[c, 128 * j : 128 * j + 128]
                acc[j] = acc[j] + dot(values, high)
                rest[j] = rest[j] + dot(values, low)
            return 0

        lax.fori_loop(c0, c1, attend, 0)
        for j in range(pairs):
            cols = slice(128 * j, 128 * j + 128)
            o_out[out_rows, cols] = one_block(acc[j]).astype(BF)
            exact_out[out_rows, cols] = one_block(acc[j] + rest[j])
        return 0

    lse_out[...] = jnp.zeros(lse_out.shape, FL)
    lax.fori_loop(0, o_out.shape[0] // QB, query_block, 0)


def attend_forward(spans, slopes, q, k, vt, bounds):
    own, width = q.shape
    wide = width // 2
    pairs = wide // 128
    keys = k.shape[0]
    chunks = keys // KC
    col = lambda i, *_: (0, i)
    return pl.pallas_call(
        forward_kernel,
        name="attend_forward",
        cost_estimate=takes(30),
        grid_spec=pltpu.PrefetchScalarGridSpec(
            num_scalar_prefetch=2,
            grid=(2,),
            in_specs=[
                pl.BlockSpec((own, wide), col),
                pl.BlockSpec((keys, wide), col),
                pl.BlockSpec((chunks, wide, KC), lambda i, *_: (0, i, 0)),
                pl.BlockSpec(bounds.shape, lambda i, *_: (0, 0)),
            ],
            out_specs=[
                pl.BlockSpec((own, wide), col),
                pl.BlockSpec((own, wide), col),
                pl.BlockSpec((8, own), lambda i, *_: (i, 0)),
            ],
            scratch_shapes=[
                pltpu.VMEM((chunks, pairs, KC, 2 * QB), FL),
                pltpu.VMEM((pairs, 2 * QB, 128), BF),
                pltpu.VMEM((pairs, 8, 2 * QB), FL),
                pltpu.VMEM((pairs, 8, 2 * QB), FL),
                pltpu.VMEM((pairs, 128, 2 * QB), FL),
                pltpu.VMEM((pairs, 128, 2 * QB), FL),
            ],
        ),
        out_shape=[
            jax.ShapeDtypeStruct((own, width), BF),
            jax.ShapeDtypeStruct((own, width), FL),
            jax.ShapeDtypeStruct((16, own), FL),
        ],
        compiler_params=params(),
    )(spans, slopes, q, k, vt, bounds)


def pieces(x):
    out = []
    for _ in range(3):
        y = x.astype(BF).astype(FL)
        out.append(y)
        x = x - y
    return out


def key_lines(side, kind):
    lane = lax.broadcasted_iota(jnp.int32, (KC, 128), 1)
    key = lax.broadcasted_iota(jnp.int32, (KC, 128), 0).astype(FL)
    x = jnp.where(lane < 3, 1.0, jnp.where(lane < 6, -side, jnp.where(lane < 9, side * key, 0.0)))
    return jnp.where(lane == kind, 1.0, x) if kind else x


def chunk_lines(base, away, side, limit):
    lane = lax.broadcasted_iota(jnp.int32, (KC, 128), 1)
    key = lax.broadcasted_iota(jnp.int32, (KC, 128), 0).astype(FL) + KC * away
    other = jnp.where(side * key < side * limit, 1.0, 0.0)
    x = base + jnp.where((lane >= 9) & (lane < 12), side * KC * away, 0.0)
    return jnp.where(lane == 12, other, x).astype(BF)


def value_lines():
    lane = lax.broadcasted_iota(jnp.int32, (KC, 128), 1)
    return (lane < 3).astype(FL).astype(BF)


def query_rows(lse, slope, spots, out_left, out_right):
    one = jnp.ones_like(lse)
    rows = pieces(-lse) + pieces(slope * spots) + pieces(slope * one) * 2
    rows += [-FAR * one, -FAR * out_left, -FAR * out_right, 0.0 * one]
    return jnp.concatenate(rows, 0).astype(BF)


def two_heads_t(x):
    line = lax.broadcasted_iota(jnp.int32, x.shape, 0)
    zero = jnp.zeros_like(x)
    return jnp.concatenate([jnp.where(line < HD, x, zero), jnp.where(line < HD, zero, x)], 1)


def block_setup(bounds, row):
    low = bounds[0:1, pl.ds(row, QB)]
    high = bounds[1:2, pl.ds(row, QB)]
    first = low[:, 0:1]
    last = high[:, QB - 1 : QB]
    base = (2 * row).astype(FL) if hasattr(row, "astype") else float(2 * row)
    out_left = jnp.where(low == first, 0.0, 1.0)
    out_right = jnp.where(high == last, 0.0, 1.0)
    spots = 2.0 * lax.broadcasted_iota(jnp.int32, (1, QB), 1).astype(FL) + 0.5
    return low - base, high - base, first - base, last - base - 0.5, twice(out_left), twice(out_right), twice(spots)


def twice(x):
    return jnp.concatenate([x, x], 1)


def fill_queries(j, q, da, lse, delta, slope, setup, q2, da2, qt, dat):
    out_left, out_right, spots = setup[4:]
    q2[j] = two_heads(q)
    da2[j] = two_heads(da)
    qt[j, 0:128] = two_heads_t(q.T)
    dat[j, 0:128] = two_heads_t(da.T)
    qt[j, 128:144] = query_rows(lse, slope, spots, out_left, out_right)
    rows = pieces(-delta) + [jnp.zeros((13, 2 * QB), FL)]
    dat[j, 128:144] = jnp.concatenate(rows, 0).astype(BF)


def own_kernel(
    spans, slopes, q, k, v, kt, da, stats, bounds, dq_out, dk, dv, slope_out, q2, da2, qt, dat, dq2, sl, base
):
    pairs = q.shape[1] // 128
    head0 = pl.program_id(0) * 2 * pairs
    total_blocks = bounds.shape[1] // QB
    quarter = k.shape[0] // KC // 4
    first = total_blocks // 4
    slope = [slope_line(slopes, head0 + 2 * j) for j in range(pairs)]
    dk[...] = jnp.zeros(dk.shape, FL)
    dv[...] = jnp.zeros(dv.shape, FL)
    sl[...] = jnp.zeros(sl.shape, FL)
    qt[...] = jnp.zeros(qt.shape, BF)
    dat[...] = jnp.zeros(dat.shape, BF)
    line = lax.broadcasted_iota(jnp.int32, (16, KC), 0)
    spot = lax.broadcasted_iota(jnp.int32, (16, KC), 1).astype(FL)
    extra = jnp.where(line == 0, 1.0, jnp.where(line == 1, spot, 0.0)).astype(BF)
    base[0] = key_lines(1.0, 13)
    base[1] = key_lines(-1.0, 14)
    own_lines = key_lines(1.0, 0).astype(BF)
    ones = value_lines()

    def query_block(b, _):
        block = first + b
        row = pl.multiple_of(block * QB, QB)
        rows = pl.ds(pl.multiple_of(b * QB, QB), QB)
        c0 = spans[block]
        c1 = spans[total_blocks + block]
        setup = block_setup(bounds, row)
        low, high, limit_left, limit_right = setup[:4]
        spots = setup[6]
        for j in range(pairs):
            cols = slice(128 * j, 128 * j + 128)
            h = 2 * j
            lse = jnp.concatenate([stats[h : h + 1, rows], stats[h + 1 : h + 2, rows]], 1)
            delta = jnp.concatenate([stats[8 + h : 9 + h, rows], stats[9 + h : 10 + h, rows]], 1)
            fill_queries(j, q[rows, cols], da[rows, cols], lse, delta, slope[j], setup, q2, da2, qt, dat)
        dq2[...] = jnp.zeros(dq2.shape, FL)

        def step(c, lines, side, away, grads, wide):
            keys = pl.ds(pl.multiple_of(c * KC, KC), KC)
            col = [slice(128 * j, 128 * j + 128) for j in range(pairs)]
            s = [dot(jnp.concatenate([k[keys, col[j]], lines], 1), qt[j]) for j in range(pairs)]
            dp = [dot(jnp.concatenate([v[keys, col[j]], ones], 1), dat[j]) for j in range(pairs)]
            if wide is not None:
                s = [s[j] - slope[j] * wide for j in range(pairs)]
            p = [jnp.exp(x) for x in s]
            ds = [(p[j] * dp[j]).astype(BF) for j in range(pairs)]
            if grads:
                mine = pl.ds(pl.multiple_of((c - quarter) * KC, KC), KC)
                new_v = [dot(p[j].astype(BF), da2[j]) for j in range(pairs)]
                new_k = [dot(ds[j], q2[j]) for j in range(pairs)]
            r = [dot(jnp.concatenate([kt[c, col[j]], extra], 0), ds[j]) for j in range(pairs)]
            for j in range(pairs):
                if grads:
                    dv[mine, col[j]] = dv[mine, col[j]] + new_v[j]
                    dk[mine, col[j]] = dk[mine, col[j]] + new_k[j]
                dq2[j] = dq2[j] + r[j][0:128]
                part = side * ((spots - KC * away) * r[j][128:129] - r[j][129:130])
                if wide is not None:
                    part = part + jnp.sum(ds[j].astype(FL) * wide, 0, keepdims=True)
                sl[j] = sl[j] + part

        key = lax.broadcasted_iota(jnp.int32, (KC, QB), 0).astype(FL)
        over = 2.0 * jnp.maximum(key - spots[:, :QB], 0.0)
        wide = twice(jnp.where((key >= low) & (key < high), over, FAR))
        step(block, own_lines, 1.0, 0.0, True, wide)

        def other(c, grads):
            before = c < block
            side = jnp.where(before, 1.0, -1.0)
            away = (c - block).astype(FL)
            limit = jnp.where(before, limit_left, limit_right)
            step(c, chunk_lines(base[jnp.where(before, 0, 1)], away, side, limit), side, away, grads, None)

        def inside(i, _):
            other(jnp.where(i < block, i, i + 1), True)
            return 0

        left = jnp.maximum(jnp.minimum(c1, quarter) - c0, 0)
        right0 = jnp.maximum(c0, 3 * quarter)

        def outside(i, _):
            other(jnp.where(i < left, c0 + i, right0 + i - left), False)
            return 0

        lax.fori_loop(jnp.maximum(c0, quarter), jnp.minimum(c1, 3 * quarter) - 1, inside, 0)
        lax.fori_loop(0, left + jnp.maximum(c1 - right0, 0), outside, 0)
        for j in range(pairs):
            dq_out[rows, 128 * j : 128 * j + 128] = (one_block(dq2[j]) * HD**-0.5).astype(BF)
        return 0

    lax.fori_loop(0, da.shape[0] // QB, query_block, 0)
    slope_out[...] = jnp.zeros(slope_out.shape, FL)
    for j in range(pairs):
        slope_out[8 * j : 8 * j + 1] = sl[j]


def attend_own(spans, slopes, q, k, v, kt, da, stats, bounds):
    own, width = q.shape
    wide = width // 2
    pairs = wide // 128
    keys = k.shape[0]
    chunks = keys // KC
    col = lambda i, *_: (0, i)
    zero = lambda i, *_: (0, 0)
    return pl.pallas_call(
        own_kernel,
        name="attend_own",
        cost_estimate=takes(30),
        grid_spec=pltpu.PrefetchScalarGridSpec(
            num_scalar_prefetch=2,
            grid=(2,),
            in_specs=[
                pl.BlockSpec((own, wide), col),
                pl.BlockSpec((keys, wide), col),
                pl.BlockSpec((keys, wide), col),
                pl.BlockSpec((chunks, wide, KC), lambda i, *_: (0, i, 0)),
                pl.BlockSpec((own, wide), col),
                pl.BlockSpec((16, own), lambda i, *_: (i, 0)),
                pl.BlockSpec(bounds.shape, zero),
            ],
            out_specs=[
                pl.BlockSpec((own, wide), col),
                pl.BlockSpec((keys // 2, wide), col),
                pl.BlockSpec((keys // 2, wide), col),
                pl.BlockSpec((8 * pairs, 2 * QB), lambda i, *_: (i, 0)),
            ],
            scratch_shapes=[
                pltpu.VMEM((pairs, 2 * QB, 128), BF),
                pltpu.VMEM((pairs, 2 * QB, 128), BF),
                pltpu.VMEM((pairs, 256, 2 * QB), BF),
                pltpu.VMEM((pairs, 256, 2 * QB), BF),
                pltpu.VMEM((pairs, 128, 2 * QB), FL),
                pltpu.VMEM((pairs, 1, 2 * QB), FL),
                pltpu.VMEM((2, KC, 128), FL),
            ],
        ),
        out_shape=[
            jax.ShapeDtypeStruct((own, width), BF),
            jax.ShapeDtypeStruct((keys // 2, width), FL),
            jax.ShapeDtypeStruct((keys // 2, width), FL),
            jax.ShapeDtypeStruct((16 * pairs, 2 * QB), FL),
        ],
        compiler_params=params(),
    )(spans, slopes, q, k, v, kt, da, stats, bounds)


def halo_kernel(
    spans,
    slopes,
    q,
    ka,
    kb,
    va,
    vb,
    low_pay,
    high_pay,
    low_stats,
    high_stats,
    bounds,
    dk0,
    dv0,
    dk_out,
    dv_out,
    q2,
    da2,
    qt,
    dat,
    st,
    k,
    v,
    dk,
    dv,
):
    half = pl.program_id(0)
    pairs = q.shape[2] // 128
    total_blocks = bounds.shape[1] // QB
    edge = ka.shape[0]
    first = edge // KC
    count = low_pay.shape[0] // QB
    dk[...] = dk0[...]
    dv[...] = dv0[...]
    for into, parts in ((k, (ka, kb)), (v, (va, vb))):
        into[0:edge] = parts[0][...]
        into[edge:] = parts[1][...]
    qt[...] = jnp.zeros(qt.shape, BF)
    dat[...] = jnp.zeros(dat.shape, BF)
    ones = value_lines()
    for side, pay in enumerate((low_stats, high_stats)):
        x = pay[...].astype(FL)
        x = (x + pltpu.roll(x, 96, 1) + pltpu.roll(x, 64, 1)).T
        st[side] = jnp.where(half == 0, x[0:16], x[16:32])

    def query_block(i, _):
        side = i // count
        nth = i - side * count
        block = jnp.where(side == 0, i, total_blocks - 2 * count + i)
        row = pl.multiple_of(block * QB, QB)
        rows = pl.ds(pl.multiple_of(nth * QB, QB), QB)
        c0 = spans[block]
        c1 = spans[total_blocks + block]

        @pl.when(c0 < c1)
        def _():
            setup = block_setup(bounds, row)
            limit = jnp.where(side == 0, setup[3], setup[2])
            sign = jnp.where(side == 0, -1.0, 1.0)
            base = jnp.where(side == 0, key_lines(-1.0, 14), key_lines(1.0, 13))
            for j in range(pairs):
                cols = slice(128 * j, 128 * j + 128)
                h = 2 * j
                lse = jnp.concatenate([st[side, h : h + 1, rows], st[side, h + 1 : h + 2, rows]], 1)
                delta = jnp.concatenate([st[side, h + 8 : h + 9, rows], st[side, h + 9 : h + 10, rows]], 1)
                d = jnp.where(side == 0, low_pay[rows, cols], high_pay[rows, cols])
                slope = slope_line(slopes, 2 * pairs * half + h)
                fill_queries(j, q[side, rows, cols], d, lse, delta, slope, setup, q2, da2, qt, dat)

            def step(c, _):
                mine = pl.ds(pl.multiple_of((c - first) * KC, KC), KC)
                lines = chunk_lines(base, (c - block).astype(FL), sign, limit)
                js = range(pairs)
                col = [slice(128 * j, 128 * j + 128) for j in js]
                p = [jnp.exp(dot(jnp.concatenate([k[mine, col[j]], lines], 1), qt[j])) for j in js]
                dp = [dot(jnp.concatenate([v[mine, col[j]], ones], 1), dat[j]) for j in js]
                new_v = [dot(p[j].astype(BF), da2[j]) for j in js]
                new_k = [dot((p[j] * dp[j]).astype(BF), q2[j]) for j in js]
                for j in js:
                    dv[mine, col[j]] = dv[mine, col[j]] + new_v[j]
                    dk[mine, col[j]] = dk[mine, col[j]] + new_k[j]
                return 0

            lax.fori_loop(c0, c1, step, 0)

        return 0

    lax.fori_loop(0, 2 * count, query_block, 0)
    dk_out[...] = dk[...].astype(BF)
    dv_out[...] = dv[...].astype(BF)


def attend_halo(spans, slopes, q, k, v, low_pay, high_pay, bounds, dk0, dv0):
    width = q.shape[2]
    wide = width // 2
    pairs = wide // 128
    keys = dk0.shape[0]
    rows = low_pay.shape[0]
    shape = jax.ShapeDtypeStruct((keys, width), BF)
    col = lambda i, *_: (0, i)
    parts = [pl.BlockSpec((keys // 2, wide), lambda i, *_: (1, i)), pl.BlockSpec((keys // 2, wide), lambda i, *_: (2, i))]
    tail = pl.BlockSpec((rows, 128), lambda i, *_: (0, width // 128))
    whole = pl.BlockSpec((keys, wide), col)
    pay = pl.BlockSpec((rows, wide), col)
    return pl.pallas_call(
        halo_kernel,
        name="attend_halo",
        cost_estimate=takes(12),
        grid_spec=pltpu.PrefetchScalarGridSpec(
            num_scalar_prefetch=2,
            grid=(2,),
            in_specs=[pl.BlockSpec((2, q.shape[1], wide), lambda i, *_: (0, 0, i))]
            + parts * 2
            + [pay, pay, tail, tail, pl.BlockSpec(bounds.shape, lambda i, *_: (0, 0)), whole, whole],
            out_specs=[whole, whole],
            scratch_shapes=[
                pltpu.VMEM((pairs, 2 * QB, 128), BF),
                pltpu.VMEM((pairs, 2 * QB, 128), BF),
                pltpu.VMEM((pairs, 256, 2 * QB), BF),
                pltpu.VMEM((pairs, 256, 2 * QB), BF),
                pltpu.VMEM((2, 16, rows), FL),
                pltpu.VMEM((keys, wide), BF),
                pltpu.VMEM((keys, wide), BF),
                pltpu.VMEM((keys, wide), FL),
                pltpu.VMEM((keys, wide), FL),
            ],
        ),
        out_shape=[shape, shape],
        compiler_params=params(),
    )(spans, slopes, q, k, k, v, v, low_pay, high_pay, low_pay, high_pay, bounds, dk0, dv0)


def normalize(z):
    centred = z - jnp.mean(z, -1, keepdims=True)
    scale = lax.rsqrt(jnp.mean(centred * centred, -1, keepdims=True) + EPS)
    return centred * scale, scale


def normalize_back(d, unit, scale):
    return scale * (d - jnp.mean(d, -1, keepdims=True) - unit * jnp.mean(d * unit, -1, keepdims=True))


def rows_sum(x):
    return jnp.sum(x, 0, keepdims=True)


def middle_kernel(
    ids,
    pool_in,
    att,
    exact_in,
    lse,
    cot_in,
    vec,
    upb,
    low,
    high,
    olow,
    ohigh,
    out,
    pay,
    pay_low,
    pay_high,
    stats,
    mixed,
    gvec,
    gup,
    keep,
    send,
    wo,
    w1,
    w2,
    active,
    slope,
    unit1,
    hid,
    hid_low,
    z,
    d2,
    dw1,
    dw2,
    dwo,
    pool,
    exact,
    cot,
    sems,
    load_sems,
):
    n, width = att.shape
    loads = [(pool_in, pool), (cot_in, cot), (exact_in, exact)]
    loads = [pltpu.make_async_copy(a, b, load_sems.at[i]) for i, (a, b) in enumerate(loads)]
    rb = width // NB
    fb = w2.shape[0] // NB
    parts = w1.shape[0]

    def rows(r, size):
        return pl.ds(pl.multiple_of(r, 16), size)

    def copies_a(block, s, p):
        pltpu.make_async_copy(block.at[pl.ds(192, 32)], wo.at[rows(s * rb, 32)], sems.at[0]).start()
        pltpu.make_async_copy(block.at[pl.ds(0, 192)], w2.at[rows(s * fb, 192)], sems.at[2]).start()

    def copies_b(block, s, p):
        pltpu.make_async_copy(block.at[pl.ds(192, 16)], wo.at[rows(s * rb + 32, 16)], sems.at[0]).start()
        for c in range(parts):
            pltpu.make_async_copy(block.at[pl.ds(48 * c, 48)], w1.at[c, rows(s * rb, 48)], sems.at[1]).start()

    load_sets(ids, low, high, olow, ohigh, copies_a, copies_b)
    for x in loads:
        x.start()
    wait_all(wo, sems.at[0])
    z[...] = dot(att[...], wo[...])
    loads[0].wait()
    rc = 128

    def row_loop(f):
        def body(i, _):
            f(pl.ds(pl.multiple_of(i * rc, rc), rc), i)
            return 0

        lax.fori_loop(0, n // rc, body, 0)

    def first_norm(r, i):
        unit, scale = normalize(pool[r, :] + z[r, :] + vec[2:3])
        h = unit * vec[3:4] + vec[4:5]
        unit1[r, :] = unit
        d2[r, 0:128] = jnp.broadcast_to(scale, (rc, 128))
        hid[r, :] = h
        hid_low[r, :] = h.astype(BF)

    row_loop(first_norm)
    wait_all(w1, sems.at[1])
    wait_all(w2, sems.at[2])
    c0 = 0.7978845608028654

    def up(c, _):
        before = jnp.maximum(c - 1, 0)
        z[...] = z[...] + dot(active[before], w2[pl.ds(pl.multiple_of(before * width, 128), width), :])
        inner = dot(hid_low[...], w1[c]) + upb[pl.ds(0, 1), pl.ds(pl.multiple_of(c * width, 128), width)]
        sq = inner * inner
        t = jnp.tanh(inner * (c0 + (0.044715 * c0) * sq))
        cdf = 0.5 + 0.5 * t
        active[c] = (inner * cdf).astype(BF)
        slope[c] = cdf + (inner * (1.0 - t * t)) * (0.5 * c0 + (1.5 * 0.044715 * c0) * sq)
        return 0

    active[0] = jnp.zeros((n, width), BF)
    z[...] = jnp.zeros(z.shape, FL)
    lax.fori_loop(0, parts, up, 0)
    z[...] = z[...] + dot(active[parts - 1], w2[pl.ds((parts - 1) * width, width), :])
    gvec[...] = jnp.zeros(gvec.shape, FL)
    loads[1].wait()

    def second_norm(r, i):
        unit, scale = normalize(hid[r, :] + (z[r, :] + vec[5:6]))
        out[r, :] = (unit * vec[6:7] + vec[7:8]).astype(BF)
        dy = cot[r, :].astype(FL)
        gvec[6:7] = gvec[6:7] + rows_sum(dy * unit)
        gvec[7:8] = gvec[7:8] + rows_sum(dy)
        d = normalize_back(dy * vec[6:7], unit, scale)
        hid[r, :] = d
        d_low = d.astype(BF)
        att_like[r, :] = d_low
        gvec[5:6] = gvec[5:6] + rows_sum(d_low.astype(FL))

    att_like = pay.at[:, 0:width]
    scale1 = d2[:, 0:1]
    row_loop(second_norm)
    z[...] = jnp.zeros(z.shape, FL)

    def down(c, _):
        ffn = pay[:, 0:width]
        far = pl.ds(pl.multiple_of(c * width, 128), width)
        d_inner = (dot_t(ffn, w2[far, :]) * slope[c]).astype(BF)
        gup[:, far] = jnp.broadcast_to(rows_sum(d_inner.astype(FL)), (8, width))
        dw2[far, :] = t_dot(active[c], ffn).astype(BF)
        dw1[c] = t_dot(hid_low[...], d_inner).astype(BF)
        z[...] = z[...] + dot_t(d_inner, w1[c])
        return 0

    lax.fori_loop(0, parts, down, 0)

    def store_sets(a_ref, b_ref):
        for p in range(NB):
            s = ids[0] ^ rel_a(p)
            pltpu.make_async_copy(dw2.at[rows(s * fb, 192)], a_ref.at[p, pl.ds(0, 192)], sems.at[3]).start()
            s = ids[0] ^ rel_b(p)
            for c in range(parts):
                pltpu.make_async_copy(
                    dw1.at[c, rows(s * rb, 48)], b_ref.at[p, pl.ds(48 * c, 48)], sems.at[3]
                ).start()

    @pl.when(ids[1] == 0)
    def _():
        store_sets(keep, send)

    @pl.when(ids[1] != 0)
    def _():
        store_sets(send, keep)

    def first_back(r, i):
        unit = unit1[r, :]
        d = hid[r, :] + z[r, :]
        gvec[3:4] = gvec[3:4] + rows_sum(d * unit)
        gvec[4:5] = gvec[4:5] + rows_sum(d)
        d = normalize_back(d * vec[3:4], unit, d2[r, 0:1])
        mixed[r, :] = d
        d_low = d.astype(BF)
        hid_low[r, :] = d_low
        gvec[2:3] = gvec[2:3] + rows_sum(d_low.astype(FL))

    row_loop(first_back)
    dwo[...] = t_dot(att[...], hid_low[...]).astype(BF)

    def store_wo(a_ref, b_ref):
        for p in range(NB):
            s = ids[0] ^ rel_a(p)
            pltpu.make_async_copy(dwo.at[rows(s * rb, 32)], a_ref.at[p, pl.ds(192, 32)], sems.at[3]).start()
            s = ids[0] ^ rel_b(p)
            pltpu.make_async_copy(dwo.at[rows(s * rb + 32, 16)], b_ref.at[p, pl.ds(192, 16)], sems.at[3]).start()
            pltpu.make_async_copy(dwo.at[rows(s * rb + 32, 16)], b_ref.at[p, pl.ds(208, 16)], sems.at[3]).start()

    @pl.when(ids[1] == 0)
    def _():
        store_wo(keep, send)

    @pl.when(ids[1] != 0)
    def _():
        store_wo(send, keep)

    z[...] = dot_t(hid_low[...], wo[...])
    heads = width // HD
    head_of = lax.broadcasted_iota(jnp.int32, (16, width), 1) // HD
    head_of = jnp.where(head_of < heads // 2, head_of, head_of - heads // 2 + 8)
    pick = (head_of == lax.broadcasted_iota(jnp.int32, (16, width), 0)).astype(FL).astype(BF)
    stats[0:8, :] = lse[0:8, :]
    stats[16:24, :] = lse[8:16, :]

    loads[2].wait()

    def last(r, i):
        d_low = z[r, :].astype(BF)
        pay[r, 0:width] = d_low
        prod = d_low.astype(FL) * exact[r, :]
        delta = jnp.zeros((16, rc), FL)
        for _ in range(3):
            piece = prod.astype(BF)
            delta = delta + dot_t(pick, piece)
            prod = prod - piece.astype(FL)
        stats[8:16, r] = delta[0:8]
        stats[24:32, r] = delta[8:16]

    row_loop(last)
    st = stats[...].T
    pieces = []
    for _ in range(3):
        piece = st.astype(BF).astype(FL)
        pieces.append(piece)
        st = st - piece
    pieces.append(jnp.zeros_like(st))
    pay_low[:, width:] = jnp.concatenate(pieces, 1)[: n // 2].astype(BF)
    pay_high[:, width:] = jnp.concatenate(pieces, 1)[n // 2 :].astype(BF)
    pay_low[:, 0:width] = pay[0 : n // 2, :]
    pay_high[:, 0:width] = pay[n // 2 :, :]
    wait_all(keep, sems.at[3])
    wait_all(send, sems.at[3])


def middle(ids, pool, att, exact, lse, cot, vec, upb, sets, set_rows):
    n, width = pool.shape
    ff = upb.shape[1]
    parts = ff // width
    whole = lambda i, *_: (0, 0)
    full = lambda x: pl.BlockSpec(x.shape, whole)
    shapes = [
        jax.ShapeDtypeStruct((n, width), BF),
        jax.ShapeDtypeStruct((n, width), BF),
        jax.ShapeDtypeStruct((n // 2, width + 128), BF),
        jax.ShapeDtypeStruct((n // 2, width + 128), BF),
        jax.ShapeDtypeStruct((32, n), FL),
        jax.ShapeDtypeStruct((n, width), FL),
        jax.ShapeDtypeStruct((8, width), FL),
        jax.ShapeDtypeStruct((8, ff), FL),
    ]
    big = jax.ShapeDtypeStruct((NB, set_rows, width), BF)
    return pl.pallas_call(
        middle_kernel,
        name="middle",
        cost_estimate=takes(36),
        grid_spec=pltpu.PrefetchScalarGridSpec(
            num_scalar_prefetch=1,
            grid=(1,),
            in_specs=[ANY, full(att), ANY, full(lse), ANY, full(vec), full(upb)]
            + [ANY] * 4,
            out_specs=[full(x) for x in shapes] + [ANY, ANY],
            scratch_shapes=[
                pltpu.VMEM((width, width), BF),
                pltpu.VMEM((parts, width, width), BF),
                pltpu.VMEM((ff, width), BF),
                pltpu.VMEM((parts, n, width), BF),
                pltpu.VMEM((parts, n, width), FL),
                pltpu.VMEM((n, width), FL),
                pltpu.VMEM((n, width), FL),
                pltpu.VMEM((n, width), BF),
                pltpu.VMEM((n, width), FL),
                pltpu.VMEM((n, 128), FL),
                pltpu.VMEM((parts, width, width), BF),
                pltpu.VMEM((ff, width), BF),
                pltpu.VMEM((width, width), BF),
                pltpu.VMEM(pool.shape, FL),
                pltpu.VMEM(exact.shape, FL),
                pltpu.VMEM(cot.shape, BF),
                pltpu.SemaphoreType.DMA((4,)),
                pltpu.SemaphoreType.DMA((3,)),
            ],
        ),
        out_shape=shapes + [big, big],
        compiler_params=params(),
    )(ids, pool, att, exact, lse, cot, vec, upb, *sets)


def weights_kernel(
    ids,
    pool_in,
    tok_in,
    dq_in,
    dk_in,
    dv_in,
    gvec,
    gup,
    sl,
    keep_low,
    keep_up,
    send_low,
    send_up,
    dwq,
    dwk,
    dwv,
    bias,
    tt,
    pool,
    tok,
    dq,
    dk,
    dv,
    sems,
    load_sems,
):
    loads = [(tok_in, tok), (pool_in, pool), (dq_in, dq), (dk_in, dk), (dv_in, dv)]
    loads = [pltpu.make_async_copy(a, b, load_sems.at[i]) for i, (a, b) in enumerate(loads)]
    for x in loads:
        x.start()
    keep = (keep_low, keep_up)
    send = (send_low, send_up)
    width = tok.shape[1]
    ff = gup.shape[1]
    rb = width // NB
    for x in loads[:3]:
        x.wait()
    tt[...] = tok[...].T
    dwq[...] = t_dot(pool[...].astype(BF), dq[...]).astype(BF)

    for x in loads[3:]:
        x.wait()

    def columns(c, _):
        cols = pl.ds(pl.multiple_of(c * 256, 256), 256)
        dwk[:, cols] = dot(tt[...], dk[:, cols]).astype(BF)
        dwv[:, cols] = dot(tt[...], dv[:, cols]).astype(BF)
        return 0

    lax.fori_loop(0, width // 256, columns, 0)

    def rows(r, size):
        return pl.ds(pl.multiple_of(r, 16), size)

    def go(src, dst):
        pltpu.make_async_copy(src, dst, sems.at[0]).start()

    def store_sets(a_ref, b_ref):
        for p in range(NB):
            s = ids[0] ^ rel_a(p)
            go(dwq.at[rows(s * rb, 48)], a_ref[p // 8].at[p % 8, pl.ds(0, 48)])
            go(dwk.at[rows(s * rb, 32)], a_ref[p // 8].at[p % 8, pl.ds(48, 32)])
            s = ids[0] ^ rel_b(p)
            go(dwk.at[rows(s * rb + 32, 16)], b_ref[p // 8].at[p % 8, pl.ds(0, 16)])
            go(dwv.at[rows(s * rb, 48)], b_ref[p // 8].at[p % 8, pl.ds(16, 48)])

    @pl.when(ids[1] == 0)
    def _():
        store_sets(keep, send)

    @pl.when(ids[1] != 0)
    def _():
        store_sets(send, keep)

    row = lax.broadcasted_iota(jnp.int32, (16, width), 0)
    g = jnp.concatenate([gvec[...], jnp.zeros((8, width), FL)], 0)
    g = jnp.where(row == 0, rows_sum(dq[...].astype(FL)), g)
    g = jnp.where(row == 1, rows_sum(dv[...].astype(FL)), g)
    block_of = div_rb(lax.broadcasted_iota(jnp.int32, (16, width), 1))
    parts = []
    for p in range(NB):
        parts.append(jnp.where(block_of == (ids[0] ^ rel_b(p)), g, 0.0).astype(BF))
    total = dot_t(jnp.concatenate(parts, 0), spread_matrix(128, width, rb))
    row = lax.broadcasted_iota(jnp.int32, (16, ff), 0)
    block_of = div_rb(lax.broadcasted_iota(jnp.int32, (16, ff), 1))
    block_of = jnp.where((row >= 8) & (row < 12), block_of - row + 8, -1)
    up = jnp.concatenate([gup[...], gup[...]], 0)
    parts = []
    for p in range(NB):
        parts.append(jnp.where(block_of == 4 * (ids[0] ^ rel_b(p)), up, 0.0).astype(BF))
    total = total + dot_t(jnp.concatenate(parts, 0), spread_matrix(128, ff, rb))
    line = jnp.zeros((1, 128), FL)
    lane = lax.broadcasted_iota(jnp.int32, (1, 128), 1)
    for j in range(sl.shape[0] // 8):
        for i in range(2):
            value = jnp.sum(sl[8 * j : 8 * j + 1, QB * i : QB * i + QB], 1, keepdims=True)
            line = jnp.where(lane == 2 * j + i, -value, line)
    row = lax.broadcasted_iota(jnp.int32, (16 * NB, 128), 0)
    total = jnp.where((row & 15) == 12, line, total)
    bias[...] = jnp.zeros(bias.shape, BF)
    bias[:, 0:128] = total.astype(BF)

    def store_bias(b_ref):
        for p in range(NB):
            go(bias.at[pl.ds(16 * p, 16)], b_ref[p // 8].at[p % 8, pl.ds(64, 16)])

    @pl.when(ids[1] == 0)
    def _():
        store_bias(send)

    @pl.when(ids[1] != 0)
    def _():
        store_bias(keep)

    for x in keep + send:
        wait_all(x, sems.at[0])


def weight_grads(ids, pool, tok, dq, dk, dv, gvec, gup, sl, set_rows):
    width = tok.shape[1]
    full = lambda x: pl.BlockSpec(x.shape, lambda i, *_: (0, 0))
    big = jax.ShapeDtypeStruct((NB // 2, set_rows, width), BF)
    square = pltpu.VMEM((width, width), BF)
    return pl.pallas_call(
        weights_kernel,
        name="weight_grads",
        cost_estimate=takes(9),
        grid_spec=pltpu.PrefetchScalarGridSpec(
            num_scalar_prefetch=1,
            grid=(1,),
            in_specs=[ANY] * 5 + [full(x) for x in (gvec, gup, sl)],
            out_specs=[ANY] * 4,
            scratch_shapes=[
                square,
                square,
                square,
                pltpu.VMEM((16 * NB, width), BF),
                pltpu.VMEM((width, tok.shape[0]), BF),
            ]
            + [pltpu.VMEM(x.shape, x.dtype) for x in (pool, tok, dq, dk, dv)]
            + [
                pltpu.SemaphoreType.DMA((1,)),
                pltpu.SemaphoreType.DMA((5,)),
            ],
        ),
        out_shape=[big] * 4,
        compiler_params=params(),
    )(ids, pool, tok, dq, dk, dv, gvec, gup, sl)


def tokens_kernel(mixed, dq, dk, dv, wq, wk, wv, out, acc):
    half = mixed.shape[0]
    up = 0.5 * (mixed[...] + dot_t(dq[...], wq[...]))
    down = dot_t(dk[...], wk[...]) + dot_t(dv[...], wv[...])
    for j in range(mixed.shape[1] // 128):
        cols = slice(128 * j, 128 * j + 128)
        for i in range(2):
            acc[j, pl.ds(i, half, stride=2)] = up[:, cols]
        out[:, cols] = acc[j] + down[:, cols]


def token_grads(mixed, dq, dk, dv, wq, wk, wv):
    rows, width = dk.shape
    step = 512
    half = pl.BlockSpec((step // 2, width), lambda i: (i, 0))
    block = pl.BlockSpec((step, width), lambda i: (i, 0))
    whole = pl.BlockSpec((width, width), lambda i: (0, 0))
    return pl.pallas_call(
        tokens_kernel,
        name="token_grads",
        cost_estimate=takes(8),
        grid=(rows // step,),
        in_specs=[half, half, block, block, whole, whole, whole],
        out_specs=block,
        out_shape=jax.ShapeDtypeStruct((rows, width), FL),
        scratch_shapes=[pltpu.VMEM((width // 128, step, 128), FL)],
        compiler_params=params(),
    )(mixed, dq, dk, dv, wq, wk, wv)


def blocks_of(x):
    return x.reshape(NB, x.shape[0] // NB, x.shape[1])


def column_parts(x, width):
    return jnp.concatenate([x[..., width * c : width * c + width] for c in range(x.shape[-1] // width)], -2)


def bias_block(small, up, width):
    rb = small[0].shape[-1]
    rows = jnp.stack(list(small) + [up[..., rb * c : rb * c + rb] for c in range(4)], -2)
    pad = [(0, 0)] * (rows.ndim - 2) + [(0, 4), (0, width - rb)]
    return jnp.pad(rows, pad)


def pack(wq, wk, wv, wo, w1, w2, bias, width):
    a1 = jnp.concatenate([wq, wk[..., :32, :]], -2)
    b1 = jnp.concatenate([wk[..., 32:, :], wv, bias], -2)
    a2 = jnp.concatenate([w2, wo[..., :32, :]], -2)
    b2 = jnp.concatenate([column_parts(w1, width), wo[..., 32:, :], wo[..., 32:, :]], -2)
    return a1, b1, a2, b2


def unpack(a1, b1, a2, b2, width):
    wq = a1[..., :48, :]
    wk = jnp.concatenate([a1[..., 48:, :], b1[..., :16, :]], -2)
    wv = b1[..., 16:64, :]
    bias = b1[..., 64:, :]
    wo = jnp.concatenate([a2[..., 192:, :], b2[..., 192:208, :]], -2)
    w2 = a2[..., :192, :]
    parts = 4
    w1 = jnp.concatenate([b2[..., 48 * c : 48 * c + 48, :] for c in range(parts)], -1)
    return wq, wk, wv, wo, w1, w2, bias


def pack_kernel(ids, wq, wk, wv, wo, w1, w2, b_up, *refs):
    vectors, (out, bias) = refs[:8], refs[8:]
    first = out.at[:, 0:80]
    second = out.at[:, 80:304]
    rb, width = wq.shape

    @pl.when(ids[1] == 0)
    def _():
        first[0, 0:48] = wq[...].astype(BF)
        first[0, 48:80] = wk[0:32].astype(BF)
        second[0, 0:192] = w2[...].astype(BF)
        second[0, 192:224] = wo[0:32].astype(BF)

    @pl.when(ids[1] != 0)
    def _():
        bias[...] = jnp.zeros(bias.shape, FL)
        for i, x in enumerate(vectors):
            bias[i : i + 1, 0:rb] = x[...]
        for c in range(4):
            bias[8 + c : 9 + c, 0:rb] = b_up[:, rb * c : rb * c + rb]
        first[0, 0:16] = wk[32:48].astype(BF)
        first[0, 16:64] = wv[...].astype(BF)
        first[0, 64:80] = bias[...].astype(BF)
        for c in range(4):
            second[0, 48 * c : 48 * c + 48] = w1[:, width * c : width * c + width].astype(BF)
        second[0, 192:208] = wo[32:48].astype(BF)
        second[0, 208:224] = wo[32:48].astype(BF)


def pack_own(ids, masters, b_up, vectors):
    width = masters[0].shape[1]
    args = list(masters) + [b_up[None]] + [x[None] for x in vectors]
    full = lambda x: pl.BlockSpec(x.shape, lambda i, *_: (0,) * len(x.shape))
    shape = jax.ShapeDtypeStruct((1, 304, width), BF)
    return pl.pallas_call(
        pack_kernel,
        name="pack",
        cost_estimate=takes(3),
        grid_spec=pltpu.PrefetchScalarGridSpec(
            num_scalar_prefetch=1,
            grid=(1,),
            in_specs=[full(x) for x in args],
            out_specs=full(shape),
            scratch_shapes=[pltpu.VMEM((16, width), FL)],
        ),
        out_shape=shape,
        compiler_params=params(),
    )(ids, *args)


def unpack_kernel(ids, low1, got1, olow1, ogot1, wq, wk, wv, *vectors):
    rb = wq.shape[0]
    mine = low1[...] + got1[...].astype(FL)
    other = olow1[...] + ogot1[...].astype(FL)

    def store(a, b):
        wq[...] = a[0:48]
        wk[0:32] = a[48:80]
        wk[32:48] = b[0:16]
        wv[...] = b[16:64]
        for i in range(8):
            vectors[i][...] = b[64 + i : 65 + i, 0:rb]
        for c in range(4):
            vectors[8][:, rb * c : rb * c + rb] = b[72 + c : 73 + c, 0:rb]
        vectors[9][...] = b[76:77, 0 : vectors[9].shape[1]]

    @pl.when(ids[1] == 0)
    def _():
        store(mine, other)

    @pl.when(ids[1] != 0)
    def _():
        store(other, mine)


def unpack_wide_kernel(ids, mine, other, wo, w1, w2):
    width = wo.shape[1]

    def store(a, b):
        for c in range(4):
            w1[:, width * c : width * c + width] = b[48 * c : 48 * c + 48]
        w2[...] = a[0:192]
        wo[0:32] = a[192:224]
        wo[32:48] = b[192:208]

    @pl.when(ids[1] == 0)
    def _():
        store(mine, other)

    @pl.when(ids[1] != 0)
    def _():
        store(other, mine)


def unpack_call(kernel, name, ids, args, dims):
    shapes = [jax.ShapeDtypeStruct(d, FL) for d in dims]
    full = lambda x: pl.BlockSpec(x.shape, lambda i, *_: (0, 0))
    return pl.pallas_call(
        kernel,
        name=name,
        cost_estimate=takes(2),
        grid_spec=pltpu.PrefetchScalarGridSpec(
            num_scalar_prefetch=1,
            grid=(1,),
            in_specs=[full(x) for x in args],
            out_specs=[full(x) for x in shapes],
        ),
        out_shape=shapes,
        compiler_params=params(),
    )(ids, *args)


def after(x, *done):
    return lax.optimization_barrier((x,) + done)[0]


def local(
    tokens,
    cotangent,
    lengths,
    w_query,
    b_query,
    w_key,
    w_value,
    b_value,
    w_output,
    b_output,
    gain_attn,
    shift_attn,
    w_up,
    b_up,
    w_down,
    b_down,
    gain_ffn,
    shift_ffn,
    distance_slope,
):
    rows_here, width = tokens.shape
    ff = w_up.shape[1]
    own = rows_here // 2
    halo = rows_here // 2
    seq = lax.axis_size("seq")
    devices = seq * lax.axis_size("dp")
    direct = seq == NB
    order = ("dp", "seq")
    up_pairs = [(i, i + 1) for i in range(devices - 1)]
    down_pairs = [(i + 1, i) for i in range(devices - 1)]

    masters = (w_query, w_key, w_value, w_output, w_up, w_down)
    vectors = (b_query, b_value, b_output, gain_attn, shift_attn, b_down, gain_ffn, shift_ffn)
    if direct:
        core = lax.axis_index("dp")
        ids = jnp.stack([lax.axis_index("seq"), core]).astype(jnp.int32)
        x = pack_own(ids, masters, b_up, vectors)
        y = x[:, 80:]
        x = x[:, :80]
        x = jnp.concatenate([x, exchange(x, 8, 4)], 0)
        x1, low_a = lax.optimization_barrier(
            (exchange(x, 4, 8), lax.ppermute(tokens[rows_here - halo : rows_here - halo // 2], order, up_pairs))
        )
        x = jnp.concatenate([x, x1], 0)
        y, part = lax.optimization_barrier((y, tokens[rows_here - halo // 2 :], x1))[:2]
        x1, y1, low_b = lax.optimization_barrier(
            (exchange(x, 2, 1), exchange(y, 8, 4), lax.ppermute(part, order, up_pairs))
        )
        low1 = jnp.concatenate([x, x1], 0)
        y = jnp.concatenate([y, y1], 0)
        high1, olow1, y1, high_a = lax.optimization_barrier(
            (
                exchange(low1, 1, 2),
                swap_core(low1),
                exchange(y, 4, 8),
                lax.ppermute(after(tokens[: halo // 2], x1), order, down_pairs),
            )
        )
        y = jnp.concatenate([y, y1], 0)
        sets1 = (low1, high1, olow1, swap_core(high1))
        y1 = exchange(y, 2, 1)
        high_b = lax.ppermute(after(tokens[halo // 2 : halo], high1), order, down_pairs)
    else:
        ids = jnp.zeros((2,), jnp.int32)
        gather = lambda x: lax.all_gather(x.astype(BF), "seq", axis=0, tiled=True)
        full = [blocks_of(gather(x)) for x in masters]
        small = [gather(x).reshape(NB, -1) for x in vectors]
        bias = bias_block(small, gather(b_up).reshape(NB, -1), width)
        a1, b1, a2, b2 = pack(*full, bias, width)
        at_a = jnp.array([rel_a(p) for p in range(NB)])
        at_b = jnp.array([rel_b(p) for p in range(NB)])
        sets1 = (a1[at_a[:8]], a1[at_a[8:]], b1[at_b[:8]], b1[at_b[8:]])
        sets2 = (a2[at_a[:8]], a2[at_a[8:]], b2[at_b[:8]], b2[at_b[8:]])
        low_a = lax.ppermute(tokens[rows_here - halo : rows_here - halo // 2], order, up_pairs)
        low_b = lax.ppermute(tokens[rows_here - halo // 2 :], order, up_pairs)
        high_a = lax.ppermute(tokens[: halo // 2], order, down_pairs)
        high_b = lax.ppermute(tokens[halo // 2 : halo], order, down_pairs)

    first_row = lax.axis_index(order) * rows_here
    total = devices * rows_here
    starts = 2 * (jnp.cumsum(lengths) - lengths)
    place = first_row - halo + 2 * jnp.arange(2 * own, dtype=jnp.int32)
    before = starts[None, :] <= place[:, None]
    begin = jnp.max(jnp.where(before, starts[None, :], 0), 1)
    end = jnp.min(jnp.where(before, total, starts[None, :]), 1)
    inside = (place >= 0) & (place < total)
    shift = first_row - halo
    begin = jnp.where(inside, begin - shift, 0)
    end = jnp.where(inside, end - shift, 0)
    bounds = jnp.pad(jnp.stack([begin, end], 0).astype(FL), ((0, 6), (0, 0)))
    blocks = 2 * own // QB
    chunks = (rows_here + 2 * halo) // KC
    low_chunk = jnp.min(jnp.where(inside, begin, 4 * total).reshape(blocks, QB), 1) // KC
    high_chunk = (jnp.max(end.reshape(blocks, QB), 1) + KC - 1) // KC
    index = jnp.arange(blocks)
    away = (index < blocks // 4) | (index >= blocks - blocks // 4)
    low_chunk = jnp.clip(low_chunk, jnp.where(away, chunks // 4, 0), chunks)
    high_chunk = jnp.clip(high_chunk, 0, jnp.where(away, chunks - chunks // 4, chunks))
    spans = jnp.concatenate([low_chunk, high_chunk]).astype(jnp.int32)

    slopes = distance_slope
    q, k, v, kt, vt, pool, wq, wk, wv, vec, upb = qkv(ids, tokens, sets1, ff)
    if direct:
        k, high_b = lax.optimization_barrier((k, high_b))
    qh, k, v, kt, vt = halo_qkv(low_a, low_b, high_a, high_b, wq, wk, wv, vec, k, v, kt, vt)
    if direct:
        y1, qh = lax.optimization_barrier((y1, qh))
        low2 = jnp.concatenate([y, y1], 0)
        bounds = after(bounds, low2)
    att, exact, lse = attend_forward(spans, slopes, q, k, vt, bounds)
    if direct:
        high2, lse = lax.optimization_barrier((exchange(low2, 1, 2), lse))
        sets2 = (low2, high2, swap_core(low2), swap_core(high2))
    out, pay, pay_low, pay_high, stats, mixed, gvec, gup, keep2, send2 = middle(
        ids, pool, att, exact, lse, cotangent, vec, upb, sets2, 224
    )
    low_pay = lax.ppermute(pay_high, order, up_pairs)
    high_pay = lax.ppermute(pay_low, order, down_pairs)
    if direct:
        got = swap_core(send2)
        up = add(keep2[8:], got[8:]).astype(BF)
        bounds = after(bounds, up)
    dq, dk, dv, sl = attend_own(spans, slopes, q, k, v, kt, pay, stats, bounds)
    if direct:
        dq, low_pay, high_pay = lax.optimization_barrier((dq, low_pay, high_pay))
    dk, dv = attend_halo(spans, slopes, qh, k, v, low_pay, high_pay, bounds, dk, dv)
    if direct:
        got1, dk = lax.optimization_barrier((exchange(up, 1, 2), dk))
        up = add(keep2[4:8], got[4:8], got1[4:]).astype(BF)
        sl = after(sl, up)
    keep1, keep1_up, send1, send1_up = weight_grads(ids, pool, tokens, dq, dk, dv, gvec, gup, sl, 80)
    if direct:
        gots = swap_core(send1)
        part, got2 = lax.optimization_barrier((add(keep1_up, swap_core(send1_up)).astype(BF), exchange(up, 2, 1)))
        low = add(keep2[:4], got[:4], got1[:4])
        up = (low[2:] + got2[2:].astype(FL)).astype(BF)
        low = low[:2] + got2[:2].astype(FL)
        mixed = after(mixed, part, up)
    grad_tokens = token_grads(mixed, dq, dk, dv, wq, wk, wv)

    if direct:
        got3, one, grad_tokens = lax.optimization_barrier((exchange(up, 4, 8), exchange(part, 1, 2), grad_tokens))
        part = add(keep1[4:8], gots[4:8], one[4:]).astype(BF)
        up = (low[1:] + got3[1:].astype(FL)).astype(BF)
        low = low[:1] + got3[:1].astype(FL)
        got4, two = lax.optimization_barrier((exchange(up, 8, 4), exchange(part, 2, 1)))
        mine = (low + got4.astype(FL))[0]
        rest = add(keep1[:4], gots[:4], one[:4])
        part = (rest[2:] + two[2:].astype(FL)).astype(BF)
        rest = rest[:2] + two[:2].astype(FL)
        three, other = lax.optimization_barrier((exchange(part, 4, 8), swap_core(mine)))
        second = (mine, other)
        part = (rest[1:] + three[1:].astype(FL)).astype(BF)
        rest = rest[:1] + three[:1].astype(FL)
        over = [(s, seq + (s ^ 8)) for s in range(seq)] + [(seq + s, s ^ 4) for s in range(seq)]
        first = (rest[0], exchange(part, 8, 4)[0], swap_core(rest)[0], lax.ppermute(part, order, over)[0])
        rb = width // NB
        go, g1, g2 = unpack_call(unpack_wide_kernel, "unpack_wide", ids, second, [(rb, width), (rb, ff), (ff // NB, width)])
        dims = [(rb, width)] * 3 + [(1, rb)] * 8 + [(1, ff // NB), (1, distance_slope.shape[0])]
        gq, gk, gv, *small = unpack_call(unpack_kernel, "unpack", ids, first, dims)
        g_up, g_slope = small[8][0], small[9][0]
        small = [x[0] for x in small[:8]]
    else:
        inv_a = [0] * NB
        inv_b = [0] * NB
        for p in range(NB):
            inv_a[rel_a(p)] = p
            inv_b[rel_b(p)] = p
        inv_a = jnp.array(inv_a)
        inv_b = jnp.array(inv_b)
        joined = [jnp.concatenate(x, 0) for x in ((keep1, keep1_up), (send1, send1_up))]
        gq, gk, gv, go, g1, g2, gb = unpack(joined[0][inv_a], joined[1][inv_b], keep2[inv_a], send2[inv_b], width)
        rb = width // NB

        def share(x):
            x = lax.psum(x.astype(FL), "dp")
            return lax.psum_scatter(x, "seq", scatter_dimension=0, tiled=True)

        gq, gk, gv, go, g1, g2 = [share(x.reshape(-1, x.shape[-1])) for x in (gq, gk, gv, go, g1, g2)]
        small = [share(gb[:, i, :rb].reshape(-1)) for i in range(8)]
        g_up = share(gb[:, 8:12, :rb].reshape(-1))
        g_slope = lax.psum(gb[0, 12, : distance_slope.shape[0]].astype(FL), order)
    return (
        out,
        grad_tokens,
        gq,
        small[0],
        gk,
        gv,
        small[1],
        go,
        small[2],
        small[3],
        small[4],
        g1,
        g_up,
        g2,
        small[5],
        small[6],
        small[7],
        g_slope,
    )


def solution(mesh):
    tall = P(("dp", "seq"), None)
    mat = P("seq", None)
    vec = P("seq")
    return jax.shard_map(
        local,
        mesh=mesh,
        in_specs=(tall, tall, P(), mat, vec, mat, mat, vec, mat, vec, vec, vec, mat, vec, mat, vec, vec, vec, P()),
        out_specs=(tall, tall, mat, vec, mat, mat, vec, mat, vec, vec, vec, mat, vec, mat, vec, vec, vec, P()),
        check_vma=False,
    )
```

```python
import functools

import jax
import jax.numpy as jnp
from jax import lax
from jax.experimental import pallas as pl
from jax.experimental.pallas import tpu as pltpu
from jax.sharding import PartitionSpec as P

HD = 64
NB = 16
QB = 128
KC = 256
EPS = 1e-05
FAR = 1e12
BF = jnp.bfloat16
FL = jnp.float32


def rel_a(p):
    return (p & 1) * 8 + ((p >> 1) & 1) * 4 + ((p >> 2) & 1) * 2 + ((p >> 3) & 1)


def rel_b(p):
    return (p & 1) * 4 + ((p >> 1) & 1) * 8 + ((p >> 2) & 1) + ((p >> 3) & 1) * 2


def dot(a, b):
    return jnp.dot(a, b, preferred_element_type=FL)


def dot_t(a, b):
    return lax.dot_general(a, b, (((1,), (1,)), ((), ())), preferred_element_type=FL)


def t_dot(a, b):
    return lax.dot_general(a, b, (((0,), (0,)), ((), ())), preferred_element_type=FL)


def exchange(x, stride_a, stride_b):
    n = lax.axis_size("seq")
    pairs = [(s, s ^ stride_a) for s in range(n)] + [(n + s, n + (s ^ stride_b)) for s in range(n)]
    return lax.ppermute(x, ("dp", "seq"), pairs)


def swap_core(x):
    return lax.ppermute(x, "dp", [(0, 1), (1, 0)])


def add(*xs):
    total = xs[0].astype(FL)
    for x in xs[1:]:
        total = total + x.astype(FL)
    return total


def params(**kw):
    return pltpu.CompilerParams(vmem_limit_bytes=58 * 1024 * 1024, **kw)


def takes(us):
    return pl.CostEstimate(flops=us * 1150 * 10**6, transcendentals=0, bytes_accessed=us * 3600 * 10**3)


ANY = pl.BlockSpec(memory_space=pl.ANY)


def load_sets(ids, low, high, olow, ohigh, copies_a, copies_b):
    def start(a_refs, b_refs):
        for p in range(NB):
            copies_a(a_refs[p // 8].at[p % 8], ids[0] ^ rel_a(p), p)
            copies_b(b_refs[p // 8].at[p % 8], ids[0] ^ rel_b(p), p)

    @pl.when(ids[1] == 0)
    def _():
        start((low, high), (olow, ohigh))

    @pl.when(ids[1] != 0)
    def _():
        start((olow, ohigh), (low, high))


def wait_all(ref, sem):
    pltpu.make_async_copy(ref, ref, sem).wait()


def spread_matrix(rows, cols, rb):
    lanes = lax.broadcasted_iota(jnp.int32, (rows, cols), 1)
    return (lax.broadcasted_iota(jnp.int32, (rows, cols), 0) == lanes - rb * div_rb(lanes)).astype(FL).astype(BF)


def div_rb(x):
    return (x * 21846) >> 20


def qkv_kernel(
    ids, tok, low, high, olow, ohigh, q_out, k_out, v_out, kt_out, vt_out, pool_out, wq, wk, wv, vec_out, up_out, bias, x32, sems
):
    width = tok.shape[1]
    rb = width // NB

    @pl.when(pl.program_id(0) == 0)
    def _():
        def rows(r, n):
            return pl.ds(pl.multiple_of(r, 16), n)

        def copies_a(block, s, p):
            pltpu.make_async_copy(block.at[pl.ds(0, 48)], wq.at[rows(s * rb, 48)], sems.at[0]).start()
            pltpu.make_async_copy(block.at[pl.ds(48, 32)], wk.at[rows(s * rb, 32)], sems.at[1]).start()

        def copies_b(block, s, p):
            pltpu.make_async_copy(block.at[pl.ds(0, 16)], wk.at[rows(s * rb + 32, 16)], sems.at[1]).start()
            pltpu.make_async_copy(block.at[pl.ds(16, 48)], wv.at[rows(s * rb, 48)], sems.at[2]).start()
            pltpu.make_async_copy(block.at[pl.ds(64, 16)], bias.at[pl.ds(16 * p, 16)], sems.at[3]).start()

        load_sets(ids, low, high, olow, ohigh, copies_a, copies_b)
        wait_all(wq, sems.at[0])
        wait_all(wk, sems.at[1])
        wait_all(wv, sems.at[2])
        wait_all(bias, sems.at[3])
        parts = bias[:, 0:128]
        wide = dot(parts, spread_matrix(128, width, rb))
        block_of = div_rb(lax.broadcasted_iota(jnp.int32, (16, width), 1))
        total = jnp.zeros((16, width), FL)
        for p in range(NB):
            total = total + jnp.where(block_of == (ids[0] ^ rel_b(p)), wide[16 * p : 16 * p + 16], 0.0)
        vec_out[...] = total
        ff = up_out.shape[1]
        wide = dot(parts, spread_matrix(128, ff, rb))
        block_of = div_rb(lax.broadcasted_iota(jnp.int32, (16, ff), 1))
        row = lax.broadcasted_iota(jnp.int32, (16, ff), 0)
        block_of = jnp.where((row >= 8) & (row < 12), block_of - row + 8, -1)
        total = jnp.zeros((16, ff), FL)
        for p in range(NB):
            total = total + jnp.where(block_of == 4 * (ids[0] ^ rel_b(p)), wide[16 * p : 16 * p + 16], 0.0)
        up_out[...] = jnp.broadcast_to(jnp.sum(total, 0, keepdims=True), up_out.shape)

    pool_out[...] = project(tok[...], wq, wk, wv, vec_out, q_out, k_out, v_out, kt_out, vt_out, x32)


def project(x, wq, wk, wv, vec, q_out, k_out, v_out, kt_out, vt_out, x32):
    width = x.shape[1]
    half = x.shape[0] // 2
    k_out[...] = dot(x, wk[...]).astype(BF)
    v_out[...] = (dot(x, wv[...]) + vec[1:2]).astype(BF)
    for c in range(x.shape[0] // KC):
        kt_out[c] = k_out[KC * c : KC * c + KC].T
        vt_out[c] = v_out[KC * c : KC * c + KC].T
    pooled = []
    for j in range(width // 128):
        x32[j] = x[:, 128 * j : 128 * j + 128].astype(FL)
        pooled.append((x32[j, pl.ds(0, half, stride=2)] + x32[j, pl.ds(1, half, stride=2)]) * 0.5)
    pooled = jnp.concatenate(pooled, 1)
    q = (dot(pooled.astype(BF), wq[...]) + vec[0:1]).astype(BF)
    q_out[...] = (q.astype(FL) * HD**-0.5).astype(BF)
    return pooled


def qkv(ids, tokens, sets, ff):
    rows, width = tokens.shape
    step = 512
    whole = lambda i, *_: (0, 0)
    square = jax.ShapeDtypeStruct((width, width), BF)
    thin = pl.BlockSpec((step // 2, width), lambda i, *_: (i, 0))
    block = pl.BlockSpec((step, width), lambda i, *_: (i, 0))
    inner = pl.BlockSpec((step, width), lambda i, *_: (i + 1, 0))
    tall = pl.BlockSpec((step // KC, width, KC), lambda i, *_: (i + 1, 0, 0))
    return pl.pallas_call(
        qkv_kernel,
        name="qkv",
        cost_estimate=takes(9),
        grid_spec=pltpu.PrefetchScalarGridSpec(
            num_scalar_prefetch=1,
            grid=(rows // step,),
            in_specs=[block, ANY, ANY, ANY, ANY],
            out_specs=[thin, inner, inner, tall, tall, thin]
            + [pl.BlockSpec((width, width), whole)] * 3
            + [pl.BlockSpec((16, width), whole), pl.BlockSpec((8, ff), whole)],
            scratch_shapes=[
                pltpu.VMEM((16 * NB, width), BF),
                pltpu.VMEM((width // 128, step, 128), FL),
                pltpu.SemaphoreType.DMA((4,)),
            ],
        ),
        out_shape=[
            jax.ShapeDtypeStruct((rows // 2, width), BF),
            jax.ShapeDtypeStruct((2 * rows, width), BF),
            jax.ShapeDtypeStruct((2 * rows, width), BF),
            jax.ShapeDtypeStruct((2 * rows // KC, width, KC), BF),
            jax.ShapeDtypeStruct((2 * rows // KC, width, KC), BF),
            jax.ShapeDtypeStruct((rows // 2, width), FL),
            square,
            square,
            square,
            jax.ShapeDtypeStruct((16, width), FL),
            jax.ShapeDtypeStruct((8, ff), FL),
        ],
        compiler_params=params(),
    )(ids, tokens, *sets)


def halo_qkv_kernel(
    low_a, low_b, high_a, high_b, wq, wk, wv, vec, k, v, kt, vt, q_out, k_out, v_out, kt_out, vt_out, x32
):
    low = pl.program_id(0) == 0
    parts = [jnp.where(low, a[...], b[...]) for a, b in ((low_a, high_a), (low_b, high_b))]
    project(jnp.concatenate(parts, 0), wq, wk, wv, vec, q_out, k_out, v_out, kt_out, vt_out, x32)


def halo_qkv(low_a, low_b, high_a, high_b, wq, wk, wv, vec, k, v, kt, vt):
    rows, width = low_a.shape
    rows = 2 * rows
    full = lambda x: pl.BlockSpec(x.shape, lambda i: (0,) * len(x.shape))
    args = (low_a, low_b, high_a, high_b, wq, wk, wv, vec)
    edge = pl.BlockSpec((rows, width), lambda i: (3 * i, 0))
    tall = pl.BlockSpec((rows // KC, width, KC), lambda i: (3 * i, 0, 0))
    return pl.pallas_call(
        halo_qkv_kernel,
        name="halo_qkv",
        cost_estimate=takes(7),
        grid=(2,),
        in_specs=[full(x) for x in args] + [ANY] * 4,
        out_specs=[pl.BlockSpec((None, rows // 2, width), lambda i: (i, 0, 0)), edge, edge, tall, tall],
        out_shape=[jax.ShapeDtypeStruct((2, rows // 2, width), BF)]
        + [jax.ShapeDtypeStruct(x.shape, x.dtype) for x in (k, v, kt, vt)],
        input_output_aliases={8: 1, 9: 2, 10: 3, 11: 4},
        scratch_shapes=[pltpu.VMEM((width // 128, rows, 128), FL)],
        compiler_params=params(),
    )(*args, k, v, kt, vt)


def two_heads(x):
    lane = lax.broadcasted_iota(jnp.int32, x.shape, 1)
    zero = jnp.zeros_like(x)
    return jnp.concatenate([jnp.where(lane < HD, x, zero), jnp.where(lane < HD, zero, x)], 0)


def one_block(x):
    r = x.shape[1] // 2
    line = lax.broadcasted_iota(jnp.int32, (128, r), 0)
    return jnp.where(line < HD, x[:, :r], x[:, r:]).T


def distances(bounds, row, c):
    low = bounds[0:1, pl.ds(row, QB)]
    high = bounds[1:2, pl.ds(row, QB)]
    query = (2 * (row + lax.broadcasted_iota(jnp.int32, (KC, QB), 1))).astype(FL) + 0.5
    key = (c * KC + lax.broadcasted_iota(jnp.int32, (KC, QB), 0)).astype(FL)
    far = jnp.where((key >= low) & (key < high), jnp.abs(query - key), FAR)
    return jnp.concatenate([far, far], 1)


def fold(x, f):
    n = x.shape[0] // 8
    parts = [x[8 * i : 8 * i + 8] for i in range(n)]
    while len(parts) > 1:
        parts = [f(parts[2 * i], parts[2 * i + 1]) for i in range(len(parts) // 2)]
    return parts[0]


def slope_line(slopes, head):
    lane = lax.broadcasted_iota(jnp.int32, (1, 2 * QB), 1)
    return jnp.where(lane < QB, slopes[head], slopes[head + 1])


def forward_kernel(
    spans, slopes, q, k, vt, bounds, o_out, exact_out, lse_out, s_scr, q2, top, total, acc, rest
):
    pairs = q.shape[1] // 128
    head0 = pl.program_id(0) * 2 * pairs
    q_first = q.shape[0] // 2
    slope = [slope_line(slopes, head0 + 2 * j) for j in range(pairs)]

    def query_block(b, _):
        row = pl.multiple_of(q_first + b * QB, QB)
        out_rows = pl.ds(pl.multiple_of(b * QB, QB), QB)
        block = row // QB
        c0 = spans[block]
        c1 = spans[spans.shape[0] // 2 + block]
        for j in range(pairs):
            q2[j] = two_heads(q[out_rows, 128 * j : 128 * j + 128])
        top[...] = jnp.full(top.shape, -3e38, FL)
        total[...] = jnp.zeros(total.shape, FL)
        acc[...] = jnp.zeros(acc.shape, FL)
        rest[...] = jnp.zeros(rest.shape, FL)

        def score(c, _):
            far = distances(bounds, row, c)
            keys = pl.ds(pl.multiple_of(c * KC, KC), KC)
            for j in range(pairs):
                s = dot_t(k[keys, 128 * j : 128 * j + 128], q2[j]) - slope[j] * far
                s_scr[c - c0, j] = s
                top[j] = jnp.maximum(top[j], fold(s, jnp.maximum))
            return 0

        lax.fori_loop(c0, c1, score, 0)
        peak = [jnp.max(top[j], 0, keepdims=True) for j in range(pairs)]

        def exponent(c, _):
            for j in range(pairs):
                e = jnp.exp(s_scr[c - c0, j] - peak[j])
                s_scr[c - c0, j] = e
                total[j] = total[j] + fold(e, jnp.add)
            return 0

        lax.fori_loop(c0, c1, exponent, 0)
        inverse = []
        for j in range(pairs):
            l = jnp.sum(total[j], 0, keepdims=True)
            t = peak[j] + jnp.log(l)
            inverse.append(1.0 / l)
            lse_out[2 * j : 2 * j + 1, out_rows] = t[:, :QB]
            lse_out[2 * j + 1 : 2 * j + 2, out_rows] = t[:, QB:]

        def attend(c, _):
            for j in range(pairs):
                p = s_scr[c - c0, j] * inverse[j]
                high = p.astype(BF)
                low = (p - high.astype(FL)).astype(BF)
                values = vt[c, 128 * j : 128 * j + 128]
                acc[j] = acc[j] + dot(values, high)
                rest[j] = rest[j] + dot(values, low)
            return 0

        lax.fori_loop(c0, c1, attend, 0)
        for j in range(pairs):
            cols = slice(128 * j, 128 * j + 128)
            o_out[out_rows, cols] = one_block(acc[j]).astype(BF)
            exact_out[out_rows, cols] = one_block(acc[j] + rest[j])
        return 0

    lse_out[...] = jnp.zeros(lse_out.shape, FL)
    lax.fori_loop(0, o_out.shape[0] // QB, query_block, 0)


def attend_forward(spans, slopes, q, k, vt, bounds):
    own, width = q.shape
    wide = width // 2
    pairs = wide // 128
    keys = k.shape[0]
    chunks = keys // KC
    col = lambda i, *_: (0, i)
    return pl.pallas_call(
        forward_kernel,
        name="attend_forward",
        cost_estimate=takes(30),
        grid_spec=pltpu.PrefetchScalarGridSpec(
            num_scalar_prefetch=2,
            grid=(2,),
            in_specs=[
                pl.BlockSpec((own, wide), col),
                pl.BlockSpec((keys, wide), col),
                pl.BlockSpec((chunks, wide, KC), lambda i, *_: (0, i, 0)),
                pl.BlockSpec(bounds.shape, lambda i, *_: (0, 0)),
            ],
            out_specs=[
                pl.BlockSpec((own, wide), col),
                pl.BlockSpec((own, wide), col),
                pl.BlockSpec((8, own), lambda i, *_: (i, 0)),
            ],
            scratch_shapes=[
                pltpu.VMEM((chunks, pairs, KC, 2 * QB), FL),
                pltpu.VMEM((pairs, 2 * QB, 128), BF),
                pltpu.VMEM((pairs, 8, 2 * QB), FL),
                pltpu.VMEM((pairs, 8, 2 * QB), FL),
                pltpu.VMEM((pairs, 128, 2 * QB), FL),
                pltpu.VMEM((pairs, 128, 2 * QB), FL),
            ],
        ),
        out_shape=[
            jax.ShapeDtypeStruct((own, width), BF),
            jax.ShapeDtypeStruct((own, width), FL),
            jax.ShapeDtypeStruct((16, own), FL),
        ],
        compiler_params=params(),
    )(spans, slopes, q, k, vt, bounds)


def pieces(x):
    out = []
    for _ in range(3):
        y = x.astype(BF).astype(FL)
        out.append(y)
        x = x - y
    return out


def key_lines(side, kind):
    lane = lax.broadcasted_iota(jnp.int32, (KC, 128), 1)
    key = lax.broadcasted_iota(jnp.int32, (KC, 128), 0).astype(FL)
    x = jnp.where(lane < 3, 1.0, jnp.where(lane < 6, -side, jnp.where(lane < 9, side * key, 0.0)))
    return jnp.where(lane == kind, 1.0, x) if kind else x


def chunk_lines(base, away, side, limit):
    lane = lax.broadcasted_iota(jnp.int32, (KC, 128), 1)
    key = lax.broadcasted_iota(jnp.int32, (KC, 128), 0).astype(FL) + KC * away
    other = jnp.where(side * key < side * limit, 1.0, 0.0)
    x = base + jnp.where((lane >= 9) & (lane < 12), side * KC * away, 0.0)
    return jnp.where(lane == 12, other, x).astype(BF)


def value_lines():
    lane = lax.broadcasted_iota(jnp.int32, (KC, 128), 1)
    return (lane < 3).astype(FL).astype(BF)


def query_rows(lse, slope, spots, out_left, out_right):
    one = jnp.ones_like(lse)
    rows = pieces(-lse) + pieces(slope * spots) + pieces(slope * one) * 2
    rows += [-FAR * one, -FAR * out_left, -FAR * out_right, 0.0 * one]
    return jnp.concatenate(rows, 0).astype(BF)


def two_heads_t(x):
    line = lax.broadcasted_iota(jnp.int32, x.shape, 0)
    zero = jnp.zeros_like(x)
    return jnp.concatenate([jnp.where(line < HD, x, zero), jnp.where(line < HD, zero, x)], 1)


def block_setup(bounds, row):
    low = bounds[0:1, pl.ds(row, QB)]
    high = bounds[1:2, pl.ds(row, QB)]
    first = low[:, 0:1]
    last = high[:, QB - 1 : QB]
    base = (2 * row).astype(FL) if hasattr(row, "astype") else float(2 * row)
    out_left = jnp.where(low == first, 0.0, 1.0)
    out_right = jnp.where(high == last, 0.0, 1.0)
    spots = 2.0 * lax.broadcasted_iota(jnp.int32, (1, QB), 1).astype(FL) + 0.5
    return low - base, high - base, first - base, last - base - 0.5, twice(out_left), twice(out_right), twice(spots)


def twice(x):
    return jnp.concatenate([x, x], 1)


def fill_queries(j, q, da, lse, delta, slope, setup, q2, da2, qt, dat):
    out_left, out_right, spots = setup[4:]
    q2[j] = two_heads(q)
    da2[j] = two_heads(da)
    qt[j, 0:128] = two_heads_t(q.T)
    dat[j, 0:128] = two_heads_t(da.T)
    qt[j, 128:144] = query_rows(lse, slope, spots, out_left, out_right)
    rows = pieces(-delta) + [jnp.zeros((13, 2 * QB), FL)]
    dat[j, 128:144] = jnp.concatenate(rows, 0).astype(BF)


def own_kernel(
    spans, slopes, q, k, v, kt, da, stats, bounds, dq_out, dk, dv, slope_out, q2, da2, qt, dat, dq2, sl, base
):
    pairs = q.shape[1] // 128
    head0 = pl.program_id(0) * 2 * pairs
    total_blocks = bounds.shape[1] // QB
    quarter = k.shape[0] // KC // 4
    first = total_blocks // 4
    slope = [slope_line(slopes, head0 + 2 * j) for j in range(pairs)]
    dk[...] = jnp.zeros(dk.shape, FL)
    dv[...] = jnp.zeros(dv.shape, FL)
    sl[...] = jnp.zeros(sl.shape, FL)
    @pl.when(pl.program_id(0) == 0)
    def _():
        qt[...] = jnp.zeros(qt.shape, BF)
        dat[...] = jnp.zeros(dat.shape, BF)
        base[0] = key_lines(1.0, 13)
        base[1] = key_lines(-1.0, 14)

    line = lax.broadcasted_iota(jnp.int32, (16, KC), 0)
    spot = lax.broadcasted_iota(jnp.int32, (16, KC), 1).astype(FL)
    extra = jnp.where(line == 0, 1.0, jnp.where(line == 1, spot, 0.0)).astype(BF)
    own_lines = key_lines(1.0, 0).astype(BF)
    ones = value_lines()

    def query_block(b, _):
        block = first + b
        row = pl.multiple_of(block * QB, QB)
        rows = pl.ds(pl.multiple_of(b * QB, QB), QB)
        c0 = spans[block]
        c1 = spans[total_blocks + block]
        setup = block_setup(bounds, row)
        low, high, limit_left, limit_right = setup[:4]
        spots = setup[6]
        for j in range(pairs):
            cols = slice(128 * j, 128 * j + 128)
            h = 2 * j
            lse = jnp.concatenate([stats[h : h + 1, rows], stats[h + 1 : h + 2, rows]], 1)
            delta = jnp.concatenate([stats[8 + h : 9 + h, rows], stats[9 + h : 10 + h, rows]], 1)
            fill_queries(j, q[rows, cols], da[rows, cols], lse, delta, slope[j], setup, q2, da2, qt, dat)
        dq2[...] = jnp.zeros(dq2.shape, FL)

        def step(c, lines, side, away, grads, wide):
            keys = pl.ds(pl.multiple_of(c * KC, KC), KC)
            col = [slice(128 * j, 128 * j + 128) for j in range(pairs)]
            s = [dot(jnp.concatenate([k[keys, col[j]], lines], 1), qt[j]) for j in range(pairs)]
            dp = [dot(jnp.concatenate([v[keys, col[j]], ones], 1), dat[j]) for j in range(pairs)]
            if wide is not None:
                s = [s[j] - slope[j] * wide for j in range(pairs)]
            p = [jnp.exp(x) for x in s]
            ds = [(p[j] * dp[j]).astype(BF) for j in range(pairs)]
            if grads:
                mine = pl.ds(pl.multiple_of((c - quarter) * KC, KC), KC)
                new_v = [dot(p[j].astype(BF), da2[j]) for j in range(pairs)]
                new_k = [dot(ds[j], q2[j]) for j in range(pairs)]
            r = [dot(jnp.concatenate([kt[c, col[j]], extra], 0), ds[j]) for j in range(pairs)]
            for j in range(pairs):
                if grads:
                    dv[mine, col[j]] = dv[mine, col[j]] + new_v[j]
                    dk[mine, col[j]] = dk[mine, col[j]] + new_k[j]
                dq2[j] = dq2[j] + r[j][0:128]
                part = side * ((spots - KC * away) * r[j][128:129] - r[j][129:130])
                if wide is not None:
                    part = part + jnp.sum(ds[j].astype(FL) * wide, 0, keepdims=True)
                sl[j] = sl[j] + part

        key = lax.broadcasted_iota(jnp.int32, (KC, QB), 0).astype(FL)
        over = 2.0 * jnp.maximum(key - spots[:, :QB], 0.0)
        wide = twice(jnp.where((key >= low) & (key < high), over, FAR))
        step(block, own_lines, 1.0, 0.0, True, wide)

        def other(c, grads):
            before = c < block
            side = jnp.where(before, 1.0, -1.0)
            away = (c - block).astype(FL)
            limit = jnp.where(before, limit_left, limit_right)
            step(c, chunk_lines(base[jnp.where(before, 0, 1)], away, side, limit), side, away, grads, None)

        def inside(i, _):
            other(jnp.where(i < block, i, i + 1), True)
            return 0

        left = jnp.maximum(jnp.minimum(c1, quarter) - c0, 0)
        right0 = jnp.maximum(c0, 3 * quarter)

        def outside(i, _):
            other(jnp.where(i < left, c0 + i, right0 + i - left), False)
            return 0

        lax.fori_loop(jnp.maximum(c0, quarter), jnp.minimum(c1, 3 * quarter) - 1, inside, 0)
        lax.fori_loop(0, left + jnp.maximum(c1 - right0, 0), outside, 0)
        for j in range(pairs):
            dq_out[rows, 128 * j : 128 * j + 128] = (one_block(dq2[j]) * HD**-0.5).astype(BF)
        return 0

    lax.fori_loop(0, da.shape[0] // QB, query_block, 0)
    slope_out[...] = jnp.zeros(slope_out.shape, FL)
    for j in range(pairs):
        slope_out[8 * j : 8 * j + 1] = sl[j]


def attend_own(spans, slopes, q, k, v, kt, da, stats, bounds):
    own, width = q.shape
    wide = width // 2
    pairs = wide // 128
    keys = k.shape[0]
    chunks = keys // KC
    col = lambda i, *_: (0, i)
    zero = lambda i, *_: (0, 0)
    return pl.pallas_call(
        own_kernel,
        name="attend_own",
        cost_estimate=takes(30),
        grid_spec=pltpu.PrefetchScalarGridSpec(
            num_scalar_prefetch=2,
            grid=(2,),
            in_specs=[
                pl.BlockSpec((own, wide), col),
                pl.BlockSpec((keys, wide), col),
                pl.BlockSpec((keys, wide), col),
                pl.BlockSpec((chunks, wide, KC), lambda i, *_: (0, i, 0)),
                pl.BlockSpec((own, wide), col),
                pl.BlockSpec((16, own), lambda i, *_: (i, 0)),
                pl.BlockSpec(bounds.shape, zero),
            ],
            out_specs=[
                pl.BlockSpec((own, wide), col),
                pl.BlockSpec((keys // 2, wide), col),
                pl.BlockSpec((keys // 2, wide), col),
                pl.BlockSpec((8 * pairs, 2 * QB), lambda i, *_: (i, 0)),
            ],
            scratch_shapes=[
                pltpu.VMEM((pairs, 2 * QB, 128), BF),
                pltpu.VMEM((pairs, 2 * QB, 128), BF),
                pltpu.VMEM((pairs, 256, 2 * QB), BF),
                pltpu.VMEM((pairs, 256, 2 * QB), BF),
                pltpu.VMEM((pairs, 128, 2 * QB), FL),
                pltpu.VMEM((pairs, 1, 2 * QB), FL),
                pltpu.VMEM((2, KC, 128), FL),
            ],
        ),
        out_shape=[
            jax.ShapeDtypeStruct((own, width), BF),
            jax.ShapeDtypeStruct((keys // 2, width), FL),
            jax.ShapeDtypeStruct((keys // 2, width), FL),
            jax.ShapeDtypeStruct((16 * pairs, 2 * QB), FL),
        ],
        compiler_params=params(),
    )(spans, slopes, q, k, v, kt, da, stats, bounds)


def halo_kernel(
    spans,
    slopes,
    q,
    ka,
    kb,
    va,
    vb,
    low_pay,
    high_pay,
    low_stats,
    high_stats,
    bounds,
    dk0,
    dv0,
    dk_out,
    dv_out,
    q2,
    da2,
    qt,
    dat,
    st,
    k,
    v,
    dk,
    dv,
):
    half = pl.program_id(0)
    pairs = q.shape[2] // 128
    total_blocks = bounds.shape[1] // QB
    edge = ka.shape[0]
    first = edge // KC
    count = low_pay.shape[0] // QB
    dk[...] = dk0[...]
    dv[...] = dv0[...]
    for into, parts in ((k, (ka, kb)), (v, (va, vb))):
        into[0:edge] = parts[0][...]
        into[edge:] = parts[1][...]

    @pl.when(pl.program_id(0) == 0)
    def _():
        qt[...] = jnp.zeros(qt.shape, BF)
        dat[...] = jnp.zeros(dat.shape, BF)

    ones = value_lines()
    for side, pay in enumerate((low_stats, high_stats)):
        x = pay[...].astype(FL)
        x = (x + pltpu.roll(x, 96, 1) + pltpu.roll(x, 64, 1)).T
        st[side] = jnp.where(half == 0, x[0:16], x[16:32])

    def query_block(i, _):
        side = i // count
        nth = i - side * count
        block = jnp.where(side == 0, i, total_blocks - 2 * count + i)
        row = pl.multiple_of(block * QB, QB)
        rows = pl.ds(pl.multiple_of(nth * QB, QB), QB)
        c0 = spans[block]
        c1 = spans[total_blocks + block]

        @pl.when(c0 < c1)
        def _():
            setup = block_setup(bounds, row)
            limit = jnp.where(side == 0, setup[3], setup[2])
            sign = jnp.where(side == 0, -1.0, 1.0)
            base = jnp.where(side == 0, key_lines(-1.0, 14), key_lines(1.0, 13))
            for j in range(pairs):
                cols = slice(128 * j, 128 * j + 128)
                h = 2 * j
                lse = jnp.concatenate([st[side, h : h + 1, rows], st[side, h + 1 : h + 2, rows]], 1)
                delta = jnp.concatenate([st[side, h + 8 : h + 9, rows], st[side, h + 9 : h + 10, rows]], 1)
                d = jnp.where(side == 0, low_pay[rows, cols], high_pay[rows, cols])
                slope = slope_line(slopes, 2 * pairs * half + h)
                fill_queries(j, q[side, rows, cols], d, lse, delta, slope, setup, q2, da2, qt, dat)

            def step(c, _):
                mine = pl.ds(pl.multiple_of((c - first) * KC, KC), KC)
                lines = chunk_lines(base, (c - block).astype(FL), sign, limit)
                js = range(pairs)
                col = [slice(128 * j, 128 * j + 128) for j in js]
                p = [jnp.exp(dot(jnp.concatenate([k[mine, col[j]], lines], 1), qt[j])) for j in js]
                dp = [dot(jnp.concatenate([v[mine, col[j]], ones], 1), dat[j]) for j in js]
                new_v = [dot(p[j].astype(BF), da2[j]) for j in js]
                new_k = [dot((p[j] * dp[j]).astype(BF), q2[j]) for j in js]
                for j in js:
                    dv[mine, col[j]] = dv[mine, col[j]] + new_v[j]
                    dk[mine, col[j]] = dk[mine, col[j]] + new_k[j]
                return 0

            lax.fori_loop(c0, c1, step, 0)

        return 0

    lax.fori_loop(0, 2 * count, query_block, 0)
    dk_out[...] = dk[...].astype(BF)
    dv_out[...] = dv[...].astype(BF)


def attend_halo(spans, slopes, q, k, v, low_pay, high_pay, bounds, dk0, dv0):
    width = q.shape[2]
    wide = width // 2
    pairs = wide // 128
    keys = dk0.shape[0]
    rows = low_pay.shape[0]
    shape = jax.ShapeDtypeStruct((keys, width), BF)
    col = lambda i, *_: (0, i)
    parts = [pl.BlockSpec((keys // 2, wide), lambda i, *_: (1, i)), pl.BlockSpec((keys // 2, wide), lambda i, *_: (2, i))]
    tail = pl.BlockSpec((rows, 128), lambda i, *_: (0, width // 128))
    whole = pl.BlockSpec((keys, wide), col)
    pay = pl.BlockSpec((rows, wide), col)
    return pl.pallas_call(
        halo_kernel,
        name="attend_halo",
        cost_estimate=takes(12),
        grid_spec=pltpu.PrefetchScalarGridSpec(
            num_scalar_prefetch=2,
            grid=(2,),
            in_specs=[pl.BlockSpec((2, q.shape[1], wide), lambda i, *_: (0, 0, i))]
            + parts * 2
            + [pay, pay, tail, tail, pl.BlockSpec(bounds.shape, lambda i, *_: (0, 0)), whole, whole],
            out_specs=[whole, whole],
            scratch_shapes=[
                pltpu.VMEM((pairs, 2 * QB, 128), BF),
                pltpu.VMEM((pairs, 2 * QB, 128), BF),
                pltpu.VMEM((pairs, 256, 2 * QB), BF),
                pltpu.VMEM((pairs, 256, 2 * QB), BF),
                pltpu.VMEM((2, 16, rows), FL),
                pltpu.VMEM((keys, wide), BF),
                pltpu.VMEM((keys, wide), BF),
                pltpu.VMEM((keys, wide), FL),
                pltpu.VMEM((keys, wide), FL),
            ],
        ),
        out_shape=[shape, shape],
        compiler_params=params(),
    )(spans, slopes, q, k, k, v, v, low_pay, high_pay, low_pay, high_pay, bounds, dk0, dv0)


def normalize(z):
    centred = z - jnp.mean(z, -1, keepdims=True)
    scale = lax.rsqrt(jnp.mean(centred * centred, -1, keepdims=True) + EPS)
    return centred * scale, scale


def normalize_back(d, unit, scale):
    return scale * (d - jnp.mean(d, -1, keepdims=True) - unit * jnp.mean(d * unit, -1, keepdims=True))


def rows_sum(x):
    return jnp.sum(x, 0, keepdims=True)


def middle_kernel(
    ids,
    pool_in,
    att,
    exact_in,
    lse,
    cot_in,
    vec,
    upb,
    low,
    high,
    olow,
    ohigh,
    out,
    pay,
    pay_low,
    pay_high,
    stats,
    mixed,
    gvec,
    gup,
    keep,
    send,
    wo,
    w1,
    w2,
    active,
    slope,
    unit1,
    hid,
    hid_low,
    z,
    d2,
    dw1,
    dw2,
    dwo,
    pool,
    exact,
    cot,
    sems,
    load_sems,
):
    n, width = att.shape
    loads = [(pool_in, pool), (cot_in, cot), (exact_in, exact)]
    loads = [pltpu.make_async_copy(a, b, load_sems.at[i]) for i, (a, b) in enumerate(loads)]
    rb = width // NB
    fb = w2.shape[0] // NB
    parts = w1.shape[0]

    def rows(r, size):
        return pl.ds(pl.multiple_of(r, 16), size)

    def copies_a(block, s, p):
        pltpu.make_async_copy(block.at[pl.ds(192, 32)], wo.at[rows(s * rb, 32)], sems.at[0]).start()
        pltpu.make_async_copy(block.at[pl.ds(0, 192)], w2.at[rows(s * fb, 192)], sems.at[2]).start()

    def copies_b(block, s, p):
        pltpu.make_async_copy(block.at[pl.ds(192, 16)], wo.at[rows(s * rb + 32, 16)], sems.at[0]).start()
        for c in range(parts):
            pltpu.make_async_copy(block.at[pl.ds(48 * c, 48)], w1.at[c, rows(s * rb, 48)], sems.at[1]).start()

    load_sets(ids, low, high, olow, ohigh, copies_a, copies_b)
    for x in loads:
        x.start()
    wait_all(wo, sems.at[0])
    z[...] = dot(att[...], wo[...])
    loads[0].wait()
    rc = 128

    def row_loop(f):
        def body(i, _):
            f(pl.ds(pl.multiple_of(i * rc, rc), rc), i)
            return 0

        lax.fori_loop(0, n // rc, body, 0)

    def first_norm(r, i):
        unit, scale = normalize(pool[r, :] + z[r, :] + vec[2:3])
        h = unit * vec[3:4] + vec[4:5]
        unit1[r, :] = unit
        d2[r, 0:128] = jnp.broadcast_to(scale, (rc, 128))
        hid[r, :] = h
        hid_low[r, :] = h.astype(BF)

    row_loop(first_norm)
    wait_all(w1, sems.at[1])
    wait_all(w2, sems.at[2])
    c0 = 0.7978845608028654

    def up(c, _):
        before = jnp.maximum(c - 1, 0)
        z[...] = z[...] + dot(active[before], w2[pl.ds(pl.multiple_of(before * width, 128), width), :])
        inner = dot(hid_low[...], w1[c]) + upb[pl.ds(0, 1), pl.ds(pl.multiple_of(c * width, 128), width)]
        sq = inner * inner
        t = jnp.tanh(inner * (c0 + (0.044715 * c0) * sq))
        cdf = 0.5 + 0.5 * t
        active[c] = (inner * cdf).astype(BF)
        slope[c] = cdf + (inner * (1.0 - t * t)) * (0.5 * c0 + (1.5 * 0.044715 * c0) * sq)
        return 0

    active[0] = jnp.zeros((n, width), BF)
    z[...] = jnp.zeros(z.shape, FL)
    lax.fori_loop(0, parts, up, 0)
    z[...] = z[...] + dot(active[parts - 1], w2[pl.ds((parts - 1) * width, width), :])
    gvec[...] = jnp.zeros(gvec.shape, FL)
    loads[1].wait()

    def second_norm(r, i):
        unit, scale = normalize(hid[r, :] + (z[r, :] + vec[5:6]))
        out[r, :] = (unit * vec[6:7] + vec[7:8]).astype(BF)
        dy = cot[r, :].astype(FL)
        gvec[6:7] = gvec[6:7] + rows_sum(dy * unit)
        gvec[7:8] = gvec[7:8] + rows_sum(dy)
        d = normalize_back(dy * vec[6:7], unit, scale)
        hid[r, :] = d
        d_low = d.astype(BF)
        att_like[r, :] = d_low
        gvec[5:6] = gvec[5:6] + rows_sum(d_low.astype(FL))

    att_like = pay.at[:, 0:width]
    scale1 = d2[:, 0:1]
    row_loop(second_norm)
    z[...] = jnp.zeros(z.shape, FL)

    def down(c, _):
        ffn = pay[:, 0:width]
        far = pl.ds(pl.multiple_of(c * width, 128), width)
        d_inner = (dot_t(ffn, w2[far, :]) * slope[c]).astype(BF)
        gup[:, far] = jnp.broadcast_to(rows_sum(d_inner.astype(FL)), (8, width))
        dw2[far, :] = t_dot(active[c], ffn).astype(BF)
        dw1[c] = t_dot(hid_low[...], d_inner).astype(BF)
        z[...] = z[...] + dot_t(d_inner, w1[c])
        return 0

    lax.fori_loop(0, parts, down, 0)

    def store_sets(a_ref, b_ref):
        for p in range(NB):
            s = ids[0] ^ rel_a(p)
            pltpu.make_async_copy(dw2.at[rows(s * fb, 192)], a_ref.at[p, pl.ds(0, 192)], sems.at[3]).start()
            s = ids[0] ^ rel_b(p)
            for c in range(parts):
                pltpu.make_async_copy(
                    dw1.at[c, rows(s * rb, 48)], b_ref.at[p, pl.ds(48 * c, 48)], sems.at[3]
                ).start()

    @pl.when(ids[1] == 0)
    def _():
        store_sets(keep, send)

    @pl.when(ids[1] != 0)
    def _():
        store_sets(send, keep)

    def first_back(r, i):
        unit = unit1[r, :]
        d = hid[r, :] + z[r, :]
        gvec[3:4] = gvec[3:4] + rows_sum(d * unit)
        gvec[4:5] = gvec[4:5] + rows_sum(d)
        d = normalize_back(d * vec[3:4], unit, d2[r, 0:1])
        mixed[r, :] = d
        d_low = d.astype(BF)
        hid_low[r, :] = d_low
        gvec[2:3] = gvec[2:3] + rows_sum(d_low.astype(FL))

    row_loop(first_back)
    dwo[...] = t_dot(att[...], hid_low[...]).astype(BF)

    def store_wo(a_ref, b_ref):
        for p in range(NB):
            s = ids[0] ^ rel_a(p)
            pltpu.make_async_copy(dwo.at[rows(s * rb, 32)], a_ref.at[p, pl.ds(192, 32)], sems.at[3]).start()
            s = ids[0] ^ rel_b(p)
            pltpu.make_async_copy(dwo.at[rows(s * rb + 32, 16)], b_ref.at[p, pl.ds(192, 16)], sems.at[3]).start()
            pltpu.make_async_copy(dwo.at[rows(s * rb + 32, 16)], b_ref.at[p, pl.ds(208, 16)], sems.at[3]).start()

    @pl.when(ids[1] == 0)
    def _():
        store_wo(keep, send)

    @pl.when(ids[1] != 0)
    def _():
        store_wo(send, keep)

    z[...] = dot_t(hid_low[...], wo[...])
    heads = width // HD
    head_of = lax.broadcasted_iota(jnp.int32, (16, width), 1) // HD
    head_of = jnp.where(head_of < heads // 2, head_of, head_of - heads // 2 + 8)
    pick = (head_of == lax.broadcasted_iota(jnp.int32, (16, width), 0)).astype(FL).astype(BF)
    stats[0:8, :] = lse[0:8, :]
    stats[16:24, :] = lse[8:16, :]

    loads[2].wait()

    def last(r, i):
        d_low = z[r, :].astype(BF)
        pay[r, 0:width] = d_low
        prod = d_low.astype(FL) * exact[r, :]
        delta = jnp.zeros((16, rc), FL)
        for _ in range(3):
            piece = prod.astype(BF)
            delta = delta + dot_t(pick, piece)
            prod = prod - piece.astype(FL)
        stats[8:16, r] = delta[0:8]
        stats[24:32, r] = delta[8:16]

    row_loop(last)
    st = stats[...].T
    pieces = []
    for _ in range(3):
        piece = st.astype(BF).astype(FL)
        pieces.append(piece)
        st = st - piece
    pieces.append(jnp.zeros_like(st))
    pay_low[:, width:] = jnp.concatenate(pieces, 1)[: n // 2].astype(BF)
    pay_high[:, width:] = jnp.concatenate(pieces, 1)[n // 2 :].astype(BF)
    pay_low[:, 0:width] = pay[0 : n // 2, :]
    pay_high[:, 0:width] = pay[n // 2 :, :]
    wait_all(keep, sems.at[3])
    wait_all(send, sems.at[3])


def middle(ids, pool, att, exact, lse, cot, vec, upb, sets, set_rows):
    n, width = pool.shape
    ff = upb.shape[1]
    parts = ff // width
    whole = lambda i, *_: (0, 0)
    full = lambda x: pl.BlockSpec(x.shape, whole)
    shapes = [
        jax.ShapeDtypeStruct((n, width), BF),
        jax.ShapeDtypeStruct((n, width), BF),
        jax.ShapeDtypeStruct((n // 2, width + 128), BF),
        jax.ShapeDtypeStruct((n // 2, width + 128), BF),
        jax.ShapeDtypeStruct((32, n), FL),
        jax.ShapeDtypeStruct((n, width), FL),
        jax.ShapeDtypeStruct((8, width), FL),
        jax.ShapeDtypeStruct((8, ff), FL),
    ]
    big = jax.ShapeDtypeStruct((NB, set_rows, width), BF)
    return pl.pallas_call(
        middle_kernel,
        name="middle",
        cost_estimate=takes(36),
        grid_spec=pltpu.PrefetchScalarGridSpec(
            num_scalar_prefetch=1,
            grid=(1,),
            in_specs=[ANY, full(att), ANY, full(lse), ANY, full(vec), full(upb)]
            + [ANY] * 4,
            out_specs=[full(x) for x in shapes] + [ANY, ANY],
            scratch_shapes=[
                pltpu.VMEM((width, width), BF),
                pltpu.VMEM((parts, width, width), BF),
                pltpu.VMEM((ff, width), BF),
                pltpu.VMEM((parts, n, width), BF),
                pltpu.VMEM((parts, n, width), FL),
                pltpu.VMEM((n, width), FL),
                pltpu.VMEM((n, width), FL),
                pltpu.VMEM((n, width), BF),
                pltpu.VMEM((n, width), FL),
                pltpu.VMEM((n, 128), FL),
                pltpu.VMEM((parts, width, width), BF),
                pltpu.VMEM((ff, width), BF),
                pltpu.VMEM((width, width), BF),
                pltpu.VMEM(pool.shape, FL),
                pltpu.VMEM(exact.shape, FL),
                pltpu.VMEM(cot.shape, BF),
                pltpu.SemaphoreType.DMA((4,)),
                pltpu.SemaphoreType.DMA((3,)),
            ],
        ),
        out_shape=shapes + [big, big],
        compiler_params=params(),
    )(ids, pool, att, exact, lse, cot, vec, upb, *sets)


def weights_kernel(
    ids,
    pool_in,
    tok_in,
    dq_in,
    dk_in,
    dv_in,
    gvec,
    gup,
    sl,
    keep_low,
    keep_up,
    send_low,
    send_up,
    dwq,
    dwk,
    dwv,
    bias,
    tt,
    pool,
    tok,
    dq,
    dk,
    dv,
    sems,
    load_sems,
):
    loads = [(tok_in, tok), (pool_in, pool), (dq_in, dq), (dk_in, dk), (dv_in, dv)]
    loads = [pltpu.make_async_copy(a, b, load_sems.at[i]) for i, (a, b) in enumerate(loads)]
    for x in loads:
        x.start()
    keep = (keep_low, keep_up)
    send = (send_low, send_up)
    width = tok.shape[1]
    ff = gup.shape[1]
    rb = width // NB
    for x in loads[:3]:
        x.wait()
    tt[...] = tok[...].T
    dwq[...] = t_dot(pool[...].astype(BF), dq[...]).astype(BF)

    for x in loads[3:]:
        x.wait()

    def columns(c, _):
        cols = pl.ds(pl.multiple_of(c * 256, 256), 256)
        dwk[:, cols] = dot(tt[...], dk[:, cols]).astype(BF)
        dwv[:, cols] = dot(tt[...], dv[:, cols]).astype(BF)
        return 0

    lax.fori_loop(0, width // 256, columns, 0)

    def rows(r, size):
        return pl.ds(pl.multiple_of(r, 16), size)

    def go(src, dst):
        pltpu.make_async_copy(src, dst, sems.at[0]).start()

    def store_sets(a_ref, b_ref):
        for p in range(NB):
            s = ids[0] ^ rel_a(p)
            go(dwq.at[rows(s * rb, 48)], a_ref[p // 8].at[p % 8, pl.ds(0, 48)])
            go(dwk.at[rows(s * rb, 32)], a_ref[p // 8].at[p % 8, pl.ds(48, 32)])
            s = ids[0] ^ rel_b(p)
            go(dwk.at[rows(s * rb + 32, 16)], b_ref[p // 8].at[p % 8, pl.ds(0, 16)])
            go(dwv.at[rows(s * rb, 48)], b_ref[p // 8].at[p % 8, pl.ds(16, 48)])

    @pl.when(ids[1] == 0)
    def _():
        store_sets(keep, send)

    @pl.when(ids[1] != 0)
    def _():
        store_sets(send, keep)

    row = lax.broadcasted_iota(jnp.int32, (16, width), 0)
    g = jnp.concatenate([gvec[...], jnp.zeros((8, width), FL)], 0)
    g = jnp.where(row == 0, rows_sum(dq[...].astype(FL)), g)
    g = jnp.where(row == 1, rows_sum(dv[...].astype(FL)), g)
    block_of = div_rb(lax.broadcasted_iota(jnp.int32, (16, width), 1))
    parts = []
    for p in range(NB):
        parts.append(jnp.where(block_of == (ids[0] ^ rel_b(p)), g, 0.0).astype(BF))
    total = dot_t(jnp.concatenate(parts, 0), spread_matrix(128, width, rb))
    row = lax.broadcasted_iota(jnp.int32, (16, ff), 0)
    block_of = div_rb(lax.broadcasted_iota(jnp.int32, (16, ff), 1))
    block_of = jnp.where((row >= 8) & (row < 12), block_of - row + 8, -1)
    up = jnp.concatenate([gup[...], gup[...]], 0)
    parts = []
    for p in range(NB):
        parts.append(jnp.where(block_of == 4 * (ids[0] ^ rel_b(p)), up, 0.0).astype(BF))
    total = total + dot_t(jnp.concatenate(parts, 0), spread_matrix(128, ff, rb))
    line = jnp.zeros((1, 128), FL)
    lane = lax.broadcasted_iota(jnp.int32, (1, 128), 1)
    for j in range(sl.shape[0] // 8):
        for i in range(2):
            value = jnp.sum(sl[8 * j : 8 * j + 1, QB * i : QB * i + QB], 1, keepdims=True)
            line = jnp.where(lane == 2 * j + i, -value, line)
    row = lax.broadcasted_iota(jnp.int32, (16 * NB, 128), 0)
    total = jnp.where((row & 15) == 12, line, total)
    bias[...] = jnp.zeros(bias.shape, BF)
    bias[:, 0:128] = total.astype(BF)

    def store_bias(b_ref):
        for p in range(NB):
            go(bias.at[pl.ds(16 * p, 16)], b_ref[p // 8].at[p % 8, pl.ds(64, 16)])

    @pl.when(ids[1] == 0)
    def _():
        store_bias(send)

    @pl.when(ids[1] != 0)
    def _():
        store_bias(keep)

    for x in keep + send:
        wait_all(x, sems.at[0])


def weight_grads(ids, pool, tok, dq, dk, dv, gvec, gup, sl, set_rows):
    width = tok.shape[1]
    full = lambda x: pl.BlockSpec(x.shape, lambda i, *_: (0, 0))
    big = jax.ShapeDtypeStruct((NB // 2, set_rows, width), BF)
    square = pltpu.VMEM((width, width), BF)
    return pl.pallas_call(
        weights_kernel,
        name="weight_grads",
        cost_estimate=takes(9),
        grid_spec=pltpu.PrefetchScalarGridSpec(
            num_scalar_prefetch=1,
            grid=(1,),
            in_specs=[ANY] * 5 + [full(x) for x in (gvec, gup, sl)],
            out_specs=[ANY] * 4,
            scratch_shapes=[
                square,
                square,
                square,
                pltpu.VMEM((16 * NB, width), BF),
                pltpu.VMEM((width, tok.shape[0]), BF),
            ]
            + [pltpu.VMEM(x.shape, x.dtype) for x in (pool, tok, dq, dk, dv)]
            + [
                pltpu.SemaphoreType.DMA((1,)),
                pltpu.SemaphoreType.DMA((5,)),
            ],
        ),
        out_shape=[big] * 4,
        compiler_params=params(),
    )(ids, pool, tok, dq, dk, dv, gvec, gup, sl)


def tokens_kernel(mixed, dq, dk, dv, wq, wk, wv, out, acc):
    half = mixed.shape[0]
    up = 0.5 * (mixed[...] + dot_t(dq[...], wq[...]))
    down = dot_t(dk[...], wk[...]) + dot_t(dv[...], wv[...])
    for j in range(mixed.shape[1] // 128):
        cols = slice(128 * j, 128 * j + 128)
        for i in range(2):
            acc[j, pl.ds(i, half, stride=2)] = up[:, cols]
        out[:, cols] = acc[j] + down[:, cols]


def token_grads(mixed, dq, dk, dv, wq, wk, wv):
    rows, width = dk.shape
    step = 512
    half = pl.BlockSpec((step // 2, width), lambda i: (i, 0))
    block = pl.BlockSpec((step, width), lambda i: (i, 0))
    whole = pl.BlockSpec((width, width), lambda i: (0, 0))
    return pl.pallas_call(
        tokens_kernel,
        name="token_grads",
        cost_estimate=takes(8),
        grid=(rows // step,),
        in_specs=[half, half, block, block, whole, whole, whole],
        out_specs=block,
        out_shape=jax.ShapeDtypeStruct((rows, width), FL),
        scratch_shapes=[pltpu.VMEM((width // 128, step, 128), FL)],
        compiler_params=params(),
    )(mixed, dq, dk, dv, wq, wk, wv)


def blocks_of(x):
    return x.reshape(NB, x.shape[0] // NB, x.shape[1])


def column_parts(x, width):
    return jnp.concatenate([x[..., width * c : width * c + width] for c in range(x.shape[-1] // width)], -2)


def bias_block(small, up, width):
    rb = small[0].shape[-1]
    rows = jnp.stack(list(small) + [up[..., rb * c : rb * c + rb] for c in range(4)], -2)
    pad = [(0, 0)] * (rows.ndim - 2) + [(0, 4), (0, width - rb)]
    return jnp.pad(rows, pad)


def pack(wq, wk, wv, wo, w1, w2, bias, width):
    a1 = jnp.concatenate([wq, wk[..., :32, :]], -2)
    b1 = jnp.concatenate([wk[..., 32:, :], wv, bias], -2)
    a2 = jnp.concatenate([w2, wo[..., :32, :]], -2)
    b2 = jnp.concatenate([column_parts(w1, width), wo[..., 32:, :], wo[..., 32:, :]], -2)
    return a1, b1, a2, b2


def unpack(a1, b1, a2, b2, width):
    wq = a1[..., :48, :]
    wk = jnp.concatenate([a1[..., 48:, :], b1[..., :16, :]], -2)
    wv = b1[..., 16:64, :]
    bias = b1[..., 64:, :]
    wo = jnp.concatenate([a2[..., 192:, :], b2[..., 192:208, :]], -2)
    w2 = a2[..., :192, :]
    parts = 4
    w1 = jnp.concatenate([b2[..., 48 * c : 48 * c + 48, :] for c in range(parts)], -1)
    return wq, wk, wv, wo, w1, w2, bias


def pack_kernel(ids, wq, wk, wv, wo, w1, w2, b_up, *refs):
    vectors, (out, bias) = refs[:8], refs[8:]
    first = out.at[:, 0:80]
    second = out.at[:, 80:304]
    rb, width = wq.shape

    @pl.when(ids[1] == 0)
    def _():
        first[0, 0:48] = wq[...].astype(BF)
        first[0, 48:80] = wk[0:32].astype(BF)
        second[0, 0:192] = w2[...].astype(BF)
        second[0, 192:224] = wo[0:32].astype(BF)

    @pl.when(ids[1] != 0)
    def _():
        bias[...] = jnp.zeros(bias.shape, FL)
        for i, x in enumerate(vectors):
            bias[i : i + 1, 0:rb] = x[...]
        for c in range(4):
            bias[8 + c : 9 + c, 0:rb] = b_up[:, rb * c : rb * c + rb]
        first[0, 0:16] = wk[32:48].astype(BF)
        first[0, 16:64] = wv[...].astype(BF)
        first[0, 64:80] = bias[...].astype(BF)
        for c in range(4):
            second[0, 48 * c : 48 * c + 48] = w1[:, width * c : width * c + width].astype(BF)
        second[0, 192:208] = wo[32:48].astype(BF)
        second[0, 208:224] = wo[32:48].astype(BF)


def pack_own(ids, masters, b_up, vectors):
    width = masters[0].shape[1]
    args = list(masters) + [b_up[None]] + [x[None] for x in vectors]
    full = lambda x: pl.BlockSpec(x.shape, lambda i, *_: (0,) * len(x.shape))
    shape = jax.ShapeDtypeStruct((1, 304, width), BF)
    return pl.pallas_call(
        pack_kernel,
        name="pack",
        cost_estimate=takes(3),
        grid_spec=pltpu.PrefetchScalarGridSpec(
            num_scalar_prefetch=1,
            grid=(1,),
            in_specs=[full(x) for x in args],
            out_specs=full(shape),
            scratch_shapes=[pltpu.VMEM((16, width), FL)],
        ),
        out_shape=shape,
        compiler_params=params(),
    )(ids, *args)


def unpack_kernel(ids, low1, got1, olow1, ogot1, wq, wk, wv, *vectors):
    rb = wq.shape[0]
    mine = low1[...] + got1[...].astype(FL)
    other = olow1[...] + ogot1[...].astype(FL)

    def store(a, b):
        wq[...] = a[0:48]
        wk[0:32] = a[48:80]
        wk[32:48] = b[0:16]
        wv[...] = b[16:64]
        for i in range(8):
            vectors[i][...] = b[64 + i : 65 + i, 0:rb]
        for c in range(4):
            vectors[8][:, rb * c : rb * c + rb] = b[72 + c : 73 + c, 0:rb]
        vectors[9][...] = b[76:77, 0 : vectors[9].shape[1]]

    @pl.when(ids[1] == 0)
    def _():
        store(mine, other)

    @pl.when(ids[1] != 0)
    def _():
        store(other, mine)


def unpack_wide_kernel(ids, mine, other, wo, w1, w2):
    width = wo.shape[1]

    def store(a, b):
        for c in range(4):
            w1[:, width * c : width * c + width] = b[48 * c : 48 * c + 48]
        w2[...] = a[0:192]
        wo[0:32] = a[192:224]
        wo[32:48] = b[192:208]

    @pl.when(ids[1] == 0)
    def _():
        store(mine, other)

    @pl.when(ids[1] != 0)
    def _():
        store(other, mine)


def unpack_call(kernel, name, ids, args, dims):
    shapes = [jax.ShapeDtypeStruct(d, FL) for d in dims]
    full = lambda x: pl.BlockSpec(x.shape, lambda i, *_: (0, 0))
    return pl.pallas_call(
        kernel,
        name=name,
        cost_estimate=takes(2),
        grid_spec=pltpu.PrefetchScalarGridSpec(
            num_scalar_prefetch=1,
            grid=(1,),
            in_specs=[full(x) for x in args],
            out_specs=[full(x) for x in shapes],
        ),
        out_shape=shapes,
        compiler_params=params(),
    )(ids, *args)


def after(x, *done):
    return lax.optimization_barrier((x,) + done)[0]


def local(
    tokens,
    cotangent,
    lengths,
    w_query,
    b_query,
    w_key,
    w_value,
    b_value,
    w_output,
    b_output,
    gain_attn,
    shift_attn,
    w_up,
    b_up,
    w_down,
    b_down,
    gain_ffn,
    shift_ffn,
    distance_slope,
):
    rows_here, width = tokens.shape
    ff = w_up.shape[1]
    own = rows_here // 2
    halo = rows_here // 2
    seq = lax.axis_size("seq")
    devices = seq * lax.axis_size("dp")
    direct = seq == NB
    order = ("dp", "seq")
    up_pairs = [(i, i + 1) for i in range(devices - 1)]
    down_pairs = [(i + 1, i) for i in range(devices - 1)]

    masters = (w_query, w_key, w_value, w_output, w_up, w_down)
    vectors = (b_query, b_value, b_output, gain_attn, shift_attn, b_down, gain_ffn, shift_ffn)
    if direct:
        core = lax.axis_index("dp")
        ids = jnp.stack([lax.axis_index("seq"), core]).astype(jnp.int32)
        x = pack_own(ids, masters, b_up, vectors)
        y = x[:, 80:]
        x = x[:, :80]
        x = jnp.concatenate([x, exchange(x, 8, 4)], 0)
        x1, low_a = lax.optimization_barrier(
            (exchange(x, 4, 8), lax.ppermute(tokens[rows_here - halo : rows_here - halo // 2], order, up_pairs))
        )
        x = jnp.concatenate([x, x1], 0)
        y, part = lax.optimization_barrier((y, tokens[rows_here - halo // 2 :], x1))[:2]
        x1, y1, low_b = lax.optimization_barrier(
            (exchange(x, 2, 1), exchange(y, 8, 4), lax.ppermute(part, order, up_pairs))
        )
        low1 = jnp.concatenate([x, x1], 0)
        y = jnp.concatenate([y, y1], 0)
        high1, olow1, y1, high_a = lax.optimization_barrier(
            (
                exchange(low1, 1, 2),
                swap_core(low1),
                exchange(y, 4, 8),
                lax.ppermute(after(tokens[: halo // 2], x1), order, down_pairs),
            )
        )
        y = jnp.concatenate([y, y1], 0)
        sets1 = (low1, high1, olow1, swap_core(high1))
        y1 = exchange(y, 2, 1)
        high_b = lax.ppermute(after(tokens[halo // 2 : halo], high1), order, down_pairs)
    else:
        ids = jnp.zeros((2,), jnp.int32)
        gather = lambda x: lax.all_gather(x.astype(BF), "seq", axis=0, tiled=True)
        full = [blocks_of(gather(x)) for x in masters]
        small = [gather(x).reshape(NB, -1) for x in vectors]
        bias = bias_block(small, gather(b_up).reshape(NB, -1), width)
        a1, b1, a2, b2 = pack(*full, bias, width)
        at_a = jnp.array([rel_a(p) for p in range(NB)])
        at_b = jnp.array([rel_b(p) for p in range(NB)])
        sets1 = (a1[at_a[:8]], a1[at_a[8:]], b1[at_b[:8]], b1[at_b[8:]])
        sets2 = (a2[at_a[:8]], a2[at_a[8:]], b2[at_b[:8]], b2[at_b[8:]])
        low_a = lax.ppermute(tokens[rows_here - halo : rows_here - halo // 2], order, up_pairs)
        low_b = lax.ppermute(tokens[rows_here - halo // 2 :], order, up_pairs)
        high_a = lax.ppermute(tokens[: halo // 2], order, down_pairs)
        high_b = lax.ppermute(tokens[halo // 2 : halo], order, down_pairs)

    first_row = lax.axis_index(order) * rows_here
    total = devices * rows_here
    starts = 2 * (jnp.cumsum(lengths) - lengths)
    place = first_row - halo + 2 * jnp.arange(2 * own, dtype=jnp.int32)
    before = starts[None, :] <= place[:, None]
    begin = jnp.max(jnp.where(before, starts[None, :], 0), 1)
    end = jnp.min(jnp.where(before, total, starts[None, :]), 1)
    inside = (place >= 0) & (place < total)
    shift = first_row - halo
    begin = jnp.where(inside, begin - shift, 0)
    end = jnp.where(inside, end - shift, 0)
    bounds = jnp.pad(jnp.stack([begin, end], 0).astype(FL), ((0, 6), (0, 0)))
    blocks = 2 * own // QB
    chunks = (rows_here + 2 * halo) // KC
    low_chunk = jnp.min(jnp.where(inside, begin, 4 * total).reshape(blocks, QB), 1) // KC
    high_chunk = (jnp.max(end.reshape(blocks, QB), 1) + KC - 1) // KC
    index = jnp.arange(blocks)
    away = (index < blocks // 4) | (index >= blocks - blocks // 4)
    low_chunk = jnp.clip(low_chunk, jnp.where(away, chunks // 4, 0), chunks)
    high_chunk = jnp.clip(high_chunk, 0, jnp.where(away, chunks - chunks // 4, chunks))
    spans = jnp.concatenate([low_chunk, high_chunk]).astype(jnp.int32)

    slopes = distance_slope
    q, k, v, kt, vt, pool, wq, wk, wv, vec, upb = qkv(ids, tokens, sets1, ff)
    if direct:
        k, high_b = lax.optimization_barrier((k, high_b))
    qh, k, v, kt, vt = halo_qkv(low_a, low_b, high_a, high_b, wq, wk, wv, vec, k, v, kt, vt)
    if direct:
        y1, qh = lax.optimization_barrier((y1, qh))
        low2 = jnp.concatenate([y, y1], 0)
        bounds = after(bounds, low2)
    att, exact, lse = attend_forward(spans, slopes, q, k, vt, bounds)
    if direct:
        high2, lse = lax.optimization_barrier((exchange(low2, 1, 2), lse))
        sets2 = (low2, high2, swap_core(low2), swap_core(high2))
    out, pay, pay_low, pay_high, stats, mixed, gvec, gup, keep2, send2 = middle(
        ids, pool, att, exact, lse, cotangent, vec, upb, sets2, 224
    )
    low_pay = lax.ppermute(pay_high, order, up_pairs)
    high_pay = lax.ppermute(pay_low, order, down_pairs)
    if direct:
        got = swap_core(send2)
        up = add(keep2[8:], got[8:]).astype(BF)
        bounds = after(bounds, up)
    dq, dk, dv, sl = attend_own(spans, slopes, q, k, v, kt, pay, stats, bounds)
    if direct:
        dq, low_pay, high_pay = lax.optimization_barrier((dq, low_pay, high_pay))
    dk, dv = attend_halo(spans, slopes, qh, k, v, low_pay, high_pay, bounds, dk, dv)
    if direct:
        got1, dk = lax.optimization_barrier((exchange(up, 1, 2), dk))
        up = add(keep2[4:8], got[4:8], got1[4:]).astype(BF)
        sl = after(sl, up)
    keep1, keep1_up, send1, send1_up = weight_grads(ids, pool, tokens, dq, dk, dv, gvec, gup, sl, 80)
    if direct:
        gots = swap_core(send1)
        part, got2 = lax.optimization_barrier((add(keep1_up, swap_core(send1_up)).astype(BF), exchange(up, 2, 1)))
        low = add(keep2[:4], got[:4], got1[:4])
        up = (low[2:] + got2[2:].astype(FL)).astype(BF)
        low = low[:2] + got2[:2].astype(FL)
        mixed = after(mixed, part, up)
    grad_tokens = token_grads(mixed, dq, dk, dv, wq, wk, wv)

    if direct:
        got3, one, grad_tokens = lax.optimization_barrier((exchange(up, 4, 8), exchange(part, 1, 2), grad_tokens))
        part = add(keep1[4:8], gots[4:8], one[4:]).astype(BF)
        up = (low[1:] + got3[1:].astype(FL)).astype(BF)
        low = low[:1] + got3[:1].astype(FL)
        got4, two = lax.optimization_barrier((exchange(up, 8, 4), exchange(part, 2, 1)))
        mine = (low + got4.astype(FL))[0]
        rest = add(keep1[:4], gots[:4], one[:4])
        part = (rest[2:] + two[2:].astype(FL)).astype(BF)
        rest = rest[:2] + two[:2].astype(FL)
        three, other = lax.optimization_barrier((exchange(part, 4, 8), swap_core(mine)))
        second = (mine, other)
        part = (rest[1:] + three[1:].astype(FL)).astype(BF)
        rest = rest[:1] + three[:1].astype(FL)
        over = [(s, seq + (s ^ 8)) for s in range(seq)] + [(seq + s, s ^ 4) for s in range(seq)]
        first = (rest[0], exchange(part, 8, 4)[0], swap_core(rest)[0], lax.ppermute(part, order, over)[0])
        rb = width // NB
        go, g1, g2 = unpack_call(unpack_wide_kernel, "unpack_wide", ids, second, [(rb, width), (rb, ff), (ff // NB, width)])
        dims = [(rb, width)] * 3 + [(1, rb)] * 8 + [(1, ff // NB), (1, distance_slope.shape[0])]
        gq, gk, gv, *small = unpack_call(unpack_kernel, "unpack", ids, first, dims)
        g_up, g_slope = small[8][0], small[9][0]
        small = [x[0] for x in small[:8]]
    else:
        inv_a = [0] * NB
        inv_b = [0] * NB
        for p in range(NB):
            inv_a[rel_a(p)] = p
            inv_b[rel_b(p)] = p
        inv_a = jnp.array(inv_a)
        inv_b = jnp.array(inv_b)
        joined = [jnp.concatenate(x, 0) for x in ((keep1, keep1_up), (send1, send1_up))]
        gq, gk, gv, go, g1, g2, gb = unpack(joined[0][inv_a], joined[1][inv_b], keep2[inv_a], send2[inv_b], width)
        rb = width // NB

        def share(x):
            x = lax.psum(x.astype(FL), "dp")
            return lax.psum_scatter(x, "seq", scatter_dimension=0, tiled=True)

        gq, gk, gv, go, g1, g2 = [share(x.reshape(-1, x.shape[-1])) for x in (gq, gk, gv, go, g1, g2)]
        small = [share(gb[:, i, :rb].reshape(-1)) for i in range(8)]
        g_up = share(gb[:, 8:12, :rb].reshape(-1))
        g_slope = lax.psum(gb[0, 12, : distance_slope.shape[0]].astype(FL), order)
    return (
        out,
        grad_tokens,
        gq,
        small[0],
        gk,
        gv,
        small[1],
        go,
        small[2],
        small[3],
        small[4],
        g1,
        g_up,
        g2,
        small[5],
        small[6],
        small[7],
        g_slope,
    )


def solution(mesh):
    tall = P(("dp", "seq"), None)
    mat = P("seq", None)
    vec = P("seq")
    return jax.shard_map(
        local,
        mesh=mesh,
        in_specs=(tall, tall, P(), mat, vec, mat, mat, vec, mat, vec, vec, vec, mat, vec, mat, vec, vec, vec, P()),
        out_specs=(tall, tall, mat, vec, mat, mat, vec, mat, vec, vec, vec, mat, vec, mat, vec, vec, vec, P()),
        check_vma=False,
    )
```
